32 devices in a mesh: wide: 16 (over z, y, x), narrow: 2 (over core).
Axes of the slice: x: 2, y: 2, z: 4, core: 2. Of those that a mesh axis runs over, the one named last changes fastest.
Arguments:
- tokens: bfloat16 [4096, 768], P('wide'), may hold values from -6 to 6
- cotangent: bfloat16 [4096, 768], P('wide'), may hold values from -6 to 6
- time_table: bfloat16 [1000, 768], replicated, may hold values from -6 to 6
- timesteps: int32 [16], P('wide'), may hold values from 0 to 999
- routes: int32 [4096, 2], P('wide'), may hold values from 0 to 7, all different within a row; in each aligned block of 256 rows (0 to 255, 256 to 511, ...) at most 96 rows name the same one
- w_ada: bfloat16 [768, 6, 768], P('wide'), may hold values from -0.21875 to 0.21875
- w_qkv: bfloat16 [768, 3, 768], P('wide', None, 'narrow'), may hold values from -0.21875 to 0.21875
- w_proj: bfloat16 [768, 768], P('wide', 'narrow'), may hold values from -0.875 to 0.875
- w_route: bfloat16 [768, 8], P('wide'), may hold values from -0.21875 to 0.21875
- w_shared_up: bfloat16 [768, 3072], P('wide', 'narrow'), may hold values from -0.21875 to 0.21875
- w_shared_down: bfloat16 [768, 3072], P('wide', 'narrow'), may hold values from -0.109375 to 0.109375
- e_up: bfloat16 [6144, 3072], P('wide', 'narrow'), may hold values from -0.21875 to 0.21875
- e_down: bfloat16 [6144, 3072], P('wide', 'narrow'), may hold values from -0.109375 to 0.109375
Outputs:
- output: bfloat16 [4096, 768], P('wide')
- tokens_grad: float32 [4096, 768], P('wide')
- ada_grad: float32 [768, 6, 768], P('wide')
- qkv_grad: float32 [768, 3, 768], P('wide', None, 'narrow')
- proj_grad: float32 [768, 768], P('wide', 'narrow')
- route_grad: float32 [768, 8], P('wide')
- shared_up_grad: float32 [768, 3072], P('wide', 'narrow')
- shared_down_grad: float32 [768, 3072], P('wide', 'narrow')
- expert_up_grad: float32 [6144, 3072], P('wide', 'narrow')
- expert_down_grad: float32 [6144, 3072], P('wide', 'narrow')
The draws below stay inside these ranges and needn't reach their ends.
Inputs may be any that keep to these rules, and one draw needn't show every extreme that they name: `routes`: in each aligned block of 256 rows (the rows of one index of wide) no expert is named by more than 96 rows, a bound that some block reaches.
All inputs are finite; a program needn't handle non-finite values.
Results may differ from the reference program's by a relative error of at most 0.02.
Values may be sent and summed in bfloat16 or wider, within the bound.
A program may use at most 128 MiB of HBM per device.

```python
import math
import jax
import jax.numpy as jnp
import numpy as np
from jax import lax

D = 768
HEADS = 12
FF = 3072
PATCHES = 256
EXPERTS = 8
NSTEPS = 1000
HEAD_DIM = 64
TOK_DEV = 256
IMAGES = 16
TOKENS = 4096
CAP = 96
N_WIDE = 16


def with_ends(array, stream_key, least, high):
    shape = array.shape
    place = [jax.random.randint(jax.random.fold_in(stream_key, axis), (), 0, shape[axis]) for axis in range(len(shape))]
    array = array.at[tuple(place)].set(least)
    longest = shape.index(max(shape))
    place[longest] = (place[longest] + 1) % shape[longest]
    return array.at[tuple(place)].set(high)


def spiked(values, own_key, source, target, parts, factor):
    owner, partner = [(jnp.arange(values.shape[dim]) // (values.shape[dim] // parts)).reshape([-1 if axis == dim else 1 for axis in range(values.ndim)]) for dim in (source, target)]
    chosen = jax.random.permutation(own_key, parts)[partner]
    strong = (owner == chosen) | (owner == (partner + parts // 2) % parts)
    return jnp.where(strong, factor * values, values)


def block_scale(stream_key, shape, cuts, low, largest):
    def one(dim, parts):
        heights = jax.random.uniform(jax.random.fold_in(jax.random.fold_in(stream_key, 6), dim), (parts,), jnp.float32, low / len(cuts), largest / len(cuts))
        return jnp.repeat(jnp.exp(heights), shape[dim] // parts).reshape((-1,) + (1,) * (len(shape) - dim - 1))

    level = one(*cuts[0])
    for cut in cuts[1:]:
        level = level * one(*cut)
    return level


def rank_table(count, slope):
    weights = [(1 << 20) // math.isqrt(grade ** slope) + 1 for grade in range(1, count + 1)]
    width = 1 + sum(weights) // (1 << 30)
    return np.cumsum(np.array([max(1, weight // width) for weight in weights]))


def ranked_ids(stream_key, extent, amount, lean):
    listing = rank_table(amount, lean)
    ticket = jax.random.randint(jax.random.fold_in(stream_key, 1), extent, 0, int(listing[amount - 1]))
    grade = jnp.searchsorted(jnp.asarray(listing, jnp.int32), ticket, side="right")
    return jax.random.permutation(jax.random.fold_in(stream_key, 2), amount)[grade].astype(jnp.int32)


def assign_block(rng, own, number, rows, amount, top, limit, lean):
    sequence = jax.random.permutation(rng, amount)
    crowded, common = portions_of(amount, rows * top, limit, lean, True), portions_of(amount, rows * top, limit, lean, False)
    places = jnp.arange(amount)

    def named(tallies, rotation):
        used = int((tallies > 0).sum())
        fixed = max(1, used // 4)
        passed = fixed + (places - fixed + rotation * (used - fixed)) % max(1, amount - fixed)
        return jnp.zeros((amount,), jnp.int32).at[sequence[jnp.where(places < fixed, places, passed)]].set(jnp.asarray(tallies, jnp.int32))

    tallies = jnp.where(number % 4 == 0, named(crowded, number // 4), named(common, number - number // 4 - 1))
    mixed = jax.random.permutation(jax.random.fold_in(own, 3), amount)
    donor, receiver = mixed[0:amount // 2 * 2:2], mixed[1:amount // 2 * 2:2]
    room = jnp.minimum(tallies[donor] - 1, limit - tallies[receiver]) // 2
    room = jnp.where((donor == sequence[0]) | (receiver == sequence[0]) | (tallies[receiver] == 0), 0, jnp.maximum(room, 0))
    passed = jax.random.randint(jax.random.fold_in(own, 4), (amount // 2,), 0, 1 << 20) % (room + 1)
    tallies = tallies.at[donor].add(-passed).at[receiver].add(passed)
    labels = jnp.searchsorted(jnp.cumsum(tallies), jnp.arange(rows * top), side="right").astype(jnp.int32)
    grid = labels.reshape(top, rows).T
    grid = grid[jax.random.permutation(jax.random.fold_in(own, 1), rows)]
    rotation = jax.random.randint(jax.random.fold_in(own, 2), (rows, 1), 0, top)
    return jnp.take_along_axis(grid, (jnp.arange(top)[None, :] + rotation) % top, axis=1)


def portions_of(number_of, total, bound, slope, full):
    weights = [(1 << 20) // math.isqrt(standing ** slope) + 1 for standing in range(1, number_of + 1)]
    largest = bound if full else min(bound, max(-(-total // number_of), total * weights[0] // sum(weights)))
    least = 1 if total - largest >= number_of - 1 else 0
    holding, surplus = [largest] + [least] * (number_of - 1), total - largest - least * (number_of - 1)
    while surplus > 0:
        movable = [i for i in range(1, number_of) if holding[i] < largest] or [i for i in range(1, number_of) if holding[i] < bound]
        mass, remaining = sum([weights[i] for i in movable]), surplus
        for i in movable:
            more = min(bound - holding[i], max(1, remaining * weights[i] // mass), surplus)
            holding[i] = holding[i] + more
            surplus = surplus - more
    return np.array(holding)


def gaussian(stream_key, dims, deviation, reach, split=(), kind=jnp.bfloat16):
    result = jax.random.normal(stream_key, dims, jnp.float32) * deviation
    if len(split) > 0:
        result = block_scale(stream_key, dims, split, -0.22, 0.18) * result
    return jnp.clip(result, min=-reach, max=reach).astype(kind)


def gaussian_with(key, dims, scale, limit, split, heavy, kind=jnp.bfloat16):
    entries = scale * jax.random.normal(key, dims, jnp.float32)
    if split:
        entries = entries * block_scale(key, dims, split, -0.22, 0.18)
    return jnp.clip(spiked(entries, jax.random.fold_in(key, 3), *heavy), -limit, limit).astype(kind)


def setup_inputs(seed: int = 0) -> dict:
    key_list = jax.random.split(jax.random.key(seed), 14)
    tokens = gaussian(key_list[0], (TOKENS, D), 1.0, 6.0, ((0, 16),))
    cotangent = gaussian_with(key_list[1], (TOKENS, D), 1.0, 6.0, ((0, 16),), (0, 1, 16, 2.0))
    time_table = gaussian(key_list[2], (NSTEPS, D), 1.0, 6.0)
    timesteps = with_ends(ranked_ids(key_list[3], (IMAGES,), NSTEPS, 2), jax.random.fold_in(key_list[3], 3), 0, NSTEPS - 1).astype(jnp.int32)
    routes_keys = jax.random.split(jax.random.fold_in(key_list[4], 1), TOKENS // TOK_DEV)
    routes_turns = jax.random.permutation(jax.random.fold_in(key_list[4], 3), TOKENS // TOK_DEV)
    routes = jax.vmap(lambda own, number: assign_block(jax.random.fold_in(key_list[4], 2), own, number, TOK_DEV, EXPERTS, 2, CAP, 2))(routes_keys, routes_turns).reshape((TOKENS, 2))
    w_ada = gaussian(key_list[5], (D, 6, D), D ** -0.5, 0.21875, ((0, 16),))
    w_qkv = gaussian(key_list[6], (D, 3, D), D ** -0.5, 0.21875, ((0, 16), (2, 2)))
    w_proj = gaussian(key_list[7], (D, D), (D // 16) ** -0.5, 0.875, ((0, 16), (1, 2)))
    w_route = gaussian(key_list[8], (D, EXPERTS), D ** -0.5, 0.21875, ((0, 16),))
    w_shared_up = gaussian(key_list[9], (D, FF), D ** -0.5, 0.21875, ((0, 16), (1, 2)))
    w_shared_down = gaussian(key_list[10], (D, FF), FF ** -0.5, 0.109375, ((0, 16), (1, 2)))
    e_up = gaussian(key_list[11], (EXPERTS * D, FF), D ** -0.5, 0.21875, ((0, 16), (1, 2)))
    e_down = gaussian(key_list[12], (EXPERTS * D, FF), FF ** -0.5, 0.109375, ((0, 16), (1, 2)))
    return {"tokens": tokens, "cotangent": cotangent, "time_table": time_table, "timesteps": timesteps, "routes": routes, "w_ada": w_ada, "w_qkv": w_qkv, "w_proj": w_proj, "w_route": w_route, "w_shared_up": w_shared_up, "w_shared_down": w_shared_down, "e_up": e_up, "e_down": e_down}


epsilon = 1e-06
highest = lax.Precision.HIGHEST

@jax.custom_vjp
def low(v):
    return lax.optimization_barrier(v.astype(jnp.bfloat16)).astype(jnp.float32)

@jax.custom_vjp
def low_back(v):
    return v

def low_keep(v):
    return (low(v), None)

def low_pass(kept, grad):
    return (grad,)

def back_keep(v):
    return (v, None)

def back_low(kept, grad):
    return (low(grad),)
low.defvjp(low_keep, low_pass)
low_back.defvjp(back_keep, back_low)

def normalize(values):
    centre = lax.optimization_barrier(jnp.mean(values, axis=-1, keepdims=True))
    shifted = values - centre
    spread = lax.optimization_barrier(jnp.mean(shifted * shifted, axis=-1, keepdims=True))
    return shifted * lax.rsqrt(spread + epsilon)

def modulate(values, offset, factor):
    return normalize(values) * (1.0 + factor[:, None, :]) + offset[:, None, :]

def gelu_tanh(values):
    return jax.nn.gelu(values, approximate=True)

def slot_table(route_block, expert_count, capacity):
    flat_routes = route_block.reshape(-1)
    matches = (flat_routes[:, None] == jnp.arange(expert_count, dtype=jnp.int32)[None, :]).astype(jnp.int32)
    earlier = jnp.cumsum(matches, axis=0, dtype=jnp.int32) - matches
    ranking = lax.optimization_barrier(jnp.sum(earlier * matches, axis=1, dtype=jnp.int32))
    return flat_routes * capacity + ranking

def reference(tokens, cotangent, time_table, timesteps, routes, w_ada, w_qkv, w_proj, w_route, w_shared_up, w_shared_down, e_up, e_down):
    cond = time_table.astype(jnp.float32)[timesteps]
    cond_act = low(jax.nn.silu(cond))
    route_blocks = routes.reshape(N_WIDE, TOK_DEV, 2)
    slots = jax.vmap(lambda block_routes: slot_table(block_routes, EXPERTS, CAP))(route_blocks)
    block_ids = jnp.broadcast_to(jnp.arange(N_WIDE, dtype=jnp.int32)[:, None], slots.shape)
    choice_token = jnp.arange(TOKENS * 2, dtype=jnp.int32).reshape(N_WIDE, 2 * TOK_DEV) // 2
    source = jnp.zeros((N_WIDE, EXPERTS * CAP), jnp.int32).at[block_ids, slots].set(choice_token)
    filled = jnp.zeros((N_WIDE, EXPERTS * CAP), jnp.float32).at[block_ids, slots].set(1.0)
    source = source.reshape(N_WIDE, EXPERTS, CAP).transpose(1, 0, 2).reshape(EXPERTS, N_WIDE * CAP)
    filled = filled.reshape(N_WIDE, EXPERTS, CAP).transpose(1, 0, 2).reshape(EXPERTS, N_WIDE * CAP)
    position = (slots // CAP * (N_WIDE * CAP) + block_ids * CAP + slots % CAP).reshape(TOKENS * 2)
    attn_group = math.gcd(IMAGES, max(1, 4096 // PATCHES))
    mlp_rows = attn_group * PATCHES
    scale_factor = HEAD_DIM ** (-0.5)

    def forward(inputs, ada_weight, qkv_weight, proj_weight, route_weight, up_weight, down_weight, expert_up, expert_down):
        modulation = jnp.dot(cond_act, ada_weight.reshape(D, 6 * D), precision=highest).reshape(IMAGES, 6, D)
        image_rows = inputs.reshape(IMAGES, PATCHES, D)
        first_in = low(modulate(image_rows, modulation[:, 0], modulation[:, 1])).reshape(TOKENS, D)

        def attend(block_in):
            projected = jnp.dot(block_in, qkv_weight.reshape(D, 3 * D), precision=highest)
            projected = projected.reshape(attn_group, PATCHES, 3, HEADS, HEAD_DIM)
            queries = low_back(low(projected[:, :, 0]))
            keys = low_back(low(projected[:, :, 1]))
            values = low_back(low(projected[:, :, 2]))
            scores = low_back(jnp.einsum('bqhd,bkhd->bhqk', queries, keys, precision=highest) * scale_factor)
            probs = low(jax.nn.softmax(scores, axis=-1))
            mixed = jnp.einsum('bhqk,bkhd->bqhd', probs, values, precision=highest)
            return low_back(low(mixed)).reshape(attn_group * PATCHES, D)
        mixed_all = lax.map(jax.checkpoint(attend), first_in.reshape(IMAGES // attn_group, attn_group * PATCHES, D))
        mixed_all = mixed_all.reshape(TOKENS, D)
        attn_out = low_back(jnp.dot(mixed_all, proj_weight.T, precision=highest))
        hidden_state = image_rows + modulation[:, 2][:, None, :] * attn_out.reshape(IMAGES, PATCHES, D)
        second_in = low(modulate(hidden_state, modulation[:, 3], modulation[:, 4])).reshape(TOKENS, D)

        def shared_block(block_in):
            shared_pre = low_back(jnp.dot(block_in, up_weight, precision=highest))
            shared_act = low(gelu_tanh(shared_pre))
            return low_back(jnp.dot(shared_act, down_weight.T, precision=highest))
        shared_out = lax.map(jax.checkpoint(shared_block), second_in.reshape(TOKENS // mlp_rows, mlp_rows, D))
        shared_out = shared_out.reshape(TOKENS, D)
        logits = low_back(jnp.dot(second_in, route_weight, precision=highest))
        chosen = jnp.take_along_axis(logits, routes, axis=1)
        gate_values = jax.nn.softmax(chosen, axis=-1)

        def expert_block(pieces):
            source_rows, filled_rows, up_piece, down_piece = pieces
            gathered = low_back(second_in[source_rows] * filled_rows[:, None])
            expert_pre = low_back(jnp.dot(gathered, up_piece, precision=highest))
            expert_act = low(gelu_tanh(expert_pre))
            return low_back(low(jnp.dot(expert_act, down_piece.T, precision=highest)))
        expert_out = lax.map(jax.checkpoint(expert_block), (source, filled, expert_up.reshape(EXPERTS, D, FF), expert_down.reshape(EXPERTS, D, FF)))
        picked = expert_out.reshape(EXPERTS * N_WIDE * CAP, D)[position].reshape(TOKENS, 2, D)
        mixture = lax.optimization_barrier(jnp.sum(gate_values[:, :, None] * picked, axis=1))
        branch = (shared_out + mixture).reshape(IMAGES, PATCHES, D)
        return (hidden_state + modulation[:, 5][:, None, :] * branch).reshape(TOKENS, D)
    output, pullback = jax.vjp(forward, tokens.astype(jnp.float32), w_ada.astype(jnp.float32), w_qkv.astype(jnp.float32), w_proj.astype(jnp.float32), w_route.astype(jnp.float32), w_shared_up.astype(jnp.float32), w_shared_down.astype(jnp.float32), e_up.astype(jnp.float32), e_down.astype(jnp.float32))
    grads = pullback(cotangent.astype(jnp.float32))
    return (output.astype(jnp.bfloat16), grads[0], grads[1], grads[2], grads[3], grads[4], grads[5], grads[6], grads[7], grads[8])
```

```python
import functools

import jax
import jax.numpy as jnp
from jax import lax
from jax.experimental import pallas as pl
from jax.experimental.pallas import tpu as pltpu
from jax.sharding import PartitionSpec as P

HEADS = 12
EXPERTS = 8
CAP = 96


epsilon = 1e-06
highest = lax.Precision.HIGHEST


def swapped(shard, axis, distance):
    return lax.ppermute(shard, axis, [(i, i ^ 1 << distance) for i in range(lax.axis_size(axis))])


def normalize(values):
    centre = jnp.mean(values, axis=-1, keepdims=True)
    shifted = values - centre
    spread = jnp.mean(shifted * shifted, axis=-1, keepdims=True)
    return shifted * lax.rsqrt(spread + epsilon)


def modulate(values, offset, factor):
    return normalize(values) * (1.0 + factor[:, None, :]) + offset[:, None, :]


def gelu_tanh(values):
    return jax.nn.gelu(values, approximate=True)


def gelu_back(values, gradient):
    return jax.vjp(gelu_tanh, values)[1](gradient)[0]


def contract(left_side, right_side, left_dims, right_dims):
    return lax.dot_general(
        left_side,
        right_side,
        ((left_dims, right_dims), ((), ())),
        preferred_element_type=jnp.float32,
    )


def slot_table(route_block):
    flat_routes = route_block.reshape(-1)
    matches = (flat_routes[:, None] == jnp.arange(EXPERTS, dtype=jnp.int32)[None, :]).astype(
        jnp.int32
    )
    earlier = jnp.cumsum(matches, axis=0, dtype=jnp.int32) - matches
    ranking = jnp.sum(earlier * matches, axis=1, dtype=jnp.int32)
    return flat_routes * CAP + ranking


def join_halves(stacked, bit_level, wide_place):
    partner = swapped(stacked, "wide", bit_level)
    upper = wide_place >> bit_level & 1 == 1
    return jnp.where(
        upper,
        jnp.concatenate([partner, stacked], axis=1),
        jnp.concatenate([stacked, partner], axis=1),
    )


def split_halves(stacked, bit_level, wide_place):
    half_rows = stacked.shape[1] // 2
    upper = wide_place >> bit_level & 1 == 1
    lower_part = stacked[:, :half_rows]
    upper_part = stacked[:, half_rows:]
    kept = jnp.where(upper, upper_part, lower_part)
    given = jnp.where(upper, lower_part, upper_part)
    return kept + swapped(given.astype(jnp.bfloat16), "wide", bit_level).astype(given.dtype)


def per_device(
    tokens,
    cotangent,
    time_table,
    timesteps,
    routes,
    w_ada,
    w_qkv,
    w_proj,
    w_route,
    w_shared_up,
    w_shared_down,
    e_up,
    e_down,
):
    images = timesteps.shape[0]
    row_count = tokens.shape[0]
    model_width = tokens.shape[1]
    patches = row_count // images
    core_count = lax.axis_size("narrow")
    wide_count = lax.axis_size("wide")
    group_size = wide_count // EXPERTS
    levels = group_size.bit_length() - 1
    slice_rows = CAP // group_size
    heads_here = HEADS // core_count
    head_dim = model_width // HEADS
    head_width = heads_here * head_dim
    scale_factor = head_dim ** (-0.5)
    wide_place = lax.axis_index("wide")
    ada_rows = w_ada.shape[0]
    step_onehot = (
        timesteps[:, None] == jnp.arange(time_table.shape[0], dtype=jnp.int32)[None, :]
    ).astype(jnp.bfloat16)
    cond = jnp.dot(step_onehot, time_table, preferred_element_type=jnp.float32)
    cond_act = jax.nn.silu(cond).astype(jnp.bfloat16)
    qkv_full, proj_full, route_full, up_full, down_full = (
        lax.all_gather(w_qkv, "wide", axis=0, tiled=True),
        lax.all_gather(w_proj, "wide", axis=0, tiled=True),
        lax.all_gather(w_route, "wide", axis=0, tiled=True),
        lax.all_gather(w_shared_up, "wide", axis=0, tiled=True),
        lax.all_gather(w_shared_down, "wide", axis=0, tiled=True),
    )
    cond_every = lax.all_gather(cond_act, "wide", axis=0, tiled=True)
    cond_own = lax.dynamic_slice_in_dim(cond_every, wide_place * ada_rows, ada_rows, 1)
    modulation_terms = jnp.dot(
        cond_own, w_ada.reshape(ada_rows, 6 * model_width), preferred_element_type=jnp.float32
    )
    modulation = lax.psum_scatter(modulation_terms, "wide", scatter_dimension=0, tiled=True)
    modulation = modulation.reshape(images, 6, model_width)
    expert_weights = jnp.stack([e_up, e_down])
    for bit_level in range(levels):
        expert_weights = join_halves(expert_weights, bit_level, wide_place)
    expert_up = expert_weights[0]
    expert_down = expert_weights[1]
    inputs = tokens.astype(jnp.float32).reshape(images, patches, model_width)
    attn_in, pull_first = jax.vjp(modulate, inputs, modulation[:, 0], modulation[:, 1])
    attn_low = attn_in.reshape(row_count, model_width).astype(jnp.bfloat16)
    projected = jnp.dot(
        attn_low, qkv_full.reshape(model_width, 3 * head_width), preferred_element_type=jnp.float32
    )
    projected = projected.reshape(images, patches, 3, heads_here, head_dim).astype(jnp.bfloat16)
    queries = projected[:, :, 0]
    keys = projected[:, :, 1]
    values = projected[:, :, 2]
    scores = (
        jnp.einsum("bqhd,bkhd->bhqk", queries, keys, preferred_element_type=jnp.float32)
        * scale_factor
    )
    highest_score = jnp.max(scores, axis=-1, keepdims=True)
    log_total = highest_score + jnp.log(
        jnp.sum(jnp.exp(scores - highest_score), axis=-1, keepdims=True)
    )
    probs_low = jnp.exp(scores - log_total).astype(jnp.bfloat16)
    mixed = jnp.einsum("bhqk,bkhd->bqhd", probs_low, values, preferred_element_type=jnp.float32)
    mixed_low = mixed.astype(jnp.bfloat16).reshape(row_count, head_width)
    attn_part = contract(mixed_low, proj_full, (1,), (1,))
    attn_out = lax.psum(attn_part.astype(jnp.bfloat16), "narrow").astype(jnp.float32)
    attn_three = attn_out.reshape(images, patches, model_width)
    hidden_state = inputs + modulation[:, 2][:, None, :] * attn_three
    mlp_in, pull_second = jax.vjp(modulate, hidden_state, modulation[:, 3], modulation[:, 4])
    mlp_low = mlp_in.reshape(row_count, model_width).astype(jnp.bfloat16)
    logits = jnp.dot(mlp_low, route_full, preferred_element_type=jnp.float32)
    selector = (routes[:, :, None] == jnp.arange(EXPERTS, dtype=jnp.int32)[None, None, :]).astype(
        jnp.float32
    )
    chosen = jnp.sum(logits[:, None, :] * selector, axis=-1)
    gate_values, pull_gate = jax.vjp(
        lambda picked_logits: jax.nn.softmax(picked_logits, axis=-1), chosen
    )
    slot_index = slot_table(routes)
    outgoing = (
        jnp.zeros((EXPERTS * CAP, model_width), jnp.bfloat16)
        .at[slot_index]
        .set(jnp.repeat(mlp_low, 2, axis=0))
    )
    arrived = lax.all_to_all(
        outgoing.reshape(wide_count, slice_rows, model_width),
        "wide",
        split_axis=0,
        concat_axis=0,
        tiled=True,
    )
    expert_in = arrived.reshape(wide_count * slice_rows, model_width)
    shared_pre = jnp.dot(mlp_low, up_full, preferred_element_type=jnp.float32)
    shared_act = gelu_tanh(shared_pre).astype(jnp.bfloat16)
    shared_part = contract(shared_act, down_full, (1,), (1,))
    expert_pre = jnp.dot(expert_in, expert_up, preferred_element_type=jnp.float32)
    expert_act = gelu_tanh(expert_pre).astype(jnp.bfloat16)
    expert_part = contract(expert_act, expert_down, (1,), (1,))
    expert_sum, shared_out = (
        lax.psum(expert_part.astype(jnp.bfloat16), "narrow").astype(jnp.float32),
        lax.psum(shared_part.astype(jnp.bfloat16), "narrow").astype(jnp.float32),
    )
    expert_out = expert_sum.astype(jnp.bfloat16)
    returned = lax.all_to_all(
        expert_out.reshape(wide_count, slice_rows, model_width),
        "wide",
        split_axis=0,
        concat_axis=0,
        tiled=True,
    )
    returned = returned.reshape(EXPERTS * CAP, model_width)
    picked = returned[slot_index].astype(jnp.float32).reshape(row_count, 2, model_width)
    mixture = jnp.sum(gate_values[:, :, None] * picked, axis=1)
    branch = (shared_out + mixture).reshape(images, patches, model_width)
    output = hidden_state + modulation[:, 5][:, None, :] * branch
    grad_out = cotangent.astype(jnp.float32).reshape(images, patches, model_width)
    grad_branch = (modulation[:, 5][:, None, :] * grad_out).reshape(row_count, model_width)
    grad_gate2 = jnp.sum(grad_out * branch, axis=1)
    grad_pick = jnp.sum(grad_branch[:, None, :] * picked, axis=-1)
    grad_rows = (
        (gate_values[:, :, None] * grad_branch[:, None, :])
        .astype(jnp.bfloat16)
        .reshape(row_count * 2, model_width)
    )
    grad_slots = jnp.zeros((EXPERTS * CAP, model_width), jnp.bfloat16).at[slot_index].set(grad_rows)
    grad_expert_out = lax.all_to_all(
        grad_slots.reshape(wide_count, slice_rows, model_width),
        "wide",
        split_axis=0,
        concat_axis=0,
        tiled=True,
    )
    grad_expert_out = grad_expert_out.reshape(wide_count * slice_rows, model_width)
    grad_shared = grad_branch.astype(jnp.bfloat16)
    shared_down_grad = contract(grad_shared, shared_act, (0,), (0,))
    grad_shared_act = jnp.dot(grad_shared, down_full, preferred_element_type=jnp.float32)
    grad_shared_pre = gelu_back(shared_pre, grad_shared_act).astype(jnp.bfloat16)
    shared_up_grad = contract(mlp_low, grad_shared_pre, (0,), (0,))
    grad_in_shared = contract(grad_shared_pre, up_full, (1,), (1,))
    grad_chosen = pull_gate(grad_pick)[0]
    grad_logits = jnp.sum(grad_chosen[:, :, None] * selector, axis=1).astype(jnp.bfloat16)
    route_grad = contract(mlp_low, grad_logits, (0,), (0,))
    grad_in_route = contract(grad_logits, route_full, (1,), (1,))
    expert_down_grad = contract(grad_expert_out, expert_act, (0,), (0,))
    grad_expert_act = jnp.dot(grad_expert_out, expert_down, preferred_element_type=jnp.float32)
    grad_expert_pre = gelu_back(expert_pre, grad_expert_act).astype(jnp.bfloat16)
    expert_up_grad = contract(expert_in, grad_expert_pre, (0,), (0,))
    grad_in_part = contract(grad_expert_pre, expert_up, (1,), (1,))
    grad_in_rows, grad_in_shared_sum = (
        lax.psum(grad_in_part.astype(jnp.bfloat16), "narrow").astype(jnp.float32),
        lax.psum(grad_in_shared.astype(jnp.bfloat16), "narrow").astype(jnp.float32),
    )
    back_rows = lax.all_to_all(
        grad_in_rows.astype(jnp.bfloat16).reshape(wide_count, slice_rows, model_width),
        "wide",
        split_axis=0,
        concat_axis=0,
        tiled=True,
    )
    back_rows = back_rows.reshape(EXPERTS * CAP, model_width)
    grad_in_expert = jnp.sum(
        back_rows[slot_index].astype(jnp.float32).reshape(row_count, 2, model_width), axis=1
    )
    grad_mlp_in = grad_in_shared_sum + grad_in_route + grad_in_expert
    grad_hidden_norm, grad_shift2, grad_scale2 = pull_second(
        grad_mlp_in.reshape(images, patches, model_width)
    )
    grad_hidden = grad_out + grad_hidden_norm
    grad_gate1 = jnp.sum(grad_hidden * attn_three, axis=1)
    grad_attn = (
        (modulation[:, 2][:, None, :] * grad_hidden)
        .reshape(row_count, model_width)
        .astype(jnp.bfloat16)
    )
    proj_grad = contract(grad_attn, mixed_low, (0,), (0,))
    grad_mixed = jnp.dot(grad_attn, proj_full, preferred_element_type=jnp.float32).astype(
        jnp.bfloat16
    )
    grad_mixed = grad_mixed.reshape(images, patches, heads_here, head_dim)
    again_scores = (
        jnp.einsum("bqhd,bkhd->bhqk", queries, keys, preferred_element_type=jnp.float32)
        * scale_factor
    )
    probs_full = jnp.exp(again_scores - log_total)
    again_low = probs_full.astype(jnp.bfloat16)
    grad_probs = jnp.einsum(
        "bqhd,bkhd->bhqk", grad_mixed, values, preferred_element_type=jnp.float32
    )
    grad_values = jnp.einsum(
        "bhqk,bqhd->bkhd", again_low, grad_mixed, preferred_element_type=jnp.float32
    )
    weighted_sum = jnp.sum(probs_full * grad_probs, axis=-1, keepdims=True)
    grad_scores = (probs_full * (grad_probs - weighted_sum)).astype(jnp.bfloat16)
    grad_queries = (
        jnp.einsum("bhqk,bkhd->bqhd", grad_scores, keys, preferred_element_type=jnp.float32)
        * scale_factor
    )
    grad_keys = (
        jnp.einsum("bhqk,bqhd->bkhd", grad_scores, queries, preferred_element_type=jnp.float32)
        * scale_factor
    )
    grad_qkv = jnp.stack([grad_queries, grad_keys, grad_values], axis=2).astype(jnp.bfloat16)
    grad_qkv = grad_qkv.reshape(row_count, 3 * head_width)
    qkv_grad = contract(attn_low, grad_qkv, (0,), (0,)).reshape(model_width, 3, head_width)
    grad_attn_part = contract(grad_qkv, qkv_full.reshape(model_width, 3 * head_width), (1,), (1,))
    grad_attn_in = lax.psum(grad_attn_part.astype(jnp.bfloat16), "narrow").astype(jnp.float32)
    grad_input_norm, grad_shift1, grad_scale1 = pull_first(
        grad_attn_in.reshape(images, patches, model_width)
    )
    tokens_grad = (grad_hidden + grad_input_norm).reshape(row_count, model_width)
    grad_modulation = jnp.stack(
        [grad_shift1, grad_scale1, grad_gate1, grad_shift2, grad_scale2, grad_gate2], axis=1
    )
    grad_modulation = grad_modulation.reshape(images, 6 * model_width)
    grad_mod_every = lax.all_gather(grad_modulation, "wide", axis=0, tiled=True)
    ada_part = jnp.dot(cond_own.astype(jnp.float32).T, grad_mod_every, precision=highest).reshape(
        ada_rows, 6, model_width
    )
    qkv_part, proj_part, route_part, shared_up_part, shared_down_part = (
        lax.psum_scatter(qkv_grad, "wide", scatter_dimension=0, tiled=True),
        lax.psum_scatter(proj_grad, "wide", scatter_dimension=0, tiled=True),
        lax.psum_scatter(route_grad, "wide", scatter_dimension=0, tiled=True),
        lax.psum_scatter(shared_up_grad, "wide", scatter_dimension=0, tiled=True),
        lax.psum_scatter(shared_down_grad, "wide", scatter_dimension=0, tiled=True),
    )
    expert_grads = jnp.stack([expert_up_grad, expert_down_grad])
    for bit_level in reversed(range(levels)):
        expert_grads = split_halves(expert_grads, bit_level, wide_place)
    return (
        output.reshape(row_count, model_width).astype(jnp.bfloat16),
        tokens_grad,
        ada_part,
        qkv_part,
        proj_part,
        route_part,
        shared_up_part,
        shared_down_part,
        expert_grads[0],
        expert_grads[1],
    )


MESH = pl.DeviceIdType.MESH
F32 = jnp.float32
BF16 = jnp.bfloat16
Z_SIZE, Y_SIZE, X_SIZE = 4, 2, 2
VMEM_LIMIT = 60 * 1024 * 1024


def place(index):
    return lax.div(index, 4), lax.rem(lax.div(index, 2), 2), lax.rem(index, 2)


def at_place(z, y, x):
    return z * 4 + y * 2 + x


class Sends:
    def __init__(self):
        self.items = []

    def go(self, make, when=None):
        self.items.append((make, when))
        guarded(when, lambda: make().start())

    def drain(self):
        for make, when in self.items:
            guarded(when, lambda make=make: make().wait_send())


def guarded(when, action):
    if when is None:
        action()
        return

    @pl.when(when)
    def _():
        action()


def both(first, second):
    if first is None:
        return second
    if second is None:
        return first
    return jnp.logical_and(first, second)


def remote(src, dst, send_sem, recv_sem, target):
    return pltpu.make_async_remote_copy(
        src_ref=src,
        dst_ref=dst,
        send_sem=send_sem,
        recv_sem=recv_sem,
        device_id=target,
        device_id_type=MESH,
    )


def greet(targets):
    barrier = pltpu.get_barrier_semaphore()
    for target in targets:
        pl.semaphore_signal(barrier, inc=1, device_id=target, device_id_type=MESH)
    pl.semaphore_wait(barrier, len(targets))


class Gather:
    def __init__(self, streams, send_sem, recv_sem, sends):
        self.streams, self.ss, self.rs, self.sends = streams, send_sem, recv_sem, sends
        self.count = [0] * len(streams)
        self.core = lax.axis_index("narrow")
        self.me = lax.axis_index("wide")
        self.z, self.y, self.x = place(self.me)
        self.to_x = at_place(self.z, self.y, 1 - self.x)
        self.to_y = at_place(self.z, 1 - self.y, self.x)
        self.can_up, self.can_down = self.z < Z_SIZE - 1, self.z > 0
        self.up, self.down = self.me + 4, self.me - 4

    def block(self, s, origin):
        shard, full, start, width, _ = self.streams[s]
        rows = shard.shape[0]
        return full.at[pl.ds(pl.multiple_of(origin * rows, 16), rows), pl.ds(start, width)]

    def send(self, s, origin, target, when=None, own=False):
        shard, full, start, width, _ = self.streams[s]
        index = self.count[s]
        self.count[s] += 1

        def make():
            dst = self.block(s, origin)
            src = shard.at[:, pl.ds(start, width)] if own else dst
            return remote(src, dst, self.ss.at[s, index], self.rs.at[s, origin], (target, self.core))

        self.sends.go(make, when)

    def wait(self, s, origin, when=None):
        def action():
            ref = self.block(s, origin)
            remote(
                ref, ref, self.ss.at[s, 0], self.rs.at[s, origin], (self.to_x, self.core)
            ).wait_recv()

        guarded(when, action)

    def spread(self, s, origin, when=None, own=False, up=True, down=True, over_y=True):
        if up:
            self.send(s, origin, self.up, both(when, self.can_up), own)
        if down:
            self.send(s, origin, self.down, both(when, self.can_down), own)
        if over_y:
            self.send(s, origin, self.to_y, when, own)

    def begin(self, s):
        self.send(s, self.me, self.to_x, own=True)
        self.spread(s, self.me, own=True)

    def after_x(self, s):
        self.wait(s, self.to_x)
        self.spread(s, self.to_x)

    def y_pair(self, s):
        if self.streams[s][4] == "xyz":
            for xx in (self.x, 1 - self.x):
                origin = at_place(self.z, 1 - self.y, xx)
                self.wait(s, origin)
                self.spread(s, origin, over_y=False)

    def after_z(self, s, distance):
        order = self.streams[s][4]
        ys = (self.y,) if order == "xzy" else (self.y, 1 - self.y)
        for step, ok in ((-distance, self.z >= distance), (distance, self.z + distance < Z_SIZE)):
            for yy in ys:
                for xx in (self.x, 1 - self.x):
                    origin = at_place(self.z + step, yy, xx)
                    self.wait(s, origin, ok)
                    self.spread(s, origin, ok, up=step < 0, down=step > 0, over_y=order == "xzy")

    def finish(self, s):
        if self.streams[s][4] == "xzy":
            for zz in range(Z_SIZE):
                for xx in range(X_SIZE):
                    self.wait(s, at_place(zz, 1 - self.y, xx))


def gather_kernel(
    ts_ref, table_ref, ada_ref, qkv_ref, proj_ref, route_ref, up_ref, down_ref,
    mod_ref, cond_ref, qkv_out, proj_out, route_out, up_out, down_out,
    ts_all, terms, landed, ts_ss, ts_rs, mod_ss, mod_rs, ag_ss, ag_rs, own_sem,
):
    me, core = lax.axis_index("wide"), lax.axis_index("narrow")
    count = lax.axis_size("wide")
    others = [lax.rem(me + k, count) for k in range(1, count)]
    greet([(other, core) for other in others])
    sends = Sends()
    for k, other in enumerate(others):
        sends.go(lambda k=k, other=other: remote(ts_ref, ts_all.at[me], ts_ss.at[k], ts_rs.at[me], (other, core)))
    half = down_ref.shape[1] // 2
    streams = [
        (qkv_ref, qkv_out, 0, qkv_ref.shape[1], "xzy"),
        (proj_ref, proj_out, 0, proj_ref.shape[1], "xzy"),
        (route_ref, route_out, 0, route_ref.shape[1], "xzy"),
        (up_ref, up_out, 0, up_ref.shape[1], "xzy"),
        (down_ref, down_out, 0, half, "xzy"),
        (down_ref, down_out, half, half, "xyz"),
    ]
    ag = Gather(streams, ag_ss, ag_rs, sends)
    ag.begin(0)
    own = []
    for i, (shard, full) in enumerate(
        ((qkv_ref, qkv_out), (proj_ref, proj_out), (route_ref, route_out), (up_ref, up_out), (down_ref, down_out))
    ):
        rows = shard.shape[0]
        own.append(
            pltpu.make_async_copy(
                shard, full.at[pl.ds(pl.multiple_of(me * rows, 16), rows), :], own_sem.at[i]
            )
        )
        own[-1].start()
    ts_all[me] = ts_ref[...]
    for other in others:
        remote(ts_ref, ts_all.at[other], ts_ss.at[0], ts_rs.at[other], (other, core)).wait_recv()
    steps = jnp.max(ts_all[...], axis=1)[:, :1]
    onehot = (
        steps == lax.broadcasted_iota(jnp.int32, (count, table_ref.shape[0]), 1)
    ).astype(F32).astype(BF16)
    cond = jnp.dot(onehot, table_ref[...], preferred_element_type=F32)
    cond_act = (cond * jax.nn.sigmoid(cond)).astype(BF16)
    cond_ref[...] = cond_act.astype(F32)
    for j in range(terms.shape[1]):
        terms[:, j, :] = jnp.dot(
            cond_act, ada_ref[:, 128 * j : 128 * (j + 1)], preferred_element_type=F32
        )
    for k, other in enumerate(others):
        sends.go(lambda k=k, other=other: remote(terms.at[other], landed.at[me], mod_ss.at[k], mod_rs.at[me], (other, core)))
    n = len(streams)
    for s in range(1, n):
        ag.begin(s)
    ag.after_x(0)
    landed[me] = terms[me]
    for other in others:
        remote(terms.at[me], landed.at[other], mod_ss.at[0], mod_rs.at[other], (other, core)).wait_recv()
    mod_ref[...] = jnp.sum(landed[...], axis=0)
    for s in range(1, n):
        ag.after_x(s)
    for distance in range(1, Z_SIZE):
        if distance == 1:
            for s in range(n):
                ag.y_pair(s)
        for s in range(n):
            ag.after_z(s, distance)
    for s in range(n):
        ag.finish(s)
    for copy in own:
        copy.wait()
    sends.drain()


def vmem(count):
    return [pl.BlockSpec(memory_space=pltpu.VMEM)] * count


def hbm(count):
    return [pl.BlockSpec(memory_space=pl.ANY)] * count


def params(collective_id):
    return pltpu.CompilerParams(
        collective_id=collective_id, has_side_effects=True, vmem_limit_bytes=VMEM_LIMIT
    )


def gather_weights(count, ts_tile, table, ada, qkv, proj, route, up, down):
    shards = (qkv, proj, route, up, down)
    vectors = ada.shape[1] // 128
    dma = pltpu.SemaphoreType.DMA
    return pl.pallas_call(
        gather_kernel,
        out_shape=[
            jax.ShapeDtypeStruct((vectors, 128), F32),
            jax.ShapeDtypeStruct((count, table.shape[1]), F32),
            *[jax.ShapeDtypeStruct((count * a.shape[0], a.shape[1]), a.dtype) for a in shards],
        ],
        in_specs=vmem(8),
        out_specs=vmem(2) + hbm(5),
        scratch_shapes=[
            pltpu.VMEM((count, 8, 128), jnp.int32),
            pltpu.VMEM((count, vectors, 128), F32),
            pltpu.VMEM((count, vectors, 128), F32),
            dma((count,)), dma((count,)), dma((count,)), dma((count,)),
            dma((6, 40)), dma((6, count)), dma((5,)),
        ],
        compiler_params=params(1),
        name="gather_weights",
    )(ts_tile, table, ada, *shards)


def swap_kernel(count, *refs):
    ins, outs, (ss, rs) = refs[:count], refs[count : 2 * count], refs[2 * count :]
    me, core = lax.axis_index("wide"), lax.axis_index("narrow")
    peer = (me, 1 - core)
    greet([peer])
    copies = [remote(ins[i], outs[i], ss.at[i], rs.at[i], peer) for i in range(count)]
    for copy in copies:
        copy.start()
    for copy in copies:
        copy.wait()


def swap_cores(collective_id, *arrays):
    count = len(arrays)
    return pl.pallas_call(
        functools.partial(swap_kernel, count),
        out_shape=[jax.ShapeDtypeStruct(a.shape, a.dtype) for a in arrays],
        in_specs=vmem(count),
        out_specs=vmem(count),
        scratch_shapes=[pltpu.SemaphoreType.DMA((count,)), pltpu.SemaphoreType.DMA((count,))],
        compiler_params=params(collective_id),
        name="swap_cores",
    )(*arrays)


def peers_far_first(me):
    z, y, x = place(me)
    found = []
    for dz in range(Z_SIZE):
        for dy in range(Y_SIZE):
            for dx in range(X_SIZE):
                if dz or dy or dx:
                    zz = lax.rem(z + dz, Z_SIZE)
                    found.append(at_place(zz, lax.rem(y + dy, 2), lax.rem(x + dx, 2)))
    return found[::-1]


def dispatch_kernel(
    rows_ref, grads_ref, rows_out, grads_out, ss, rs, pass_ss, pass_rs, own_sem
):
    me, core = lax.axis_index("wide"), lax.axis_index("narrow")
    others = peers_far_first(me)
    peer = (me, 1 - core)
    greet([(other, core) for other in others] + [peer])
    size = rows_ref.shape[0] // lax.axis_size("wide")
    sends = Sends()

    def rows(index):
        return pl.ds(pl.multiple_of(index * size, 16), size)

    pairs = ((rows_ref, rows_out), (grads_ref, grads_out))
    for k, other in enumerate(others):
        for a, (src, dst) in enumerate(pairs):
            sends.go(
                lambda k=k, other=other, a=a, src=src, dst=dst: remote(
                    src.at[rows(other), :], dst.at[core, rows(me), :],
                    ss.at[a, k], rs.at[a, me], (other, core),
                )
            )
    for a, (src, dst) in enumerate(pairs):
        sends.go(
            lambda a=a, src=src, dst=dst: remote(
                src.at[rows(me), :], dst.at[core, rows(me), :], pass_ss.at[a, 15], pass_rs.at[a, me], peer
            )
        )
        own = pltpu.make_async_copy(src.at[rows(me), :], dst.at[core, rows(me), :], own_sem.at[a])
        own.start()
        own.wait()
    for k, other in enumerate(others[::-1]):
        for a, (src, dst) in enumerate(pairs):
            here = dst.at[core, rows(other), :]
            remote(here, here, ss.at[a, 0], rs.at[a, other], peer).wait_recv()
            sends.go(
                lambda k=k, other=other, a=a, here=here: remote(
                    here, here, pass_ss.at[a, k], pass_rs.at[a, other], peer
                )
            )
    for other in [me] + others[::-1]:
        for a, (src, dst) in enumerate(pairs):
            there = dst.at[1 - core, rows(other), :]
            remote(there, there, pass_ss.at[a, 0], pass_rs.at[a, other], peer).wait_recv()
    sends.drain()


def dispatch(rows, grads):
    total, width = rows.shape
    dma = pltpu.SemaphoreType.DMA
    return pl.pallas_call(
        dispatch_kernel,
        out_shape=[jax.ShapeDtypeStruct((2, total, width), BF16)] * 2,
        in_specs=vmem(2),
        out_specs=hbm(2),
        scratch_shapes=[dma((2, 16)), dma((2, 16)), dma((2, 16)), dma((2, 16)), dma((2,))],
        compiler_params=params(2),
        name="dispatch",
    )(rows, grads)


def bring_back_kernel(
    out_ref, grad_ref, shared_ref, shared_grad_ref,
    out_back, grad_back, shared_sum, shared_grad_sum,
    their_out, their_grad, their_shared, their_shared_grad, sum_out, sum_grad,
    near_ss, near_rs, ss, rs, own_sem,
):
    me, core = lax.axis_index("wide"), lax.axis_index("narrow")
    others = peers_far_first(me)
    peer = (me, 1 - core)
    greet([(other, core) for other in others] + [peer])
    count = lax.axis_size("wide")
    size = out_ref.shape[1] // count
    sends = Sends()

    def rows(index):
        return pl.ds(pl.multiple_of(index * size, 16), size)

    triples = ((out_ref, their_out, sum_out, out_back), (grad_ref, their_grad, sum_grad, grad_back))
    order = others + [me]
    for k, other in enumerate(order):
        for a, (src, theirs, _, _) in enumerate(triples):
            sends.go(
                lambda k=k, other=other, a=a, src=src, theirs=theirs: remote(
                    src.at[1 - core, rows(other), :], theirs.at[rows(other), :],
                    near_ss.at[a, k], near_rs.at[a, other], peer,
                )
            )
    small = ((shared_ref, their_shared, shared_sum), (shared_grad_ref, their_shared_grad, shared_grad_sum))
    for a, (src, theirs, _) in enumerate(small):
        sends.go(lambda a=a, src=src, theirs=theirs: remote(src.at[1 - core], theirs, near_ss.at[a, 16], near_rs.at[a, 16], peer))
    for k, other in enumerate(order):
        for a, (src, theirs, total, back) in enumerate(triples):
            here = theirs.at[rows(other), :]
            remote(here, here, near_ss.at[a, 0], near_rs.at[a, other], peer).wait_recv()
            total[rows(other), :] = (
                src[core, rows(other), :].astype(F32) + theirs[rows(other), :].astype(F32)
            ).astype(BF16)
            if k < len(others):
                sends.go(
                    lambda k=k, other=other, a=a, total=total, back=back: remote(
                        total.at[rows(other), :], back.at[rows(me), :],
                        ss.at[a, k], rs.at[a, me], (other, core),
                    )
                )
            else:
                own = pltpu.make_async_copy(total.at[rows(me), :], back.at[rows(me), :], own_sem.at[a])
                own.start()
                own.wait()
    for a, (src, theirs, result) in enumerate(small):
        remote(theirs, theirs, near_ss.at[a, 0], near_rs.at[a, 16], peer).wait_recv()
        result[...] = src[core].astype(F32) + theirs[...].astype(F32)
    for other in others[::-1]:
        for a, (_, _, _, back) in enumerate(triples):
            here = back.at[rows(other), :]
            remote(here, here, ss.at[a, 0], rs.at[a, other], peer).wait_recv()
    sends.drain()


def bring_back(out_part, grad_part, shared_part, shared_grad_part):
    _, total, width = out_part.shape
    local = shared_part.shape[1]
    dma = pltpu.SemaphoreType.DMA
    return pl.pallas_call(
        bring_back_kernel,
        out_shape=[jax.ShapeDtypeStruct((total, width), BF16)] * 2
        + [jax.ShapeDtypeStruct((local, width), F32)] * 2,
        in_specs=vmem(4),
        out_specs=vmem(4),
        scratch_shapes=[
            pltpu.VMEM((total, width), BF16), pltpu.VMEM((total, width), BF16),
            pltpu.VMEM((local, width), BF16), pltpu.VMEM((local, width), BF16),
            pltpu.VMEM((total, width), BF16), pltpu.VMEM((total, width), BF16),
            dma((2, 17)), dma((2, 17)), dma((2, 16)), dma((2, 16)), dma((2,)),
        ],
        compiler_params=params(3),
        name="bring_back",
    )(out_part, grad_part, shared_part, shared_grad_part)


def reduce_kernel(count, *refs):
    terms, vectors = refs[:count], refs[count]
    outs, every = refs[count + 1 : 2 * count + 1], refs[2 * count + 1]
    rest = refs[2 * count + 2 :]
    work, from_y = rest[:count], rest[count : 2 * count]
    from_z, from_x = rest[2 * count : 3 * count], rest[3 * count : 4 * count]
    y_ss, y_rs, z_ss, z_rs, x_ss, x_rs, vec_ss, vec_rs, load_sem = rest[4 * count :]
    me, core = lax.axis_index("wide"), lax.axis_index("narrow")
    z, y, x = place(me)
    others = peers_far_first(me)
    greet([(other, core) for other in others])
    sends = Sends()
    for k, other in enumerate(others):
        sends.go(lambda k=k, other=other: remote(vectors, every.at[me], vec_ss.at[k], vec_rs.at[me], (other, core)))
    every[me] = vectors[...]
    to_x, to_y = at_place(z, y, 1 - x), at_place(z, 1 - y, x)
    upper = z >= 2
    dest_z = [
        jnp.where(upper, 0, 3), jnp.where(upper, 1, 2), jnp.where(upper, 5 - z, 1 - z), z
    ]

    def rows(i, index):
        size = terms[i].shape[0] // lax.axis_size("wide")
        return pl.ds(pl.multiple_of(index * size, 16), size)

    for k in range(4):
        for i in range(count):
            for xx in range(2):
                there = at_place(dest_z[k], 1 - y, xx)
                sends.go(
                    lambda k=k, i=i, xx=xx, there=there: remote(
                        terms[i].at[rows(i, there), :], from_y[i].at[dest_z[k], xx],
                        y_ss.at[i, k * 2 + xx], y_rs.at[i, dest_z[k] * 2 + xx], (to_y, core),
                    )
                )

    def landed(ref, recv_sem):
        remote(ref, ref, y_ss.at[0, 0], recv_sem, (to_y, core)).wait_recv()

    for k in range(4):
        zz = dest_z[k]
        going_up = zz > z
        for i in range(count):
            for xx in range(2):
                landed(from_y[i].at[zz, xx], y_rs.at[i, zz * 2 + xx])
                here = rows(i, at_place(zz, y, xx))
                work[i][zz, xx] = (
                    terms[i][here, :].astype(F32) + from_y[i][zz, xx].astype(F32)
                ).astype(BF16)

                def add(came, i=i, xx=xx, zz=zz):
                    landed(from_z[i].at[came, zz, xx], z_rs.at[i, (came * 4 + zz) * 2 + xx])
                    work[i][zz, xx] = (
                        work[i][zz, xx].astype(F32) + from_z[i][came, zz, xx].astype(F32)
                    ).astype(BF16)

                def pass_on(came, target, i=i, xx=xx, zz=zz, k=k):
                    return lambda: remote(
                        work[i].at[zz, xx], from_z[i].at[came, zz, xx],
                        z_ss.at[i, k * 2 + xx], z_rs.at[i, (came * 4 + zz) * 2 + xx], (target, core),
                    )

                if k < 3:
                    guarded(jnp.logical_and(going_up, z > 0), lambda: add(0))
                    guarded(jnp.logical_and(zz < z, z < 3), lambda: add(1))
                    sends.go(pass_on(0, me + 4), going_up)
                    sends.go(pass_on(1, me - 4), zz < z)
                else:
                    guarded(z > 0, lambda: add(0))
                    guarded(z < 3, lambda: add(1))
        if k == 3:
            for i in range(count):
                sends.go(
                    lambda i=i: remote(work[i].at[z, 1 - x], from_x[i], x_ss.at[i], x_rs.at[i], (to_x, core))
                )
    for i in range(count):
        landed(from_x[i], x_rs.at[i])
        outs[i][...] = work[i][z, x].astype(F32) + from_x[i][...].astype(F32)
    for other in others:
        landed(every.at[other], vec_rs.at[other])
    sends.drain()


def reduce_rows(vectors, *terms):
    count = len(terms)
    shapes = [(t.shape[0] // 16, t.shape[1]) for t in terms]
    dma = pltpu.SemaphoreType.DMA
    return pl.pallas_call(
        functools.partial(reduce_kernel, count),
        out_shape=[jax.ShapeDtypeStruct(s, F32) for s in shapes]
        + [jax.ShapeDtypeStruct((16, *vectors.shape), F32)],
        in_specs=vmem(count + 1),
        out_specs=vmem(count + 1),
        scratch_shapes=[pltpu.VMEM((4, 2, *s), BF16) for s in shapes]
        + [pltpu.VMEM((4, 2, *s), BF16) for s in shapes]
        + [pltpu.VMEM((2, 4, 2, *s), BF16) for s in shapes]
        + [pltpu.VMEM(s, BF16) for s in shapes]
        + [
            dma((count, 8)), dma((count, 8)), dma((count, 6)), dma((count, 16)),
            dma((count,)), dma((count,)), dma((16,)), dma((16,)), dma((1,)),
        ],
        compiler_params=params(4),
        name="reduce_rows",
    )(*terms, vectors)


def normalized(values):
    centre = jnp.mean(values, axis=-1, keepdims=True)
    shifted = values - centre
    spread = jnp.mean(shifted * shifted, axis=-1, keepdims=True)
    rate = lax.rsqrt(spread + epsilon)
    return shifted * rate, rate


def norm_back(normal, rate, gradient):
    mean = jnp.mean(gradient, axis=-1, keepdims=True)
    along = jnp.mean(gradient * normal, axis=-1, keepdims=True)
    return rate * (gradient - mean - normal * along)


def halves(array, core):
    width = array.shape[-1] // 2
    return jnp.stack([array[:, :width], array[:, width:]])


def own_half(array, core):
    width = array.shape[-1] // 2
    return lax.dynamic_slice_in_dim(array, core * width, width, array.ndim - 1)


def per_device_direct(
    tokens, cotangent, time_table, timesteps, routes, w_ada, w_qkv, w_proj,
    w_route, w_shared_up, w_shared_down, e_up, e_down,
):
    row_count, model_width = tokens.shape
    core = lax.axis_index("narrow")
    core_count = lax.axis_size("narrow")
    wide_count = lax.axis_size("wide")
    heads_here = HEADS // core_count
    head_dim = model_width // HEADS
    head_width = heads_here * head_dim
    half = model_width // 2
    scale_factor = head_dim ** (-0.5)
    wide_place = lax.axis_index("wide")
    upper = wide_place % 2 == 1
    ada_rows = w_ada.shape[0]

    partner = [(i, i ^ 1) for i in range(wide_count)]
    up_other = lax.ppermute(e_up, "wide", partner)
    down_other = lax.ppermute(e_down, "wide", partner)

    table = lax.dynamic_slice_in_dim(time_table, wide_place * ada_rows, ada_rows, 1)
    table = jnp.pad(table, ((0, -table.shape[0] % 128), (0, 0)))
    ts_tile = jnp.broadcast_to(timesteps[:, None], (8, 128)).astype(jnp.int32)
    mod, cond_own, qkv_full, proj_full, route_full, up_full, down_full = gather_weights(
        wide_count,
        ts_tile,
        table,
        w_ada.reshape(ada_rows, 6 * model_width),
        w_qkv.reshape(ada_rows, 3 * head_width),
        w_proj,
        jnp.pad(w_route, ((0, 0), (0, 128 - EXPERTS))),
        w_shared_up,
        w_shared_down,
    )
    modulation = mod.reshape(6, model_width)
    shift1, scale1, gate1, shift2, scale2, gate2 = [modulation[j][None, :] for j in range(6)]

    inputs = tokens.astype(F32)
    normal1, rate1 = normalized(inputs)
    attn_low = (normal1 * (1.0 + scale1) + shift1).astype(BF16)
    projected = jnp.dot(attn_low, qkv_full, preferred_element_type=F32).astype(BF16)
    projected = projected.reshape(row_count, 3, heads_here, head_dim)
    queries, keys, values = projected[:, 0], projected[:, 1], projected[:, 2]
    scores = jnp.einsum("qhd,khd->hqk", queries, keys, preferred_element_type=F32) * scale_factor
    top = jnp.max(scores, axis=-1, keepdims=True)
    log_total = top + jnp.log(jnp.sum(jnp.exp(scores - top), axis=-1, keepdims=True))
    probs_full = jnp.exp(scores - log_total)
    probs_low = probs_full.astype(BF16)
    mixed = jnp.einsum("hqk,khd->qhd", probs_low, values, preferred_element_type=F32)
    mixed_low = mixed.astype(BF16).reshape(row_count, head_width)
    attn_part = contract(mixed_low, proj_full, (1,), (1,)).astype(BF16)
    (attn_theirs,) = swap_cores(5, attn_part)
    attn_out = attn_part.astype(F32) + attn_theirs.astype(F32)
    hidden = inputs + gate1 * attn_out
    normal2, rate2 = normalized(hidden)
    mlp_low = (normal2 * (1.0 + scale2) + shift2).astype(BF16)
    logits = jnp.dot(mlp_low, route_full, preferred_element_type=F32)
    lanes = jnp.arange(route_full.shape[1], dtype=jnp.int32)
    pick = [(routes[:, k : k + 1] == lanes[None, :]).astype(F32) for k in range(2)]
    chosen = [jnp.sum(logits * pick[k], axis=-1, keepdims=True) for k in range(2)]
    peak = jnp.maximum(chosen[0], chosen[1])
    weight = [jnp.exp(chosen[k] - peak) for k in range(2)]
    gates = [weight[k] / (weight[0] + weight[1]) for k in range(2)]

    flat = routes.reshape(-1)
    matches = (flat[:, None] == jnp.arange(EXPERTS, dtype=jnp.int32)[None, :]).astype(BF16)
    steps = jnp.arange(flat.shape[0], dtype=jnp.int32)
    before = (steps[None, :] < steps[:, None]).astype(BF16)
    earlier = jnp.dot(before, matches, preferred_element_type=F32)
    ranking = jnp.sum(earlier * matches.astype(F32), axis=1).astype(jnp.int32)
    slots = (flat * CAP + ranking).reshape(row_count, 2)
    slot_ids = jnp.arange(EXPERTS * CAP, dtype=jnp.int32)
    place_in = [(slot_ids[:, None] == slots[None, :, k]).astype(BF16) for k in range(2)]
    take_out = [(slots[:, k : k + 1] == slot_ids[None, :]).astype(BF16) for k in range(2)]

    grad_out = cotangent.astype(F32)
    grad_branch = gate2 * grad_out
    grad_branch_half = own_half(grad_branch, core)
    rows_half = jnp.dot(
        place_in[0] + place_in[1], own_half(mlp_low, core), preferred_element_type=F32
    ).astype(BF16)
    grads_half = sum(
        jnp.dot(
            place_in[k], (gates[k] * grad_branch_half).astype(BF16), preferred_element_type=F32
        )
        for k in range(2)
    ).astype(BF16)
    expert_in, grad_expert_out = dispatch(rows_half, grads_half)

    shared_pre = jnp.dot(mlp_low, up_full, preferred_element_type=F32)
    shared_act = gelu_tanh(shared_pre).astype(BF16)
    shared_part = contract(shared_act, down_full, (1,), (1,)).astype(BF16)
    grad_shared = grad_branch.astype(BF16)
    shared_down_grad = contract(grad_shared, shared_act, (0,), (0,)).astype(BF16)
    grad_shared_act = jnp.dot(grad_shared, down_full, preferred_element_type=F32)
    grad_shared_pre = gelu_back(shared_pre, grad_shared_act).astype(BF16)
    shared_up_grad = contract(mlp_low, grad_shared_pre, (0,), (0,)).astype(BF16)
    grad_in_shared = contract(grad_shared_pre, up_full, (1,), (1,)).astype(BF16)

    in_low, in_high = expert_in[0], expert_in[1]
    in_own, in_other = jnp.where(upper, in_high, in_low), jnp.where(upper, in_low, in_high)
    g_low, g_high = grad_expert_out[0], grad_expert_out[1]
    g_own, g_other = jnp.where(upper, g_high, g_low), jnp.where(upper, g_low, g_high)
    expert_pre = jnp.dot(in_own, e_up, preferred_element_type=F32) + jnp.dot(
        in_other, up_other, preferred_element_type=F32
    )
    expert_act = gelu_tanh(expert_pre).astype(BF16)
    out_own = contract(expert_act, e_down, (1,), (1,)).astype(BF16)
    out_other = contract(expert_act, down_other, (1,), (1,)).astype(BF16)
    grad_expert_act = jnp.dot(g_own, e_down, preferred_element_type=F32) + jnp.dot(
        g_other, down_other, preferred_element_type=F32
    )
    grad_expert_pre = gelu_back(expert_pre, grad_expert_act).astype(BF16)
    gi_own = contract(grad_expert_pre, e_up, (1,), (1,)).astype(BF16)
    gi_other = contract(grad_expert_pre, up_other, (1,), (1,)).astype(BF16)
    up_send = contract(in_other, grad_expert_pre, (0,), (0,)).astype(BF16)
    down_send = contract(g_other, expert_act, (0,), (0,)).astype(BF16)
    up_came = lax.ppermute(up_send, "wide", partner)
    down_came = lax.ppermute(down_send, "wide", partner)
    up_kept = contract(in_own, grad_expert_pre, (0,), (0,))
    down_kept = contract(g_own, expert_act, (0,), (0,))

    def in_order(own, other):
        return jnp.stack([jnp.where(upper, other, own), jnp.where(upper, own, other)])

    returned, back_rows, shared_half, grad_shared_half = bring_back(
        in_order(out_own, out_other),
        in_order(gi_own, gi_other),
        halves(shared_part, core),
        halves(grad_in_shared, core),
    )
    picked = [jnp.dot(take_out[k], returned, preferred_element_type=F32) for k in range(2)]
    branch_half = shared_half + gates[0] * picked[0] + gates[1] * picked[1]
    grad_mlp_half = grad_shared_half + jnp.dot(
        take_out[0] + take_out[1], back_rows, preferred_element_type=F32
    )
    gate_terms = jnp.concatenate(
        [jnp.sum(grad_branch_half * picked[k], axis=-1, keepdims=True) for k in range(2)], axis=1
    )
    gate_terms = jnp.pad(gate_terms, ((0, 0), (0, 126)))
    branch_theirs, grad_mlp_theirs, gate_theirs = swap_cores(
        6, branch_half, grad_mlp_half, gate_terms
    )

    def whole(mine, theirs):
        first = core == 0
        return jnp.concatenate(
            [jnp.where(first, mine, theirs), jnp.where(first, theirs, mine)], axis=1
        )

    branch = whole(branch_half, branch_theirs)
    grad_gates = gate_terms + gate_theirs
    inner = gates[0] * grad_gates[:, 0:1] + gates[1] * grad_gates[:, 1:2]
    grad_chosen = [gates[k] * (grad_gates[:, k : k + 1] - inner) for k in range(2)]
    grad_logits = (grad_chosen[0] * pick[0] + grad_chosen[1] * pick[1]).astype(BF16)
    route_grad = contract(mlp_low, grad_logits, (0,), (0,)).astype(BF16)
    grad_mlp_in = whole(grad_mlp_half, grad_mlp_theirs) + contract(
        grad_logits, route_full, (1,), (1,)
    )
    output = hidden + gate2 * branch
    grad_gate2 = jnp.sum(grad_out * branch, axis=0)
    grad_shift2 = jnp.sum(grad_mlp_in, axis=0)
    grad_scale2 = jnp.sum(grad_mlp_in * normal2, axis=0)
    grad_hidden = grad_out + norm_back(normal2, rate2, grad_mlp_in * (1.0 + scale2))
    grad_gate1 = jnp.sum(grad_hidden * attn_out, axis=0)
    grad_attn = (gate1 * grad_hidden).astype(BF16)
    proj_grad = contract(grad_attn, mixed_low, (0,), (0,)).astype(BF16)
    grad_mixed = jnp.dot(grad_attn, proj_full, preferred_element_type=F32).astype(BF16)
    grad_mixed = grad_mixed.reshape(row_count, heads_here, head_dim)
    grad_probs = jnp.einsum("qhd,khd->hqk", grad_mixed, values, preferred_element_type=F32)
    grad_values = jnp.einsum("hqk,qhd->khd", probs_low, grad_mixed, preferred_element_type=F32)
    weighted = jnp.sum(probs_full * grad_probs, axis=-1, keepdims=True)
    grad_scores = (probs_full * (grad_probs - weighted)).astype(BF16)
    grad_queries = (
        jnp.einsum("hqk,khd->qhd", grad_scores, keys, preferred_element_type=F32) * scale_factor
    )
    grad_keys = (
        jnp.einsum("hqk,qhd->khd", grad_scores, queries, preferred_element_type=F32)
        * scale_factor
    )
    grad_qkv = jnp.stack([grad_queries, grad_keys, grad_values], axis=1).astype(BF16)
    grad_qkv = grad_qkv.reshape(row_count, 3 * head_width)
    qkv_grad = contract(attn_low, grad_qkv, (0,), (0,)).astype(BF16)
    grad_attn_part = contract(grad_qkv, qkv_full, (1,), (1,)).astype(BF16)
    (grad_attn_theirs,) = swap_cores(7, grad_attn_part)
    grad_attn_in = grad_attn_part.astype(F32) + grad_attn_theirs.astype(F32)
    grad_shift1 = jnp.sum(grad_attn_in, axis=0)
    grad_scale1 = jnp.sum(grad_attn_in * normal1, axis=0)
    tokens_grad = grad_hidden + norm_back(normal1, rate1, grad_attn_in * (1.0 + scale1))
    grad_mod = jnp.stack(
        [grad_shift1, grad_scale1, grad_gate1, grad_shift2, grad_scale2, grad_gate2]
    ).reshape(-1, 128)
    qkv_sum, proj_sum, route_sum, up_sum, down_sum, mod_every = reduce_rows(
        grad_mod, qkv_grad, proj_grad, route_grad, shared_up_grad, shared_down_grad
    )
    ada_grad = jnp.dot(
        cond_own.T, mod_every.reshape(wide_count, 6 * model_width), precision=highest
    ).reshape(ada_rows, 6, model_width)
    return (
        output.astype(BF16),
        tokens_grad,
        ada_grad,
        qkv_sum.reshape(ada_rows, 3, head_width),
        proj_sum,
        route_sum[:, :EXPERTS],
        up_sum,
        down_sum,
        up_kept + up_came.astype(F32),
        down_kept + down_came.astype(F32),
    )


def solution(mesh):
    placed = (
        P("wide", None),
        P("wide", None),
        P(),
        P("wide"),
        P("wide", None),
        P("wide", None, None),
        P("wide", None, "narrow"),
        P("wide", "narrow"),
        P("wide", None),
        P("wide", "narrow"),
        P("wide", "narrow"),
        P("wide", "narrow"),
        P("wide", "narrow"),
    )
    direct = mesh.shape["wide"] == 16 and mesh.shape["narrow"] == 2
    return jax.shard_map(
        per_device_direct if direct else per_device,
        mesh=mesh,
        in_specs=placed,
        out_specs=(
            P("wide", None),
            P("wide", None),
            P("wide", None, None),
            P("wide", None, "narrow"),
            P("wide", "narrow"),
            P("wide", None),
            P("wide", "narrow"),
            P("wide", "narrow"),
            P("wide", "narrow"),
            P("wide", "narrow"),
        ),
        check_vma=False,
    )
```

```python
import functools

import jax
import jax.numpy as jnp
from jax import lax
from jax.experimental import pallas as pl
from jax.experimental.pallas import tpu as pltpu
from jax.sharding import PartitionSpec as P

HEADS = 12
EXPERTS = 8
CAP = 96


epsilon = 1e-06
highest = lax.Precision.HIGHEST


def swapped(shard, axis, distance):
    return lax.ppermute(shard, axis, [(i, i ^ 1 << distance) for i in range(lax.axis_size(axis))])


def normalize(values):
    centre = jnp.mean(values, axis=-1, keepdims=True)
    shifted = values - centre
    spread = jnp.mean(shifted * shifted, axis=-1, keepdims=True)
    return shifted * lax.rsqrt(spread + epsilon)


def modulate(values, offset, factor):
    return normalize(values) * (1.0 + factor[:, None, :]) + offset[:, None, :]


def gelu_tanh(values):
    return jax.nn.gelu(values, approximate=True)


def gelu_back(values, gradient):
    return jax.vjp(gelu_tanh, values)[1](gradient)[0]


def contract(left_side, right_side, left_dims, right_dims):
    return lax.dot_general(
        left_side,
        right_side,
        ((left_dims, right_dims), ((), ())),
        preferred_element_type=jnp.float32,
    )


def slot_table(route_block):
    flat_routes = route_block.reshape(-1)
    matches = (flat_routes[:, None] == jnp.arange(EXPERTS, dtype=jnp.int32)[None, :]).astype(
        jnp.int32
    )
    earlier = jnp.cumsum(matches, axis=0, dtype=jnp.int32) - matches
    ranking = jnp.sum(earlier * matches, axis=1, dtype=jnp.int32)
    return flat_routes * CAP + ranking


def join_halves(stacked, bit_level, wide_place):
    partner = swapped(stacked, "wide", bit_level)
    upper = wide_place >> bit_level & 1 == 1
    return jnp.where(
        upper,
        jnp.concatenate([partner, stacked], axis=1),
        jnp.concatenate([stacked, partner], axis=1),
    )


def split_halves(stacked, bit_level, wide_place):
    half_rows = stacked.shape[1] // 2
    upper = wide_place >> bit_level & 1 == 1
    lower_part = stacked[:, :half_rows]
    upper_part = stacked[:, half_rows:]
    kept = jnp.where(upper, upper_part, lower_part)
    given = jnp.where(upper, lower_part, upper_part)
    return kept + swapped(given.astype(jnp.bfloat16), "wide", bit_level).astype(given.dtype)


def per_device(
    tokens,
    cotangent,
    time_table,
    timesteps,
    routes,
    w_ada,
    w_qkv,
    w_proj,
    w_route,
    w_shared_up,
    w_shared_down,
    e_up,
    e_down,
):
    images = timesteps.shape[0]
    row_count = tokens.shape[0]
    model_width = tokens.shape[1]
    patches = row_count // images
    core_count = lax.axis_size("narrow")
    wide_count = lax.axis_size("wide")
    group_size = wide_count // EXPERTS
    levels = group_size.bit_length() - 1
    slice_rows = CAP // group_size
    heads_here = HEADS // core_count
    head_dim = model_width // HEADS
    head_width = heads_here * head_dim
    scale_factor = head_dim ** (-0.5)
    wide_place = lax.axis_index("wide")
    ada_rows = w_ada.shape[0]
    step_onehot = (
        timesteps[:, None] == jnp.arange(time_table.shape[0], dtype=jnp.int32)[None, :]
    ).astype(jnp.bfloat16)
    cond = jnp.dot(step_onehot, time_table, preferred_element_type=jnp.float32)
    cond_act = jax.nn.silu(cond).astype(jnp.bfloat16)
    qkv_full, proj_full, route_full, up_full, down_full = (
        lax.all_gather(w_qkv, "wide", axis=0, tiled=True),
        lax.all_gather(w_proj, "wide", axis=0, tiled=True),
        lax.all_gather(w_route, "wide", axis=0, tiled=True),
        lax.all_gather(w_shared_up, "wide", axis=0, tiled=True),
        lax.all_gather(w_shared_down, "wide", axis=0, tiled=True),
    )
    cond_every = lax.all_gather(cond_act, "wide", axis=0, tiled=True)
    cond_own = lax.dynamic_slice_in_dim(cond_every, wide_place * ada_rows, ada_rows, 1)
    modulation_terms = jnp.dot(
        cond_own, w_ada.reshape(ada_rows, 6 * model_width), preferred_element_type=jnp.float32
    )
    modulation = lax.psum_scatter(modulation_terms, "wide", scatter_dimension=0, tiled=True)
    modulation = modulation.reshape(images, 6, model_width)
    expert_weights = jnp.stack([e_up, e_down])
    for bit_level in range(levels):
        expert_weights = join_halves(expert_weights, bit_level, wide_place)
    expert_up = expert_weights[0]
    expert_down = expert_weights[1]
    inputs = tokens.astype(jnp.float32).reshape(images, patches, model_width)
    attn_in, pull_first = jax.vjp(modulate, inputs, modulation[:, 0], modulation[:, 1])
    attn_low = attn_in.reshape(row_count, model_width).astype(jnp.bfloat16)
    projected = jnp.dot(
        attn_low, qkv_full.reshape(model_width, 3 * head_width), preferred_element_type=jnp.float32
    )
    projected = projected.reshape(images, patches, 3, heads_here, head_dim).astype(jnp.bfloat16)
    queries = projected[:, :, 0]
    keys = projected[:, :, 1]
    values = projected[:, :, 2]
    scores = (
        jnp.einsum("bqhd,bkhd->bhqk", queries, keys, preferred_element_type=jnp.float32)
        * scale_factor
    )
    highest_score = jnp.max(scores, axis=-1, keepdims=True)
    log_total = highest_score + jnp.log(
        jnp.sum(jnp.exp(scores - highest_score), axis=-1, keepdims=True)
    )
    probs_low = jnp.exp(scores - log_total).astype(jnp.bfloat16)
    mixed = jnp.einsum("bhqk,bkhd->bqhd", probs_low, values, preferred_element_type=jnp.float32)
    mixed_low = mixed.astype(jnp.bfloat16).reshape(row_count, head_width)
    attn_part = contract(mixed_low, proj_full, (1,), (1,))
    attn_out = lax.psum(attn_part.astype(jnp.bfloat16), "narrow").astype(jnp.float32)
    attn_three = attn_out.reshape(images, patches, model_width)
    hidden_state = inputs + modulation[:, 2][:, None, :] * attn_three
    mlp_in, pull_second = jax.vjp(modulate, hidden_state, modulation[:, 3], modulation[:, 4])
    mlp_low = mlp_in.reshape(row_count, model_width).astype(jnp.bfloat16)
    logits = jnp.dot(mlp_low, route_full, preferred_element_type=jnp.float32)
    selector = (routes[:, :, None] == jnp.arange(EXPERTS, dtype=jnp.int32)[None, None, :]).astype(
        jnp.float32
    )
    chosen = jnp.sum(logits[:, None, :] * selector, axis=-1)
    gate_values, pull_gate = jax.vjp(
        lambda picked_logits: jax.nn.softmax(picked_logits, axis=-1), chosen
    )
    slot_index = slot_table(routes)
    outgoing = (
        jnp.zeros((EXPERTS * CAP, model_width), jnp.bfloat16)
        .at[slot_index]
        .set(jnp.repeat(mlp_low, 2, axis=0))
    )
    arrived = lax.all_to_all(
        outgoing.reshape(wide_count, slice_rows, model_width),
        "wide",
        split_axis=0,
        concat_axis=0,
        tiled=True,
    )
    expert_in = arrived.reshape(wide_count * slice_rows, model_width)
    shared_pre = jnp.dot(mlp_low, up_full, preferred_element_type=jnp.float32)
    shared_act = gelu_tanh(shared_pre).astype(jnp.bfloat16)
    shared_part = contract(shared_act, down_full, (1,), (1,))
    expert_pre = jnp.dot(expert_in, expert_up, preferred_element_type=jnp.float32)
    expert_act = gelu_tanh(expert_pre).astype(jnp.bfloat16)
    expert_part = contract(expert_act, expert_down, (1,), (1,))
    expert_sum, shared_out = (
        lax.psum(expert_part.astype(jnp.bfloat16), "narrow").astype(jnp.float32),
        lax.psum(shared_part.astype(jnp.bfloat16), "narrow").astype(jnp.float32),
    )
    expert_out = expert_sum.astype(jnp.bfloat16)
    returned = lax.all_to_all(
        expert_out.reshape(wide_count, slice_rows, model_width),
        "wide",
        split_axis=0,
        concat_axis=0,
        tiled=True,
    )
    returned = returned.reshape(EXPERTS * CAP, model_width)
    picked = returned[slot_index].astype(jnp.float32).reshape(row_count, 2, model_width)
    mixture = jnp.sum(gate_values[:, :, None] * picked, axis=1)
    branch = (shared_out + mixture).reshape(images, patches, model_width)
    output = hidden_state + modulation[:, 5][:, None, :] * branch
    grad_out = cotangent.astype(jnp.float32).reshape(images, patches, model_width)
    grad_branch = (modulation[:, 5][:, None, :] * grad_out).reshape(row_count, model_width)
    grad_gate2 = jnp.sum(grad_out * branch, axis=1)
    grad_pick = jnp.sum(grad_branch[:, None, :] * picked, axis=-1)
    grad_rows = (
        (gate_values[:, :, None] * grad_branch[:, None, :])
        .astype(jnp.bfloat16)
        .reshape(row_count * 2, model_width)
    )
    grad_slots = jnp.zeros((EXPERTS * CAP, model_width), jnp.bfloat16).at[slot_index].set(grad_rows)
    grad_expert_out = lax.all_to_all(
        grad_slots.reshape(wide_count, slice_rows, model_width),
        "wide",
        split_axis=0,
        concat_axis=0,
        tiled=True,
    )
    grad_expert_out = grad_expert_out.reshape(wide_count * slice_rows, model_width)
    grad_shared = grad_branch.astype(jnp.bfloat16)
    shared_down_grad = contract(grad_shared, shared_act, (0,), (0,))
    grad_shared_act = jnp.dot(grad_shared, down_full, preferred_element_type=jnp.float32)
    grad_shared_pre = gelu_back(shared_pre, grad_shared_act).astype(jnp.bfloat16)
    shared_up_grad = contract(mlp_low, grad_shared_pre, (0,), (0,))
    grad_in_shared = contract(grad_shared_pre, up_full, (1,), (1,))
    grad_chosen = pull_gate(grad_pick)[0]
    grad_logits = jnp.sum(grad_chosen[:, :, None] * selector, axis=1).astype(jnp.bfloat16)
    route_grad = contract(mlp_low, grad_logits, (0,), (0,))
    grad_in_route = contract(grad_logits, route_full, (1,), (1,))
    expert_down_grad = contract(grad_expert_out, expert_act, (0,), (0,))
    grad_expert_act = jnp.dot(grad_expert_out, expert_down, preferred_element_type=jnp.float32)
    grad_expert_pre = gelu_back(expert_pre, grad_expert_act).astype(jnp.bfloat16)
    expert_up_grad = contract(expert_in, grad_expert_pre, (0,), (0,))
    grad_in_part = contract(grad_expert_pre, expert_up, (1,), (1,))
    grad_in_rows, grad_in_shared_sum = (
        lax.psum(grad_in_part.astype(jnp.bfloat16), "narrow").astype(jnp.float32),
        lax.psum(grad_in_shared.astype(jnp.bfloat16), "narrow").astype(jnp.float32),
    )
    back_rows = lax.all_to_all(
        grad_in_rows.astype(jnp.bfloat16).reshape(wide_count, slice_rows, model_width),
        "wide",
        split_axis=0,
        concat_axis=0,
        tiled=True,
    )
    back_rows = back_rows.reshape(EXPERTS * CAP, model_width)
    grad_in_expert = jnp.sum(
        back_rows[slot_index].astype(jnp.float32).reshape(row_count, 2, model_width), axis=1
    )
    grad_mlp_in = grad_in_shared_sum + grad_in_route + grad_in_expert
    grad_hidden_norm, grad_shift2, grad_scale2 = pull_second(
        grad_mlp_in.reshape(images, patches, model_width)
    )
    grad_hidden = grad_out + grad_hidden_norm
    grad_gate1 = jnp.sum(grad_hidden * attn_three, axis=1)
    grad_attn = (
        (modulation[:, 2][:, None, :] * grad_hidden)
        .reshape(row_count, model_width)
        .astype(jnp.bfloat16)
    )
    proj_grad = contract(grad_attn, mixed_low, (0,), (0,))
    grad_mixed = jnp.dot(grad_attn, proj_full, preferred_element_type=jnp.float32).astype(
        jnp.bfloat16
    )
    grad_mixed = grad_mixed.reshape(images, patches, heads_here, head_dim)
    again_scores = (
        jnp.einsum("bqhd,bkhd->bhqk", queries, keys, preferred_element_type=jnp.float32)
        * scale_factor
    )
    probs_full = jnp.exp(again_scores - log_total)
    again_low = probs_full.astype(jnp.bfloat16)
    grad_probs = jnp.einsum(
        "bqhd,bkhd->bhqk", grad_mixed, values, preferred_element_type=jnp.float32
    )
    grad_values = jnp.einsum(
        "bhqk,bqhd->bkhd", again_low, grad_mixed, preferred_element_type=jnp.float32
    )
    weighted_sum = jnp.sum(probs_full * grad_probs, axis=-1, keepdims=True)
    grad_scores = (probs_full * (grad_probs - weighted_sum)).astype(jnp.bfloat16)
    grad_queries = (
        jnp.einsum("bhqk,bkhd->bqhd", grad_scores, keys, preferred_element_type=jnp.float32)
        * scale_factor
    )
    grad_keys = (
        jnp.einsum("bhqk,bqhd->bkhd", grad_scores, queries, preferred_element_type=jnp.float32)
        * scale_factor
    )
    grad_qkv = jnp.stack([grad_queries, grad_keys, grad_values], axis=2).astype(jnp.bfloat16)
    grad_qkv = grad_qkv.reshape(row_count, 3 * head_width)
    qkv_grad = contract(attn_low, grad_qkv, (0,), (0,)).reshape(model_width, 3, head_width)
    grad_attn_part = contract(grad_qkv, qkv_full.reshape(model_width, 3 * head_width), (1,), (1,))
    grad_attn_in = lax.psum(grad_attn_part.astype(jnp.bfloat16), "narrow").astype(jnp.float32)
    grad_input_norm, grad_shift1, grad_scale1 = pull_first(
        grad_attn_in.reshape(images, patches, model_width)
    )
    tokens_grad = (grad_hidden + grad_input_norm).reshape(row_count, model_width)
    grad_modulation = jnp.stack(
        [grad_shift1, grad_scale1, grad_gate1, grad_shift2, grad_scale2, grad_gate2], axis=1
    )
    grad_modulation = grad_modulation.reshape(images, 6 * model_width)
    grad_mod_every = lax.all_gather(grad_modulation, "wide", axis=0, tiled=True)
    ada_part = jnp.dot(cond_own.astype(jnp.float32).T, grad_mod_every, precision=highest).reshape(
        ada_rows, 6, model_width
    )
    qkv_part, proj_part, route_part, shared_up_part, shared_down_part = (
        lax.psum_scatter(qkv_grad, "wide", scatter_dimension=0, tiled=True),
        lax.psum_scatter(proj_grad, "wide", scatter_dimension=0, tiled=True),
        lax.psum_scatter(route_grad, "wide", scatter_dimension=0, tiled=True),
        lax.psum_scatter(shared_up_grad, "wide", scatter_dimension=0, tiled=True),
        lax.psum_scatter(shared_down_grad, "wide", scatter_dimension=0, tiled=True),
    )
    expert_grads = jnp.stack([expert_up_grad, expert_down_grad])
    for bit_level in reversed(range(levels)):
        expert_grads = split_halves(expert_grads, bit_level, wide_place)
    return (
        output.reshape(row_count, model_width).astype(jnp.bfloat16),
        tokens_grad,
        ada_part,
        qkv_part,
        proj_part,
        route_part,
        shared_up_part,
        shared_down_part,
        expert_grads[0],
        expert_grads[1],
    )


MESH = pl.DeviceIdType.MESH
F32 = jnp.float32
BF16 = jnp.bfloat16
Z_SIZE, Y_SIZE, X_SIZE = 4, 2, 2
VMEM_LIMIT = 60 * 1024 * 1024


def place(index):
    return lax.div(index, 4), lax.rem(lax.div(index, 2), 2), lax.rem(index, 2)


def at_place(z, y, x):
    return z * 4 + y * 2 + x


class Sends:
    def __init__(self):
        self.items = []

    def go(self, make, when=None):
        self.items.append((make, when))
        guarded(when, lambda: make().start())

    def drain(self):
        for make, when in self.items:
            guarded(when, lambda make=make: make().wait_send())


def guarded(when, action):
    if when is None:
        action()
        return

    @pl.when(when)
    def _():
        action()


def both(first, second):
    if first is None:
        return second
    if second is None:
        return first
    return jnp.logical_and(first, second)


def remote(src, dst, send_sem, recv_sem, target):
    return pltpu.make_async_remote_copy(
        src_ref=src,
        dst_ref=dst,
        send_sem=send_sem,
        recv_sem=recv_sem,
        device_id=target,
        device_id_type=MESH,
    )


def greet(targets):
    barrier = pltpu.get_barrier_semaphore()
    for target in targets:
        pl.semaphore_signal(barrier, inc=1, device_id=target, device_id_type=MESH)
    pl.semaphore_wait(barrier, len(targets))


class Gather:
    def __init__(self, streams, send_sem, recv_sem, sends):
        self.streams, self.ss, self.rs, self.sends = streams, send_sem, recv_sem, sends
        self.count = [0] * len(streams)
        self.core = lax.axis_index("narrow")
        self.me = lax.axis_index("wide")
        self.z, self.y, self.x = place(self.me)
        self.to_x = at_place(self.z, self.y, 1 - self.x)
        self.to_y = at_place(self.z, 1 - self.y, self.x)
        self.can_up, self.can_down = self.z < Z_SIZE - 1, self.z > 0
        self.up, self.down = self.me + 4, self.me - 4

    def block(self, s, origin):
        shard, full, start, width, _ = self.streams[s]
        rows = shard.shape[0]
        return full.at[pl.ds(pl.multiple_of(origin * rows, 16), rows), pl.ds(start, width)]

    def send(self, s, origin, target, when=None, own=False):
        shard, full, start, width, _ = self.streams[s]
        index = self.count[s]
        self.count[s] += 1

        def make():
            dst = self.block(s, origin)
            src = shard.at[:, pl.ds(start, width)] if own else dst
            return remote(src, dst, self.ss.at[s, index], self.rs.at[s, origin], (target, self.core))

        self.sends.go(make, when)

    def wait(self, s, origin, when=None):
        def action():
            ref = self.block(s, origin)
            remote(
                ref, ref, self.ss.at[s, 0], self.rs.at[s, origin], (self.to_x, self.core)
            ).wait_recv()

        guarded(when, action)

    def spread(self, s, origin, when=None, own=False, up=True, down=True, over_y=True):
        if up:
            self.send(s, origin, self.up, both(when, self.can_up), own)
        if down:
            self.send(s, origin, self.down, both(when, self.can_down), own)
        if over_y:
            self.send(s, origin, self.to_y, when, own)

    def begin(self, s):
        self.send(s, self.me, self.to_x, own=True)
        self.spread(s, self.me, own=True)

    def after_x(self, s):
        self.wait(s, self.to_x)
        self.spread(s, self.to_x)

    def y_pair(self, s):
        if self.streams[s][4] == "xyz":
            for xx in (self.x, 1 - self.x):
                origin = at_place(self.z, 1 - self.y, xx)
                self.wait(s, origin)
                self.spread(s, origin, over_y=False)

    def after_z(self, s, distance):
        order = self.streams[s][4]
        ys = (self.y,) if order == "xzy" else (self.y, 1 - self.y)
        for step, ok in ((-distance, self.z >= distance), (distance, self.z + distance < Z_SIZE)):
            for yy in ys:
                for xx in (self.x, 1 - self.x):
                    origin = at_place(self.z + step, yy, xx)
                    self.wait(s, origin, ok)
                    self.spread(s, origin, ok, up=step < 0, down=step > 0, over_y=order == "xzy")

    def finish(self, s):
        if self.streams[s][4] == "xzy":
            for zz in range(Z_SIZE):
                for xx in range(X_SIZE):
                    self.wait(s, at_place(zz, 1 - self.y, xx))


def vmem(count):
    return [pl.BlockSpec(memory_space=pltpu.VMEM)] * count


def hbm(count):
    return [pl.BlockSpec(memory_space=pl.ANY)] * count


def params(collective_id):
    return pltpu.CompilerParams(
        collective_id=collective_id, has_side_effects=True, vmem_limit_bytes=VMEM_LIMIT
    )


def swap_kernel(count, *refs):
    ins, outs, (ss, rs) = refs[:count], refs[count : 2 * count], refs[2 * count :]
    me, core = lax.axis_index("wide"), lax.axis_index("narrow")
    peer = (me, 1 - core)
    greet([peer])
    copies = [remote(ins[i], outs[i], ss.at[i], rs.at[i], peer) for i in range(count)]
    for copy in copies:
        copy.start()
    for copy in copies:
        copy.wait()


def swap_cores(collective_id, *arrays):
    count = len(arrays)
    return pl.pallas_call(
        functools.partial(swap_kernel, count),
        out_shape=[jax.ShapeDtypeStruct(a.shape, a.dtype) for a in arrays],
        in_specs=vmem(count),
        out_specs=vmem(count),
        scratch_shapes=[pltpu.SemaphoreType.DMA((count,)), pltpu.SemaphoreType.DMA((count,))],
        compiler_params=params(collective_id),
        name="swap_cores",
    )(*arrays)


def peers_far_first(me):
    z, y, x = place(me)
    found = []
    for dz in range(Z_SIZE):
        for dy in range(Y_SIZE):
            for dx in range(X_SIZE):
                if dz or dy or dx:
                    zz = lax.rem(z + dz, Z_SIZE)
                    found.append(at_place(zz, lax.rem(y + dy, 2), lax.rem(x + dx, 2)))
    return found[::-1]


def bring_back_kernel(
    out_ref, grad_ref, shared_ref, shared_grad_ref,
    out_back, grad_back, shared_sum, shared_grad_sum,
    their_out, their_grad, their_shared, their_shared_grad, sum_out, sum_grad,
    near_ss, near_rs, ss, rs, own_sem,
):
    me, core = lax.axis_index("wide"), lax.axis_index("narrow")
    others = peers_far_first(me)
    peer = (me, 1 - core)
    greet([(other, core) for other in others] + [peer])
    count = lax.axis_size("wide")
    size = out_ref.shape[1] // count
    sends = Sends()

    def rows(index):
        return pl.ds(pl.multiple_of(index * size, 16), size)

    triples = ((out_ref, their_out, sum_out, out_back), (grad_ref, their_grad, sum_grad, grad_back))
    order = others + [me]
    for k, other in enumerate(order):
        for a, (src, theirs, _, _) in enumerate(triples):
            sends.go(
                lambda k=k, other=other, a=a, src=src, theirs=theirs: remote(
                    src.at[1 - core, rows(other), :], theirs.at[rows(other), :],
                    near_ss.at[a, k], near_rs.at[a, other], peer,
                )
            )
    small = ((shared_ref, their_shared, shared_sum), (shared_grad_ref, their_shared_grad, shared_grad_sum))
    for a, (src, theirs, _) in enumerate(small):
        sends.go(lambda a=a, src=src, theirs=theirs: remote(src.at[1 - core], theirs, near_ss.at[a, 16], near_rs.at[a, 16], peer))
    for k, other in enumerate(order):
        for a, (src, theirs, total, back) in enumerate(triples):
            here = theirs.at[rows(other), :]
            remote(here, here, near_ss.at[a, 0], near_rs.at[a, other], peer).wait_recv()
            total[rows(other), :] = (
                src[core, rows(other), :].astype(F32) + theirs[rows(other), :].astype(F32)
            ).astype(BF16)
            if k < len(others):
                sends.go(
                    lambda k=k, other=other, a=a, total=total, back=back: remote(
                        total.at[rows(other), :], back.at[rows(me), :],
                        ss.at[a, k], rs.at[a, me], (other, core),
                    )
                )
            else:
                own = pltpu.make_async_copy(total.at[rows(me), :], back.at[rows(me), :], own_sem.at[a])
                own.start()
                own.wait()
    for a, (src, theirs, result) in enumerate(small):
        remote(theirs, theirs, near_ss.at[a, 0], near_rs.at[a, 16], peer).wait_recv()
        result[...] = src[core].astype(F32) + theirs[...].astype(F32)
    for other in others[::-1]:
        for a, (_, _, _, back) in enumerate(triples):
            here = back.at[rows(other), :]
            remote(here, here, ss.at[a, 0], rs.at[a, other], peer).wait_recv()
    sends.drain()


def bring_back(out_part, grad_part, shared_part, shared_grad_part):
    _, total, width = out_part.shape
    local = shared_part.shape[1]
    dma = pltpu.SemaphoreType.DMA
    return pl.pallas_call(
        bring_back_kernel,
        out_shape=[jax.ShapeDtypeStruct((total, width), BF16)] * 2
        + [jax.ShapeDtypeStruct((local, width), F32)] * 2,
        in_specs=vmem(4),
        out_specs=vmem(4),
        scratch_shapes=[
            pltpu.VMEM((total, width), BF16), pltpu.VMEM((total, width), BF16),
            pltpu.VMEM((local, width), BF16), pltpu.VMEM((local, width), BF16),
            pltpu.VMEM((total, width), BF16), pltpu.VMEM((total, width), BF16),
            dma((2, 17)), dma((2, 17)), dma((2, 16)), dma((2, 16)), dma((2,)),
        ],
        compiler_params=params(3),
        name="bring_back",
    )(out_part, grad_part, shared_part, shared_grad_part)


def reduce_kernel(count, *refs):
    terms, vectors = refs[:count], refs[count]
    outs, every = refs[count + 1 : 2 * count + 1], refs[2 * count + 1]
    rest = refs[2 * count + 2 :]
    work, from_y = rest[:count], rest[count : 2 * count]
    from_z, from_x = rest[2 * count : 3 * count], rest[3 * count : 4 * count]
    y_ss, y_rs, z_ss, z_rs, x_ss, x_rs, vec_ss, vec_rs, load_sem = rest[4 * count :]
    me, core = lax.axis_index("wide"), lax.axis_index("narrow")
    z, y, x = place(me)
    others = peers_far_first(me)
    greet([(other, core) for other in others])
    sends = Sends()
    for k, other in enumerate(others):
        sends.go(lambda k=k, other=other: remote(vectors, every.at[me], vec_ss.at[k], vec_rs.at[me], (other, core)))
    every[me] = vectors[...]
    to_x, to_y = at_place(z, y, 1 - x), at_place(z, 1 - y, x)
    upper = z >= 2
    dest_z = [
        jnp.where(upper, 0, 3), jnp.where(upper, 1, 2), jnp.where(upper, 5 - z, 1 - z), z
    ]

    def rows(i, index):
        size = terms[i].shape[0] // lax.axis_size("wide")
        return pl.ds(pl.multiple_of(index * size, 16), size)

    for k in range(4):
        for i in range(count):
            for xx in range(2):
                there = at_place(dest_z[k], 1 - y, xx)
                sends.go(
                    lambda k=k, i=i, xx=xx, there=there: remote(
                        terms[i].at[rows(i, there), :], from_y[i].at[dest_z[k], xx],
                        y_ss.at[i, k * 2 + xx], y_rs.at[i, dest_z[k] * 2 + xx], (to_y, core),
                    )
                )

    def landed(ref, recv_sem):
        remote(ref, ref, y_ss.at[0, 0], recv_sem, (to_y, core)).wait_recv()

    for k in range(4):
        zz = dest_z[k]
        going_up = zz > z
        for i in range(count):
            for xx in range(2):
                landed(from_y[i].at[zz, xx], y_rs.at[i, zz * 2 + xx])
                here = rows(i, at_place(zz, y, xx))
                work[i][zz, xx] = (
                    terms[i][here, :].astype(F32) + from_y[i][zz, xx].astype(F32)
                ).astype(BF16)

                def add(came, i=i, xx=xx, zz=zz):
                    landed(from_z[i].at[came, zz, xx], z_rs.at[i, (came * 4 + zz) * 2 + xx])
                    work[i][zz, xx] = (
                        work[i][zz, xx].astype(F32) + from_z[i][came, zz, xx].astype(F32)
                    ).astype(BF16)

                def pass_on(came, target, i=i, xx=xx, zz=zz, k=k):
                    return lambda: remote(
                        work[i].at[zz, xx], from_z[i].at[came, zz, xx],
                        z_ss.at[i, k * 2 + xx], z_rs.at[i, (came * 4 + zz) * 2 + xx], (target, core),
                    )

                if k < 3:
                    guarded(jnp.logical_and(going_up, z > 0), lambda: add(0))
                    guarded(jnp.logical_and(zz < z, z < 3), lambda: add(1))
                    sends.go(pass_on(0, me + 4), going_up)
                    sends.go(pass_on(1, me - 4), zz < z)
                else:
                    guarded(z > 0, lambda: add(0))
                    guarded(z < 3, lambda: add(1))
        if k == 3:
            for i in range(count):
                sends.go(
                    lambda i=i: remote(work[i].at[z, 1 - x], from_x[i], x_ss.at[i], x_rs.at[i], (to_x, core))
                )
    for i in range(count):
        landed(from_x[i], x_rs.at[i])
        outs[i][...] = work[i][z, x].astype(F32) + from_x[i][...].astype(F32)
    for other in others:
        landed(every.at[other], vec_rs.at[other])
    sends.drain()


def reduce_rows(vectors, *terms):
    count = len(terms)
    shapes = [(t.shape[0] // 16, t.shape[1]) for t in terms]
    dma = pltpu.SemaphoreType.DMA
    return pl.pallas_call(
        functools.partial(reduce_kernel, count),
        out_shape=[jax.ShapeDtypeStruct(s, F32) for s in shapes]
        + [jax.ShapeDtypeStruct((16, *vectors.shape), F32)],
        in_specs=vmem(count + 1),
        out_specs=vmem(count + 1),
        scratch_shapes=[pltpu.VMEM((4, 2, *s), BF16) for s in shapes]
        + [pltpu.VMEM((4, 2, *s), BF16) for s in shapes]
        + [pltpu.VMEM((2, 4, 2, *s), BF16) for s in shapes]
        + [pltpu.VMEM(s, BF16) for s in shapes]
        + [
            dma((count, 8)), dma((count, 8)), dma((count, 6)), dma((count, 16)),
            dma((count,)), dma((count,)), dma((16,)), dma((16,)), dma((1,)),
        ],
        compiler_params=params(4),
        name="reduce_rows",
    )(*terms, vectors)


def lanes_of(ref, vector):
    rows = ref.shape[0] // 6
    return jnp.concatenate(
        [ref[rows * vector + i : rows * vector + i + 1, :] for i in range(rows)], axis=1
    )


def head_masks(rows):
    lane = lax.broadcasted_iota(jnp.int32, (rows, 128), 1)
    first = (lane < 64).astype(F32)
    return first, 1.0 - first


def choice_masks(routes_ref):
    rows = routes_ref.shape[0]
    lane = lax.broadcasted_iota(jnp.int32, (rows, 128), 1)
    named = [(routes_ref[:, k : k + 1] == lane).astype(F32) for k in range(2)]
    above = lax.broadcasted_iota(jnp.int32, (rows, rows), 0)
    along = lax.broadcasted_iota(jnp.int32, (rows, rows), 1)
    before = jnp.dot(
        (along < above).astype(F32).astype(BF16),
        (named[0] + named[1]).astype(BF16),
        preferred_element_type=F32,
    )
    slot = lax.broadcasted_iota(jnp.int32, (rows, EXPERTS * CAP), 1)
    takes = []
    for k in range(2):
        rank = jnp.sum(before * named[k], axis=1, keepdims=True)
        own = routes_ref[:, k : k + 1].astype(F32) * CAP + rank
        takes.append((slot == own.astype(jnp.int32)).astype(F32).astype(BF16))
    return named, takes


def attend(attn_low, qkv_ref, act_ref, probs_ref, mixed_ref, pump):
    rows, width = attn_low.shape[0], mixed_ref.shape[1]
    for j in range(3):
        act_ref[:, width * j : width * (j + 1)] = jnp.dot(
            attn_low, qkv_ref[:, width * j : width * (j + 1)], preferred_element_type=F32
        ).astype(BF16)
        pump()
    masks = head_masks(rows)
    scale_factor = 64 ** (-0.5)
    for pair in range(width // 128):
        q, k, v = [
            act_ref[:, width * j + 128 * pair : width * j + 128 * (pair + 1)] for j in range(3)
        ]
        mixed = None
        for h in range(2):
            scores = contract(q * masks[h].astype(BF16), k, (1,), (1,)) * scale_factor
            top = jnp.max(scores, axis=-1, keepdims=True)
            weights = jnp.exp(scores - top)
            probs = weights / jnp.sum(weights, axis=-1, keepdims=True)
            probs_ref[2 * pair + h] = probs
            part = jnp.dot(probs.astype(BF16), v, preferred_element_type=F32) * masks[h]
            mixed = part if mixed is None else mixed + part
            pump()
        mixed_ref[:, 128 * pair : 128 * (pair + 1)] = mixed.astype(BF16)


def forward_kernel(
    ts_ref, table_ref, ada_ref, qkv_ref, proj_ref, route_ref, up_ref, down_ref,
    eup_ref, edown_ref, tok_ref, cot_ref, routes_ref,
    mod_ref, cond_ref, qkv_out, proj_out, route_out, act_ref, probs_ref, mixed_ref,
    attn_ref, attn_low_ref, mlp_ref, gshared_ref, gates_ref,
    up_out, down_out, eup_out, edown_out, rows_out, grads_out,
    ts_all, terms, landed, part, theirs, gate_row, rows_send, grads_send,
    ts_ss, ts_rs, mod_ss, mod_rs, ag_ss, ag_rs, own_sem, join_ss, join_rs, swap_sem,
    ss, rs, pass_ss, pass_rs, own_a,
):
    me, core = lax.axis_index("wide"), lax.axis_index("narrow")
    count = lax.axis_size("wide")
    others = peers_far_first(me)
    peer = (me, 1 - core)
    greet([(other, core) for other in others] + [peer])
    sends = Sends()
    for k, other in enumerate(others):
        sends.go(lambda k=k, other=other: remote(ts_ref, ts_all.at[me], ts_ss.at[k], ts_rs.at[me], (other, core)))
    half = down_ref.shape[1] // 2
    streams = [
        (qkv_ref, qkv_out, 0, qkv_ref.shape[1], "xzy"),
        (proj_ref, proj_out, 0, proj_ref.shape[1], "xzy"),
        (route_ref, route_out, 0, route_ref.shape[1], "xzy"),
        (up_ref, up_out, 0, up_ref.shape[1], "xzy"),
        (down_ref, down_out, 0, half, "xzy"),
        (down_ref, down_out, half, half, "xyz"),
    ]
    ag = Gather(streams, ag_ss, ag_rs, sends)
    for s in range(3):
        ag.begin(s)
    own = []
    for i, (shard, full) in enumerate(
        ((qkv_ref, qkv_out), (proj_ref, proj_out), (route_ref, route_out), (up_ref, up_out), (down_ref, down_out))
    ):
        rows = shard.shape[0]
        own.append(
            pltpu.make_async_copy(
                shard, full.at[pl.ds(pl.multiple_of(me * rows, 16), rows), :], own_sem.at[i]
            )
        )
        own[-1].start()

    tokens = tok_ref[...].astype(F32)
    normal1, _ = normalized(tokens)

    ts_all[me] = ts_ref[...]
    for other in others[::-1]:
        remote(ts_ref, ts_all.at[other], ts_ss.at[0], ts_rs.at[other], (other, core)).wait_recv()
    steps = jnp.max(ts_all[...], axis=1)[:, :1]
    onehot = (
        steps == lax.broadcasted_iota(jnp.int32, (count, table_ref.shape[0]), 1)
    ).astype(F32).astype(BF16)
    cond = jnp.dot(onehot, table_ref[...], preferred_element_type=F32)
    cond_act = (cond * jax.nn.sigmoid(cond)).astype(BF16)
    cond_ref[...] = cond_act.astype(F32)
    chunks = terms.shape[1] // 6
    for j in range(6):
        vector = jnp.dot(
            cond_act,
            ada_ref[:, 128 * chunks * j : 128 * chunks * (j + 1)],
            preferred_element_type=F32,
        )
        for i in range(chunks):
            terms[:, chunks * j + i, :] = vector[:, 128 * i : 128 * (i + 1)]
    for k, other in enumerate(others):
        sends.go(lambda k=k, other=other: remote(terms.at[other], landed.at[me], mod_ss.at[k], mod_rs.at[me], (other, core)))
    for s in range(3):
        ag.after_x(s)

    pieces = 4
    joins = []
    for a, (src, dst) in enumerate(((eup_ref, eup_out), (edown_ref, edown_out))):
        size = src.shape[0] // pieces
        for p in range(pieces):
            cut = pl.ds(p * size, size)
            joins.append(
                lambda a=a, p=p, src=src, dst=dst, cut=cut: remote(
                    src.at[cut, :], dst.at[cut, :],
                    join_ss.at[a * pieces + p], join_rs.at[a * pieces + p], (ag.to_x, core),
                )
            )

    for distance in range(1, Z_SIZE):
        for s in range(3):
            ag.after_z(s, distance)
    for s in range(3, len(streams)):
        ag.begin(s)
    for make in joins[:4]:
        sends.go(make)
    landed[me] = terms[me]
    for other in others[::-1]:
        remote(terms.at[me], landed.at[other], mod_ss.at[0], mod_rs.at[other], (other, core)).wait_recv()
    mod_ref[...] = jnp.sum(landed[...], axis=0)
    shift1, scale1, gate1, shift2, scale2, gate2 = [lanes_of(mod_ref, j) for j in range(6)]
    attn_low_ref[...] = (normal1 * (1.0 + scale1) + shift1).astype(BF16)
    bulk = range(3, len(streams))
    queue = [lambda s=s: ag.after_x(s) for s in bulk]
    queue += [lambda s=s: ag.y_pair(s) for s in bulk]
    queue += [lambda s=s, d=d: ag.after_z(s, d) for d in range(1, Z_SIZE) for s in bulk]

    def pump():
        if queue:
            queue.pop(0)()

    ag.finish(0)
    own[0].wait()
    attend(attn_low_ref[...], qkv_out, act_ref, probs_ref, mixed_ref, pump)
    ag.finish(1)
    own[1].wait()
    part[...] = contract(mixed_ref[...], proj_out[...], (1,), (1,)).astype(BF16)
    swap = remote(part, theirs, swap_sem.at[0], swap_sem.at[1], peer)
    swap.start()
    named, takes = choice_masks(routes_ref)
    gate_row[...] = jnp.broadcast_to(gate2, gate_row.shape)
    gshared_ref[...] = (gate2 * cot_ref[...].astype(F32)).astype(BF16)
    pump()
    swap.wait()
    attn_out = part[...].astype(F32) + theirs[...].astype(F32)
    attn_ref[...] = attn_out
    hidden = tok_ref[...].astype(F32) + gate1 * attn_out
    normal2, _ = normalized(hidden)
    mlp_ref[...] = (normal2 * (1.0 + scale2) + shift2).astype(BF16)
    ag.finish(2)
    own[2].wait()
    logits = jnp.dot(mlp_ref[...], route_out[...], preferred_element_type=F32)
    chosen = [jnp.sum(logits * named[k], axis=1, keepdims=True) for k in range(2)]
    peak = jnp.maximum(chosen[0], chosen[1])
    weight = [jnp.exp(chosen[k] - peak) for k in range(2)]
    total = weight[0] + weight[1]
    gates = [weight[k] / total for k in range(2)]
    lane = lax.broadcasted_iota(jnp.int32, gates_ref.shape, 1)
    gates_ref[...] = jnp.where(lane == 0, gates[0], jnp.where(lane == 1, gates[1], 0.0))
    width = rows_send.shape[1]
    mine = pl.ds(pl.multiple_of(core * width, 128), width)
    grad_half = gate_row[0:1, mine] * cot_ref[:, mine].astype(F32)
    rows_send[...] = contract(takes[0] + takes[1], mlp_ref[:, mine], (0,), (0,)).astype(BF16)
    grads_send[...] = (
        contract(takes[0], (gates[0] * grad_half).astype(BF16), (0,), (0,))
        + contract(takes[1], (gates[1] * grad_half).astype(BF16), (0,), (0,))
    ).astype(BF16)

    size = rows_send.shape[0] // count

    def rows(index):
        return pl.ds(pl.multiple_of(index * size, 16), size)

    pairs = ((rows_send, rows_out), (grads_send, grads_out))
    for k, other in enumerate(others):
        for a, (src, dst) in enumerate(pairs):
            sends.go(
                lambda k=k, other=other, a=a, src=src, dst=dst: remote(
                    src.at[rows(other), :], dst.at[core, rows(me), :],
                    ss.at[a, k], rs.at[a, me], (other, core),
                )
            )
    for make in joins[4:]:
        sends.go(make)
    kept = []
    for a, (src, dst) in enumerate(pairs):
        sends.go(
            lambda a=a, src=src, dst=dst: remote(
                src.at[rows(me), :], dst.at[core, rows(me), :], pass_ss.at[a, 15], pass_rs.at[a, me], peer
            )
        )
        kept.append(pltpu.make_async_copy(src.at[rows(me), :], dst.at[core, rows(me), :], own_a.at[a]))
        kept[-1].start()
    while queue:
        pump()
    for k, other in enumerate(others[::-1]):
        for a, (src, dst) in enumerate(pairs):
            here = dst.at[core, rows(other), :]
            remote(here, here, ss.at[a, 0], rs.at[a, other], peer).wait_recv()
            sends.go(
                lambda k=k, other=other, a=a, here=here: remote(
                    here, here, pass_ss.at[a, k], pass_rs.at[a, other], peer
                )
            )
    for s in range(3, len(streams)):
        ag.finish(s)
    for i, make in enumerate(joins):
        make().wait_recv()
    for other in [me] + others[::-1]:
        for a, (src, dst) in enumerate(pairs):
            there = dst.at[1 - core, rows(other), :]
            remote(there, there, pass_ss.at[a, 0], pass_rs.at[a, other], peer).wait_recv()
    for copy in own[3:] + kept:
        copy.wait()
    sends.drain()


def forward(ts_tile, table, ada, qkv, proj, route, up, down, e_up, e_down, tokens, cotangent, routes):
    count = 16
    shards = (qkv, proj, route, up, down)
    vectors = ada.shape[1] // 128
    patches, width = tokens.shape
    slots = EXPERTS * CAP
    dma = pltpu.SemaphoreType.DMA
    shape = jax.ShapeDtypeStruct

    def full(a):
        return shape((count * a.shape[0], a.shape[1]), a.dtype)

    return pl.pallas_call(
        forward_kernel,
        out_shape=[
            shape((vectors, 128), F32), shape((count, table.shape[1]), F32),
            full(qkv), full(proj), full(route),
            shape((patches, qkv.shape[1]), BF16), shape((proj.shape[1] // 64, patches, patches), F32),
            shape((patches, proj.shape[1]), BF16), shape((patches, width), F32),
            shape((patches, width), BF16), shape((patches, width), BF16),
            shape((patches, width), BF16), shape((patches, 128), F32),
            full(up), full(down), shape(e_up.shape, BF16), shape(e_down.shape, BF16),
            shape((2, slots, width // 2), BF16), shape((2, slots, width // 2), BF16),
        ],
        in_specs=vmem(8) + hbm(2) + vmem(3),
        out_specs=vmem(13) + hbm(6),
        scratch_shapes=[
            pltpu.VMEM((count, 8, 128), jnp.int32),
            pltpu.VMEM((count, vectors, 128), F32),
            pltpu.VMEM((count, vectors, 128), F32),
            pltpu.VMEM((patches, width), BF16), pltpu.VMEM((patches, width), BF16),
            pltpu.VMEM((8, width), F32),
            pltpu.VMEM((slots, width // 2), BF16), pltpu.VMEM((slots, width // 2), BF16),
            dma((16,)), dma((16,)), dma((16,)), dma((16,)),
            dma((6, 40)), dma((6, 16)), dma((5,)), dma((8,)), dma((8,)), dma((2,)),
            dma((2, 16)), dma((2, 16)), dma((2, 16)), dma((2, 16)), dma((2,)),
        ],
        compiler_params=params(1),
        name="forward",
    )(ts_tile, table, ada, *shards, e_up, e_down, tokens, cotangent, routes)


def normalized(values):
    centre = jnp.mean(values, axis=-1, keepdims=True)
    shifted = values - centre
    spread = jnp.mean(shifted * shifted, axis=-1, keepdims=True)
    rate = lax.rsqrt(spread + epsilon)
    return shifted * rate, rate


def norm_back(normal, rate, gradient):
    mean = jnp.mean(gradient, axis=-1, keepdims=True)
    along = jnp.mean(gradient * normal, axis=-1, keepdims=True)
    return rate * (gradient - mean - normal * along)


def halves(array, core):
    width = array.shape[-1] // 2
    return jnp.stack([array[:, :width], array[:, width:]])


def own_half(array, core):
    width = array.shape[-1] // 2
    return lax.dynamic_slice_in_dim(array, core * width, width, array.ndim - 1)


def per_device_direct(
    tokens, cotangent, time_table, timesteps, routes, w_ada, w_qkv, w_proj,
    w_route, w_shared_up, w_shared_down, e_up, e_down,
):
    row_count, model_width = tokens.shape
    core = lax.axis_index("narrow")
    core_count = lax.axis_size("narrow")
    wide_count = lax.axis_size("wide")
    heads_here = HEADS // core_count
    head_dim = model_width // HEADS
    head_width = heads_here * head_dim
    half = model_width // 2
    scale_factor = head_dim ** (-0.5)
    wide_place = lax.axis_index("wide")
    upper = wide_place % 2 == 1
    ada_rows = w_ada.shape[0]

    partner = [(i, i ^ 1) for i in range(wide_count)]
    table = lax.dynamic_slice_in_dim(time_table, wide_place * ada_rows, ada_rows, 1)
    table = jnp.pad(table, ((0, -table.shape[0] % 128), (0, 0)))
    ts_tile = jnp.broadcast_to(timesteps[:, None], (8, 128)).astype(jnp.int32)
    (
        mod, cond_own, qkv_full, proj_full, route_full, activated, probs_full, mixed_low,
        attn_out, attn_low, mlp_low, grad_shared, gate_lanes,
        up_full, down_full, up_other, down_other, expert_in, grad_expert_out,
    ) = forward(
        ts_tile,
        table,
        w_ada.reshape(ada_rows, 6 * model_width),
        w_qkv.reshape(ada_rows, 3 * head_width),
        w_proj,
        jnp.pad(w_route, ((0, 0), (0, 128 - EXPERTS))),
        w_shared_up,
        w_shared_down,
        e_up,
        e_down,
        tokens,
        cotangent,
        routes,
    )
    modulation = mod.reshape(6, model_width)
    shift1, scale1, gate1, shift2, scale2, gate2 = [modulation[j][None, :] for j in range(6)]
    inputs = tokens.astype(F32)
    normal1, rate1 = normalized(inputs)
    activated = activated.reshape(row_count, 3, heads_here, head_dim)
    queries, keys, values = activated[:, 0], activated[:, 1], activated[:, 2]
    probs_low = probs_full.astype(BF16)
    hidden = inputs + gate1 * attn_out
    normal2, rate2 = normalized(hidden)
    lanes = jnp.arange(route_full.shape[1], dtype=jnp.int32)
    pick = [(routes[:, k : k + 1] == lanes[None, :]).astype(F32) for k in range(2)]
    gates = [gate_lanes[:, k : k + 1] for k in range(2)]
    flat = routes.reshape(-1)
    matches = (flat[:, None] == jnp.arange(EXPERTS, dtype=jnp.int32)[None, :]).astype(BF16)
    steps = jnp.arange(flat.shape[0], dtype=jnp.int32)
    before = (steps[None, :] < steps[:, None]).astype(BF16)
    earlier = jnp.dot(before, matches, preferred_element_type=F32)
    ranking = jnp.sum(earlier * matches.astype(F32), axis=1).astype(jnp.int32)
    slots = (flat * CAP + ranking).reshape(row_count, 2)
    slot_ids = jnp.arange(EXPERTS * CAP, dtype=jnp.int32)
    take_out = [(slots[:, k : k + 1] == slot_ids[None, :]).astype(BF16) for k in range(2)]
    grad_out = cotangent.astype(F32)
    grad_branch_half = own_half(gate2 * grad_out, core)

    shared_pre = jnp.dot(mlp_low, up_full, preferred_element_type=F32)
    shared_act = gelu_tanh(shared_pre).astype(BF16)
    shared_part = contract(shared_act, down_full, (1,), (1,)).astype(BF16)
    shared_down_grad = contract(grad_shared, shared_act, (0,), (0,)).astype(BF16)
    grad_shared_act = jnp.dot(grad_shared, down_full, preferred_element_type=F32)
    grad_shared_pre = gelu_back(shared_pre, grad_shared_act).astype(BF16)
    shared_up_grad = contract(mlp_low, grad_shared_pre, (0,), (0,)).astype(BF16)
    grad_in_shared = contract(grad_shared_pre, up_full, (1,), (1,)).astype(BF16)

    in_low, in_high = expert_in[0], expert_in[1]
    in_own, in_other = jnp.where(upper, in_high, in_low), jnp.where(upper, in_low, in_high)
    g_low, g_high = grad_expert_out[0], grad_expert_out[1]
    g_own, g_other = jnp.where(upper, g_high, g_low), jnp.where(upper, g_low, g_high)
    expert_pre = jnp.dot(in_own, e_up, preferred_element_type=F32) + jnp.dot(
        in_other, up_other, preferred_element_type=F32
    )
    expert_act = gelu_tanh(expert_pre).astype(BF16)
    out_own = contract(expert_act, e_down, (1,), (1,)).astype(BF16)
    out_other = contract(expert_act, down_other, (1,), (1,)).astype(BF16)
    grad_expert_act = jnp.dot(g_own, e_down, preferred_element_type=F32) + jnp.dot(
        g_other, down_other, preferred_element_type=F32
    )
    grad_expert_pre = gelu_back(expert_pre, grad_expert_act).astype(BF16)
    gi_own = contract(grad_expert_pre, e_up, (1,), (1,)).astype(BF16)
    gi_other = contract(grad_expert_pre, up_other, (1,), (1,)).astype(BF16)
    up_send = contract(in_other, grad_expert_pre, (0,), (0,)).astype(BF16)
    down_send = contract(g_other, expert_act, (0,), (0,)).astype(BF16)
    up_came = lax.ppermute(up_send, "wide", partner)
    down_came = lax.ppermute(down_send, "wide", partner)
    up_kept = contract(in_own, grad_expert_pre, (0,), (0,))
    down_kept = contract(g_own, expert_act, (0,), (0,))

    def in_order(own, other):
        return jnp.stack([jnp.where(upper, other, own), jnp.where(upper, own, other)])

    returned, back_rows, shared_half, grad_shared_half = bring_back(
        in_order(out_own, out_other),
        in_order(gi_own, gi_other),
        halves(shared_part, core),
        halves(grad_in_shared, core),
    )
    picked = [jnp.dot(take_out[k], returned, preferred_element_type=F32) for k in range(2)]
    branch_half = shared_half + gates[0] * picked[0] + gates[1] * picked[1]
    grad_mlp_half = grad_shared_half + jnp.dot(
        take_out[0] + take_out[1], back_rows, preferred_element_type=F32
    )
    gate_terms = jnp.concatenate(
        [jnp.sum(grad_branch_half * picked[k], axis=-1, keepdims=True) for k in range(2)], axis=1
    )
    gate_terms = jnp.pad(gate_terms, ((0, 0), (0, 126)))
    branch_theirs, grad_mlp_theirs, gate_theirs = swap_cores(
        6, branch_half, grad_mlp_half, gate_terms
    )

    def whole(mine, theirs):
        first = core == 0
        return jnp.concatenate(
            [jnp.where(first, mine, theirs), jnp.where(first, theirs, mine)], axis=1
        )

    branch = whole(branch_half, branch_theirs)
    grad_gates = gate_terms + gate_theirs
    inner = gates[0] * grad_gates[:, 0:1] + gates[1] * grad_gates[:, 1:2]
    grad_chosen = [gates[k] * (grad_gates[:, k : k + 1] - inner) for k in range(2)]
    grad_logits = (grad_chosen[0] * pick[0] + grad_chosen[1] * pick[1]).astype(BF16)
    route_grad = contract(mlp_low, grad_logits, (0,), (0,)).astype(BF16)
    grad_mlp_in = whole(grad_mlp_half, grad_mlp_theirs) + contract(
        grad_logits, route_full, (1,), (1,)
    )
    output = hidden + gate2 * branch
    grad_gate2 = jnp.sum(grad_out * branch, axis=0)
    grad_shift2 = jnp.sum(grad_mlp_in, axis=0)
    grad_scale2 = jnp.sum(grad_mlp_in * normal2, axis=0)
    grad_hidden = grad_out + norm_back(normal2, rate2, grad_mlp_in * (1.0 + scale2))
    grad_gate1 = jnp.sum(grad_hidden * attn_out, axis=0)
    grad_attn = (gate1 * grad_hidden).astype(BF16)
    proj_grad = contract(grad_attn, mixed_low, (0,), (0,)).astype(BF16)
    grad_mixed = jnp.dot(grad_attn, proj_full, preferred_element_type=F32).astype(BF16)
    grad_mixed = grad_mixed.reshape(row_count, heads_here, head_dim)
    grad_probs = jnp.einsum("qhd,khd->hqk", grad_mixed, values, preferred_element_type=F32)
    grad_values = jnp.einsum("hqk,qhd->khd", probs_low, grad_mixed, preferred_element_type=F32)
    weighted = jnp.sum(probs_full * grad_probs, axis=-1, keepdims=True)
    grad_scores = (probs_full * (grad_probs - weighted)).astype(BF16)
    grad_queries = (
        jnp.einsum("hqk,khd->qhd", grad_scores, keys, preferred_element_type=F32) * scale_factor
    )
    grad_keys = (
        jnp.einsum("hqk,qhd->khd", grad_scores, queries, preferred_element_type=F32)
        * scale_factor
    )
    grad_qkv = jnp.stack([grad_queries, grad_keys, grad_values], axis=1).astype(BF16)
    grad_qkv = grad_qkv.reshape(row_count, 3 * head_width)
    qkv_grad = contract(attn_low, grad_qkv, (0,), (0,)).astype(BF16)
    grad_attn_part = contract(grad_qkv, qkv_full, (1,), (1,)).astype(BF16)
    (grad_attn_theirs,) = swap_cores(7, grad_attn_part)
    grad_attn_in = grad_attn_part.astype(F32) + grad_attn_theirs.astype(F32)
    grad_shift1 = jnp.sum(grad_attn_in, axis=0)
    grad_scale1 = jnp.sum(grad_attn_in * normal1, axis=0)
    tokens_grad = grad_hidden + norm_back(normal1, rate1, grad_attn_in * (1.0 + scale1))
    grad_mod = jnp.stack(
        [grad_shift1, grad_scale1, grad_gate1, grad_shift2, grad_scale2, grad_gate2]
    ).reshape(-1, 128)
    qkv_sum, proj_sum, route_sum, up_sum, down_sum, mod_every = reduce_rows(
        grad_mod, qkv_grad, proj_grad, route_grad, shared_up_grad, shared_down_grad
    )
    ada_grad = jnp.dot(
        cond_own.T, mod_every.reshape(wide_count, 6 * model_width), precision=highest
    ).reshape(ada_rows, 6, model_width)
    return (
        output.astype(BF16),
        tokens_grad,
        ada_grad,
        qkv_sum.reshape(ada_rows, 3, head_width),
        proj_sum,
        route_sum[:, :EXPERTS],
        up_sum,
        down_sum,
        up_kept + up_came.astype(F32),
        down_kept + down_came.astype(F32),
    )


def solution(mesh):
    placed = (
        P("wide", None),
        P("wide", None),
        P(),
        P("wide"),
        P("wide", None),
        P("wide", None, None),
        P("wide", None, "narrow"),
        P("wide", "narrow"),
        P("wide", None),
        P("wide", "narrow"),
        P("wide", "narrow"),
        P("wide", "narrow"),
        P("wide", "narrow"),
    )
    direct = mesh.shape["wide"] == 16 and mesh.shape["narrow"] == 2
    return jax.shard_map(
        per_device_direct if direct else per_device,
        mesh=mesh,
        in_specs=placed,
        out_specs=(
            P("wide", None),
            P("wide", None),
            P("wide", None, None),
            P("wide", None, "narrow"),
            P("wide", "narrow"),
            P("wide", None),
            P("wide", "narrow"),
            P("wide", "narrow"),
            P("wide", "narrow"),
            P("wide", "narrow"),
        ),
        check_vma=False,
    )
```

```python
import functools
import types

import jax
import jax.numpy as jnp
from jax import lax
from jax.experimental import pallas as pl
from jax.experimental.pallas import tpu as pltpu
from jax.sharding import PartitionSpec as P

WIDE, NARROW = "wide", "narrow"
HEADS = 12
EXPERTS = 8
CAP = 96


epsilon = 1e-06
highest = lax.Precision.HIGHEST


def swapped(shard, axis, distance):
    return lax.ppermute(shard, axis, [(i, i ^ 1 << distance) for i in range(lax.axis_size(axis))])


def normalize(values):
    centre = jnp.mean(values, axis=-1, keepdims=True)
    shifted = values - centre
    spread = jnp.mean(shifted * shifted, axis=-1, keepdims=True)
    return shifted * lax.rsqrt(spread + epsilon)


def modulate(values, offset, factor):
    return normalize(values) * (1.0 + factor[:, None, :]) + offset[:, None, :]


def gelu_tanh(values):
    return jax.nn.gelu(values, approximate=True)


def gelu_back(values, gradient):
    return jax.vjp(gelu_tanh, values)[1](gradient)[0]


def contract(left_side, right_side, left_dims, right_dims):
    return lax.dot_general(
        left_side,
        right_side,
        ((left_dims, right_dims), ((), ())),
        preferred_element_type=jnp.float32,
    )


def slot_table(route_block):
    flat_routes = route_block.reshape(-1)
    matches = (flat_routes[:, None] == jnp.arange(EXPERTS, dtype=jnp.int32)[None, :]).astype(
        jnp.int32
    )
    earlier = jnp.cumsum(matches, axis=0, dtype=jnp.int32) - matches
    ranking = jnp.sum(earlier * matches, axis=1, dtype=jnp.int32)
    return flat_routes * CAP + ranking


def join_halves(stacked, bit_level, wide_place):
    partner = swapped(stacked, WIDE, bit_level)
    upper = wide_place >> bit_level & 1 == 1
    return jnp.where(
        upper,
        jnp.concatenate([partner, stacked], axis=1),
        jnp.concatenate([stacked, partner], axis=1),
    )


def split_halves(stacked, bit_level, wide_place):
    half_rows = stacked.shape[1] // 2
    upper = wide_place >> bit_level & 1 == 1
    lower_part = stacked[:, :half_rows]
    upper_part = stacked[:, half_rows:]
    kept = jnp.where(upper, upper_part, lower_part)
    given = jnp.where(upper, lower_part, upper_part)
    return kept + swapped(given.astype(jnp.bfloat16), WIDE, bit_level).astype(given.dtype)


def per_device(
    tokens,
    cotangent,
    time_table,
    timesteps,
    routes,
    w_ada,
    w_qkv,
    w_proj,
    w_route,
    w_shared_up,
    w_shared_down,
    e_up,
    e_down,
):
    images = timesteps.shape[0]
    row_count = tokens.shape[0]
    model_width = tokens.shape[1]
    patches = row_count // images
    core_count = lax.axis_size(NARROW)
    wide_count = lax.axis_size(WIDE)
    group_size = wide_count // EXPERTS
    levels = group_size.bit_length() - 1
    slice_rows = CAP // group_size
    heads_here = HEADS // core_count
    head_dim = model_width // HEADS
    head_width = heads_here * head_dim
    scale_factor = head_dim ** (-0.5)
    wide_place = lax.axis_index(WIDE)
    ada_rows = w_ada.shape[0]
    step_onehot = (
        timesteps[:, None] == jnp.arange(time_table.shape[0], dtype=jnp.int32)[None, :]
    ).astype(jnp.bfloat16)
    cond = jnp.dot(step_onehot, time_table, preferred_element_type=jnp.float32)
    cond_act = jax.nn.silu(cond).astype(jnp.bfloat16)
    qkv_full, proj_full, route_full, up_full, down_full = (
        lax.all_gather(w_qkv, WIDE, axis=0, tiled=True),
        lax.all_gather(w_proj, WIDE, axis=0, tiled=True),
        lax.all_gather(w_route, WIDE, axis=0, tiled=True),
        lax.all_gather(w_shared_up, WIDE, axis=0, tiled=True),
        lax.all_gather(w_shared_down, WIDE, axis=0, tiled=True),
    )
    cond_every = lax.all_gather(cond_act, WIDE, axis=0, tiled=True)
    cond_own = lax.dynamic_slice_in_dim(cond_every, wide_place * ada_rows, ada_rows, 1)
    modulation_terms = jnp.dot(
        cond_own, w_ada.reshape(ada_rows, 6 * model_width), preferred_element_type=jnp.float32
    )
    modulation = lax.psum_scatter(modulation_terms, WIDE, scatter_dimension=0, tiled=True)
    modulation = modulation.reshape(images, 6, model_width)
    expert_weights = jnp.stack([e_up, e_down])
    for bit_level in range(levels):
        expert_weights = join_halves(expert_weights, bit_level, wide_place)
    expert_up = expert_weights[0]
    expert_down = expert_weights[1]
    inputs = tokens.astype(jnp.float32).reshape(images, patches, model_width)
    attn_in, pull_first = jax.vjp(modulate, inputs, modulation[:, 0], modulation[:, 1])
    attn_low = attn_in.reshape(row_count, model_width).astype(jnp.bfloat16)
    projected = jnp.dot(
        attn_low, qkv_full.reshape(model_width, 3 * head_width), preferred_element_type=jnp.float32
    )
    projected = projected.reshape(images, patches, 3, heads_here, head_dim).astype(jnp.bfloat16)
    queries = projected[:, :, 0]
    keys = projected[:, :, 1]
    values = projected[:, :, 2]
    scores = (
        jnp.einsum("bqhd,bkhd->bhqk", queries, keys, preferred_element_type=jnp.float32)
        * scale_factor
    )
    highest_score = jnp.max(scores, axis=-1, keepdims=True)
    log_total = highest_score + jnp.log(
        jnp.sum(jnp.exp(scores - highest_score), axis=-1, keepdims=True)
    )
    probs_low = jnp.exp(scores - log_total).astype(jnp.bfloat16)
    mixed = jnp.einsum("bhqk,bkhd->bqhd", probs_low, values, preferred_element_type=jnp.float32)
    mixed_low = mixed.astype(jnp.bfloat16).reshape(row_count, head_width)
    attn_part = contract(mixed_low, proj_full, (1,), (1,))
    attn_out = lax.psum(attn_part.astype(jnp.bfloat16), NARROW).astype(jnp.float32)
    attn_three = attn_out.reshape(images, patches, model_width)
    hidden_state = inputs + modulation[:, 2][:, None, :] * attn_three
    mlp_in, pull_second = jax.vjp(modulate, hidden_state, modulation[:, 3], modulation[:, 4])
    mlp_low = mlp_in.reshape(row_count, model_width).astype(jnp.bfloat16)
    logits = jnp.dot(mlp_low, route_full, preferred_element_type=jnp.float32)
    selector = (routes[:, :, None] == jnp.arange(EXPERTS, dtype=jnp.int32)[None, None, :]).astype(
        jnp.float32
    )
    chosen = jnp.sum(logits[:, None, :] * selector, axis=-1)
    gate_values, pull_gate = jax.vjp(
        lambda picked_logits: jax.nn.softmax(picked_logits, axis=-1), chosen
    )
    slot_index = slot_table(routes)
    outgoing = (
        jnp.zeros((EXPERTS * CAP, model_width), jnp.bfloat16)
        .at[slot_index]
        .set(jnp.repeat(mlp_low, 2, axis=0))
    )
    arrived = lax.all_to_all(
        outgoing.reshape(wide_count, slice_rows, model_width),
        WIDE,
        split_axis=0,
        concat_axis=0,
        tiled=True,
    )
    expert_in = arrived.reshape(wide_count * slice_rows, model_width)
    shared_pre = jnp.dot(mlp_low, up_full, preferred_element_type=jnp.float32)
    shared_act = gelu_tanh(shared_pre).astype(jnp.bfloat16)
    shared_part = contract(shared_act, down_full, (1,), (1,))
    expert_pre = jnp.dot(expert_in, expert_up, preferred_element_type=jnp.float32)
    expert_act = gelu_tanh(expert_pre).astype(jnp.bfloat16)
    expert_part = contract(expert_act, expert_down, (1,), (1,))
    expert_sum, shared_out = (
        lax.psum(expert_part.astype(jnp.bfloat16), NARROW).astype(jnp.float32),
        lax.psum(shared_part.astype(jnp.bfloat16), NARROW).astype(jnp.float32),
    )
    expert_out = expert_sum.astype(jnp.bfloat16)
    returned = lax.all_to_all(
        expert_out.reshape(wide_count, slice_rows, model_width),
        WIDE,
        split_axis=0,
        concat_axis=0,
        tiled=True,
    )
    returned = returned.reshape(EXPERTS * CAP, model_width)
    picked = returned[slot_index].astype(jnp.float32).reshape(row_count, 2, model_width)
    mixture = jnp.sum(gate_values[:, :, None] * picked, axis=1)
    branch = (shared_out + mixture).reshape(images, patches, model_width)
    output = hidden_state + modulation[:, 5][:, None, :] * branch
    grad_out = cotangent.astype(jnp.float32).reshape(images, patches, model_width)
    grad_branch = (modulation[:, 5][:, None, :] * grad_out).reshape(row_count, model_width)
    grad_gate2 = jnp.sum(grad_out * branch, axis=1)
    grad_pick = jnp.sum(grad_branch[:, None, :] * picked, axis=-1)
    grad_rows = (
        (gate_values[:, :, None] * grad_branch[:, None, :])
        .astype(jnp.bfloat16)
        .reshape(row_count * 2, model_width)
    )
    grad_slots = jnp.zeros((EXPERTS * CAP, model_width), jnp.bfloat16).at[slot_index].set(grad_rows)
    grad_expert_out = lax.all_to_all(
        grad_slots.reshape(wide_count, slice_rows, model_width),
        WIDE,
        split_axis=0,
        concat_axis=0,
        tiled=True,
    )
    grad_expert_out = grad_expert_out.reshape(wide_count * slice_rows, model_width)
    grad_shared = grad_branch.astype(jnp.bfloat16)
    shared_down_grad = contract(grad_shared, shared_act, (0,), (0,))
    grad_shared_act = jnp.dot(grad_shared, down_full, preferred_element_type=jnp.float32)
    grad_shared_pre = gelu_back(shared_pre, grad_shared_act).astype(jnp.bfloat16)
    shared_up_grad = contract(mlp_low, grad_shared_pre, (0,), (0,))
    grad_in_shared = contract(grad_shared_pre, up_full, (1,), (1,))
    grad_chosen = pull_gate(grad_pick)[0]
    grad_logits = jnp.sum(grad_chosen[:, :, None] * selector, axis=1).astype(jnp.bfloat16)
    route_grad = contract(mlp_low, grad_logits, (0,), (0,))
    grad_in_route = contract(grad_logits, route_full, (1,), (1,))
    expert_down_grad = contract(grad_expert_out, expert_act, (0,), (0,))
    grad_expert_act = jnp.dot(grad_expert_out, expert_down, preferred_element_type=jnp.float32)
    grad_expert_pre = gelu_back(expert_pre, grad_expert_act).astype(jnp.bfloat16)
    expert_up_grad = contract(expert_in, grad_expert_pre, (0,), (0,))
    grad_in_part = contract(grad_expert_pre, expert_up, (1,), (1,))
    grad_in_rows, grad_in_shared_sum = (
        lax.psum(grad_in_part.astype(jnp.bfloat16), NARROW).astype(jnp.float32),
        lax.psum(grad_in_shared.astype(jnp.bfloat16), NARROW).astype(jnp.float32),
    )
    back_rows = lax.all_to_all(
        grad_in_rows.astype(jnp.bfloat16).reshape(wide_count, slice_rows, model_width),
        WIDE,
        split_axis=0,
        concat_axis=0,
        tiled=True,
    )
    back_rows = back_rows.reshape(EXPERTS * CAP, model_width)
    grad_in_expert = jnp.sum(
        back_rows[slot_index].astype(jnp.float32).reshape(row_count, 2, model_width), axis=1
    )
    grad_mlp_in = grad_in_shared_sum + grad_in_route + grad_in_expert
    grad_hidden_norm, grad_shift2, grad_scale2 = pull_second(
        grad_mlp_in.reshape(images, patches, model_width)
    )
    grad_hidden = grad_out + grad_hidden_norm
    grad_gate1 = jnp.sum(grad_hidden * attn_three, axis=1)
    grad_attn = (
        (modulation[:, 2][:, None, :] * grad_hidden)
        .reshape(row_count, model_width)
        .astype(jnp.bfloat16)
    )
    proj_grad = contract(grad_attn, mixed_low, (0,), (0,))
    grad_mixed = jnp.dot(grad_attn, proj_full, preferred_element_type=jnp.float32).astype(
        jnp.bfloat16
    )
    grad_mixed = grad_mixed.reshape(images, patches, heads_here, head_dim)
    again_scores = (
        jnp.einsum("bqhd,bkhd->bhqk", queries, keys, preferred_element_type=jnp.float32)
        * scale_factor
    )
    probs_full = jnp.exp(again_scores - log_total)
    again_low = probs_full.astype(jnp.bfloat16)
    grad_probs = jnp.einsum(
        "bqhd,bkhd->bhqk", grad_mixed, values, preferred_element_type=jnp.float32
    )
    grad_values = jnp.einsum(
        "bhqk,bqhd->bkhd", again_low, grad_mixed, preferred_element_type=jnp.float32
    )
    weighted_sum = jnp.sum(probs_full * grad_probs, axis=-1, keepdims=True)
    grad_scores = (probs_full * (grad_probs - weighted_sum)).astype(jnp.bfloat16)
    grad_queries = (
        jnp.einsum("bhqk,bkhd->bqhd", grad_scores, keys, preferred_element_type=jnp.float32)
        * scale_factor
    )
    grad_keys = (
        jnp.einsum("bhqk,bqhd->bkhd", grad_scores, queries, preferred_element_type=jnp.float32)
        * scale_factor
    )
    grad_qkv = jnp.stack([grad_queries, grad_keys, grad_values], axis=2).astype(jnp.bfloat16)
    grad_qkv = grad_qkv.reshape(row_count, 3 * head_width)
    qkv_grad = contract(attn_low, grad_qkv, (0,), (0,)).reshape(model_width, 3, head_width)
    grad_attn_part = contract(grad_qkv, qkv_full.reshape(model_width, 3 * head_width), (1,), (1,))
    grad_attn_in = lax.psum(grad_attn_part.astype(jnp.bfloat16), NARROW).astype(jnp.float32)
    grad_input_norm, grad_shift1, grad_scale1 = pull_first(
        grad_attn_in.reshape(images, patches, model_width)
    )
    tokens_grad = (grad_hidden + grad_input_norm).reshape(row_count, model_width)
    grad_modulation = jnp.stack(
        [grad_shift1, grad_scale1, grad_gate1, grad_shift2, grad_scale2, grad_gate2], axis=1
    )
    grad_modulation = grad_modulation.reshape(images, 6 * model_width)
    grad_mod_every = lax.all_gather(grad_modulation, WIDE, axis=0, tiled=True)
    ada_part = jnp.dot(cond_own.astype(jnp.float32).T, grad_mod_every, precision=highest).reshape(
        ada_rows, 6, model_width
    )
    qkv_part, proj_part, route_part, shared_up_part, shared_down_part = (
        lax.psum_scatter(qkv_grad, WIDE, scatter_dimension=0, tiled=True),
        lax.psum_scatter(proj_grad, WIDE, scatter_dimension=0, tiled=True),
        lax.psum_scatter(route_grad, WIDE, scatter_dimension=0, tiled=True),
        lax.psum_scatter(shared_up_grad, WIDE, scatter_dimension=0, tiled=True),
        lax.psum_scatter(shared_down_grad, WIDE, scatter_dimension=0, tiled=True),
    )
    expert_grads = jnp.stack([expert_up_grad, expert_down_grad])
    for bit_level in reversed(range(levels)):
        expert_grads = split_halves(expert_grads, bit_level, wide_place)
    return (
        output.reshape(row_count, model_width).astype(jnp.bfloat16),
        tokens_grad,
        ada_part,
        qkv_part,
        proj_part,
        route_part,
        shared_up_part,
        shared_down_part,
        expert_grads[0],
        expert_grads[1],
    )


MESH = pl.DeviceIdType.MESH
F32 = jnp.float32
BF16 = jnp.bfloat16
Z_SIZE, Y_SIZE, X_SIZE = 4, 2, 2
VMEM_LIMIT = 60 * 1024 * 1024


def place(index):
    return lax.div(index, 4), lax.rem(lax.div(index, 2), 2), lax.rem(index, 2)


def at_place(z, y, x):
    return z * 4 + y * 2 + x


class Sends:
    def __init__(self):
        self.items = []

    def go(self, make, when=None):
        self.items.append((make, when))
        guarded(when, lambda: make().start())

    def drain(self):
        for make, when in self.items:
            guarded(when, lambda make=make: make().wait_send())


def guarded(when, action):
    if when is None:
        action()
        return

    @pl.when(when)
    def _():
        action()


def both(first, second):
    if first is None:
        return second
    if second is None:
        return first
    return jnp.logical_and(first, second)


def remote(src, dst, send_sem, recv_sem, target):
    return pltpu.make_async_remote_copy(
        src_ref=src,
        dst_ref=dst,
        send_sem=send_sem,
        recv_sem=recv_sem,
        device_id=target,
        device_id_type=MESH,
    )


def greet(targets):
    barrier = pltpu.get_barrier_semaphore()
    for target in targets:
        pl.semaphore_signal(barrier, inc=1, device_id=target, device_id_type=MESH)
    pl.semaphore_wait(barrier, len(targets))


class Gather:
    def __init__(self, streams, send_sem, recv_sem, sends):
        self.streams, self.ss, self.rs, self.sends = streams, send_sem, recv_sem, sends
        self.count = [0] * len(streams)
        self.core = lax.axis_index(NARROW)
        self.me = lax.axis_index(WIDE)
        self.z, self.y, self.x = place(self.me)
        self.to_x = at_place(self.z, self.y, 1 - self.x)
        self.to_y = at_place(self.z, 1 - self.y, self.x)
        self.can_up, self.can_down = self.z < Z_SIZE - 1, self.z > 0
        self.up, self.down = self.me + 4, self.me - 4

    def block(self, s, origin):
        shard, full, start, width, _ = self.streams[s]
        rows = shard.shape[0]
        return full.at[pl.ds(pl.multiple_of(origin * rows, 16), rows), pl.ds(start, width)]

    def send(self, s, origin, target, when=None, own=False):
        shard, full, start, width, _ = self.streams[s]
        index = self.count[s]
        self.count[s] += 1

        def make():
            dst = self.block(s, origin)
            src = shard.at[:, pl.ds(start, width)] if own else dst
            return remote(src, dst, self.ss.at[s, index], self.rs.at[s, origin], (target, self.core))

        self.sends.go(make, when)

    def wait(self, s, origin, when=None):
        def action():
            ref = self.block(s, origin)
            remote(
                ref, ref, self.ss.at[s, 0], self.rs.at[s, origin], (self.to_x, self.core)
            ).wait_recv()

        guarded(when, action)

    def spread(self, s, origin, when=None, own=False, up=True, down=True, over_y=True):
        if up:
            self.send(s, origin, self.up, both(when, self.can_up), own)
        if down:
            self.send(s, origin, self.down, both(when, self.can_down), own)
        if over_y:
            self.send(s, origin, self.to_y, when, own)

    def begin(self, s):
        self.send(s, self.me, self.to_x, own=True)
        self.spread(s, self.me, own=True)

    def after_x(self, s):
        self.wait(s, self.to_x)
        self.spread(s, self.to_x)

    def y_pair(self, s):
        if self.streams[s][4] == "xyz":
            for xx in (self.x, 1 - self.x):
                origin = at_place(self.z, 1 - self.y, xx)
                self.wait(s, origin)
                self.spread(s, origin, over_y=False)

    def after_z(self, s, distance):
        order = self.streams[s][4]
        ys = (self.y,) if order == "xzy" else (self.y, 1 - self.y)
        for step, ok in ((-distance, self.z >= distance), (distance, self.z + distance < Z_SIZE)):
            for yy in ys:
                for xx in (self.x, 1 - self.x):
                    origin = at_place(self.z + step, yy, xx)
                    self.wait(s, origin, ok)
                    self.spread(s, origin, ok, up=step < 0, down=step > 0, over_y=order == "xzy")

    def finish(self, s):
        if self.streams[s][4] == "xzy":
            for zz in range(Z_SIZE):
                for xx in range(X_SIZE):
                    self.wait(s, at_place(zz, 1 - self.y, xx))


def vmem(count):
    return [pl.BlockSpec(memory_space=pltpu.VMEM)] * count


def hbm(count):
    return [pl.BlockSpec(memory_space=pl.ANY)] * count


def params(collective_id):
    return pltpu.CompilerParams(
        collective_id=collective_id, has_side_effects=True, vmem_limit_bytes=VMEM_LIMIT
    )


def peers_far_first(me):
    z, y, x = place(me)
    found = []
    for dz in range(Z_SIZE):
        for dy in range(Y_SIZE):
            for dx in range(X_SIZE):
                if dz or dy or dx:
                    zz = lax.rem(z + dz, Z_SIZE)
                    found.append(at_place(zz, lax.rem(y + dy, 2), lax.rem(x + dx, 2)))
    return found[::-1]


def lanes_of(ref, vector):
    rows = ref.shape[0] // 6
    return jnp.concatenate(
        [ref[rows * vector + i : rows * vector + i + 1, :] for i in range(rows)], axis=1
    )


def head_masks(rows):
    lane = lax.broadcasted_iota(jnp.int32, (rows, 128), 1)
    first = (lane < 64).astype(F32)
    return first, 1.0 - first


def choice_masks(routes_ref):
    rows = routes_ref.shape[0]
    lane = lax.broadcasted_iota(jnp.int32, (rows, 128), 1)
    named = [(routes_ref[:, k : k + 1] == lane).astype(F32) for k in range(2)]
    above = lax.broadcasted_iota(jnp.int32, (rows, rows), 0)
    along = lax.broadcasted_iota(jnp.int32, (rows, rows), 1)
    before = jnp.dot(
        (along < above).astype(F32).astype(BF16),
        (named[0] + named[1]).astype(BF16),
        preferred_element_type=F32,
    )
    slot = lax.broadcasted_iota(jnp.int32, (rows, EXPERTS * CAP), 1)
    takes = []
    for k in range(2):
        rank = jnp.sum(before * named[k], axis=1, keepdims=True)
        own = routes_ref[:, k : k + 1].astype(F32) * CAP + rank
        takes.append((slot == own.astype(jnp.int32)).astype(F32).astype(BF16))
    return named, takes


def attend(attn_low, qkv_ref, act_ref, probs_ref, mixed_ref, pump):
    rows, width = attn_low.shape[0], mixed_ref.shape[1]
    for j in range(3):
        act_ref[:, width * j : width * (j + 1)] = jnp.dot(
            attn_low, qkv_ref[:, width * j : width * (j + 1)], preferred_element_type=F32
        ).astype(BF16)
        pump()
    masks = head_masks(rows)
    scale_factor = 64 ** (-0.5)
    for pair in range(width // 128):
        q, k, v = [
            act_ref[:, width * j + 128 * pair : width * j + 128 * (pair + 1)] for j in range(3)
        ]
        mixed = None
        for h in range(2):
            scores = contract(q * masks[h].astype(BF16), k, (1,), (1,)) * scale_factor
            top = jnp.max(scores, axis=-1, keepdims=True)
            weights = jnp.exp(scores - top)
            probs = weights / jnp.sum(weights, axis=-1, keepdims=True)
            probs_ref[2 * pair + h] = probs
            part = jnp.dot(probs.astype(BF16), v, preferred_element_type=F32) * masks[h]
            mixed = part if mixed is None else mixed + part
            pump()
        mixed_ref[:, 128 * pair : 128 * (pair + 1)] = mixed.astype(BF16)


def forward_kernel(
    ts_ref, table_ref, ada_ref, qkv_ref, proj_ref, route_ref, up_ref, down_ref,
    eup_ref, edown_ref, tok_ref, cot_ref, routes_ref,
    mod_ref, cond_ref, qkv_out, proj_out, route_out, act_ref, probs_ref, mixed_ref,
    attn_ref, attn_low_ref, mlp_ref, gshared_ref, gates_ref,
    up_out, down_out, eup_out, edown_out, rows_out, grads_out,
    ts_all, terms, landed, part, theirs, gate_row, rows_send, grads_send,
    ts_ss, ts_rs, mod_ss, mod_rs, ag_ss, ag_rs, own_sem, join_ss, join_rs, swap_sem,
    ss, rs, pass_ss, pass_rs, own_a,
):
    me, core = lax.axis_index(WIDE), lax.axis_index(NARROW)
    count = lax.axis_size(WIDE)
    others = peers_far_first(me)
    peer = (me, 1 - core)
    greet([(other, core) for other in others] + [peer])
    sends = Sends()
    for k, other in enumerate(others):
        sends.go(lambda k=k, other=other: remote(ts_ref, ts_all.at[me], ts_ss.at[k], ts_rs.at[me], (other, core)))
    half = down_ref.shape[1] // 2
    streams = [
        (qkv_ref, qkv_out, 0, qkv_ref.shape[1], "xzy"),
        (proj_ref, proj_out, 0, proj_ref.shape[1], "xzy"),
        (route_ref, route_out, 0, route_ref.shape[1], "xzy"),
        (up_ref, up_out, 0, up_ref.shape[1], "xzy"),
        (down_ref, down_out, 0, half, "xzy"),
        (down_ref, down_out, half, half, "xyz"),
    ]
    ag = Gather(streams, ag_ss, ag_rs, sends)
    for s in range(3):
        ag.begin(s)
    own = []
    for i, (shard, full) in enumerate(
        ((qkv_ref, qkv_out), (proj_ref, proj_out), (route_ref, route_out), (up_ref, up_out), (down_ref, down_out))
    ):
        rows = shard.shape[0]
        own.append(
            pltpu.make_async_copy(
                shard, full.at[pl.ds(pl.multiple_of(me * rows, 16), rows), :], own_sem.at[i]
            )
        )
        own[-1].start()

    tokens = tok_ref[...].astype(F32)
    normal1, _ = normalized(tokens)

    ts_all[me] = ts_ref[...]
    for other in others[::-1]:
        remote(ts_ref, ts_all.at[other], ts_ss.at[0], ts_rs.at[other], (other, core)).wait_recv()
    steps = jnp.max(ts_all[...], axis=1)[:, :1]
    onehot = (
        steps == lax.broadcasted_iota(jnp.int32, (count, table_ref.shape[0]), 1)
    ).astype(F32).astype(BF16)
    cond = jnp.dot(onehot, table_ref[...], preferred_element_type=F32)
    cond_act = (cond * jax.nn.sigmoid(cond)).astype(BF16)
    cond_ref[...] = cond_act.astype(F32)
    chunks = terms.shape[1] // 6
    for j in range(6):
        vector = jnp.dot(
            cond_act,
            ada_ref[:, 128 * chunks * j : 128 * chunks * (j + 1)],
            preferred_element_type=F32,
        )
        for i in range(chunks):
            terms[:, chunks * j + i, :] = vector[:, 128 * i : 128 * (i + 1)]
    for k, other in enumerate(others):
        sends.go(lambda k=k, other=other: remote(terms.at[other], landed.at[me], mod_ss.at[k], mod_rs.at[me], (other, core)))
    for s in range(3):
        ag.after_x(s)

    pieces = 4
    joins = []
    for a, (src, dst) in enumerate(((eup_ref, eup_out), (edown_ref, edown_out))):
        size = src.shape[0] // pieces
        for p in range(pieces):
            cut = pl.ds(p * size, size)
            joins.append(
                lambda a=a, p=p, src=src, dst=dst, cut=cut: remote(
                    src.at[cut, :], dst.at[cut, :],
                    join_ss.at[a * pieces + p], join_rs.at[a * pieces + p], (ag.to_x, core),
                )
            )

    for distance in range(1, Z_SIZE):
        for s in range(3):
            ag.after_z(s, distance)
    for s in range(3, len(streams)):
        ag.begin(s)
    for make in joins[:4]:
        sends.go(make)
    landed[me] = terms[me]
    for other in others[::-1]:
        remote(terms.at[me], landed.at[other], mod_ss.at[0], mod_rs.at[other], (other, core)).wait_recv()
    mod_ref[...] = jnp.sum(landed[...], axis=0)
    shift1, scale1, gate1, shift2, scale2, gate2 = [lanes_of(mod_ref, j) for j in range(6)]
    attn_low_ref[...] = (normal1 * (1.0 + scale1) + shift1).astype(BF16)
    bulk = range(3, len(streams))
    queue = [lambda s=s: ag.after_x(s) for s in bulk]
    queue += [lambda s=s: ag.y_pair(s) for s in bulk]
    queue += [lambda s=s, d=d: ag.after_z(s, d) for d in range(1, Z_SIZE) for s in bulk]

    def pump():
        if queue:
            queue.pop(0)()

    ag.finish(0)
    own[0].wait()
    attend(attn_low_ref[...], qkv_out, act_ref, probs_ref, mixed_ref, pump)
    ag.finish(1)
    own[1].wait()
    part[...] = contract(mixed_ref[...], proj_out[...], (1,), (1,)).astype(BF16)
    swap = remote(part, theirs, swap_sem.at[0], swap_sem.at[1], peer)
    swap.start()
    named, takes = choice_masks(routes_ref)
    gate_row[...] = jnp.broadcast_to(gate2, gate_row.shape)
    gshared_ref[...] = (gate2 * cot_ref[...].astype(F32)).astype(BF16)
    pump()
    swap.wait()
    attn_out = part[...].astype(F32) + theirs[...].astype(F32)
    attn_ref[...] = attn_out
    hidden = tok_ref[...].astype(F32) + gate1 * attn_out
    normal2, _ = normalized(hidden)
    mlp_ref[...] = (normal2 * (1.0 + scale2) + shift2).astype(BF16)
    ag.finish(2)
    own[2].wait()
    logits = jnp.dot(mlp_ref[...], route_out[...], preferred_element_type=F32)
    chosen = [jnp.sum(logits * named[k], axis=1, keepdims=True) for k in range(2)]
    peak = jnp.maximum(chosen[0], chosen[1])
    weight = [jnp.exp(chosen[k] - peak) for k in range(2)]
    total = weight[0] + weight[1]
    gates = [weight[k] / total for k in range(2)]
    lane = lax.broadcasted_iota(jnp.int32, gates_ref.shape, 1)
    gates_ref[...] = jnp.where(lane == 0, gates[0], jnp.where(lane == 1, gates[1], 0.0))
    width = rows_send.shape[1]
    mine = pl.ds(pl.multiple_of(core * width, 128), width)
    grad_half = gate_row[0:1, mine] * cot_ref[:, mine].astype(F32)
    rows_send[...] = contract(takes[0] + takes[1], mlp_ref[:, mine], (0,), (0,)).astype(BF16)
    grads_send[...] = (
        contract(takes[0], (gates[0] * grad_half).astype(BF16), (0,), (0,))
        + contract(takes[1], (gates[1] * grad_half).astype(BF16), (0,), (0,))
    ).astype(BF16)

    size = rows_send.shape[0] // count

    def rows(index):
        return pl.ds(pl.multiple_of(index * size, 16), size)

    pairs = ((rows_send, rows_out), (grads_send, grads_out))
    for k, other in enumerate(others):
        for a, (src, dst) in enumerate(pairs):
            sends.go(
                lambda k=k, other=other, a=a, src=src, dst=dst: remote(
                    src.at[rows(other), :], dst.at[core, rows(me), :],
                    ss.at[a, k], rs.at[a, me], (other, core),
                )
            )
    for make in joins[4:]:
        sends.go(make)
    kept = []
    for a, (src, dst) in enumerate(pairs):
        sends.go(
            lambda a=a, src=src, dst=dst: remote(
                src.at[rows(me), :], dst.at[core, rows(me), :], pass_ss.at[a, 15], pass_rs.at[a, me], peer
            )
        )
        kept.append(pltpu.make_async_copy(src.at[rows(me), :], dst.at[core, rows(me), :], own_a.at[a]))
        kept[-1].start()
    while queue:
        pump()
    for k, other in enumerate(others[::-1]):
        for a, (src, dst) in enumerate(pairs):
            here = dst.at[core, rows(other), :]
            remote(here, here, ss.at[a, 0], rs.at[a, other], peer).wait_recv()
            sends.go(
                lambda k=k, other=other, a=a, here=here: remote(
                    here, here, pass_ss.at[a, k], pass_rs.at[a, other], peer
                )
            )
    for s in range(3, len(streams)):
        ag.finish(s)
    for i, make in enumerate(joins):
        make().wait_recv()
    for other in [me] + others[::-1]:
        for a, (src, dst) in enumerate(pairs):
            there = dst.at[1 - core, rows(other), :]
            remote(there, there, pass_ss.at[a, 0], pass_rs.at[a, other], peer).wait_recv()
    for copy in own[3:] + kept:
        copy.wait()
    sends.drain()


def forward(ts_tile, table, ada, qkv, proj, route, up, down, e_up, e_down, tokens, cotangent, routes):
    count = 16
    shards = (qkv, proj, route, up, down)
    vectors = ada.shape[1] // 128
    patches, width = tokens.shape
    slots = EXPERTS * CAP
    dma = pltpu.SemaphoreType.DMA
    shape = jax.ShapeDtypeStruct

    def full(a):
        return shape((count * a.shape[0], a.shape[1]), a.dtype)

    return pl.pallas_call(
        forward_kernel,
        out_shape=[
            shape((vectors, 128), F32), shape((count, table.shape[1]), F32),
            full(qkv), full(proj), full(route),
            shape((patches, qkv.shape[1]), BF16), shape((proj.shape[1] // 64, patches, patches), F32),
            shape((patches, proj.shape[1]), BF16), shape((patches, width), F32),
            shape((patches, width), BF16), shape((patches, width), BF16),
            shape((patches, width), BF16), shape((patches, 128), F32),
            full(up), full(down), shape(e_up.shape, BF16), shape(e_down.shape, BF16),
            shape((2, slots, width // 2), BF16), shape((2, slots, width // 2), BF16),
        ],
        in_specs=vmem(8) + hbm(2) + vmem(3),
        out_specs=vmem(13) + hbm(6),
        scratch_shapes=[
            pltpu.VMEM((count, 8, 128), jnp.int32),
            pltpu.VMEM((count, vectors, 128), F32),
            pltpu.VMEM((count, vectors, 128), F32),
            pltpu.VMEM((patches, width), BF16), pltpu.VMEM((patches, width), BF16),
            pltpu.VMEM((8, width), F32),
            pltpu.VMEM((slots, width // 2), BF16), pltpu.VMEM((slots, width // 2), BF16),
            dma((16,)), dma((16,)), dma((16,)), dma((16,)),
            dma((6, 40)), dma((6, 16)), dma((5,)), dma((8,)), dma((8,)), dma((2,)),
            dma((2, 16)), dma((2, 16)), dma((2, 16)), dma((2, 16)), dma((2,)),
        ],
        compiler_params=params(1),
        name="forward",
    )(ts_tile, table, ada, *shards, e_up, e_down, tokens, cotangent, routes)


def normalized(values):
    centre = jnp.mean(values, axis=-1, keepdims=True)
    shifted = values - centre
    spread = jnp.mean(shifted * shifted, axis=-1, keepdims=True)
    rate = lax.rsqrt(spread + epsilon)
    return shifted * rate, rate


def norm_back(normal, rate, gradient):
    mean = jnp.mean(gradient, axis=-1, keepdims=True)
    along = jnp.mean(gradient * normal, axis=-1, keepdims=True)
    return rate * (gradient - mean - normal * along)


class Sums:
    def __init__(self, specs, r, sends):
        self.specs, self.r, self.sends = specs, r, sends
        self.me, self.core = lax.axis_index(WIDE), lax.axis_index(NARROW)
        self.z, self.y, self.x = place(self.me)
        z = self.z
        upper = z >= 2
        self.dest = [
            jnp.where(upper, 0, 3), jnp.where(upper, 1, 2), jnp.where(upper, 5 - z, 1 - z), z
        ]
        self.near = {
            "y": at_place(z, 1 - self.y, self.x), "x": at_place(z, self.y, 1 - self.x)
        }

    def part(self, ref, axis, zz, other):
        if axis == "y":
            return ref.at[zz, 1 - self.y if other else self.y]
        return ref.at[zz, :, 1 - self.x if other else self.x]

    def landed(self, ref, sem):
        remote(ref, ref, self.r.first_ss.at[0, 0], sem, (self.near["x"], self.core)).wait_recv()

    def load(self, i, k):
        terms, axis, work = self.specs[i][:3]
        zz = self.dest[k]
        return pltpu.make_async_copy(
            self.part(terms, axis, zz, False), work.at[zz], self.r.load_sem.at[i, k]
        )

    def start(self, i, k):
        terms, axis, _, came = self.specs[i][:4]
        zz = self.dest[k]
        self.load(i, k).start()
        self.sends.go(
            lambda: remote(
                self.part(terms, axis, zz, True), came.at[zz],
                self.r.first_ss.at[i, k], self.r.first_rs.at[i, zz], (self.near[axis], self.core),
            )
        )

    def step(self, i, k):
        _, axis, work, came, along, last = self.specs[i][:6]
        z, zz, core = self.z, self.dest[k], self.core
        self.load(i, k).wait()
        self.landed(came.at[zz], self.r.first_rs.at[i, zz])
        if k < 3:
            rising = zz > z
            way = jnp.where(rising, 0, 1)
            more = jnp.where(rising, z > 0, z < 3)

            @pl.when(more)
            def _():
                self.landed(along.at[way, zz], self.r.z_rs.at[i, way * 4 + zz])
                add_blocks(work.at[zz], came.at[zz], along.at[way, zz])

            @pl.when(jnp.logical_not(more))
            def _():
                add_blocks(work.at[zz], came.at[zz])

            target = jnp.where(rising, self.me + 4, self.me - 4)
            self.sends.go(
                lambda: remote(
                    work.at[zz], along.at[way, zz],
                    self.r.z_ss.at[i, k], self.r.z_rs.at[i, way * 4 + zz], (target, core),
                )
            )
            return
        add_blocks(work.at[z], came.at[z])
        for way, there in ((0, z > 0), (1, z < 3)):

            @pl.when(there)
            def _(way=way):
                self.landed(along.at[way, z], self.r.z_rs.at[i, way * 4 + z])
                add_blocks(work.at[z], along.at[way, z])

        side, final = (self.x, "x") if axis == "y" else (self.y, "y")
        self.sends.go(
            lambda: remote(
                work.at[z, 1 - side], last,
                self.r.last_ss.at[i], self.r.last_rs.at[i], (self.near[final], core),
            )
        )

    def finish(self, i):
        _, axis, work, _, _, last, store = self.specs[i]
        self.landed(last, self.r.last_rs.at[i])
        side = self.x if axis == "y" else self.y
        store(work[self.z, side].astype(F32) + last[...].astype(F32))


def add_blocks(total, *terms):
    size = total.shape[1]
    per = size // 16

    def body(n, _):
        block, at = lax.div(n, per), pl.ds(pl.multiple_of(lax.rem(n, per) * 16, 16), 16)
        value = total[block, at, :].astype(F32)
        for term in terms:
            value = value + term[block, at, :].astype(F32)
        total[block, at, :] = value.astype(BF16)
        return 0

    lax.fori_loop(0, 2 * per, body, 0)


def backward_kernel(names, fetched, *refs):
    r = types.SimpleNamespace(**dict(zip(names, refs, strict=True)))
    me, core = lax.axis_index(WIDE), lax.axis_index(NARROW)
    count = lax.axis_size(WIDE)
    z, y, x = place(me)
    others = peers_far_first(me)
    peer = (me, 1 - core)
    greet([(other, core) for other in others] + [peer])
    sends = Sends()
    size = r.total0.shape[0] // count
    width = r.total0.shape[1]
    mine = pl.ds(pl.multiple_of(core * width, 128), width)
    theirs_half = pl.ds(pl.multiple_of((1 - core) * width, 128), width)

    def rows(index):
        return pl.ds(pl.multiple_of(index * size, 16), size)

    def arrived(ref, sem):
        remote(ref, ref, r.near_ss.at[0, 0], sem, peer).wait_recv()

    triples = ((r.out, r.their0, r.total0, r.back0), (r.grad, r.their1, r.total1, r.back1))
    order = others + [me]
    for a, (src, _, total, _) in enumerate(triples):
        pltpu.make_async_copy(src.at[core], total, r.own_sem.at[a]).start()
    for k, other in enumerate(order):
        for a, (src, theirs, _, _) in enumerate(triples):
            sends.go(
                lambda k=k, other=other, a=a, src=src, theirs=theirs: remote(
                    src.at[1 - core, rows(other), :], theirs.at[rows(other), :],
                    r.near_ss.at[a, k], r.near_rs.at[a, other], peer,
                )
            )

    def store_to(ref):
        def store(value):
            ref[...] = value

        return store

    def store_qkv(value):
        for j in range(3):
            r.qkv_o[:, j, :] = value[:, width * j : width * (j + 1)]

    specs = [
        (r.up, "y", r.up_w, r.up_c, r.up_a, r.up_l, store_to(r.up_o)),
        (r.down, "x", r.down_w, r.down_c, r.down_a, r.down_l, store_to(r.down_o)),
        (r.proj_t, "y", r.proj_w, r.proj_c, r.proj_a, r.proj_l, store_to(r.proj_o)),
        (r.route_t, "y", r.route_w, r.route_c, r.route_a, r.route_l, store_to(r.route_o)),
        (r.qkv_t, "y", r.qkv_w, r.qkv_c, r.qkv_a, r.qkv_l, store_qkv),
    ]
    sums = Sums(specs, r, sends)
    for i in range(2):
        sums.start(i, 0)
    fetches = {}
    for n, name in enumerate(fetched):
        fetches[name] = pltpu.make_async_copy(getattr(r, name), getattr(r, name + "_v"), r.fetch_sem.at[n])
        fetches[name].start()
    for a, (src, _, total, _) in enumerate(triples):
        pltpu.make_async_copy(src.at[core], total, r.own_sem.at[a]).wait()
    for k, other in enumerate(order):
        for a, (_, theirs, total, back) in enumerate(triples):
            arrived(theirs.at[rows(other), :], r.near_rs.at[a, other])
            both_cores = (
                total[rows(other), :].astype(F32) + theirs[rows(other), :].astype(F32)
            ).astype(BF16)
            total[rows(other), :] = both_cores
            if k < len(others):
                sends.go(
                    lambda k=k, other=other, a=a, total=total, back=back: remote(
                        total.at[rows(other), :], back.at[rows(me), :],
                        r.ss.at[a, k], r.rs.at[a, me], (other, core),
                    )
                )
            else:
                back[rows(me), :] = both_cores
    small = ((r.shared, r.their2), (r.gshared, r.their3))
    for a, (src, theirs) in enumerate(small):
        sends.go(
            lambda a=a, src=src, theirs=theirs: remote(
                src.at[:, theirs_half], theirs, r.near_ss.at[a, 16], r.near_rs.at[a, 16], peer
            )
        )
    for k in range(1, 4):
        for i in range(2):
            sums.start(i, k)
    queue = [lambda i=i, k=k: sums.step(i, k) for k in range(4) for i in range(2)]

    def pump(steps=1):
        for _ in range(steps):
            if queue:
                queue.pop(0)()

    shift1, scale1, gate1, shift2, scale2, gate2 = [lanes_of(r.mod, j) for j in range(6)]
    named, takes = choice_masks(r.routes)
    gates = [r.gates[:, k : k + 1] for k in range(2)]
    lanes_per = 256
    for name in fetched[:4]:
        fetches[name].wait()
    kept_pairs = ((r.inown_v, r.gpre_v, r.keep0, r.eup_o), (r.gown_v, r.eact_v, r.keep1, r.edown_o))
    for a, (left, right, keep, result) in enumerate(kept_pairs):

        def body(n, _, left=left, right=right, keep=keep):
            at = pl.ds(pl.multiple_of(n * lanes_per, 128), lanes_per)
            keep[:, at] = contract(left[...], right[:, at], (0,), (0,))
            return 0

        lax.fori_loop(0, right.shape[1] // lanes_per, body, 0)
        pltpu.make_async_copy(keep, result, r.keep_sem.at[a]).start()
    pump(2)
    for a, (_, theirs) in enumerate(small):
        arrived(theirs, r.near_rs.at[a, 16])
    for other in others[::-1]:
        for a, (_, _, _, back) in enumerate(triples):
            arrived(back.at[rows(other), :], r.rs.at[a, other])
    for name in fetched[4:6]:
        fetches[name].wait()
    picked = [jnp.dot(takes[k], r.back0[...], preferred_element_type=F32) for k in range(2)]
    r.branch[:, mine] = (
        r.shared_v[:, mine].astype(F32) + r.their2[...].astype(F32)
        + gates[0] * picked[0] + gates[1] * picked[1]
    )
    r.gmlp[:, mine] = (
        r.gshared_v[:, mine].astype(F32) + r.their3[...].astype(F32)
        + jnp.dot(takes[0] + takes[1], r.back1[...], preferred_element_type=F32)
    )
    for k in range(6):
        r.gate_row[k : k + 1, :] = lanes_of(r.mod, k)
    grad_half = r.gate_row[5:6, mine] * r.cot[:, mine].astype(F32)
    terms = [jnp.sum(grad_half * picked[k], axis=-1, keepdims=True) for k in range(2)]
    lane = lax.broadcasted_iota(jnp.int32, r.gsum.shape, 1)
    r.gsum[...] = jnp.where(lane == 0, terms[0], jnp.where(lane == 1, terms[1], 0.0))
    swaps = [
        remote(r.branch.at[:, mine], r.branch.at[:, mine], r.swap_ss.at[0], r.swap_rs.at[0], peer),
        remote(r.gmlp.at[:, mine], r.gmlp.at[:, mine], r.swap_ss.at[1], r.swap_rs.at[1], peer),
        remote(r.gsum, r.gsum_c, r.swap_ss.at[2], r.swap_rs.at[2], peer),
    ]
    for swap in swaps:
        swap.start()
    for name in fetched[6:]:
        fetches[name].wait()
    hidden = r.tok[...].astype(F32) + gate1 * r.attn_v[...]
    normal2, rate2 = normalized(hidden)
    r.normal[...] = normal2
    grad_out = r.cot[...].astype(F32)
    arrived(r.branch.at[:, theirs_half], r.swap_rs.at[0])
    arrived(r.gmlp.at[:, theirs_half], r.swap_rs.at[1])
    arrived(r.gsum_c, r.swap_rs.at[2])
    for swap in swaps:
        swap.wait_send()

    def put(vector, value):
        for i in range(value.shape[1] // 128):
            at = value.shape[1] // 128 * vector + i
            r.vec[at : at + 1, :] = value[:, 128 * i : 128 * (i + 1)]

    branch = r.branch[...]
    r.out_o[...] = (hidden + gate2 * branch).astype(BF16)
    put(5, jnp.sum(grad_out * branch, axis=0, keepdims=True))
    grad_gates = [r.gsum[:, k : k + 1] + r.gsum_c[:, k : k + 1] for k in range(2)]
    inner = gates[0] * grad_gates[0] + gates[1] * grad_gates[1]
    grad_chosen = [gates[k] * (grad_gates[k] - inner) for k in range(2)]
    grad_logits = (grad_chosen[0] * named[0] + grad_chosen[1] * named[1]).astype(BF16)
    grad_mlp = r.gmlp[...] + contract(grad_logits, r.routew_v[...], (1,), (1,))
    normal2 = r.normal[...]
    put(3, jnp.sum(grad_mlp, axis=0, keepdims=True))
    put(4, jnp.sum(grad_mlp * normal2, axis=0, keepdims=True))
    r.ghid[...] = grad_out + norm_back(normal2, rate2, grad_mlp * (1.0 + scale2))
    grad_hidden = r.ghid[...]
    put(2, jnp.sum(grad_hidden * r.attn_v[...], axis=0, keepdims=True))
    r.gattn[...] = (gate1 * grad_hidden).astype(BF16)
    blocks = (2, 2, 2, size)

    def weight_terms(target, left, right):
        columns = right.shape[1]
        cut = 384
        for n in range(columns // cut if columns > cut else 1):
            lo, hi = cut * n, min(columns, cut * (n + 1))
            for h in range(2):
                value = contract(left[:, 384 * h : 384 * (h + 1)], right[:, lo:hi], (0,), (0,))
                target[2 * h : 2 * h + 2, :, :, :, lo:hi] = value.astype(BF16).reshape(
                    *blocks, hi - lo
                )

    weight_terms(r.proj_t, r.gattn, r.mixed_v)
    weight_terms(r.route_t, r.mlp_v, grad_logits)
    pump(1)
    r.gmix[...] = jnp.dot(r.gattn[...], r.projw_v[...], preferred_element_type=F32).astype(BF16)
    for k in range(4):
        for i in (2, 3):
            sums.start(i, k)
    masks = head_masks(r.gmix.shape[0])
    scale_factor = 64 ** (-0.5)
    for pair in range(width // 128):
        at = [slice(width * j + 128 * pair, width * j + 128 * (pair + 1)) for j in range(3)]
        q, k, v = [r.act_v[:, at[j]] for j in range(3)]
        gm = r.gmix[:, at[0]]
        found = [None] * 3
        for h in range(2):
            probs = r.probs_v[2 * pair + h]
            grad_probs = contract(gm * masks[h].astype(BF16), v, (1,), (1,))
            weighted = jnp.sum(probs * grad_probs, axis=-1, keepdims=True)
            grad_scores = (probs * (grad_probs - weighted)).astype(BF16)
            parts = (
                jnp.dot(grad_scores, k, preferred_element_type=F32) * scale_factor,
                contract(grad_scores, q, (0,), (0,)) * scale_factor,
                contract(probs.astype(BF16), gm, (0,), (0,)),
            )
            found = [
                part * masks[h] if old is None else old + part * masks[h]
                for part, old in zip(parts, found, strict=True)
            ]
            pump(1)
        for j in range(3):
            r.gqkv[:, at[j]] = found[j].astype(BF16)
    r.gpart[...] = contract(r.gqkv[...], r.qkvw_v[...], (1,), (1,)).astype(BF16)
    swap = remote(r.gpart, r.gpart_c, r.swap_ss.at[3], r.swap_rs.at[3], peer)
    swap.start()
    weight_terms(r.qkv_t, r.attnlow_v, r.gqkv)
    for k in range(4):
        sums.start(4, k)
    tokens = r.tok[...].astype(F32)
    normal1, rate1 = normalized(tokens)
    swap.wait()
    grad_in = r.gpart[...].astype(F32) + r.gpart_c[...].astype(F32)
    put(0, jnp.sum(grad_in, axis=0, keepdims=True))
    put(1, jnp.sum(grad_in * normal1, axis=0, keepdims=True))
    for k, other in enumerate(others):
        sends.go(
            lambda k=k, other=other: remote(
                r.vec, r.every.at[me], r.vec_ss.at[k], r.vec_rs.at[me], (other, core)
            )
        )
    r.tokens_o[...] = r.ghid[...] + norm_back(normal1, rate1, grad_in * (1.0 + scale1))
    while queue:
        pump()
    for k in range(4):
        for i in (2, 3, 4):
            sums.step(i, k)
    for i in range(2):
        sums.finish(i)
    r.every[me] = r.vec[...]
    for other in others[::-1]:
        arrived(r.every.at[other], r.vec_rs.at[other])
    cond = r.cond[...]
    chunks = r.vec.shape[0] // 6
    for j in range(6):
        for i in range(chunks):
            r.ada_o[:, j, 128 * i : 128 * (i + 1)] = lax.dot_general(
                cond, r.every[:, chunks * j + i, :], (((0,), (0,)), ((), ())),
                precision=highest, preferred_element_type=F32,
            )
    for i in (2, 3, 4):
        sums.finish(i)
    for a, (_, _, keep, result) in enumerate(kept_pairs):
        pltpu.make_async_copy(keep, result, r.keep_sem.at[a]).wait()
    sends.drain()


def backward(given, far, near):
    count = 16
    dma = pltpu.SemaphoreType.DMA
    shape = jax.ShapeDtypeStruct
    operands = far | given | near
    a = types.SimpleNamespace(**operands)
    patches, width = a.tok.shape
    slots, half = a.out.shape[1:]
    head_width = a.mixed.shape[1]
    hidden = a.gpre.shape[1]
    size = a.up.shape[3]
    vectors = a.mod.shape[0]
    columns = dict(
        up=a.up.shape[4], down=a.down.shape[4], proj=head_width, route=128, qkv=3 * head_width
    )
    results = dict(
        out_o=shape((patches, width), BF16),
        tokens_o=shape((patches, width), F32),
        ada_o=shape((size, 6, width), F32),
        qkv_o=shape((size, 3, head_width), F32),
        proj_o=shape((size, head_width), F32),
        route_o=shape((size, 128), F32),
        up_o=shape((size, columns["up"]), F32),
        down_o=shape((size, columns["down"]), F32),
        eup_o=shape((half, hidden), F32),
        edown_o=shape((half, hidden), F32),
    )
    v = pltpu.VMEM
    scratch = {name + "_v": v(array.shape, array.dtype) for name, array in given.items()}
    for name, wide in columns.items():
        scratch[name + "_w"] = v((4, 2, size, wide), BF16)
        scratch[name + "_c"] = v((4, 2, size, wide), BF16)
        scratch[name + "_a"] = v((2, 4, 2, size, wide), BF16)
        scratch[name + "_l"] = v((size, wide), BF16)
        scratch[name + "_t"] = v((4, 2, 2, size, wide), BF16)
    del scratch["up_t"], scratch["down_t"]
    row_half, rows_full, low_full = v((slots, half), BF16), v((patches, width), F32), v((patches, width), BF16)
    scratch |= dict(
        their0=row_half, their1=row_half, total0=row_half, total1=row_half,
        back0=row_half, back1=row_half,
        their2=v((patches, half), BF16), their3=v((patches, half), BF16),
        keep0=v((half, hidden), F32), keep1=v((half, hidden), F32),
        branch=rows_full, gmlp=rows_full, normal=rows_full, ghid=rows_full,
        gattn=low_full, gpart=low_full, gpart_c=low_full,
        gmix=v((patches, head_width), BF16), gqkv=v((patches, 3 * head_width), BF16),
        gsum=v((patches, 128), F32), gsum_c=v((patches, 128), F32), gate_row=v((8, width), F32),
        vec=v((vectors, 128), F32), every=v((count, vectors, 128), F32),
        near_ss=dma((2, 17)), near_rs=dma((2, 17)), ss=dma((2, 16)), rs=dma((2, 16)),
        own_sem=dma((2,)), fetch_sem=dma((len(given),)), keep_sem=dma((2,)),
        first_ss=dma((5, 4)), first_rs=dma((5, 4)), load_sem=dma((5, 4)),
        z_ss=dma((5, 3)), z_rs=dma((5, 8)), last_ss=dma((5,)), last_rs=dma((5,)),
        swap_ss=dma((4,)), swap_rs=dma((4,)), vec_ss=dma((16,)), vec_rs=dma((16,)),
    )
    names = tuple(operands) + tuple(results) + tuple(scratch)
    found = pl.pallas_call(
        functools.partial(backward_kernel, names, tuple(given)),
        out_shape=list(results.values()),
        in_specs=hbm(len(far) + len(given)) + vmem(len(near)),
        out_specs=vmem(8) + hbm(2),
        scratch_shapes=list(scratch.values()),
        compiler_params=params(3),
        name="backward",
    )(*operands.values())
    return types.SimpleNamespace(**dict(zip(results, found, strict=True)))


def per_device_direct(
    tokens, cotangent, time_table, timesteps, routes, w_ada, w_qkv, w_proj,
    w_route, w_shared_up, w_shared_down, e_up, e_down,
):
    row_count, model_width = tokens.shape
    core = lax.axis_index(NARROW)
    core_count = lax.axis_size(NARROW)
    wide_count = lax.axis_size(WIDE)
    heads_here = HEADS // core_count
    head_dim = model_width // HEADS
    head_width = heads_here * head_dim
    half = model_width // 2
    scale_factor = head_dim ** (-0.5)
    wide_place = lax.axis_index(WIDE)
    upper = wide_place % 2 == 1
    ada_rows = w_ada.shape[0]

    partner = [(i, i ^ 1) for i in range(wide_count)]
    table = lax.dynamic_slice_in_dim(time_table, wide_place * ada_rows, ada_rows, 1)
    table = jnp.pad(table, ((0, -table.shape[0] % 128), (0, 0)))
    ts_tile = jnp.broadcast_to(timesteps[:, None], (8, 128)).astype(jnp.int32)
    (
        mod, cond_own, qkv_full, proj_full, route_full, activated, probs_full, mixed_low,
        attn_out, attn_low, mlp_low, grad_shared, gate_lanes,
        up_full, down_full, up_other, down_other, expert_in, grad_expert_out,
    ) = forward(
        ts_tile,
        table,
        w_ada.reshape(ada_rows, 6 * model_width),
        w_qkv.reshape(ada_rows, 3 * head_width),
        w_proj,
        jnp.pad(w_route, ((0, 0), (0, 128 - EXPERTS))),
        w_shared_up,
        w_shared_down,
        e_up,
        e_down,
        tokens,
        cotangent,
        routes,
    )

    shared_pre = jnp.dot(mlp_low, up_full, preferred_element_type=F32)
    shared_act = gelu_tanh(shared_pre).astype(BF16)
    shared_part = contract(shared_act, down_full, (1,), (1,)).astype(BF16)
    shared_down_grad = contract(grad_shared, shared_act, (0,), (0,)).astype(BF16)
    grad_shared_act = jnp.dot(grad_shared, down_full, preferred_element_type=F32)
    grad_shared_pre = gelu_back(shared_pre, grad_shared_act).astype(BF16)
    shared_up_grad = contract(mlp_low, grad_shared_pre, (0,), (0,)).astype(BF16)
    grad_in_shared = contract(grad_shared_pre, up_full, (1,), (1,)).astype(BF16)

    in_low, in_high = expert_in[0], expert_in[1]
    in_own, in_other = jnp.where(upper, in_high, in_low), jnp.where(upper, in_low, in_high)
    g_low, g_high = grad_expert_out[0], grad_expert_out[1]
    g_own, g_other = jnp.where(upper, g_high, g_low), jnp.where(upper, g_low, g_high)
    expert_pre = jnp.dot(in_own, e_up, preferred_element_type=F32) + jnp.dot(
        in_other, up_other, preferred_element_type=F32
    )
    expert_act = gelu_tanh(expert_pre).astype(BF16)
    out_own = contract(expert_act, e_down, (1,), (1,)).astype(BF16)
    out_other = contract(expert_act, down_other, (1,), (1,)).astype(BF16)
    grad_expert_act = jnp.dot(g_own, e_down, preferred_element_type=F32) + jnp.dot(
        g_other, down_other, preferred_element_type=F32
    )
    grad_expert_pre = gelu_back(expert_pre, grad_expert_act).astype(BF16)
    gi_own = contract(grad_expert_pre, e_up, (1,), (1,)).astype(BF16)
    gi_other = contract(grad_expert_pre, up_other, (1,), (1,)).astype(BF16)
    up_send = contract(in_other, grad_expert_pre, (0,), (0,)).astype(BF16)
    down_send = contract(g_other, expert_act, (0,), (0,)).astype(BF16)
    up_came = lax.ppermute(up_send, WIDE, partner)
    down_came = lax.ppermute(down_send, WIDE, partner)

    got = backward(
        dict(
            inown=in_own, gpre=grad_expert_pre, gown=g_own, eact=expert_act,
            shared=shared_part, gshared=grad_in_shared,
            attn=attn_out, mlp=mlp_low, attnlow=attn_low, act=activated,
            probs=probs_full, mixed=mixed_low,
            qkvw=qkv_full, projw=proj_full, routew=route_full,
        ),
        dict(
            out=jnp.stack([jnp.where(upper, out_other, out_own), jnp.where(upper, out_own, out_other)]),
            grad=jnp.stack([jnp.where(upper, gi_other, gi_own), jnp.where(upper, gi_own, gi_other)]),
            up=shared_up_grad.reshape(Z_SIZE, Y_SIZE, X_SIZE, ada_rows, -1),
            down=shared_down_grad.reshape(Z_SIZE, Y_SIZE, X_SIZE, ada_rows, -1),
        ),
        dict(tok=tokens, cot=cotangent, mod=mod, cond=cond_own, routes=routes, gates=gate_lanes),
    )
    return (
        got.out_o,
        got.tokens_o,
        got.ada_o,
        got.qkv_o,
        got.proj_o,
        got.route_o[:, :EXPERTS],
        got.up_o,
        got.down_o,
        got.eup_o + up_came.astype(F32),
        got.edown_o + down_came.astype(F32),
    )


def solution(mesh):
    placed = (
        P(WIDE, None),
        P(WIDE, None),
        P(),
        P(WIDE),
        P(WIDE, None),
        P(WIDE, None, None),
        P(WIDE, None, NARROW),
        P(WIDE, NARROW),
        P(WIDE, None),
        P(WIDE, NARROW),
        P(WIDE, NARROW),
        P(WIDE, NARROW),
        P(WIDE, NARROW),
    )
    direct = mesh.shape[WIDE] == 16 and mesh.shape[NARROW] == 2
    return jax.shard_map(
        per_device_direct if direct else per_device,
        mesh=mesh,
        in_specs=placed,
        out_specs=(
            P(WIDE, None),
            P(WIDE, None),
            P(WIDE, None, None),
            P(WIDE, None, NARROW),
            P(WIDE, NARROW),
            P(WIDE, None),
            P(WIDE, NARROW),
            P(WIDE, NARROW),
            P(WIDE, NARROW),
            P(WIDE, NARROW),
        ),
        check_vma=False,
    )
```

```python
import functools
import types

import jax
import jax.numpy as jnp
from jax import lax
from jax.experimental import pallas as pl
from jax.experimental.pallas import tpu as pltpu
from jax.sharding import PartitionSpec as P

WIDE, NARROW = "wide", "narrow"
HEADS = 12
EXPERTS = 8
CAP = 96


epsilon = 1e-06
highest = lax.Precision.HIGHEST


def swapped(shard, axis, distance):
    return lax.ppermute(shard, axis, [(i, i ^ 1 << distance) for i in range(lax.axis_size(axis))])


def normalize(values):
    centre = jnp.mean(values, axis=-1, keepdims=True)
    shifted = values - centre
    spread = jnp.mean(shifted * shifted, axis=-1, keepdims=True)
    return shifted * lax.rsqrt(spread + epsilon)


def modulate(values, offset, factor):
    return normalize(values) * (1.0 + factor[:, None, :]) + offset[:, None, :]


def gelu_tanh(values):
    return jax.nn.gelu(values, approximate=True)


def gelu_back(values, gradient):
    return jax.vjp(gelu_tanh, values)[1](gradient)[0]


def contract(left_side, right_side, left_dims, right_dims):
    return lax.dot_general(
        left_side,
        right_side,
        ((left_dims, right_dims), ((), ())),
        preferred_element_type=jnp.float32,
    )


def slot_table(route_block):
    flat_routes = route_block.reshape(-1)
    matches = (flat_routes[:, None] == jnp.arange(EXPERTS, dtype=jnp.int32)[None, :]).astype(
        jnp.int32
    )
    earlier = jnp.cumsum(matches, axis=0, dtype=jnp.int32) - matches
    ranking = jnp.sum(earlier * matches, axis=1, dtype=jnp.int32)
    return flat_routes * CAP + ranking


def join_halves(stacked, bit_level, wide_place):
    partner = swapped(stacked, WIDE, bit_level)
    upper = wide_place >> bit_level & 1 == 1
    return jnp.where(
        upper,
        jnp.concatenate([partner, stacked], axis=1),
        jnp.concatenate([stacked, partner], axis=1),
    )


def split_halves(stacked, bit_level, wide_place):
    half_rows = stacked.shape[1] // 2
    upper = wide_place >> bit_level & 1 == 1
    lower_part = stacked[:, :half_rows]
    upper_part = stacked[:, half_rows:]
    kept = jnp.where(upper, upper_part, lower_part)
    given = jnp.where(upper, lower_part, upper_part)
    return kept + swapped(given.astype(jnp.bfloat16), WIDE, bit_level).astype(given.dtype)


def per_device(
    tokens,
    cotangent,
    time_table,
    timesteps,
    routes,
    w_ada,
    w_qkv,
    w_proj,
    w_route,
    w_shared_up,
    w_shared_down,
    e_up,
    e_down,
):
    images = timesteps.shape[0]
    row_count = tokens.shape[0]
    model_width = tokens.shape[1]
    patches = row_count // images
    core_count = lax.axis_size(NARROW)
    wide_count = lax.axis_size(WIDE)
    group_size = wide_count // EXPERTS
    levels = group_size.bit_length() - 1
    slice_rows = CAP // group_size
    heads_here = HEADS // core_count
    head_dim = model_width // HEADS
    head_width = heads_here * head_dim
    scale_factor = head_dim ** (-0.5)
    wide_place = lax.axis_index(WIDE)
    ada_rows = w_ada.shape[0]
    step_onehot = (
        timesteps[:, None] == jnp.arange(time_table.shape[0], dtype=jnp.int32)[None, :]
    ).astype(jnp.bfloat16)
    cond = jnp.dot(step_onehot, time_table, preferred_element_type=jnp.float32)
    cond_act = jax.nn.silu(cond).astype(jnp.bfloat16)
    qkv_full, proj_full, route_full, up_full, down_full = (
        lax.all_gather(w_qkv, WIDE, axis=0, tiled=True),
        lax.all_gather(w_proj, WIDE, axis=0, tiled=True),
        lax.all_gather(w_route, WIDE, axis=0, tiled=True),
        lax.all_gather(w_shared_up, WIDE, axis=0, tiled=True),
        lax.all_gather(w_shared_down, WIDE, axis=0, tiled=True),
    )
    cond_every = lax.all_gather(cond_act, WIDE, axis=0, tiled=True)
    cond_own = lax.dynamic_slice_in_dim(cond_every, wide_place * ada_rows, ada_rows, 1)
    modulation_terms = jnp.dot(
        cond_own, w_ada.reshape(ada_rows, 6 * model_width), preferred_element_type=jnp.float32
    )
    modulation = lax.psum_scatter(modulation_terms, WIDE, scatter_dimension=0, tiled=True)
    modulation = modulation.reshape(images, 6, model_width)
    expert_weights = jnp.stack([e_up, e_down])
    for bit_level in range(levels):
        expert_weights = join_halves(expert_weights, bit_level, wide_place)
    expert_up = expert_weights[0]
    expert_down = expert_weights[1]
    inputs = tokens.astype(jnp.float32).reshape(images, patches, model_width)
    attn_in, pull_first = jax.vjp(modulate, inputs, modulation[:, 0], modulation[:, 1])
    attn_low = attn_in.reshape(row_count, model_width).astype(jnp.bfloat16)
    projected = jnp.dot(
        attn_low, qkv_full.reshape(model_width, 3 * head_width), preferred_element_type=jnp.float32
    )
    projected = projected.reshape(images, patches, 3, heads_here, head_dim).astype(jnp.bfloat16)
    queries = projected[:, :, 0]
    keys = projected[:, :, 1]
    values = projected[:, :, 2]
    scores = (
        jnp.einsum("bqhd,bkhd->bhqk", queries, keys, preferred_element_type=jnp.float32)
        * scale_factor
    )
    highest_score = jnp.max(scores, axis=-1, keepdims=True)
    log_total = highest_score + jnp.log(
        jnp.sum(jnp.exp(scores - highest_score), axis=-1, keepdims=True)
    )
    probs_low = jnp.exp(scores - log_total).astype(jnp.bfloat16)
    mixed = jnp.einsum("bhqk,bkhd->bqhd", probs_low, values, preferred_element_type=jnp.float32)
    mixed_low = mixed.astype(jnp.bfloat16).reshape(row_count, head_width)
    attn_part = contract(mixed_low, proj_full, (1,), (1,))
    attn_out = lax.psum(attn_part.astype(jnp.bfloat16), NARROW).astype(jnp.float32)
    attn_three = attn_out.reshape(images, patches, model_width)
    hidden_state = inputs + modulation[:, 2][:, None, :] * attn_three
    mlp_in, pull_second = jax.vjp(modulate, hidden_state, modulation[:, 3], modulation[:, 4])
    mlp_low = mlp_in.reshape(row_count, model_width).astype(jnp.bfloat16)
    logits = jnp.dot(mlp_low, route_full, preferred_element_type=jnp.float32)
    selector = (routes[:, :, None] == jnp.arange(EXPERTS, dtype=jnp.int32)[None, None, :]).astype(
        jnp.float32
    )
    chosen = jnp.sum(logits[:, None, :] * selector, axis=-1)
    gate_values, pull_gate = jax.vjp(
        lambda picked_logits: jax.nn.softmax(picked_logits, axis=-1), chosen
    )
    slot_index = slot_table(routes)
    outgoing = (
        jnp.zeros((EXPERTS * CAP, model_width), jnp.bfloat16)
        .at[slot_index]
        .set(jnp.repeat(mlp_low, 2, axis=0))
    )
    arrived = lax.all_to_all(
        outgoing.reshape(wide_count, slice_rows, model_width),
        WIDE,
        split_axis=0,
        concat_axis=0,
        tiled=True,
    )
    expert_in = arrived.reshape(wide_count * slice_rows, model_width)
    shared_pre = jnp.dot(mlp_low, up_full, preferred_element_type=jnp.float32)
    shared_act = gelu_tanh(shared_pre).astype(jnp.bfloat16)
    shared_part = contract(shared_act, down_full, (1,), (1,))
    expert_pre = jnp.dot(expert_in, expert_up, preferred_element_type=jnp.float32)
    expert_act = gelu_tanh(expert_pre).astype(jnp.bfloat16)
    expert_part = contract(expert_act, expert_down, (1,), (1,))
    expert_sum, shared_out = (
        lax.psum(expert_part.astype(jnp.bfloat16), NARROW).astype(jnp.float32),
        lax.psum(shared_part.astype(jnp.bfloat16), NARROW).astype(jnp.float32),
    )
    expert_out = expert_sum.astype(jnp.bfloat16)
    returned = lax.all_to_all(
        expert_out.reshape(wide_count, slice_rows, model_width),
        WIDE,
        split_axis=0,
        concat_axis=0,
        tiled=True,
    )
    returned = returned.reshape(EXPERTS * CAP, model_width)
    picked = returned[slot_index].astype(jnp.float32).reshape(row_count, 2, model_width)
    mixture = jnp.sum(gate_values[:, :, None] * picked, axis=1)
    branch = (shared_out + mixture).reshape(images, patches, model_width)
    output = hidden_state + modulation[:, 5][:, None, :] * branch
    grad_out = cotangent.astype(jnp.float32).reshape(images, patches, model_width)
    grad_branch = (modulation[:, 5][:, None, :] * grad_out).reshape(row_count, model_width)
    grad_gate2 = jnp.sum(grad_out * branch, axis=1)
    grad_pick = jnp.sum(grad_branch[:, None, :] * picked, axis=-1)
    grad_rows = (
        (gate_values[:, :, None] * grad_branch[:, None, :])
        .astype(jnp.bfloat16)
        .reshape(row_count * 2, model_width)
    )
    grad_slots = jnp.zeros((EXPERTS * CAP, model_width), jnp.bfloat16).at[slot_index].set(grad_rows)
    grad_expert_out = lax.all_to_all(
        grad_slots.reshape(wide_count, slice_rows, model_width),
        WIDE,
        split_axis=0,
        concat_axis=0,
        tiled=True,
    )
    grad_expert_out = grad_expert_out.reshape(wide_count * slice_rows, model_width)
    grad_shared = grad_branch.astype(jnp.bfloat16)
    shared_down_grad = contract(grad_shared, shared_act, (0,), (0,))
    grad_shared_act = jnp.dot(grad_shared, down_full, preferred_element_type=jnp.float32)
    grad_shared_pre = gelu_back(shared_pre, grad_shared_act).astype(jnp.bfloat16)
    shared_up_grad = contract(mlp_low, grad_shared_pre, (0,), (0,))
    grad_in_shared = contract(grad_shared_pre, up_full, (1,), (1,))
    grad_chosen = pull_gate(grad_pick)[0]
    grad_logits = jnp.sum(grad_chosen[:, :, None] * selector, axis=1).astype(jnp.bfloat16)
    route_grad = contract(mlp_low, grad_logits, (0,), (0,))
    grad_in_route = contract(grad_logits, route_full, (1,), (1,))
    expert_down_grad = contract(grad_expert_out, expert_act, (0,), (0,))
    grad_expert_act = jnp.dot(grad_expert_out, expert_down, preferred_element_type=jnp.float32)
    grad_expert_pre = gelu_back(expert_pre, grad_expert_act).astype(jnp.bfloat16)
    expert_up_grad = contract(expert_in, grad_expert_pre, (0,), (0,))
    grad_in_part = contract(grad_expert_pre, expert_up, (1,), (1,))
    grad_in_rows, grad_in_shared_sum = (
        lax.psum(grad_in_part.astype(jnp.bfloat16), NARROW).astype(jnp.float32),
        lax.psum(grad_in_shared.astype(jnp.bfloat16), NARROW).astype(jnp.float32),
    )
    back_rows = lax.all_to_all(
        grad_in_rows.astype(jnp.bfloat16).reshape(wide_count, slice_rows, model_width),
        WIDE,
        split_axis=0,
        concat_axis=0,
        tiled=True,
    )
    back_rows = back_rows.reshape(EXPERTS * CAP, model_width)
    grad_in_expert = jnp.sum(
        back_rows[slot_index].astype(jnp.float32).reshape(row_count, 2, model_width), axis=1
    )
    grad_mlp_in = grad_in_shared_sum + grad_in_route + grad_in_expert
    grad_hidden_norm, grad_shift2, grad_scale2 = pull_second(
        grad_mlp_in.reshape(images, patches, model_width)
    )
    grad_hidden = grad_out + grad_hidden_norm
    grad_gate1 = jnp.sum(grad_hidden * attn_three, axis=1)
    grad_attn = (
        (modulation[:, 2][:, None, :] * grad_hidden)
        .reshape(row_count, model_width)
        .astype(jnp.bfloat16)
    )
    proj_grad = contract(grad_attn, mixed_low, (0,), (0,))
    grad_mixed = jnp.dot(grad_attn, proj_full, preferred_element_type=jnp.float32).astype(
        jnp.bfloat16
    )
    grad_mixed = grad_mixed.reshape(images, patches, heads_here, head_dim)
    again_scores = (
        jnp.einsum("bqhd,bkhd->bhqk", queries, keys, preferred_element_type=jnp.float32)
        * scale_factor
    )
    probs_full = jnp.exp(again_scores - log_total)
    again_low = probs_full.astype(jnp.bfloat16)
    grad_probs = jnp.einsum(
        "bqhd,bkhd->bhqk", grad_mixed, values, preferred_element_type=jnp.float32
    )
    grad_values = jnp.einsum(
        "bhqk,bqhd->bkhd", again_low, grad_mixed, preferred_element_type=jnp.float32
    )
    weighted_sum = jnp.sum(probs_full * grad_probs, axis=-1, keepdims=True)
    grad_scores = (probs_full * (grad_probs - weighted_sum)).astype(jnp.bfloat16)
    grad_queries = (
        jnp.einsum("bhqk,bkhd->bqhd", grad_scores, keys, preferred_element_type=jnp.float32)
        * scale_factor
    )
    grad_keys = (
        jnp.einsum("bhqk,bqhd->bkhd", grad_scores, queries, preferred_element_type=jnp.float32)
        * scale_factor
    )
    grad_qkv = jnp.stack([grad_queries, grad_keys, grad_values], axis=2).astype(jnp.bfloat16)
    grad_qkv = grad_qkv.reshape(row_count, 3 * head_width)
    qkv_grad = contract(attn_low, grad_qkv, (0,), (0,)).reshape(model_width, 3, head_width)
    grad_attn_part = contract(grad_qkv, qkv_full.reshape(model_width, 3 * head_width), (1,), (1,))
    grad_attn_in = lax.psum(grad_attn_part.astype(jnp.bfloat16), NARROW).astype(jnp.float32)
    grad_input_norm, grad_shift1, grad_scale1 = pull_first(
        grad_attn_in.reshape(images, patches, model_width)
    )
    tokens_grad = (grad_hidden + grad_input_norm).reshape(row_count, model_width)
    grad_modulation = jnp.stack(
        [grad_shift1, grad_scale1, grad_gate1, grad_shift2, grad_scale2, grad_gate2], axis=1
    )
    grad_modulation = grad_modulation.reshape(images, 6 * model_width)
    grad_mod_every = lax.all_gather(grad_modulation, WIDE, axis=0, tiled=True)
    ada_part = jnp.dot(cond_own.astype(jnp.float32).T, grad_mod_every, precision=highest).reshape(
        ada_rows, 6, model_width
    )
    qkv_part, proj_part, route_part, shared_up_part, shared_down_part = (
        lax.psum_scatter(qkv_grad, WIDE, scatter_dimension=0, tiled=True),
        lax.psum_scatter(proj_grad, WIDE, scatter_dimension=0, tiled=True),
        lax.psum_scatter(route_grad, WIDE, scatter_dimension=0, tiled=True),
        lax.psum_scatter(shared_up_grad, WIDE, scatter_dimension=0, tiled=True),
        lax.psum_scatter(shared_down_grad, WIDE, scatter_dimension=0, tiled=True),
    )
    expert_grads = jnp.stack([expert_up_grad, expert_down_grad])
    for bit_level in reversed(range(levels)):
        expert_grads = split_halves(expert_grads, bit_level, wide_place)
    return (
        output.reshape(row_count, model_width).astype(jnp.bfloat16),
        tokens_grad,
        ada_part,
        qkv_part,
        proj_part,
        route_part,
        shared_up_part,
        shared_down_part,
        expert_grads[0],
        expert_grads[1],
    )


MESH = pl.DeviceIdType.MESH
F32 = jnp.float32
BF16 = jnp.bfloat16
Z_SIZE, Y_SIZE, X_SIZE = 4, 2, 2
VMEM_LIMIT = 60 * 1024 * 1024


def place(index):
    return lax.div(index, 4), lax.rem(lax.div(index, 2), 2), lax.rem(index, 2)


def at_place(z, y, x):
    return z * 4 + y * 2 + x


class Sends:
    def __init__(self):
        self.items = []

    def go(self, make, when=None):
        self.items.append((make, when))
        guarded(when, lambda: make().start())

    def drain(self):
        for make, when in self.items:
            guarded(when, lambda make=make: make().wait_send())


def guarded(when, action):
    if when is None:
        action()
        return

    @pl.when(when)
    def _():
        action()


def both(first, second):
    if first is None:
        return second
    if second is None:
        return first
    return jnp.logical_and(first, second)


def remote(src, dst, send_sem, recv_sem, target):
    return pltpu.make_async_remote_copy(
        src_ref=src,
        dst_ref=dst,
        send_sem=send_sem,
        recv_sem=recv_sem,
        device_id=target,
        device_id_type=MESH,
    )


def greet(targets):
    barrier = pltpu.get_barrier_semaphore()
    for target in targets:
        pl.semaphore_signal(barrier, inc=1, device_id=target, device_id_type=MESH)
    pl.semaphore_wait(barrier, len(targets))


class Gather:
    def __init__(self, streams, send_sem, recv_sem, sends):
        self.streams, self.ss, self.rs, self.sends = streams, send_sem, recv_sem, sends
        self.count = [0] * len(streams)
        self.core = lax.axis_index(NARROW)
        self.me = lax.axis_index(WIDE)
        self.z, self.y, self.x = place(self.me)
        self.to_x = at_place(self.z, self.y, 1 - self.x)
        self.to_y = at_place(self.z, 1 - self.y, self.x)
        self.can_up, self.can_down = self.z < Z_SIZE - 1, self.z > 0
        self.up, self.down = self.me + 4, self.me - 4

    def block(self, s, origin):
        shard, full, start, width = self.streams[s][:4]
        rows = shard.shape[0]
        return full.at[pl.ds(pl.multiple_of(origin * rows, 16), rows), pl.ds(start, width)]

    def send(self, s, origin, target, when=None, own=False, over_x=False):
        shard, full, start, width, _, parted = self.streams[s]
        index = self.count[s]
        self.count[s] += 1

        def make():
            dst = self.block(s, origin)
            first = start
            if parted:
                first = pl.multiple_of((1 - self.x if over_x else self.x) * full.shape[1] + start, 128)
            src = shard.at[:, pl.ds(first, width)] if own else dst
            return remote(src, dst, self.ss.at[s, index], self.rs.at[s, origin], (target, self.core))

        self.sends.go(make, when)

    def wait(self, s, origin, when=None):
        def action():
            ref = self.block(s, origin)
            remote(
                ref, ref, self.ss.at[s, 0], self.rs.at[s, origin], (self.to_x, self.core)
            ).wait_recv()

        guarded(when, action)

    def spread(self, s, origin, when=None, own=False, up=True, down=True, over_y=True):
        if up:
            self.send(s, origin, self.up, both(when, self.can_up), own)
        if down:
            self.send(s, origin, self.down, both(when, self.can_down), own)
        if over_y:
            self.send(s, origin, self.to_y, when, own)

    def begin(self, s):
        self.send(s, self.me, self.to_x, own=True, over_x=True)
        self.spread(s, self.me, own=True)

    def after_x(self, s):
        self.wait(s, self.to_x)
        self.spread(s, self.to_x)

    def y_pair(self, s):
        if self.streams[s][4] == "xyz":
            for xx in (self.x, 1 - self.x):
                origin = at_place(self.z, 1 - self.y, xx)
                self.wait(s, origin)
                self.spread(s, origin, over_y=False)

    def after_z(self, s, distance):
        order = self.streams[s][4]
        ys = (self.y,) if order == "xzy" else (self.y, 1 - self.y)
        for step, ok in ((-distance, self.z >= distance), (distance, self.z + distance < Z_SIZE)):
            for yy in ys:
                for xx in (self.x, 1 - self.x):
                    origin = at_place(self.z + step, yy, xx)
                    self.wait(s, origin, ok)
                    self.spread(s, origin, ok, up=step < 0, down=step > 0, over_y=order == "xzy")

    def finish(self, s):
        if self.streams[s][4] == "xzy":
            for zz in range(Z_SIZE):
                for xx in range(X_SIZE):
                    self.wait(s, at_place(zz, 1 - self.y, xx))


def vmem(count):
    return [pl.BlockSpec(memory_space=pltpu.VMEM)] * count


def hbm(count):
    return [pl.BlockSpec(memory_space=pl.ANY)] * count


def params(collective_id, vmem_limit=VMEM_LIMIT):
    return pltpu.CompilerParams(
        collective_id=collective_id, has_side_effects=True, vmem_limit_bytes=vmem_limit
    )


def peers_far_first(me):
    z, y, x = place(me)
    found = []
    for dz in range(Z_SIZE):
        for dy in range(Y_SIZE):
            for dx in range(X_SIZE):
                if dz or dy or dx:
                    zz = lax.rem(z + dz, Z_SIZE)
                    found.append(at_place(zz, lax.rem(y + dy, 2), lax.rem(x + dx, 2)))
    return found[::-1]


def lanes_of(ref, vector):
    rows = ref.shape[0] // 6
    return jnp.concatenate(
        [ref[rows * vector + i : rows * vector + i + 1, :] for i in range(rows)], axis=1
    )


def head_masks(rows):
    lane = lax.broadcasted_iota(jnp.int32, (rows, 128), 1)
    first = (lane < 64).astype(F32)
    return first, 1.0 - first


def choice_masks(routes_ref):
    rows = routes_ref.shape[0]
    lane = lax.broadcasted_iota(jnp.int32, (rows, 128), 1)
    named = [(routes_ref[:, k : k + 1] == lane).astype(F32) for k in range(2)]
    above = lax.broadcasted_iota(jnp.int32, (rows, rows), 0)
    along = lax.broadcasted_iota(jnp.int32, (rows, rows), 1)
    before = jnp.dot(
        (along < above).astype(F32).astype(BF16),
        (named[0] + named[1]).astype(BF16),
        preferred_element_type=F32,
    )
    slot = lax.broadcasted_iota(jnp.int32, (rows, EXPERTS * CAP), 1)
    takes = []
    for k in range(2):
        rank = jnp.sum(before * named[k], axis=1, keepdims=True)
        own = routes_ref[:, k : k + 1].astype(F32) * CAP + rank
        takes.append((slot == own.astype(jnp.int32)).astype(F32).astype(BF16))
    return named, takes


def attend(attn_low, qkv_ref, act_ref, probs_ref, mixed_ref, pump):
    rows, width = attn_low.shape[0], mixed_ref.shape[1]
    for j in range(3):
        act_ref[:, width * j : width * (j + 1)] = jnp.dot(
            attn_low, qkv_ref[:, width * j : width * (j + 1)], preferred_element_type=F32
        ).astype(BF16)
        pump()
    masks = head_masks(rows)
    scale_factor = 64 ** (-0.5)
    for pair in range(width // 128):
        q, k, v = [
            act_ref[:, width * j + 128 * pair : width * j + 128 * (pair + 1)] for j in range(3)
        ]
        mixed = None
        for h in range(2):
            scores = contract(q * masks[h].astype(BF16), k, (1,), (1,)) * scale_factor
            top = jnp.max(scores, axis=-1, keepdims=True)
            weights = jnp.exp(scores - top)
            probs = weights / jnp.sum(weights, axis=-1, keepdims=True)
            probs_ref[2 * pair + h] = probs
            part = jnp.dot(probs.astype(BF16), v, preferred_element_type=F32) * masks[h]
            mixed = part if mixed is None else mixed + part
            pump()
        mixed_ref[:, 128 * pair : 128 * (pair + 1)] = mixed.astype(BF16)


def forward_kernel(
    ts_ref, table_ref, ada_ref, qkv_ref, proj_ref, route_ref, up_ref, down_ref,
    eup_ref, edown_ref, tok_ref, cot_ref, routes_ref,
    mod_ref, cond_ref, qkv_out, proj_out, route_out, act_ref, probs_ref, mixed_ref,
    attn_ref, attn_low_ref, mlp_ref, gshared_ref, gates_ref,
    up_out, down_out, eup_out, edown_out, rows_out, grads_out,
    ts_all, terms, landed, part, theirs, gate_row, rows_send, grads_send,
    ts_ss, ts_rs, mod_ss, mod_rs, ag_ss, ag_rs, own_sem, join_ss, join_rs, swap_sem,
    ss, rs, pass_ss, pass_rs, own_a, pair_ss, pair_rs,
):
    me, core = lax.axis_index(WIDE), lax.axis_index(NARROW)
    count = lax.axis_size(WIDE)
    others = peers_far_first(me)
    peer = (me, 1 - core)
    greet([(other, core) for other in others] + [peer])
    sends = Sends()
    for k, other in enumerate(others):
        sends.go(lambda k=k, other=other: remote(ts_ref, ts_all.at[me], ts_ss.at[k], ts_rs.at[me], (other, core)))
    half = down_out.shape[1] // 2
    streams = [
        (qkv_ref, qkv_out, 0, qkv_ref.shape[1], "xzy", False),
        (proj_ref, proj_out, 0, proj_ref.shape[1], "xzy", False),
        (route_ref, route_out, 0, route_ref.shape[1], "xzy", False),
        (up_ref, up_out, 0, up_out.shape[1], "xzy", True),
        (down_ref, down_out, 0, half, "xzy", True),
        (down_ref, down_out, half, half, "xyz", True),
    ]
    ag = Gather(streams, ag_ss, ag_rs, sends)
    for s in range(3):
        ag.begin(s)
    own = []
    for i, (shard, full) in enumerate(
        ((qkv_ref, qkv_out), (proj_ref, proj_out), (route_ref, route_out), (up_ref, up_out), (down_ref, down_out))
    ):
        rows, wide = shard.shape[0], full.shape[1]
        side = pl.multiple_of(ag.x * wide, 128) if wide < shard.shape[1] else 0
        own.append(
            pltpu.make_async_copy(
                shard.at[:, pl.ds(side, wide)],
                full.at[pl.ds(pl.multiple_of(me * rows, 16), rows), :], own_sem.at[i]
            )
        )
        own[-1].start()

    tokens = tok_ref[...].astype(F32)
    normal1, _ = normalized(tokens)

    ts_all[me] = ts_ref[...]
    for other in others[::-1]:
        remote(ts_ref, ts_all.at[other], ts_ss.at[0], ts_rs.at[other], (other, core)).wait_recv()
    steps = jnp.max(ts_all[...], axis=1)[:, :1]
    onehot = (
        steps == lax.broadcasted_iota(jnp.int32, (count, table_ref.shape[0]), 1)
    ).astype(F32).astype(BF16)
    cond = jnp.dot(onehot, table_ref[...], preferred_element_type=F32)
    cond_act = (cond * jax.nn.sigmoid(cond)).astype(BF16)
    cond_ref[...] = cond_act.astype(F32)
    chunks = terms.shape[1] // 6
    for j in range(6):
        vector = jnp.dot(
            cond_act,
            ada_ref[:, 128 * chunks * j : 128 * chunks * (j + 1)],
            preferred_element_type=F32,
        )
        for i in range(chunks):
            terms[:, chunks * j + i, :] = vector[:, 128 * i : 128 * (i + 1)]
    for k, other in enumerate(others):
        sends.go(lambda k=k, other=other: remote(terms.at[other], landed.at[me], mod_ss.at[k], mod_rs.at[me], (other, core)))
    for s in range(3):
        ag.after_x(s)

    pieces = 4
    joins = []
    for a, (src, dst) in enumerate(((eup_ref, eup_out), (edown_ref, edown_out))):
        size = src.shape[0] // pieces
        for p in range(pieces):
            cut = pl.ds(p * size, size)
            joins.append(
                lambda a=a, p=p, src=src, dst=dst, cut=cut: remote(
                    src.at[cut, :], dst.at[cut, :],
                    join_ss.at[a * pieces + p], join_rs.at[a * pieces + p], (ag.to_x, core),
                )
            )

    for distance in range(1, Z_SIZE):
        for s in range(3):
            ag.after_z(s, distance)
    for s in range(3, len(streams)):
        ag.begin(s)
    for make in joins[:4]:
        sends.go(make)
    landed[me] = terms[me]
    for other in others[::-1]:
        remote(terms.at[me], landed.at[other], mod_ss.at[0], mod_rs.at[other], (other, core)).wait_recv()
    mod_ref[...] = jnp.sum(landed[...], axis=0)
    shift1, scale1, gate1, shift2, scale2, gate2 = [lanes_of(mod_ref, j) for j in range(6)]
    attn_low_ref[...] = (normal1 * (1.0 + scale1) + shift1).astype(BF16)
    patches = tok_ref.shape[0]
    first, second = pl.ds(0, patches), pl.ds(patches, patches)
    gate_row[...] = jnp.broadcast_to(gate2, gate_row.shape)
    gshared_ref[first, :] = (gate2 * cot_ref[...].astype(F32)).astype(BF16)
    width = rows_send.shape[1]
    mine = pl.ds(pl.multiple_of(core * width, 128), width)
    theirs_half = pl.ds(pl.multiple_of((1 - core) * width, 128), width)
    across = [
        remote(ref.at[first, mine], ref.at[second, mine], pair_ss.at[i], pair_rs.at[i], (ag.to_x, core))
        for i, ref in enumerate((gshared_ref, mlp_ref))
    ]
    handed = [
        remote(ref.at[second, mine], ref.at[second, mine], pair_ss.at[2 + i], pair_rs.at[2 + i], peer)
        for i, ref in enumerate((gshared_ref, mlp_ref))
    ]
    came = [
        remote(ref.at[second, theirs_half], ref.at[second, theirs_half], pair_ss.at[2 + i], pair_rs.at[2 + i], peer)
        for i, ref in enumerate((gshared_ref, mlp_ref))
    ]
    across[0].start()
    bulk = range(3, len(streams))
    queue = [lambda s=s: ag.after_x(s) for s in bulk]
    queue += [lambda s=s: ag.y_pair(s) for s in bulk]
    queue += [lambda s=s, d=d: ag.after_z(s, d) for d in range(1, Z_SIZE) for s in bulk]

    def pump():
        if queue:
            queue.pop(0)()

    ag.finish(0)
    own[0].wait()
    attend(attn_low_ref[...], qkv_out, act_ref, probs_ref, mixed_ref, pump)
    ag.finish(1)
    own[1].wait()
    part[...] = contract(mixed_ref[...], proj_out[...], (1,), (1,)).astype(BF16)
    swap = remote(part, theirs, swap_sem.at[0], swap_sem.at[1], peer)
    swap.start()
    named, takes = choice_masks(routes_ref)
    pump()
    swap.wait()
    attn_out = part[...].astype(F32) + theirs[...].astype(F32)
    attn_ref[...] = attn_out
    hidden = tok_ref[...].astype(F32) + gate1 * attn_out
    normal2, _ = normalized(hidden)
    mlp_ref[first, :] = (normal2 * (1.0 + scale2) + shift2).astype(BF16)
    ag.finish(2)
    own[2].wait()
    logits = jnp.dot(mlp_ref[first, :], route_out[...], preferred_element_type=F32)
    chosen = [jnp.sum(logits * named[k], axis=1, keepdims=True) for k in range(2)]
    peak = jnp.maximum(chosen[0], chosen[1])
    weight = [jnp.exp(chosen[k] - peak) for k in range(2)]
    total = weight[0] + weight[1]
    gates = [weight[k] / total for k in range(2)]
    lane = lax.broadcasted_iota(jnp.int32, gates_ref.shape, 1)
    gates_ref[...] = jnp.where(lane == 0, gates[0], jnp.where(lane == 1, gates[1], 0.0))
    grad_half = gate_row[0:1, mine] * cot_ref[:, mine].astype(F32)
    rows_send[...] = contract(takes[0] + takes[1], mlp_ref[first, mine], (0,), (0,)).astype(BF16)
    grads_send[...] = (
        contract(takes[0], (gates[0] * grad_half).astype(BF16), (0,), (0,))
        + contract(takes[1], (gates[1] * grad_half).astype(BF16), (0,), (0,))
    ).astype(BF16)

    size = rows_send.shape[0] // count

    def rows(index):
        return pl.ds(pl.multiple_of(index * size, 16), size)

    pairs = ((rows_send, rows_out), (grads_send, grads_out))
    for k, other in enumerate(others):
        for a, (src, dst) in enumerate(pairs):
            sends.go(
                lambda k=k, other=other, a=a, src=src, dst=dst: remote(
                    src.at[rows(other), :], dst.at[core, rows(me), :],
                    ss.at[a, k], rs.at[a, me], (other, core),
                )
            )
    across[1].start()
    across[0].wait()
    handed[0].start()
    for make in joins[4:]:
        sends.go(make)
    kept = []
    for a, (src, dst) in enumerate(pairs):
        sends.go(
            lambda a=a, src=src, dst=dst: remote(
                src.at[rows(me), :], dst.at[core, rows(me), :], pass_ss.at[a, 15], pass_rs.at[a, me], peer
            )
        )
        kept.append(pltpu.make_async_copy(src.at[rows(me), :], dst.at[core, rows(me), :], own_a.at[a]))
        kept[-1].start()
    while queue:
        pump()
    across[1].wait()
    handed[1].start()
    for k, other in enumerate(others[::-1]):
        for a, (src, dst) in enumerate(pairs):
            here = dst.at[core, rows(other), :]
            remote(here, here, ss.at[a, 0], rs.at[a, other], peer).wait_recv()
            sends.go(
                lambda k=k, other=other, a=a, here=here: remote(
                    here, here, pass_ss.at[a, k], pass_rs.at[a, other], peer
                )
            )
    for s in range(3, len(streams)):
        ag.finish(s)
    for i, make in enumerate(joins):
        make().wait_recv()
    for other in [me] + others[::-1]:
        for a, (src, dst) in enumerate(pairs):
            there = dst.at[1 - core, rows(other), :]
            remote(there, there, pass_ss.at[a, 0], pass_rs.at[a, other], peer).wait_recv()
    for i in range(2):
        handed[i].wait_send()
        came[i].wait_recv()
    for copy in own[3:] + kept:
        copy.wait()
    sends.drain()


def forward(ts_tile, table, ada, qkv, proj, route, up, down, e_up, e_down, tokens, cotangent, routes):
    count = 16
    shards = (qkv, proj, route, up, down)
    vectors = ada.shape[1] // 128
    patches, width = tokens.shape
    slots = EXPERTS * CAP
    dma = pltpu.SemaphoreType.DMA
    shape = jax.ShapeDtypeStruct

    def full(a):
        return shape((count * a.shape[0], a.shape[1]), a.dtype)

    def parted(a):
        return shape((count * a.shape[0], a.shape[1] // X_SIZE), a.dtype)

    return pl.pallas_call(
        forward_kernel,
        out_shape=[
            shape((vectors, 128), F32), shape((count, table.shape[1]), F32),
            full(qkv), full(proj), full(route),
            shape((patches, qkv.shape[1]), BF16), shape((proj.shape[1] // 64, patches, patches), F32),
            shape((patches, proj.shape[1]), BF16), shape((patches, width), F32),
            shape((patches, width), BF16), shape((2 * patches, width), BF16),
            shape((2 * patches, width), BF16), shape((patches, 128), F32),
            parted(up), parted(down), shape(e_up.shape, BF16), shape(e_down.shape, BF16),
            shape((2, slots, width // 2), BF16), shape((2, slots, width // 2), BF16),
        ],
        in_specs=vmem(8) + hbm(2) + vmem(3),
        out_specs=vmem(13) + hbm(6),
        scratch_shapes=[
            pltpu.VMEM((count, 8, 128), jnp.int32),
            pltpu.VMEM((count, vectors, 128), F32),
            pltpu.VMEM((count, vectors, 128), F32),
            pltpu.VMEM((patches, width), BF16), pltpu.VMEM((patches, width), BF16),
            pltpu.VMEM((8, width), F32),
            pltpu.VMEM((slots, width // 2), BF16), pltpu.VMEM((slots, width // 2), BF16),
            dma((16,)), dma((16,)), dma((16,)), dma((16,)),
            dma((6, 40)), dma((6, 16)), dma((5,)), dma((8,)), dma((8,)), dma((2,)),
            dma((2, 16)), dma((2, 16)), dma((2, 16)), dma((2, 16)), dma((2,)), dma((4,)), dma((4,)),
        ],
        compiler_params=params(1),
        name="forward",
    )(ts_tile, table, ada, *shards, e_up, e_down, tokens, cotangent, routes)


def normalized(values):
    centre = jnp.mean(values, axis=-1, keepdims=True)
    shifted = values - centre
    spread = jnp.mean(shifted * shifted, axis=-1, keepdims=True)
    rate = lax.rsqrt(spread + epsilon)
    return shifted * rate, rate


def norm_back(normal, rate, gradient):
    mean = jnp.mean(gradient, axis=-1, keepdims=True)
    along = jnp.mean(gradient * normal, axis=-1, keepdims=True)
    return rate * (gradient - mean - normal * along)


class Sums:
    def __init__(self, specs, r, sends):
        self.specs, self.r, self.sends = specs, r, sends
        self.me, self.core = lax.axis_index(WIDE), lax.axis_index(NARROW)
        self.z, self.y, self.x = place(self.me)
        z = self.z
        upper = z >= 2
        self.dest = [
            jnp.where(upper, 0, 3), jnp.where(upper, 1, 2), jnp.where(upper, 5 - z, 1 - z), z
        ]
        self.near = {
            "y": at_place(z, 1 - self.y, self.x), "x": at_place(z, self.y, 1 - self.x)
        }

    def part(self, ref, axis, zz, other):
        if axis == "y":
            return ref.at[zz, 1 - self.y if other else self.y]
        return ref.at[zz, :, 1 - self.x if other else self.x]

    def slot(self, zz, way, at):
        return jnp.where(jnp.logical_and(zz == at, way == 1), 4, zz)

    def landed(self, ref, sem):
        remote(ref, ref, self.r.first_ss.at[0, 0], sem, (self.near["x"], self.core)).wait_recv()

    def load(self, i, k):
        terms, axis, work = self.specs[i][:3]
        zz = self.dest[k]
        return pltpu.make_async_copy(
            self.part(terms, axis, zz, False), work.at[zz], self.r.load_sem.at[i, k]
        )

    def start(self, i, k):
        terms, axis, _, came = self.specs[i][:4]
        zz = self.dest[k]
        self.load(i, k).start()
        self.sends.go(
            lambda: remote(
                self.part(terms, axis, zz, True), came.at[zz],
                self.r.first_ss.at[i, k], self.r.first_rs.at[i, zz], (self.near[axis], self.core),
            )
        )

    def step(self, i, k):
        _, axis, work, came, along, last = self.specs[i][:6]
        z, zz, core = self.z, self.dest[k], self.core
        self.load(i, k).wait()
        self.landed(came.at[zz], self.r.first_rs.at[i, zz])
        if k < 3:
            rising = zz > z
            way = jnp.where(rising, 0, 1)
            more = jnp.where(rising, z > 0, z < 3)

            @pl.when(more)
            def _():
                self.landed(along.at[zz], self.r.z_rs.at[i, zz])
                add_blocks(work.at[zz], came.at[zz], along.at[zz])

            @pl.when(jnp.logical_not(more))
            def _():
                add_blocks(work.at[zz], came.at[zz])

            target = jnp.where(rising, self.me + 4, self.me - 4)
            slot = self.slot(zz, way, jnp.where(rising, z + 1, z - 1))
            self.sends.go(
                lambda: remote(
                    work.at[zz], along.at[slot],
                    self.r.z_ss.at[i, k], self.r.z_rs.at[i, slot], (target, core),
                )
            )
            return
        add_blocks(work.at[z], came.at[z])
        for way, there in ((0, z > 0), (1, z < 3)):

            @pl.when(there)
            def _(way=way):
                slot = self.slot(z, way, z)
                self.landed(along.at[slot], self.r.z_rs.at[i, slot])
                add_blocks(work.at[z], along.at[slot])

        side, final = (self.x, "x") if axis == "y" else (self.y, "y")
        self.sends.go(
            lambda: remote(
                work.at[z, 1 - side], last,
                self.r.last_ss.at[i], self.r.last_rs.at[i], (self.near[final], core),
            )
        )

    def finish(self, i):
        _, axis, work, _, _, last, store = self.specs[i]
        self.landed(last, self.r.last_rs.at[i])
        side = self.x if axis == "y" else self.y
        store(work[self.z, side].astype(F32), last[...].astype(F32))


def add_blocks(total, *terms):
    size = total.shape[1]
    per = size // 16

    def body(n, _):
        block, at = lax.div(n, per), pl.ds(pl.multiple_of(lax.rem(n, per) * 16, 16), 16)
        value = total[block, at, :].astype(F32)
        for term in terms:
            value = value + term[block, at, :].astype(F32)
        total[block, at, :] = value.astype(BF16)
        return 0

    lax.fori_loop(0, 2 * per, body, 0)


def gelu_pair(value, gradient):
    root = 0.7978845608028654
    square = value * value
    bend = jnp.tanh(root * (value + 0.044715 * value * square))
    half = 0.5 * (1.0 + bend)
    slope = half + 0.5 * value * (1.0 - bend * bend) * (root * (1.0 + 0.134145 * square))
    return (value * half).astype(BF16), (slope * gradient).astype(BF16)


def columns_of(total, tile, body):
    def turn(n, _):
        body(pl.ds(pl.multiple_of(n * tile, 128), tile))
        return 0

    lax.fori_loop(0, total // tile, turn, 0)


def backward_kernel(names, fetched, *refs):
    r = types.SimpleNamespace(**dict(zip(names, refs, strict=True)))
    me, core = lax.axis_index(WIDE), lax.axis_index(NARROW)
    count = lax.axis_size(WIDE)
    z, y, x = place(me)
    others = peers_far_first(me)
    peer = (me, 1 - core)
    across = (at_place(z, y, 1 - x), core)
    fetches = {}
    for n, name in enumerate(fetched):
        fetches[name] = pltpu.make_async_copy(getattr(r, name), getattr(r, name + "_v"), r.fetch_sem.at[n])
        fetches[name].start()
    greet([(other, core) for other in others] + [peer])
    sends = Sends()
    slots, width = r.their0.shape
    size = slots // count
    patches = r.tok.shape[0]
    mine = pl.ds(pl.multiple_of(core * width, 128), width)
    theirs_half = pl.ds(pl.multiple_of((1 - core) * width, 128), width)

    def rows(index):
        return pl.ds(pl.multiple_of(index * size, 16), size)

    def arrived(ref, sem):
        remote(ref, ref, r.near_ss.at[0, 0], sem, peer).wait_recv()

    for name in fetched[:6]:
        fetches[name].wait()
    hidden_units = r.eup_v.shape[1]
    for n in range(2):
        r.ein_t[n] = r.ein_v[n].T
        r.eg_t[n] = r.eg_v[n].T

    def expert_hidden(at):
        def through(rows_ref, own, other):
            return jnp.dot(rows_ref[x], own[:, at], preferred_element_type=F32) + jnp.dot(
                rows_ref[1 - x], other[:, at], preferred_element_type=F32
            )

        r.eact[:, at], r.epre[:, at] = gelu_pair(
            through(r.ein_v, r.eup_v, r.upo_v), through(r.eg_v, r.edn_v, r.dno_v)
        )

    columns_of(hidden_units, 256, expert_hidden)

    for target, left, own, other in (
        (r.ein_v, r.eact, r.edn_v, r.dno_v), (r.eg_v, r.epre, r.eup_v, r.upo_v),
    ):
        target[x] = contract(left[...], own[...], (1,), (1,)).astype(BF16)
        target[1 - x] = contract(left[...], other[...], (1,), (1,)).astype(BF16)

    triples = ((r.ein_v, r.their0, r.back0), (r.eg_v, r.their1, r.back1))
    order = others + [me]
    for k, other in enumerate(order):
        for a, (src, theirs, _) in enumerate(triples):
            sends.go(
                lambda k=k, other=other, a=a, src=src, theirs=theirs: remote(
                    src.at[1 - core, rows(other), :], theirs.at[rows(other), :],
                    r.near_ss.at[a, k], r.near_rs.at[a, other], peer,
                )
            )
    def given_terms(at):
        r.eup_v[:, at] = jnp.dot(r.ein_t[1 - x], r.epre[:, at], preferred_element_type=F32).astype(BF16)
        r.upo_v[:, at] = jnp.dot(r.eg_t[1 - x], r.eact[:, at], preferred_element_type=F32).astype(BF16)

    columns_of(hidden_units, 256, given_terms)
    pieces = 2
    cut = r.eup_v.shape[0] // pieces
    trades = []
    for a, (give, take) in enumerate(((r.eup_v, r.take0), (r.upo_v, r.take1))):
        for p in range(pieces):
            piece = pl.ds(p * cut, cut)
            trades.append(
                lambda a=a, p=p, give=give, take=take, piece=piece: remote(
                    give.at[piece, :], take.at[piece, :],
                    r.trade_ss.at[a * pieces + p], r.trade_rs.at[a * pieces + p], across,
                )
            )
    for k, other in enumerate(order):
        for a, (src, theirs, back) in enumerate(triples):
            arrived(theirs.at[rows(other), :], r.near_rs.at[a, other])
            both_cores = (
                src[core, rows(other), :].astype(F32) + theirs[rows(other), :].astype(F32)
            ).astype(BF16)
            if k < len(others):
                src[core, rows(other), :] = both_cores
                sends.go(
                    lambda k=k, other=other, a=a, src=src, back=back: remote(
                        src.at[core, rows(other), :], back.at[rows(me), :],
                        r.ss.at[a, k], r.rs.at[a, me], (other, core),
                    )
                )
            else:
                back[rows(me), :] = both_cores

    for name in fetched[6:10]:
        fetches[name].wait()
    r.mlp_t[...] = r.mlp_v[...].T
    r.gsh_t[...] = r.gsh_v[...].T

    def shared_hidden(at):
        r.sact[:, at], r.spre[:, at] = gelu_pair(
            jnp.dot(r.mlp_v[...], r.up_v[:, at], preferred_element_type=F32),
            jnp.dot(r.gsh_v[...], r.down_v[:, at], preferred_element_type=F32),
        )

    columns_of(r.up_v.shape[1], 256, shared_hidden)
    blocks = (2, 2, 2, size)

    def shared_terms(at):
        for target, left, right in ((r.up_t, r.mlp_t, r.spre), (r.down_t, r.gsh_t, r.sact)):
            for h in range(2):
                value = jnp.dot(
                    left[384 * h : 384 * (h + 1), :], right[:, at], preferred_element_type=F32
                )
                target[2 * h : 2 * h + 2, :, :, :, at] = value.astype(BF16).reshape(
                    *blocks, value.shape[1]
                )

    columns_of(r.up_v.shape[1], 256, shared_terms)

    def shared_out(at):
        r.part0[:, at] = contract(r.sact[...], r.down_v[at, :], (1,), (1,)).astype(BF16)
        r.gsh_v[:, at] = contract(r.spre[...], r.up_v[at, :], (1,), (1,)).astype(BF16)

    columns_of(r.part0.shape[1], 256, shared_out)

    def store_to(ref):
        def store(own, came):
            ref[...] = own + came

        return store

    def store_sides(ref):
        def store(own, came):
            half = own.shape[1]
            ref[:, pl.ds(pl.multiple_of(x * half, 128), half)] = own
            ref[:, pl.ds(pl.multiple_of((1 - x) * half, 128), half)] = came

        return store

    def store_qkv(own, came):
        for j in range(3):
            at = slice(width * j, width * (j + 1))
            r.qkv_o[:, j, :] = own[:, at] + came[:, at]

    specs = [
        (r.up_t, "y", r.up_w, r.up_c, r.up_a, r.up_l, store_sides(r.up_o)),
        (r.down_t, "y", r.down_w, r.down_c, r.down_a, r.down_l, store_sides(r.down_o)),
        (r.proj_t, "y", r.proj_w, r.proj_c, r.proj_a, r.proj_l, store_to(r.proj_o)),
        (r.route_t, "y", r.route_w, r.route_c, r.route_a, r.route_l, store_to(r.route_o)),
        (r.qkv_t, "y", r.qkv_w, r.qkv_c, r.qkv_a, r.qkv_l, store_qkv),
    ]
    sums = Sums(specs, r, sends)
    small = ((r.part0, r.their2, r.branch, r.pass0, r.came0), (r.gsh_v, r.their3, r.gmlp, r.pass1, r.came1))
    for a, (part, theirs, _, _, _) in enumerate(small):
        sends.go(
            lambda a=a, part=part, theirs=theirs: remote(
                part.at[:, theirs_half], theirs, r.near_ss.at[a, 16], r.near_rs.at[a, 16], peer
            )
        )
    for k in range(4):
        for i in range(2):
            sums.start(i, k)
    for a, (part, theirs, total, passed, came) in enumerate(small):
        arrived(theirs, r.near_rs.at[a, 16])
        total[:, mine] = part[:patches, mine].astype(F32) + theirs[:patches, :].astype(F32)
        passed[...] = (part[patches:, mine].astype(F32) + theirs[patches:, :].astype(F32)).astype(BF16)
        sends.go(
            lambda a=a, passed=passed, came=came: remote(
                passed, came, r.pass_ss.at[a], r.pass_rs.at[a], across
            )
        )
    for trade in trades:
        sends.go(trade)
    queue = [lambda i=i, k=k: sums.step(i, k) for k in range(4) for i in range(2)]

    def pump(steps=1):
        for _ in range(steps):
            if queue:
                queue.pop(0)()

    shift1, scale1, gate1, shift2, scale2, gate2 = [lanes_of(r.mod, j) for j in range(6)]
    named, takes = choice_masks(r.routes)
    gates = [r.gates[:, k : k + 1] for k in range(2)]
    pump(2)
    for other in others[::-1]:
        for a, (_, _, back) in enumerate(triples):
            arrived(back.at[rows(other), :], r.rs.at[a, other])
    for a in range(2):
        arrived(small[a][4], r.pass_rs.at[a])
    picked = [jnp.dot(takes[k], r.back0[...], preferred_element_type=F32) for k in range(2)]
    r.branch[:, mine] = (
        r.branch[:, mine] + r.came0[...].astype(F32)
        + gates[0] * picked[0] + gates[1] * picked[1]
    )
    r.gmlp[:, mine] = (
        r.gmlp[:, mine] + r.came1[...].astype(F32)
        + jnp.dot(takes[0] + takes[1], r.back1[...], preferred_element_type=F32)
    )
    for k in range(6):
        r.gate_row[k : k + 1, :] = lanes_of(r.mod, k)
    grad_half = r.gate_row[5:6, mine] * r.cot[:, mine].astype(F32)
    terms = [jnp.sum(grad_half * picked[k], axis=-1, keepdims=True) for k in range(2)]
    lane = lax.broadcasted_iota(jnp.int32, r.gsum.shape, 1)
    r.gsum[...] = jnp.where(lane == 0, terms[0], jnp.where(lane == 1, terms[1], 0.0))
    swaps = [
        remote(r.branch.at[:, mine], r.branch.at[:, mine], r.swap_ss.at[0], r.swap_rs.at[0], peer),
        remote(r.gmlp.at[:, mine], r.gmlp.at[:, mine], r.swap_ss.at[1], r.swap_rs.at[1], peer),
        remote(r.gsum, r.gsum_c, r.swap_ss.at[2], r.swap_rs.at[2], peer),
    ]
    for swap in swaps:
        swap.start()
    for name in fetched[10:]:
        fetches[name].wait()
    hidden = r.tok[...].astype(F32) + gate1 * r.attn_v[...]
    normal2, rate2 = normalized(hidden)
    r.normal[...] = normal2
    grad_out = r.cot[...].astype(F32)
    arrived(r.branch.at[:, theirs_half], r.swap_rs.at[0])
    arrived(r.gmlp.at[:, theirs_half], r.swap_rs.at[1])
    arrived(r.gsum_c, r.swap_rs.at[2])
    for swap in swaps:
        swap.wait_send()

    def put(vector, value):
        for i in range(value.shape[1] // 128):
            at = value.shape[1] // 128 * vector + i
            r.vec[at : at + 1, :] = value[:, 128 * i : 128 * (i + 1)]

    branch = r.branch[...]
    r.out_o[...] = (hidden + gate2 * branch).astype(BF16)
    put(5, jnp.sum(grad_out * branch, axis=0, keepdims=True))
    grad_gates = [r.gsum[:, k : k + 1] + r.gsum_c[:, k : k + 1] for k in range(2)]
    inner = gates[0] * grad_gates[0] + gates[1] * grad_gates[1]
    grad_chosen = [gates[k] * (grad_gates[k] - inner) for k in range(2)]
    grad_logits = (grad_chosen[0] * named[0] + grad_chosen[1] * named[1]).astype(BF16)
    grad_mlp = r.gmlp[...] + contract(grad_logits, r.routew_v[...], (1,), (1,))
    normal2 = r.normal[...]
    put(3, jnp.sum(grad_mlp, axis=0, keepdims=True))
    put(4, jnp.sum(grad_mlp * normal2, axis=0, keepdims=True))
    r.ghid[...] = grad_out + norm_back(normal2, rate2, grad_mlp * (1.0 + scale2))
    grad_hidden = r.ghid[...]
    put(2, jnp.sum(grad_hidden * r.attn_v[...], axis=0, keepdims=True))
    r.gattn[...] = (gate1 * grad_hidden).astype(BF16)

    def weight_terms(target, left, right):
        columns = right.shape[1]
        cut = 384
        for n in range(columns // cut if columns > cut else 1):
            lo, hi = cut * n, min(columns, cut * (n + 1))
            for h in range(2):
                value = contract(left[:, 384 * h : 384 * (h + 1)], right[:, lo:hi], (0,), (0,))
                target[2 * h : 2 * h + 2, :, :, :, lo:hi] = value.astype(BF16).reshape(
                    *blocks, hi - lo
                )

    weight_terms(r.proj_t, r.gattn, r.mixed_v)
    weight_terms(r.route_t, r.mlp_v[:patches, :], grad_logits)
    pump(1)
    r.gmix[...] = jnp.dot(r.gattn[...], r.projw_v[...], preferred_element_type=F32).astype(BF16)
    for k in range(4):
        for i in (2, 3):
            sums.start(i, k)
    masks = head_masks(r.gmix.shape[0])
    scale_factor = 64 ** (-0.5)
    for pair in range(width // 128):
        at = [slice(width * j + 128 * pair, width * j + 128 * (pair + 1)) for j in range(3)]
        q, k, v = [r.act_v[:, at[j]] for j in range(3)]
        gm = r.gmix[:, at[0]]
        found = [None] * 3
        for h in range(2):
            probs = r.probs_v[2 * pair + h]
            grad_probs = contract(gm * masks[h].astype(BF16), v, (1,), (1,))
            weighted = jnp.sum(probs * grad_probs, axis=-1, keepdims=True)
            grad_scores = (probs * (grad_probs - weighted)).astype(BF16)
            parts = (
                jnp.dot(grad_scores, k, preferred_element_type=F32) * scale_factor,
                contract(grad_scores, q, (0,), (0,)) * scale_factor,
                contract(probs.astype(BF16), gm, (0,), (0,)),
            )
            found = [
                part * masks[h] if old is None else old + part * masks[h]
                for part, old in zip(parts, found, strict=True)
            ]
            pump(1)
        for j in range(3):
            r.gqkv[:, at[j]] = found[j].astype(BF16)
    r.gpart[...] = contract(r.gqkv[...], r.qkvw_v[...], (1,), (1,)).astype(BF16)
    swap = remote(r.gpart, r.gpart_c, r.swap_ss.at[3], r.swap_rs.at[3], peer)
    swap.start()
    weight_terms(r.qkv_t, r.attnlow_v, r.gqkv)
    for k in range(4):
        sums.start(4, k)
    tokens = r.tok[...].astype(F32)
    normal1, rate1 = normalized(tokens)
    swap.wait()
    grad_in = r.gpart[...].astype(F32) + r.gpart_c[...].astype(F32)
    put(0, jnp.sum(grad_in, axis=0, keepdims=True))
    put(1, jnp.sum(grad_in * normal1, axis=0, keepdims=True))
    for k, other in enumerate(others):
        sends.go(
            lambda k=k, other=other: remote(
                r.vec, r.every.at[me], r.vec_ss.at[k], r.vec_rs.at[me], (other, core)
            )
        )
    r.tokens_o[...] = r.ghid[...] + norm_back(normal1, rate1, grad_in * (1.0 + scale1))
    while queue:
        pump()
    for k in range(4):
        for i in (2, 3, 4):
            sums.step(i, k)
    for a in range(2 * pieces):
        take = (r.take0, r.take1)[a // pieces]
        arrived(take.at[pl.ds(a % pieces * cut, cut), :], r.trade_rs.at[a])
    for left, right, take, result in (
        (r.ein_t, r.epre, r.take0, r.eup_o), (r.eg_t, r.eact, r.take1, r.edown_o),
    ):

        def outward(n, slot, result=result):
            at = pl.ds(pl.multiple_of(n * 512 + slot * 256, 128), 256)
            return at, pltpu.make_async_copy(r.stage.at[slot], result.at[:, at], r.keep_sem.at[slot])

        def turn(n, _, left=left, right=right, take=take, outward=outward):
            for slot in range(2):
                at, copy = outward(n, slot)
                guarded(n > 0, lambda: outward(n - 1, slot)[1].wait())
                r.stage[slot] = jnp.dot(
                    left[x], right[:, at], preferred_element_type=F32
                ) + take[:, at].astype(F32)
                copy.start()
            return 0

        turns = hidden_units // 512
        lax.fori_loop(0, turns, turn, 0)
        for slot in range(2):
            outward(turns - 1, slot)[1].wait()
    for i in range(2):
        sums.finish(i)
    r.every[me] = r.vec[...]
    for other in others[::-1]:
        arrived(r.every.at[other], r.vec_rs.at[other])
    cond = r.cond[...]
    chunks = r.vec.shape[0] // 6
    for j in range(6):
        for i in range(chunks):
            r.ada_o[:, j, 128 * i : 128 * (i + 1)] = lax.dot_general(
                cond, r.every[:, chunks * j + i, :], (((0,), (0,)), ((), ())),
                precision=highest, preferred_element_type=F32,
            )
    for i in (2, 3, 4):
        sums.finish(i)
    sends.drain()


def backward(given, near):
    count = 16
    dma = pltpu.SemaphoreType.DMA
    shape = jax.ShapeDtypeStruct
    operands = given | near
    a = types.SimpleNamespace(**operands)
    patches, width = a.tok.shape
    slots, half = a.ein.shape[1:]
    head_width = a.mixed.shape[1]
    hidden = a.eup.shape[1]
    quarter = a.up.shape[1]
    size = slots // count
    vectors = a.mod.shape[0]
    columns = dict(up=quarter, down=quarter, proj=head_width, route=128, qkv=3 * head_width)
    results = dict(
        out_o=shape((patches, width), BF16),
        tokens_o=shape((patches, width), F32),
        ada_o=shape((size, 6, width), F32),
        qkv_o=shape((size, 3, head_width), F32),
        proj_o=shape((size, head_width), F32),
        route_o=shape((size, 128), F32),
        up_o=shape((size, 2 * quarter), F32),
        down_o=shape((size, 2 * quarter), F32),
        eup_o=shape((half, hidden), F32),
        edown_o=shape((half, hidden), F32),
    )
    v = pltpu.VMEM
    scratch = {name + "_v": v(array.shape, array.dtype) for name, array in given.items()}
    for name, wide in columns.items():
        scratch[name + "_w"] = v((4, 2, size, wide), BF16)
        scratch[name + "_c"] = v((4, 2, size, wide), BF16)
        scratch[name + "_a"] = v((5, 2, size, wide), BF16)
        scratch[name + "_l"] = v((size, wide), BF16)
        scratch[name + "_t"] = v((4, 2, 2, size, wide), BF16)

    def low(*sizes):
        return v(sizes, BF16)

    def full(*sizes):
        return v(sizes, F32)

    scratch |= dict(
        ein_t=low(2, half, slots), eg_t=low(2, half, slots),
        eact=low(slots, hidden), epre=low(slots, hidden),
        take0=low(half, hidden), take1=low(half, hidden),
        stage=full(2, half, 256),
        their0=low(slots, half), their1=low(slots, half), back0=low(slots, half), back1=low(slots, half),
        mlp_t=low(width, 2 * patches), gsh_t=low(width, 2 * patches),
        sact=low(2 * patches, quarter), spre=low(2 * patches, quarter),
        part0=low(2 * patches, width),
        their2=low(2 * patches, half), their3=low(2 * patches, half),
        pass0=low(patches, half), pass1=low(patches, half), came0=low(patches, half), came1=low(patches, half),
        branch=full(patches, width), gmlp=full(patches, width),
        normal=full(patches, width), ghid=full(patches, width),
        gattn=low(patches, width), gpart=low(patches, width), gpart_c=low(patches, width),
        gmix=low(patches, head_width), gqkv=low(patches, 3 * head_width),
        gsum=full(patches, 128), gsum_c=full(patches, 128), gate_row=full(8, width),
        vec=full(vectors, 128), every=full(count, vectors, 128),
        near_ss=dma((2, 17)), near_rs=dma((2, 17)), ss=dma((2, 16)), rs=dma((2, 16)),
        fetch_sem=dma((len(given),)), keep_sem=dma((2,)), trade_ss=dma((4,)), trade_rs=dma((4,)),
        first_ss=dma((5, 4)), first_rs=dma((5, 4)), load_sem=dma((5, 4)),
        z_ss=dma((5, 3)), z_rs=dma((5, 5)), last_ss=dma((5,)), last_rs=dma((5,)),
        swap_ss=dma((4,)), swap_rs=dma((4,)), vec_ss=dma((16,)), vec_rs=dma((16,)),
        pass_ss=dma((2,)), pass_rs=dma((2,)),
    )
    names = tuple(operands) + tuple(results) + tuple(scratch)
    found = pl.pallas_call(
        functools.partial(backward_kernel, names, tuple(given)),
        out_shape=list(results.values()),
        in_specs=hbm(len(given)) + vmem(len(near)),
        out_specs=vmem(8) + hbm(2),
        scratch_shapes=list(scratch.values()),
        compiler_params=params(3, 64_000_000),
        name="backward",
    )(*operands.values())
    return types.SimpleNamespace(**dict(zip(results, found, strict=True)))


def per_device_direct(
    tokens, cotangent, time_table, timesteps, routes, w_ada, w_qkv, w_proj,
    w_route, w_shared_up, w_shared_down, e_up, e_down,
):
    row_count, model_width = tokens.shape
    core = lax.axis_index(NARROW)
    core_count = lax.axis_size(NARROW)
    wide_count = lax.axis_size(WIDE)
    heads_here = HEADS // core_count
    head_dim = model_width // HEADS
    head_width = heads_here * head_dim
    half = model_width // 2
    scale_factor = head_dim ** (-0.5)
    wide_place = lax.axis_index(WIDE)
    upper = wide_place % 2 == 1
    ada_rows = w_ada.shape[0]

    table = lax.dynamic_slice_in_dim(time_table, wide_place * ada_rows, ada_rows, 1)
    table = jnp.pad(table, ((0, -table.shape[0] % 128), (0, 0)))
    ts_tile = jnp.broadcast_to(timesteps[:, None], (8, 128)).astype(jnp.int32)
    (
        mod, cond_own, qkv_full, proj_full, route_full, activated, probs_full, mixed_low,
        attn_out, attn_low, mlp_low, grad_shared, gate_lanes,
        up_full, down_full, up_other, down_other, expert_in, grad_expert_out,
    ) = forward(
        ts_tile,
        table,
        w_ada.reshape(ada_rows, 6 * model_width),
        w_qkv.reshape(ada_rows, 3 * head_width),
        w_proj,
        jnp.pad(w_route, ((0, 0), (0, 128 - EXPERTS))),
        w_shared_up,
        w_shared_down,
        e_up,
        e_down,
        tokens,
        cotangent,
        routes,
    )
    got = backward(
        dict(
            ein=expert_in, eg=grad_expert_out, eup=e_up, upo=up_other, edn=e_down, dno=down_other,
            mlp=mlp_low, gsh=grad_shared, up=up_full, down=down_full,
            attn=attn_out, attnlow=attn_low, act=activated,
            probs=probs_full, mixed=mixed_low, qkvw=qkv_full, projw=proj_full, routew=route_full,
        ),
        dict(tok=tokens, cot=cotangent, mod=mod, cond=cond_own, routes=routes, gates=gate_lanes),
    )
    return (
        got.out_o,
        got.tokens_o,
        got.ada_o,
        got.qkv_o,
        got.proj_o,
        got.route_o[:, :EXPERTS],
        got.up_o,
        got.down_o,
        got.eup_o,
        got.edown_o,
    )


def solution(mesh):
    placed = (
        P(WIDE, None),
        P(WIDE, None),
        P(),
        P(WIDE),
        P(WIDE, None),
        P(WIDE, None, None),
        P(WIDE, None, NARROW),
        P(WIDE, NARROW),
        P(WIDE, None),
        P(WIDE, NARROW),
        P(WIDE, NARROW),
        P(WIDE, NARROW),
        P(WIDE, NARROW),
    )
    direct = mesh.shape[WIDE] == 16 and mesh.shape[NARROW] == 2
    return jax.shard_map(
        per_device_direct if direct else per_device,
        mesh=mesh,
        in_specs=placed,
        out_specs=(
            P(WIDE, None),
            P(WIDE, None),
            P(WIDE, None, None),
            P(WIDE, None, NARROW),
            P(WIDE, NARROW),
            P(WIDE, None),
            P(WIDE, NARROW),
            P(WIDE, NARROW),
            P(WIDE, NARROW),
            P(WIDE, NARROW),
        ),
        check_vma=False,
    )
```

```python
import functools
import types

import jax
import jax.numpy as jnp
from jax import lax
from jax.experimental import pallas as pl
from jax.experimental.pallas import tpu as pltpu
from jax.sharding import PartitionSpec as P

WIDE, NARROW = "wide", "narrow"
HEADS = 12
EXPERTS = 8
CAP = 96


epsilon = 1e-06
highest = lax.Precision.HIGHEST


def swapped(shard, axis, distance):
    return lax.ppermute(shard, axis, [(i, i ^ 1 << distance) for i in range(lax.axis_size(axis))])


def normalize(values):
    centre = jnp.mean(values, axis=-1, keepdims=True)
    shifted = values - centre
    spread = jnp.mean(shifted * shifted, axis=-1, keepdims=True)
    return shifted * lax.rsqrt(spread + epsilon)


def modulate(values, offset, factor):
    return normalize(values) * (1.0 + factor[:, None, :]) + offset[:, None, :]


def gelu_tanh(values):
    return jax.nn.gelu(values, approximate=True)


def gelu_back(values, gradient):
    return jax.vjp(gelu_tanh, values)[1](gradient)[0]


def contract(left_side, right_side, left_dims, right_dims):
    return lax.dot_general(
        left_side,
        right_side,
        ((left_dims, right_dims), ((), ())),
        preferred_element_type=jnp.float32,
    )


def slot_table(route_block):
    flat_routes = route_block.reshape(-1)
    matches = (flat_routes[:, None] == jnp.arange(EXPERTS, dtype=jnp.int32)[None, :]).astype(
        jnp.int32
    )
    earlier = jnp.cumsum(matches, axis=0, dtype=jnp.int32) - matches
    ranking = jnp.sum(earlier * matches, axis=1, dtype=jnp.int32)
    return flat_routes * CAP + ranking


def join_halves(stacked, bit_level, wide_place):
    partner = swapped(stacked, WIDE, bit_level)
    upper = wide_place >> bit_level & 1 == 1
    return jnp.where(
        upper,
        jnp.concatenate([partner, stacked], axis=1),
        jnp.concatenate([stacked, partner], axis=1),
    )


def split_halves(stacked, bit_level, wide_place):
    half_rows = stacked.shape[1] // 2
    upper = wide_place >> bit_level & 1 == 1
    lower_part = stacked[:, :half_rows]
    upper_part = stacked[:, half_rows:]
    kept = jnp.where(upper, upper_part, lower_part)
    given = jnp.where(upper, lower_part, upper_part)
    return kept + swapped(given.astype(jnp.bfloat16), WIDE, bit_level).astype(given.dtype)


def per_device(
    tokens,
    cotangent,
    time_table,
    timesteps,
    routes,
    w_ada,
    w_qkv,
    w_proj,
    w_route,
    w_shared_up,
    w_shared_down,
    e_up,
    e_down,
):
    images = timesteps.shape[0]
    row_count = tokens.shape[0]
    model_width = tokens.shape[1]
    patches = row_count // images
    core_count = lax.axis_size(NARROW)
    wide_count = lax.axis_size(WIDE)
    group_size = wide_count // EXPERTS
    levels = group_size.bit_length() - 1
    slice_rows = CAP // group_size
    heads_here = HEADS // core_count
    head_dim = model_width // HEADS
    head_width = heads_here * head_dim
    scale_factor = head_dim ** (-0.5)
    wide_place = lax.axis_index(WIDE)
    ada_rows = w_ada.shape[0]
    step_onehot = (
        timesteps[:, None] == jnp.arange(time_table.shape[0], dtype=jnp.int32)[None, :]
    ).astype(jnp.bfloat16)
    cond = jnp.dot(step_onehot, time_table, preferred_element_type=jnp.float32)
    cond_act = jax.nn.silu(cond).astype(jnp.bfloat16)
    qkv_full, proj_full, route_full, up_full, down_full = (
        lax.all_gather(w_qkv, WIDE, axis=0, tiled=True),
        lax.all_gather(w_proj, WIDE, axis=0, tiled=True),
        lax.all_gather(w_route, WIDE, axis=0, tiled=True),
        lax.all_gather(w_shared_up, WIDE, axis=0, tiled=True),
        lax.all_gather(w_shared_down, WIDE, axis=0, tiled=True),
    )
    cond_every = lax.all_gather(cond_act, WIDE, axis=0, tiled=True)
    cond_own = lax.dynamic_slice_in_dim(cond_every, wide_place * ada_rows, ada_rows, 1)
    modulation_terms = jnp.dot(
        cond_own, w_ada.reshape(ada_rows, 6 * model_width), preferred_element_type=jnp.float32
    )
    modulation = lax.psum_scatter(modulation_terms, WIDE, scatter_dimension=0, tiled=True)
    modulation = modulation.reshape(images, 6, model_width)
    expert_weights = jnp.stack([e_up, e_down])
    for bit_level in range(levels):
        expert_weights = join_halves(expert_weights, bit_level, wide_place)
    expert_up = expert_weights[0]
    expert_down = expert_weights[1]
    inputs = tokens.astype(jnp.float32).reshape(images, patches, model_width)
    attn_in, pull_first = jax.vjp(modulate, inputs, modulation[:, 0], modulation[:, 1])
    attn_low = attn_in.reshape(row_count, model_width).astype(jnp.bfloat16)
    projected = jnp.dot(
        attn_low, qkv_full.reshape(model_width, 3 * head_width), preferred_element_type=jnp.float32
    )
    projected = projected.reshape(images, patches, 3, heads_here, head_dim).astype(jnp.bfloat16)
    queries = projected[:, :, 0]
    keys = projected[:, :, 1]
    values = projected[:, :, 2]
    scores = (
        jnp.einsum("bqhd,bkhd->bhqk", queries, keys, preferred_element_type=jnp.float32)
        * scale_factor
    )
    highest_score = jnp.max(scores, axis=-1, keepdims=True)
    log_total = highest_score + jnp.log(
        jnp.sum(jnp.exp(scores - highest_score), axis=-1, keepdims=True)
    )
    probs_low = jnp.exp(scores - log_total).astype(jnp.bfloat16)
    mixed = jnp.einsum("bhqk,bkhd->bqhd", probs_low, values, preferred_element_type=jnp.float32)
    mixed_low = mixed.astype(jnp.bfloat16).reshape(row_count, head_width)
    attn_part = contract(mixed_low, proj_full, (1,), (1,))
    attn_out = lax.psum(attn_part.astype(jnp.bfloat16), NARROW).astype(jnp.float32)
    attn_three = attn_out.reshape(images, patches, model_width)
    hidden_state = inputs + modulation[:, 2][:, None, :] * attn_three
    mlp_in, pull_second = jax.vjp(modulate, hidden_state, modulation[:, 3], modulation[:, 4])
    mlp_low = mlp_in.reshape(row_count, model_width).astype(jnp.bfloat16)
    logits = jnp.dot(mlp_low, route_full, preferred_element_type=jnp.float32)
    selector = (routes[:, :, None] == jnp.arange(EXPERTS, dtype=jnp.int32)[None, None, :]).astype(
        jnp.float32
    )
    chosen = jnp.sum(logits[:, None, :] * selector, axis=-1)
    gate_values, pull_gate = jax.vjp(
        lambda picked_logits: jax.nn.softmax(picked_logits, axis=-1), chosen
    )
    slot_index = slot_table(routes)
    outgoing = (
        jnp.zeros((EXPERTS * CAP, model_width), jnp.bfloat16)
        .at[slot_index]
        .set(jnp.repeat(mlp_low, 2, axis=0))
    )
    arrived = lax.all_to_all(
        outgoing.reshape(wide_count, slice_rows, model_width),
        WIDE,
        split_axis=0,
        concat_axis=0,
        tiled=True,
    )
    expert_in = arrived.reshape(wide_count * slice_rows, model_width)
    shared_pre = jnp.dot(mlp_low, up_full, preferred_element_type=jnp.float32)
    shared_act = gelu_tanh(shared_pre).astype(jnp.bfloat16)
    shared_part = contract(shared_act, down_full, (1,), (1,))
    expert_pre = jnp.dot(expert_in, expert_up, preferred_element_type=jnp.float32)
    expert_act = gelu_tanh(expert_pre).astype(jnp.bfloat16)
    expert_part = contract(expert_act, expert_down, (1,), (1,))
    expert_sum, shared_out = (
        lax.psum(expert_part.astype(jnp.bfloat16), NARROW).astype(jnp.float32),
        lax.psum(shared_part.astype(jnp.bfloat16), NARROW).astype(jnp.float32),
    )
    expert_out = expert_sum.astype(jnp.bfloat16)
    returned = lax.all_to_all(
        expert_out.reshape(wide_count, slice_rows, model_width),
        WIDE,
        split_axis=0,
        concat_axis=0,
        tiled=True,
    )
    returned = returned.reshape(EXPERTS * CAP, model_width)
    picked = returned[slot_index].astype(jnp.float32).reshape(row_count, 2, model_width)
    mixture = jnp.sum(gate_values[:, :, None] * picked, axis=1)
    branch = (shared_out + mixture).reshape(images, patches, model_width)
    output = hidden_state + modulation[:, 5][:, None, :] * branch
    grad_out = cotangent.astype(jnp.float32).reshape(images, patches, model_width)
    grad_branch = (modulation[:, 5][:, None, :] * grad_out).reshape(row_count, model_width)
    grad_gate2 = jnp.sum(grad_out * branch, axis=1)
    grad_pick = jnp.sum(grad_branch[:, None, :] * picked, axis=-1)
    grad_rows = (
        (gate_values[:, :, None] * grad_branch[:, None, :])
        .astype(jnp.bfloat16)
        .reshape(row_count * 2, model_width)
    )
    grad_slots = jnp.zeros((EXPERTS * CAP, model_width), jnp.bfloat16).at[slot_index].set(grad_rows)
    grad_expert_out = lax.all_to_all(
        grad_slots.reshape(wide_count, slice_rows, model_width),
        WIDE,
        split_axis=0,
        concat_axis=0,
        tiled=True,
    )
    grad_expert_out = grad_expert_out.reshape(wide_count * slice_rows, model_width)
    grad_shared = grad_branch.astype(jnp.bfloat16)
    shared_down_grad = contract(grad_shared, shared_act, (0,), (0,))
    grad_shared_act = jnp.dot(grad_shared, down_full, preferred_element_type=jnp.float32)
    grad_shared_pre = gelu_back(shared_pre, grad_shared_act).astype(jnp.bfloat16)
    shared_up_grad = contract(mlp_low, grad_shared_pre, (0,), (0,))
    grad_in_shared = contract(grad_shared_pre, up_full, (1,), (1,))
    grad_chosen = pull_gate(grad_pick)[0]
    grad_logits = jnp.sum(grad_chosen[:, :, None] * selector, axis=1).astype(jnp.bfloat16)
    route_grad = contract(mlp_low, grad_logits, (0,), (0,))
    grad_in_route = contract(grad_logits, route_full, (1,), (1,))
    expert_down_grad = contract(grad_expert_out, expert_act, (0,), (0,))
    grad_expert_act = jnp.dot(grad_expert_out, expert_down, preferred_element_type=jnp.float32)
    grad_expert_pre = gelu_back(expert_pre, grad_expert_act).astype(jnp.bfloat16)
    expert_up_grad = contract(expert_in, grad_expert_pre, (0,), (0,))
    grad_in_part = contract(grad_expert_pre, expert_up, (1,), (1,))
    grad_in_rows, grad_in_shared_sum = (
        lax.psum(grad_in_part.astype(jnp.bfloat16), NARROW).astype(jnp.float32),
        lax.psum(grad_in_shared.astype(jnp.bfloat16), NARROW).astype(jnp.float32),
    )
    back_rows = lax.all_to_all(
        grad_in_rows.astype(jnp.bfloat16).reshape(wide_count, slice_rows, model_width),
        WIDE,
        split_axis=0,
        concat_axis=0,
        tiled=True,
    )
    back_rows = back_rows.reshape(EXPERTS * CAP, model_width)
    grad_in_expert = jnp.sum(
        back_rows[slot_index].astype(jnp.float32).reshape(row_count, 2, model_width), axis=1
    )
    grad_mlp_in = grad_in_shared_sum + grad_in_route + grad_in_expert
    grad_hidden_norm, grad_shift2, grad_scale2 = pull_second(
        grad_mlp_in.reshape(images, patches, model_width)
    )
    grad_hidden = grad_out + grad_hidden_norm
    grad_gate1 = jnp.sum(grad_hidden * attn_three, axis=1)
    grad_attn = (
        (modulation[:, 2][:, None, :] * grad_hidden)
        .reshape(row_count, model_width)
        .astype(jnp.bfloat16)
    )
    proj_grad = contract(grad_attn, mixed_low, (0,), (0,))
    grad_mixed = jnp.dot(grad_attn, proj_full, preferred_element_type=jnp.float32).astype(
        jnp.bfloat16
    )
    grad_mixed = grad_mixed.reshape(images, patches, heads_here, head_dim)
    again_scores = (
        jnp.einsum("bqhd,bkhd->bhqk", queries, keys, preferred_element_type=jnp.float32)
        * scale_factor
    )
    probs_full = jnp.exp(again_scores - log_total)
    again_low = probs_full.astype(jnp.bfloat16)
    grad_probs = jnp.einsum(
        "bqhd,bkhd->bhqk", grad_mixed, values, preferred_element_type=jnp.float32
    )
    grad_values = jnp.einsum(
        "bhqk,bqhd->bkhd", again_low, grad_mixed, preferred_element_type=jnp.float32
    )
    weighted_sum = jnp.sum(probs_full * grad_probs, axis=-1, keepdims=True)
    grad_scores = (probs_full * (grad_probs - weighted_sum)).astype(jnp.bfloat16)
    grad_queries = (
        jnp.einsum("bhqk,bkhd->bqhd", grad_scores, keys, preferred_element_type=jnp.float32)
        * scale_factor
    )
    grad_keys = (
        jnp.einsum("bhqk,bqhd->bkhd", grad_scores, queries, preferred_element_type=jnp.float32)
        * scale_factor
    )
    grad_qkv = jnp.stack([grad_queries, grad_keys, grad_values], axis=2).astype(jnp.bfloat16)
    grad_qkv = grad_qkv.reshape(row_count, 3 * head_width)
    qkv_grad = contract(attn_low, grad_qkv, (0,), (0,)).reshape(model_width, 3, head_width)
    grad_attn_part = contract(grad_qkv, qkv_full.reshape(model_width, 3 * head_width), (1,), (1,))
    grad_attn_in = lax.psum(grad_attn_part.astype(jnp.bfloat16), NARROW).astype(jnp.float32)
    grad_input_norm, grad_shift1, grad_scale1 = pull_first(
        grad_attn_in.reshape(images, patches, model_width)
    )
    tokens_grad = (grad_hidden + grad_input_norm).reshape(row_count, model_width)
    grad_modulation = jnp.stack(
        [grad_shift1, grad_scale1, grad_gate1, grad_shift2, grad_scale2, grad_gate2], axis=1
    )
    grad_modulation = grad_modulation.reshape(images, 6 * model_width)
    grad_mod_every = lax.all_gather(grad_modulation, WIDE, axis=0, tiled=True)
    ada_part = jnp.dot(cond_own.astype(jnp.float32).T, grad_mod_every, precision=highest).reshape(
        ada_rows, 6, model_width
    )
    qkv_part, proj_part, route_part, shared_up_part, shared_down_part = (
        lax.psum_scatter(qkv_grad, WIDE, scatter_dimension=0, tiled=True),
        lax.psum_scatter(proj_grad, WIDE, scatter_dimension=0, tiled=True),
        lax.psum_scatter(route_grad, WIDE, scatter_dimension=0, tiled=True),
        lax.psum_scatter(shared_up_grad, WIDE, scatter_dimension=0, tiled=True),
        lax.psum_scatter(shared_down_grad, WIDE, scatter_dimension=0, tiled=True),
    )
    expert_grads = jnp.stack([expert_up_grad, expert_down_grad])
    for bit_level in reversed(range(levels)):
        expert_grads = split_halves(expert_grads, bit_level, wide_place)
    return (
        output.reshape(row_count, model_width).astype(jnp.bfloat16),
        tokens_grad,
        ada_part,
        qkv_part,
        proj_part,
        route_part,
        shared_up_part,
        shared_down_part,
        expert_grads[0],
        expert_grads[1],
    )


MESH = pl.DeviceIdType.MESH
F32 = jnp.float32
BF16 = jnp.bfloat16
Z_SIZE, Y_SIZE, X_SIZE = 4, 2, 2
VMEM_LIMIT = 60 * 1024 * 1024


def place(index):
    return lax.div(index, 4), lax.rem(lax.div(index, 2), 2), lax.rem(index, 2)


def at_place(z, y, x):
    return z * 4 + y * 2 + x


class Sends:
    def __init__(self):
        self.items = []

    def go(self, make, when=None):
        self.items.append((make, when))
        guarded(when, lambda: make().start())

    def drain(self):
        for make, when in self.items:
            guarded(when, lambda make=make: make().wait_send())


def guarded(when, action):
    if when is None:
        action()
        return

    @pl.when(when)
    def _():
        action()


def both(first, second):
    if first is None:
        return second
    if second is None:
        return first
    return jnp.logical_and(first, second)


def remote(src, dst, send_sem, recv_sem, target):
    return pltpu.make_async_remote_copy(
        src_ref=src,
        dst_ref=dst,
        send_sem=send_sem,
        recv_sem=recv_sem,
        device_id=target,
        device_id_type=MESH,
    )


def greet(targets):
    barrier = pltpu.get_barrier_semaphore()
    for target in targets:
        pl.semaphore_signal(barrier, inc=1, device_id=target, device_id_type=MESH)
    pl.semaphore_wait(barrier, len(targets))


class Gather:
    def __init__(self, streams, send_sem, recv_sem, sends):
        self.streams, self.ss, self.rs, self.sends = streams, send_sem, recv_sem, sends
        self.count = [0] * len(streams)
        self.core = lax.axis_index(NARROW)
        self.me = lax.axis_index(WIDE)
        self.z, self.y, self.x = place(self.me)
        self.to_x = at_place(self.z, self.y, 1 - self.x)
        self.to_y = at_place(self.z, 1 - self.y, self.x)
        self.can_up, self.can_down = self.z < Z_SIZE - 1, self.z > 0
        self.up, self.down = self.me + 4, self.me - 4

    def block(self, s, origin):
        shard, full, start, width = self.streams[s][:4]
        rows = shard.shape[0]
        return full.at[pl.ds(pl.multiple_of(origin * rows, 16), rows), pl.ds(start, width)]

    def send(self, s, origin, target, when=None, own=False, over_x=False):
        shard, full, start, width, _, parted = self.streams[s]
        index = self.count[s]
        self.count[s] += 1

        def make():
            dst = self.block(s, origin)
            first = start
            if parted:
                first = pl.multiple_of((1 - self.x if over_x else self.x) * full.shape[1] + start, 128)
            src = shard.at[:, pl.ds(first, width)] if own else dst
            return remote(src, dst, self.ss.at[s, index], self.rs.at[s, origin], (target, self.core))

        self.sends.go(make, when)

    def wait(self, s, origin, when=None):
        def action():
            ref = self.block(s, origin)
            remote(
                ref, ref, self.ss.at[s, 0], self.rs.at[s, origin], (self.to_x, self.core)
            ).wait_recv()

        guarded(when, action)

    def spread(self, s, origin, when=None, own=False, up=True, down=True, over_y=True):
        if up:
            self.send(s, origin, self.up, both(when, self.can_up), own)
        if down:
            self.send(s, origin, self.down, both(when, self.can_down), own)
        if over_y:
            self.send(s, origin, self.to_y, when, own)

    def begin_x(self, s):
        self.send(s, self.me, self.to_x, own=True, over_x=True)

    def begin(self, s):
        self.begin_x(s)
        self.spread(s, self.me, own=True)

    def after_x(self, s):
        self.wait(s, self.to_x)
        self.spread(s, self.to_x)

    def y_pair(self, s):
        if self.streams[s][4] == "xyz":
            for xx in (self.x, 1 - self.x):
                origin = at_place(self.z, 1 - self.y, xx)
                self.wait(s, origin)
                self.spread(s, origin, over_y=False)

    def after_z(self, s, distance):
        order = self.streams[s][4]
        ys = (self.y,) if order == "xzy" else (self.y, 1 - self.y)
        for step, ok in ((-distance, self.z >= distance), (distance, self.z + distance < Z_SIZE)):
            for yy in ys:
                for xx in (self.x, 1 - self.x):
                    origin = at_place(self.z + step, yy, xx)
                    self.wait(s, origin, ok)
                    self.spread(s, origin, ok, up=step < 0, down=step > 0, over_y=order == "xzy")

    def finish(self, s):
        if self.streams[s][4] == "xzy":
            for zz in range(Z_SIZE):
                for xx in range(X_SIZE):
                    self.wait(s, at_place(zz, 1 - self.y, xx))


def vmem(count):
    return [pl.BlockSpec(memory_space=pltpu.VMEM)] * count


def hbm(count):
    return [pl.BlockSpec(memory_space=pl.ANY)] * count


def params(collective_id, vmem_limit=VMEM_LIMIT):
    return pltpu.CompilerParams(
        collective_id=collective_id, has_side_effects=True, vmem_limit_bytes=vmem_limit
    )


def peers_far_first(me):
    z, y, x = place(me)
    found = []
    for dz in range(Z_SIZE):
        for dy in range(Y_SIZE):
            for dx in range(X_SIZE):
                if dz or dy or dx:
                    zz = lax.rem(z + dz, Z_SIZE)
                    found.append(at_place(zz, lax.rem(y + dy, 2), lax.rem(x + dx, 2)))
    return found[::-1]


def lanes_of(ref, vector):
    rows = ref.shape[0] // 6
    return jnp.concatenate(
        [ref[rows * vector + i : rows * vector + i + 1, :] for i in range(rows)], axis=1
    )


def head_masks(rows):
    lane = lax.broadcasted_iota(jnp.int32, (rows, 128), 1)
    first = (lane < 64).astype(F32)
    return first, 1.0 - first


def choice_masks(routes_ref):
    rows = routes_ref.shape[0]
    lane = lax.broadcasted_iota(jnp.int32, (rows, 128), 1)
    named = [(routes_ref[:, k : k + 1] == lane).astype(F32) for k in range(2)]
    above = lax.broadcasted_iota(jnp.int32, (rows, rows), 0)
    along = lax.broadcasted_iota(jnp.int32, (rows, rows), 1)
    before = jnp.dot(
        (along < above).astype(F32).astype(BF16),
        (named[0] + named[1]).astype(BF16),
        preferred_element_type=F32,
    )
    slot = lax.broadcasted_iota(jnp.int32, (rows, EXPERTS * CAP), 1)
    takes = []
    for k in range(2):
        rank = jnp.sum(before * named[k], axis=1, keepdims=True)
        own = routes_ref[:, k : k + 1].astype(F32) * CAP + rank
        takes.append((slot == own.astype(jnp.int32)).astype(F32).astype(BF16))
    return named, takes


def attend(attn_low, qkv_ref, act_ref, probs_ref, mixed_ref, pump):
    rows, width = attn_low.shape[0], mixed_ref.shape[1]
    for j in range(3):
        act_ref[:, width * j : width * (j + 1)] = jnp.dot(
            attn_low, qkv_ref[:, width * j : width * (j + 1)], preferred_element_type=F32
        ).astype(BF16)
        pump()
    masks = head_masks(rows)
    scale_factor = 64 ** (-0.5)
    for pair in range(width // 128):
        q, k, v = [
            act_ref[:, width * j + 128 * pair : width * j + 128 * (pair + 1)] for j in range(3)
        ]
        mixed = None
        for h in range(2):
            scores = contract(q * masks[h].astype(BF16), k, (1,), (1,)) * scale_factor
            top = jnp.max(scores, axis=-1, keepdims=True)
            weights = jnp.exp(scores - top)
            probs = weights / jnp.sum(weights, axis=-1, keepdims=True)
            probs_ref[2 * pair + h] = probs
            part = jnp.dot(probs.astype(BF16), v, preferred_element_type=F32) * masks[h]
            mixed = part if mixed is None else mixed + part
            pump()
        mixed_ref[:, 128 * pair : 128 * (pair + 1)] = mixed.astype(BF16)


def forward_kernel(
    ts_ref, table_ref, ada_ref, qkv_ref, proj_ref, route_ref, up_ref, down_ref,
    eup_ref, edown_ref, tok_ref, cot_ref, routes_ref,
    mod_ref, cond_ref, qkv_out, proj_out, route_out, act_ref, probs_ref, mixed_ref,
    attn_ref, attn_low_ref, mlp_ref, gshared_ref, gates_ref,
    up_out, down_out, eup_out, edown_out, rows_out, grads_out,
    ts_all, terms, landed, part, theirs, gate_row, rows_send, grads_send,
    ts_ss, ts_rs, mod_ss, mod_rs, ag_ss, ag_rs, own_sem, join_ss, join_rs, swap_sem,
    ss, rs, pass_ss, pass_rs, own_a, pair_ss, pair_rs, qkv_own,
):
    me, core = lax.axis_index(WIDE), lax.axis_index(NARROW)
    count = lax.axis_size(WIDE)
    others = peers_far_first(me)
    peer = (me, 1 - core)
    greet([(other, core) for other in others] + [peer])
    sends = Sends()
    for k, other in enumerate(others):
        sends.go(lambda k=k, other=other: remote(ts_ref, ts_all.at[me], ts_ss.at[k], ts_rs.at[me], (other, core)))
    half = down_out.shape[1] // 2
    streams = [
        (qkv_own, qkv_out, 0, qkv_own.shape[1], "xzy", False),
        (proj_ref, proj_out, 0, proj_ref.shape[1], "xzy", False),
        (route_ref, route_out, 0, route_ref.shape[1], "xzy", False),
        (up_ref, up_out, 0, up_out.shape[1], "xzy", True),
        (down_ref, down_out, 0, half, "xzy", True),
        (down_ref, down_out, half, half, "xyz", True),
    ]
    for j in range(3):
        at = qkv_ref.shape[2] * j
        qkv_own[:, at : at + qkv_ref.shape[2]] = qkv_ref[j]
    ag = Gather(streams, ag_ss, ag_rs, sends)
    for s in range(3):
        ag.begin(s)
    pieces = 8
    joins = []
    for a, (src, dst) in enumerate(((eup_ref, eup_out), (edown_ref, edown_out))):
        size = src.shape[0] // pieces
        for p in range(pieces):
            cut = pl.ds(p * size, size)
            joins.append(
                lambda a=a, p=p, src=src, dst=dst, cut=cut: remote(
                    src.at[cut, :], dst.at[cut, :],
                    join_ss.at[a * pieces + p], join_rs.at[a * pieces + p], (ag.to_x, core),
                )
            )
    waiting = joins[::2] + joins[1::2]

    def join(steps):
        for _ in range(steps):
            if waiting:
                sends.go(waiting.pop(0))

    join(1)
    own = []
    for i, (shard, full) in enumerate(
        ((qkv_own, qkv_out), (proj_ref, proj_out), (route_ref, route_out), (up_ref, up_out), (down_ref, down_out))
    ):
        rows, wide = shard.shape[0], full.shape[1]
        side = pl.multiple_of(ag.x * wide, 128) if wide < shard.shape[1] else 0
        own.append(
            pltpu.make_async_copy(
                shard.at[:, pl.ds(side, wide)],
                full.at[pl.ds(pl.multiple_of(me * rows, 16), rows), :], own_sem.at[i]
            )
        )
        own[-1].start()

    tokens = tok_ref[...].astype(F32)
    normal1, _ = normalized(tokens)

    ts_all[me] = ts_ref[...]
    for other in others[::-1]:
        remote(ts_ref, ts_all.at[other], ts_ss.at[0], ts_rs.at[other], (other, core)).wait_recv()
    steps = jnp.max(ts_all[...], axis=1)[:, :1]
    onehot = (
        steps == lax.broadcasted_iota(jnp.int32, (count, table_ref.shape[0]), 1)
    ).astype(F32).astype(BF16)
    cond = jnp.dot(onehot, table_ref[...], preferred_element_type=F32)
    cond_act = (cond * jax.nn.sigmoid(cond)).astype(BF16)
    cond_ref[...] = cond_act.astype(F32)
    chunks = terms.shape[1] // 6
    for j in range(6):
        vector = jnp.dot(cond_act, ada_ref[j], preferred_element_type=F32)
        for i in range(chunks):
            terms[:, chunks * j + i, :] = vector[:, 128 * i : 128 * (i + 1)]
    for k, other in enumerate(others):
        sends.go(lambda k=k, other=other: remote(terms.at[other], landed.at[me], mod_ss.at[k], mod_rs.at[me], (other, core)))
    join(2)
    for s in range(3):
        ag.after_x(s)
    for s in range(3, len(streams)):
        ag.begin_x(s)
    join(2)

    for distance in range(1, Z_SIZE):
        for s in range(3):
            ag.after_z(s, distance)
        join(2)
    for s in range(3, len(streams)):
        ag.spread(s, ag.me, own=True)
    landed[me] = terms[me]
    for other in others[::-1]:
        remote(terms.at[me], landed.at[other], mod_ss.at[0], mod_rs.at[other], (other, core)).wait_recv()
    mod_ref[...] = jnp.sum(landed[...], axis=0)
    shift1, scale1, gate1, shift2, scale2, gate2 = [lanes_of(mod_ref, j) for j in range(6)]
    attn_low_ref[...] = (normal1 * (1.0 + scale1) + shift1).astype(BF16)
    patches = tok_ref.shape[0]
    first, second = pl.ds(0, patches), pl.ds(patches, patches)
    gate_row[...] = jnp.broadcast_to(gate2, gate_row.shape)
    gshared_ref[first, :] = (gate2 * cot_ref[...].astype(F32)).astype(BF16)
    width = rows_send.shape[1]
    mine = pl.ds(pl.multiple_of(core * width, 128), width)
    theirs_half = pl.ds(pl.multiple_of((1 - core) * width, 128), width)
    across = [
        remote(ref.at[first, mine], ref.at[second, mine], pair_ss.at[i], pair_rs.at[i], (ag.to_x, core))
        for i, ref in enumerate((gshared_ref, mlp_ref))
    ]
    handed = [
        remote(ref.at[second, mine], ref.at[second, mine], pair_ss.at[2 + i], pair_rs.at[2 + i], peer)
        for i, ref in enumerate((gshared_ref, mlp_ref))
    ]
    came = [
        remote(ref.at[second, theirs_half], ref.at[second, theirs_half], pair_ss.at[2 + i], pair_rs.at[2 + i], peer)
        for i, ref in enumerate((gshared_ref, mlp_ref))
    ]
    across[0].start()
    bulk = range(3, len(streams))
    queue = [lambda s=s: ag.after_x(s) for s in bulk]
    queue += [lambda s=s: ag.y_pair(s) for s in bulk]
    queue += [lambda s=s, d=d: ag.after_z(s, d) for d in range(1, Z_SIZE) for s in bulk]

    def pump():
        join(1)
        if queue:
            queue.pop(0)()

    ag.finish(0)
    own[0].wait()
    attend(attn_low_ref[...], qkv_out, act_ref, probs_ref, mixed_ref, pump)
    ag.finish(1)
    own[1].wait()
    part[...] = contract(mixed_ref[...], proj_out[...], (1,), (1,)).astype(BF16)
    swap = remote(part, theirs, swap_sem.at[0], swap_sem.at[1], peer)
    swap.start()
    named, takes = choice_masks(routes_ref)
    pump()
    swap.wait()
    attn_out = part[...].astype(F32) + theirs[...].astype(F32)
    attn_ref[...] = attn_out
    hidden = tok_ref[...].astype(F32) + gate1 * attn_out
    normal2, _ = normalized(hidden)
    mlp_ref[first, :] = (normal2 * (1.0 + scale2) + shift2).astype(BF16)
    ag.finish(2)
    own[2].wait()
    logits = jnp.dot(mlp_ref[first, :], route_out[...], preferred_element_type=F32)
    chosen = [jnp.sum(logits * named[k], axis=1, keepdims=True) for k in range(2)]
    peak = jnp.maximum(chosen[0], chosen[1])
    weight = [jnp.exp(chosen[k] - peak) for k in range(2)]
    total = weight[0] + weight[1]
    gates = [weight[k] / total for k in range(2)]
    lane = lax.broadcasted_iota(jnp.int32, gates_ref.shape, 1)
    gates_ref[...] = jnp.where(lane == 0, gates[0], jnp.where(lane == 1, gates[1], 0.0))
    grad_half = gate_row[0:1, mine] * cot_ref[:, mine].astype(F32)
    rows_send[...] = contract(takes[0] + takes[1], mlp_ref[first, mine], (0,), (0,)).astype(BF16)
    grads_send[...] = (
        contract(takes[0], (gates[0] * grad_half).astype(BF16), (0,), (0,))
        + contract(takes[1], (gates[1] * grad_half).astype(BF16), (0,), (0,))
    ).astype(BF16)

    size = rows_send.shape[0] // count

    def rows(index):
        return pl.ds(pl.multiple_of(index * size, 16), size)

    pairs = ((rows_send, rows_out), (grads_send, grads_out))
    for k, other in enumerate(others):
        for a, (src, dst) in enumerate(pairs):
            sends.go(
                lambda k=k, other=other, a=a, src=src, dst=dst: remote(
                    src.at[rows(other), :], dst.at[core, rows(me), :],
                    ss.at[a, k], rs.at[a, me], (other, core),
                )
            )
    across[1].start()
    across[0].wait()
    handed[0].start()
    join(len(joins))
    kept = []
    for a, (src, dst) in enumerate(pairs):
        sends.go(
            lambda a=a, src=src, dst=dst: remote(
                src.at[rows(me), :], dst.at[core, rows(me), :], pass_ss.at[a, 15], pass_rs.at[a, me], peer
            )
        )
        kept.append(pltpu.make_async_copy(src.at[rows(me), :], dst.at[core, rows(me), :], own_a.at[a]))
        kept[-1].start()
    while queue:
        pump()
    across[1].wait()
    handed[1].start()
    for k, other in enumerate(others[::-1]):
        for a, (src, dst) in enumerate(pairs):
            here = dst.at[core, rows(other), :]
            remote(here, here, ss.at[a, 0], rs.at[a, other], peer).wait_recv()
            sends.go(
                lambda k=k, other=other, a=a, here=here: remote(
                    here, here, pass_ss.at[a, k], pass_rs.at[a, other], peer
                )
            )
    for s in range(3, len(streams)):
        ag.finish(s)
    for i, make in enumerate(joins):
        make().wait_recv()
    for other in [me] + others[::-1]:
        for a, (src, dst) in enumerate(pairs):
            there = dst.at[1 - core, rows(other), :]
            remote(there, there, pass_ss.at[a, 0], pass_rs.at[a, other], peer).wait_recv()
    for i in range(2):
        handed[i].wait_send()
        came[i].wait_recv()
    for copy in own[3:] + kept:
        copy.wait()
    sends.drain()


def forward(ts_tile, table, ada, qkv, proj, route, up, down, e_up, e_down, tokens, cotangent, routes):
    count = 16
    shards = (qkv, proj, route, up, down)
    vectors = 6 * ada.shape[2] // 128
    patches, width = tokens.shape
    slots = EXPERTS * CAP
    dma = pltpu.SemaphoreType.DMA
    shape = jax.ShapeDtypeStruct

    def full(a):
        return shape((count * a.shape[0], a.shape[1]), a.dtype)

    def parted(a):
        return shape((count * a.shape[0], a.shape[1] // X_SIZE), a.dtype)

    return pl.pallas_call(
        forward_kernel,
        out_shape=[
            shape((vectors, 128), F32), shape((count, table.shape[1]), F32),
            shape((count * qkv.shape[1], 3 * qkv.shape[2]), BF16), full(proj), full(route),
            shape((patches, 3 * qkv.shape[2]), BF16), shape((proj.shape[1] // 64, patches, patches), F32),
            shape((patches, proj.shape[1]), BF16), shape((patches, width), F32),
            shape((patches, width), BF16), shape((2 * patches, width), BF16),
            shape((2 * patches, width), BF16), shape((patches, 128), F32),
            parted(up), parted(down), shape(e_up.shape, BF16), shape(e_down.shape, BF16),
            shape((2, slots, width // 2), BF16), shape((2, slots, width // 2), BF16),
        ],
        in_specs=vmem(8) + hbm(2) + vmem(3),
        out_specs=vmem(13) + hbm(6),
        scratch_shapes=[
            pltpu.VMEM((count, 8, 128), jnp.int32),
            pltpu.VMEM((count, vectors, 128), F32),
            pltpu.VMEM((count, vectors, 128), F32),
            pltpu.VMEM((patches, width), BF16), pltpu.VMEM((patches, width), BF16),
            pltpu.VMEM((8, width), F32),
            pltpu.VMEM((slots, width // 2), BF16), pltpu.VMEM((slots, width // 2), BF16),
            dma((16,)), dma((16,)), dma((16,)), dma((16,)),
            dma((6, 40)), dma((6, 16)), dma((5,)), dma((16,)), dma((16,)), dma((2,)),
            dma((2, 16)), dma((2, 16)), dma((2, 16)), dma((2, 16)), dma((2,)), dma((4,)), dma((4,)),
            pltpu.VMEM((qkv.shape[1], 3 * qkv.shape[2]), BF16),
        ],
        compiler_params=params(1),
        name="forward",
    )(ts_tile, table, ada, *shards, e_up, e_down, tokens, cotangent, routes)


def normalized(values):
    centre = jnp.mean(values, axis=-1, keepdims=True)
    shifted = values - centre
    spread = jnp.mean(shifted * shifted, axis=-1, keepdims=True)
    rate = lax.rsqrt(spread + epsilon)
    return shifted * rate, rate


def norm_back(normal, rate, gradient):
    mean = jnp.mean(gradient, axis=-1, keepdims=True)
    along = jnp.mean(gradient * normal, axis=-1, keepdims=True)
    return rate * (gradient - mean - normal * along)


class Sums:
    def __init__(self, specs, r, sends):
        self.specs, self.r, self.sends = specs, r, sends
        self.me, self.core = lax.axis_index(WIDE), lax.axis_index(NARROW)
        self.z, self.y, self.x = place(self.me)
        z = self.z
        upper = z >= 2
        self.dest = [
            jnp.where(upper, 0, 3), jnp.where(upper, 1, 2), jnp.where(upper, 5 - z, 1 - z), z
        ]
        self.near = {
            "y": at_place(z, 1 - self.y, self.x), "x": at_place(z, self.y, 1 - self.x)
        }

    def part(self, ref, axis, zz, other):
        if axis == "y":
            return ref.at[zz, 1 - self.y if other else self.y]
        return ref.at[zz, :, 1 - self.x if other else self.x]

    def slot(self, zz, way, at):
        return jnp.where(jnp.logical_and(zz == at, way == 1), 4, zz)

    def landed(self, ref, sem):
        remote(ref, ref, self.r.first_ss.at[0, 0], sem, (self.near["x"], self.core)).wait_recv()

    def load(self, i, k):
        terms, axis, work = self.specs[i][:3]
        zz = self.dest[k]
        return pltpu.make_async_copy(
            self.part(terms, axis, zz, False), work.at[zz], self.r.load_sem.at[i, k]
        )

    def start(self, i, k):
        terms, axis, _, came = self.specs[i][:4]
        zz = self.dest[k]
        self.load(i, k).start()
        self.sends.go(
            lambda: remote(
                self.part(terms, axis, zz, True), came.at[zz],
                self.r.first_ss.at[i, k], self.r.first_rs.at[i, zz], (self.near[axis], self.core),
            )
        )

    def step(self, i, k):
        _, axis, work, came, along, last = self.specs[i][:6]
        z, zz, core = self.z, self.dest[k], self.core
        self.load(i, k).wait()
        self.landed(came.at[zz], self.r.first_rs.at[i, zz])
        if k < 3:
            rising = zz > z
            way = jnp.where(rising, 0, 1)
            more = jnp.where(rising, z > 0, z < 3)

            @pl.when(more)
            def _():
                self.landed(along.at[zz], self.r.z_rs.at[i, zz])
                add_blocks(work.at[zz], came.at[zz], along.at[zz])

            @pl.when(jnp.logical_not(more))
            def _():
                add_blocks(work.at[zz], came.at[zz])

            target = jnp.where(rising, self.me + 4, self.me - 4)
            slot = self.slot(zz, way, jnp.where(rising, z + 1, z - 1))
            self.sends.go(
                lambda: remote(
                    work.at[zz], along.at[slot],
                    self.r.z_ss.at[i, k], self.r.z_rs.at[i, slot], (target, core),
                )
            )
            return
        add_blocks(work.at[z], came.at[z])
        for way, there in ((0, z > 0), (1, z < 3)):

            @pl.when(there)
            def _(way=way):
                slot = self.slot(z, way, z)
                self.landed(along.at[slot], self.r.z_rs.at[i, slot])
                add_blocks(work.at[z], along.at[slot])

        side, final = (self.x, "x") if axis == "y" else (self.y, "y")
        self.sends.go(
            lambda: remote(
                work.at[z, 1 - side], last,
                self.r.last_ss.at[i], self.r.last_rs.at[i], (self.near[final], core),
            )
        )

    def finish(self, i):
        _, axis, work, _, _, last, store = self.specs[i]
        self.landed(last, self.r.last_rs.at[i])
        side = self.x if axis == "y" else self.y
        store(work[self.z, side].astype(F32), last[...].astype(F32))


def add_blocks(total, *terms):
    size = total.shape[1]
    per = size // 16

    def body(n, _):
        block, at = lax.div(n, per), pl.ds(pl.multiple_of(lax.rem(n, per) * 16, 16), 16)
        value = total[block, at, :].astype(F32)
        for term in terms:
            value = value + term[block, at, :].astype(F32)
        total[block, at, :] = value.astype(BF16)
        return 0

    lax.fori_loop(0, 2 * per, body, 0)


def gelu_pair(value, gradient):
    root = 0.7978845608028654
    square = value * value
    bend = jnp.tanh(root * (value + 0.044715 * value * square))
    half = 0.5 * (1.0 + bend)
    slope = half + 0.5 * value * (1.0 - bend * bend) * (root * (1.0 + 0.134145 * square))
    return (value * half).astype(BF16), (slope * gradient).astype(BF16)


def columns_of(total, tile, body):
    def turn(n, _):
        body(pl.ds(pl.multiple_of(n * tile, 128), tile))
        return 0

    lax.fori_loop(0, total // tile, turn, 0)


def backward_kernel(names, fetched, *refs):
    r = types.SimpleNamespace(**dict(zip(names, refs, strict=True)))
    me, core = lax.axis_index(WIDE), lax.axis_index(NARROW)
    count = lax.axis_size(WIDE)
    z, y, x = place(me)
    others = peers_far_first(me)
    peer = (me, 1 - core)
    across = (at_place(z, y, 1 - x), core)
    fetches = {}
    for n, name in enumerate(fetched):
        fetches[name] = pltpu.make_async_copy(getattr(r, name), getattr(r, name + "_v"), r.fetch_sem.at[n])
        fetches[name].start()
    greet([(other, core) for other in others] + [peer])
    sends = Sends()
    slots, width = r.their0.shape
    size = slots // count
    patches = r.tok.shape[0]
    mine = pl.ds(pl.multiple_of(core * width, 128), width)
    theirs_half = pl.ds(pl.multiple_of((1 - core) * width, 128), width)

    def rows(index):
        return pl.ds(pl.multiple_of(index * size, 16), size)

    def arrived(ref, sem):
        remote(ref, ref, r.near_ss.at[0, 0], sem, peer).wait_recv()

    for name in fetched[:6]:
        fetches[name].wait()
    hidden_units = r.eup_v.shape[1]
    for n in range(2):
        r.ein_t[n] = r.ein_v[n].T
        r.eg_t[n] = r.eg_v[n].T

    def expert_hidden(at):
        def through(rows_ref, own, other):
            return jnp.dot(rows_ref[x], own[:, at], preferred_element_type=F32) + jnp.dot(
                rows_ref[1 - x], other[:, at], preferred_element_type=F32
            )

        r.eact[:, at], r.epre[:, at] = gelu_pair(
            through(r.ein_v, r.eup_v, r.upo_v), through(r.eg_v, r.edn_v, r.dno_v)
        )

    columns_of(hidden_units, 256, expert_hidden)

    for target, left, own, other in (
        (r.ein_v, r.eact, r.edn_v, r.dno_v), (r.eg_v, r.epre, r.eup_v, r.upo_v),
    ):
        target[x] = contract(left[...], own[...], (1,), (1,)).astype(BF16)
        target[1 - x] = contract(left[...], other[...], (1,), (1,)).astype(BF16)

    triples = ((r.ein_v, r.their0, r.back0), (r.eg_v, r.their1, r.back1))
    order = others + [me]
    for k, other in enumerate(order):
        for a, (src, theirs, _) in enumerate(triples):
            sends.go(
                lambda k=k, other=other, a=a, src=src, theirs=theirs: remote(
                    src.at[1 - core, rows(other), :], theirs.at[rows(other), :],
                    r.near_ss.at[a, k], r.near_rs.at[a, other], peer,
                )
            )
    def given_terms(at):
        r.eup_v[:, at] = jnp.dot(r.ein_t[1 - x], r.epre[:, at], preferred_element_type=F32).astype(BF16)
        r.upo_v[:, at] = jnp.dot(r.eg_t[1 - x], r.eact[:, at], preferred_element_type=F32).astype(BF16)

    columns_of(hidden_units, 256, given_terms)
    pieces = 2
    cut = r.eup_v.shape[0] // pieces
    trades = []
    for a, (give, take) in enumerate(((r.eup_v, r.take0), (r.upo_v, r.take1))):
        for p in range(pieces):
            piece = pl.ds(p * cut, cut)
            trades.append(
                lambda a=a, p=p, give=give, take=take, piece=piece: remote(
                    give.at[piece, :], take.at[piece, :],
                    r.trade_ss.at[a * pieces + p], r.trade_rs.at[a * pieces + p], across,
                )
            )
    for k, other in enumerate(order):
        for a, (src, theirs, back) in enumerate(triples):
            arrived(theirs.at[rows(other), :], r.near_rs.at[a, other])
            both_cores = (
                src[core, rows(other), :].astype(F32) + theirs[rows(other), :].astype(F32)
            ).astype(BF16)
            if k < len(others):
                src[core, rows(other), :] = both_cores
                sends.go(
                    lambda k=k, other=other, a=a, src=src, back=back: remote(
                        src.at[core, rows(other), :], back.at[rows(me), :],
                        r.ss.at[a, k], r.rs.at[a, me], (other, core),
                    )
                )
            else:
                back[rows(me), :] = both_cores

    for name in fetched[6:10]:
        fetches[name].wait()
    r.mlp_t[...] = r.mlp_v[...].T
    r.gsh_t[...] = r.gsh_v[...].T

    def shared_hidden(at):
        r.sact[:, at], r.spre[:, at] = gelu_pair(
            jnp.dot(r.mlp_v[...], r.up_v[:, at], preferred_element_type=F32),
            jnp.dot(r.gsh_v[...], r.down_v[:, at], preferred_element_type=F32),
        )

    columns_of(r.up_v.shape[1], 256, shared_hidden)
    blocks = (2, 2, 2, size)

    def shared_terms(at):
        for target, left, right in ((r.up_t, r.mlp_t, r.spre), (r.down_t, r.gsh_t, r.sact)):
            for h in range(2):
                value = jnp.dot(
                    left[384 * h : 384 * (h + 1), :], right[:, at], preferred_element_type=F32
                )
                target[2 * h : 2 * h + 2, :, :, :, at] = value.astype(BF16).reshape(
                    *blocks, value.shape[1]
                )

    columns_of(r.up_v.shape[1], 256, shared_terms)

    def shared_out(at):
        r.part0[:, at] = contract(r.sact[...], r.down_v[at, :], (1,), (1,)).astype(BF16)
        r.gsh_v[:, at] = contract(r.spre[...], r.up_v[at, :], (1,), (1,)).astype(BF16)

    columns_of(r.part0.shape[1], 256, shared_out)

    def store_to(ref):
        def store(own, came):
            ref[...] = own + came

        return store

    def store_sides(ref):
        def store(own, came):
            half = own.shape[1]
            ref[:, pl.ds(pl.multiple_of(x * half, 128), half)] = own
            ref[:, pl.ds(pl.multiple_of((1 - x) * half, 128), half)] = came

        return store

    def store_qkv(own, came):
        for j in range(3):
            at = slice(width * j, width * (j + 1))
            r.qkv_o[j] = own[:, at] + came[:, at]

    specs = [
        (r.up_t, "y", r.up_w, r.up_c, r.up_a, r.up_l, store_sides(r.up_o)),
        (r.down_t, "y", r.down_w, r.down_c, r.down_a, r.down_l, store_sides(r.down_o)),
        (r.proj_t, "y", r.proj_w, r.proj_c, r.proj_a, r.proj_l, store_to(r.proj_o)),
        (r.route_t, "y", r.route_w, r.route_c, r.route_a, r.route_l, store_to(r.route_o)),
        (r.qkv_t, "y", r.qkv_w, r.qkv_c, r.qkv_a, r.qkv_l, store_qkv),
    ]
    sums = Sums(specs, r, sends)
    small = ((r.part0, r.their2, r.branch, r.pass0, r.came0), (r.gsh_v, r.their3, r.gmlp, r.pass1, r.came1))
    for a, (part, theirs, _, _, _) in enumerate(small):
        sends.go(
            lambda a=a, part=part, theirs=theirs: remote(
                part.at[:, theirs_half], theirs, r.near_ss.at[a, 16], r.near_rs.at[a, 16], peer
            )
        )
    for k in range(4):
        for i in range(2):
            sums.start(i, k)
    for a, (part, theirs, total, passed, came) in enumerate(small):
        arrived(theirs, r.near_rs.at[a, 16])
        total[:, mine] = part[:patches, mine].astype(F32) + theirs[:patches, :].astype(F32)
        passed[...] = (part[patches:, mine].astype(F32) + theirs[patches:, :].astype(F32)).astype(BF16)
        sends.go(
            lambda a=a, passed=passed, came=came: remote(
                passed, came, r.pass_ss.at[a], r.pass_rs.at[a], across
            )
        )
    for trade in trades:
        sends.go(trade)
    queue = [lambda i=i, k=k: sums.step(i, k) for k in range(4) for i in range(2)]

    def pump(steps=1):
        for _ in range(steps):
            if queue:
                queue.pop(0)()

    shift1, scale1, gate1, shift2, scale2, gate2 = [lanes_of(r.mod, j) for j in range(6)]
    named, takes = choice_masks(r.routes)
    gates = [r.gates[:, k : k + 1] for k in range(2)]
    pump(2)
    for other in others[::-1]:
        for a, (_, _, back) in enumerate(triples):
            arrived(back.at[rows(other), :], r.rs.at[a, other])
    for a in range(2):
        arrived(small[a][4], r.pass_rs.at[a])
    picked = [jnp.dot(takes[k], r.back0[...], preferred_element_type=F32) for k in range(2)]
    r.branch[:, mine] = (
        r.branch[:, mine] + r.came0[...].astype(F32)
        + gates[0] * picked[0] + gates[1] * picked[1]
    )
    r.gmlp[:, mine] = (
        r.gmlp[:, mine] + r.came1[...].astype(F32)
        + jnp.dot(takes[0] + takes[1], r.back1[...], preferred_element_type=F32)
    )
    for k in range(6):
        r.gate_row[k : k + 1, :] = lanes_of(r.mod, k)
    grad_half = r.gate_row[5:6, mine] * r.cot[:, mine].astype(F32)
    terms = [jnp.sum(grad_half * picked[k], axis=-1, keepdims=True) for k in range(2)]
    lane = lax.broadcasted_iota(jnp.int32, r.gsum.shape, 1)
    r.gsum[...] = jnp.where(lane == 0, terms[0], jnp.where(lane == 1, terms[1], 0.0))
    swaps = [
        remote(r.branch.at[:, mine], r.branch.at[:, mine], r.swap_ss.at[0], r.swap_rs.at[0], peer),
        remote(r.gmlp.at[:, mine], r.gmlp.at[:, mine], r.swap_ss.at[1], r.swap_rs.at[1], peer),
        remote(r.gsum, r.gsum_c, r.swap_ss.at[2], r.swap_rs.at[2], peer),
    ]
    for swap in swaps:
        swap.start()
    for name in fetched[10:]:
        fetches[name].wait()
    hidden = r.tok[...].astype(F32) + gate1 * r.attn_v[...]
    normal2, rate2 = normalized(hidden)
    r.normal[...] = normal2
    grad_out = r.cot[...].astype(F32)
    arrived(r.branch.at[:, theirs_half], r.swap_rs.at[0])
    arrived(r.gmlp.at[:, theirs_half], r.swap_rs.at[1])
    arrived(r.gsum_c, r.swap_rs.at[2])
    for swap in swaps:
        swap.wait_send()

    def put(vector, value):
        for i in range(value.shape[1] // 128):
            at = value.shape[1] // 128 * vector + i
            r.vec[at : at + 1, :] = value[:, 128 * i : 128 * (i + 1)]

    branch = r.branch[...]
    r.out_o[...] = (hidden + gate2 * branch).astype(BF16)
    put(5, jnp.sum(grad_out * branch, axis=0, keepdims=True))
    grad_gates = [r.gsum[:, k : k + 1] + r.gsum_c[:, k : k + 1] for k in range(2)]
    inner = gates[0] * grad_gates[0] + gates[1] * grad_gates[1]
    grad_chosen = [gates[k] * (grad_gates[k] - inner) for k in range(2)]
    grad_logits = (grad_chosen[0] * named[0] + grad_chosen[1] * named[1]).astype(BF16)
    grad_mlp = r.gmlp[...] + contract(grad_logits, r.routew_v[...], (1,), (1,))
    normal2 = r.normal[...]
    put(3, jnp.sum(grad_mlp, axis=0, keepdims=True))
    put(4, jnp.sum(grad_mlp * normal2, axis=0, keepdims=True))
    r.ghid[...] = grad_out + norm_back(normal2, rate2, grad_mlp * (1.0 + scale2))
    grad_hidden = r.ghid[...]
    put(2, jnp.sum(grad_hidden * r.attn_v[...], axis=0, keepdims=True))
    r.gattn[...] = (gate1 * grad_hidden).astype(BF16)

    def weight_terms(target, left, right):
        columns = right.shape[1]
        cut = 384
        for n in range(columns // cut if columns > cut else 1):
            lo, hi = cut * n, min(columns, cut * (n + 1))
            for h in range(2):
                value = contract(left[:, 384 * h : 384 * (h + 1)], right[:, lo:hi], (0,), (0,))
                target[2 * h : 2 * h + 2, :, :, :, lo:hi] = value.astype(BF16).reshape(
                    *blocks, hi - lo
                )

    weight_terms(r.proj_t, r.gattn, r.mixed_v)
    weight_terms(r.route_t, r.mlp_v[:patches, :], grad_logits)
    pump(1)
    r.gmix[...] = jnp.dot(r.gattn[...], r.projw_v[...], preferred_element_type=F32).astype(BF16)
    for k in range(4):
        for i in (2, 3):
            sums.start(i, k)
    masks = head_masks(r.gmix.shape[0])
    scale_factor = 64 ** (-0.5)
    for pair in range(width // 128):
        at = [slice(width * j + 128 * pair, width * j + 128 * (pair + 1)) for j in range(3)]
        q, k, v = [r.act_v[:, at[j]] for j in range(3)]
        gm = r.gmix[:, at[0]]
        found = [None] * 3
        for h in range(2):
            probs = r.probs_v[2 * pair + h]
            grad_probs = contract(gm * masks[h].astype(BF16), v, (1,), (1,))
            weighted = jnp.sum(probs * grad_probs, axis=-1, keepdims=True)
            grad_scores = (probs * (grad_probs - weighted)).astype(BF16)
            parts = (
                jnp.dot(grad_scores, k, preferred_element_type=F32) * scale_factor,
                contract(grad_scores, q, (0,), (0,)) * scale_factor,
                contract(probs.astype(BF16), gm, (0,), (0,)),
            )
            found = [
                part * masks[h] if old is None else old + part * masks[h]
                for part, old in zip(parts, found, strict=True)
            ]
            pump(1)
        for j in range(3):
            r.gqkv[:, at[j]] = found[j].astype(BF16)
    r.gpart[...] = contract(r.gqkv[...], r.qkvw_v[...], (1,), (1,)).astype(BF16)
    swap = remote(r.gpart, r.gpart_c, r.swap_ss.at[3], r.swap_rs.at[3], peer)
    swap.start()
    weight_terms(r.qkv_t, r.attnlow_v, r.gqkv)
    for k in range(4):
        sums.start(4, k)
    tokens = r.tok[...].astype(F32)
    normal1, rate1 = normalized(tokens)
    swap.wait()
    grad_in = r.gpart[...].astype(F32) + r.gpart_c[...].astype(F32)
    put(0, jnp.sum(grad_in, axis=0, keepdims=True))
    put(1, jnp.sum(grad_in * normal1, axis=0, keepdims=True))
    for k, other in enumerate(others):
        sends.go(
            lambda k=k, other=other: remote(
                r.vec, r.every.at[me], r.vec_ss.at[k], r.vec_rs.at[me], (other, core)
            )
        )
    r.tokens_o[...] = r.ghid[...] + norm_back(normal1, rate1, grad_in * (1.0 + scale1))
    while queue:
        pump()
    for k in range(4):
        for i in (2, 3, 4):
            sums.step(i, k)
    for a in range(2 * pieces):
        take = (r.take0, r.take1)[a // pieces]
        arrived(take.at[pl.ds(a % pieces * cut, cut), :], r.trade_rs.at[a])
    for left, right, take, result in (
        (r.ein_t, r.epre, r.take0, r.eup_o), (r.eg_t, r.eact, r.take1, r.edown_o),
    ):

        def outward(n, slot, result=result):
            at = pl.ds(pl.multiple_of(n * 512 + slot * 256, 128), 256)
            return at, pltpu.make_async_copy(r.stage.at[slot], result.at[:, at], r.keep_sem.at[slot])

        def turn(n, _, left=left, right=right, take=take, outward=outward):
            for slot in range(2):
                at, copy = outward(n, slot)
                guarded(n > 0, lambda: outward(n - 1, slot)[1].wait())
                r.stage[slot] = jnp.dot(
                    left[x], right[:, at], preferred_element_type=F32
                ) + take[:, at].astype(F32)
                copy.start()
            return 0

        turns = hidden_units // 512
        lax.fori_loop(0, turns, turn, 0)
        for slot in range(2):
            outward(turns - 1, slot)[1].wait()
    for i in range(2):
        sums.finish(i)
    r.every[me] = r.vec[...]
    for other in others[::-1]:
        arrived(r.every.at[other], r.vec_rs.at[other])
    cond = r.cond[...]
    chunks = r.vec.shape[0] // 6
    for j in range(6):
        for i in range(chunks):
            r.ada_o[j, :, 128 * i : 128 * (i + 1)] = lax.dot_general(
                cond, r.every[:, chunks * j + i, :], (((0,), (0,)), ((), ())),
                precision=highest, preferred_element_type=F32,
            )
    for i in (2, 3, 4):
        sums.finish(i)
    sends.drain()


def backward(given, near):
    count = 16
    dma = pltpu.SemaphoreType.DMA
    shape = jax.ShapeDtypeStruct
    operands = given | near
    a = types.SimpleNamespace(**operands)
    patches, width = a.tok.shape
    slots, half = a.ein.shape[1:]
    head_width = a.mixed.shape[1]
    hidden = a.eup.shape[1]
    quarter = a.up.shape[1]
    size = slots // count
    vectors = a.mod.shape[0]
    columns = dict(up=quarter, down=quarter, proj=head_width, route=128, qkv=3 * head_width)
    results = dict(
        out_o=shape((patches, width), BF16),
        tokens_o=shape((patches, width), F32),
        ada_o=shape((6, size, width), F32),
        qkv_o=shape((3, size, head_width), F32),
        proj_o=shape((size, head_width), F32),
        route_o=shape((size, 128), F32),
        up_o=shape((size, 2 * quarter), F32),
        down_o=shape((size, 2 * quarter), F32),
        eup_o=shape((half, hidden), F32),
        edown_o=shape((half, hidden), F32),
    )
    v = pltpu.VMEM
    scratch = {name + "_v": v(array.shape, array.dtype) for name, array in given.items()}
    for name, wide in columns.items():
        scratch[name + "_w"] = v((4, 2, size, wide), BF16)
        scratch[name + "_c"] = v((4, 2, size, wide), BF16)
        scratch[name + "_a"] = v((5, 2, size, wide), BF16)
        scratch[name + "_l"] = v((size, wide), BF16)
        scratch[name + "_t"] = v((4, 2, 2, size, wide), BF16)

    def low(*sizes):
        return v(sizes, BF16)

    def full(*sizes):
        return v(sizes, F32)

    scratch |= dict(
        ein_t=low(2, half, slots), eg_t=low(2, half, slots),
        eact=low(slots, hidden), epre=low(slots, hidden),
        take0=low(half, hidden), take1=low(half, hidden),
        stage=full(2, half, 256),
        their0=low(slots, half), their1=low(slots, half), back0=low(slots, half), back1=low(slots, half),
        mlp_t=low(width, 2 * patches), gsh_t=low(width, 2 * patches),
        sact=low(2 * patches, quarter), spre=low(2 * patches, quarter),
        part0=low(2 * patches, width),
        their2=low(2 * patches, half), their3=low(2 * patches, half),
        pass0=low(patches, half), pass1=low(patches, half), came0=low(patches, half), came1=low(patches, half),
        branch=full(patches, width), gmlp=full(patches, width),
        normal=full(patches, width), ghid=full(patches, width),
        gattn=low(patches, width), gpart=low(patches, width), gpart_c=low(patches, width),
        gmix=low(patches, head_width), gqkv=low(patches, 3 * head_width),
        gsum=full(patches, 128), gsum_c=full(patches, 128), gate_row=full(8, width),
        vec=full(vectors, 128), every=full(count, vectors, 128),
        near_ss=dma((2, 17)), near_rs=dma((2, 17)), ss=dma((2, 16)), rs=dma((2, 16)),
        fetch_sem=dma((len(given),)), keep_sem=dma((2,)), trade_ss=dma((4,)), trade_rs=dma((4,)),
        first_ss=dma((5, 4)), first_rs=dma((5, 4)), load_sem=dma((5, 4)),
        z_ss=dma((5, 3)), z_rs=dma((5, 5)), last_ss=dma((5,)), last_rs=dma((5,)),
        swap_ss=dma((4,)), swap_rs=dma((4,)), vec_ss=dma((16,)), vec_rs=dma((16,)),
        pass_ss=dma((2,)), pass_rs=dma((2,)),
    )
    names = tuple(operands) + tuple(results) + tuple(scratch)
    found = pl.pallas_call(
        functools.partial(backward_kernel, names, tuple(given)),
        out_shape=list(results.values()),
        in_specs=hbm(len(given)) + vmem(len(near)),
        out_specs=vmem(8) + hbm(2),
        scratch_shapes=list(scratch.values()),
        compiler_params=params(3, 64_000_000),
        name="backward",
    )(*operands.values())
    return types.SimpleNamespace(**dict(zip(results, found, strict=True)))


def per_device_direct(
    tokens, cotangent, time_table, timesteps, routes, w_ada, w_qkv, w_proj,
    w_route, w_shared_up, w_shared_down, e_up, e_down,
):
    row_count, model_width = tokens.shape
    core = lax.axis_index(NARROW)
    core_count = lax.axis_size(NARROW)
    wide_count = lax.axis_size(WIDE)
    heads_here = HEADS // core_count
    head_dim = model_width // HEADS
    head_width = heads_here * head_dim
    half = model_width // 2
    scale_factor = head_dim ** (-0.5)
    wide_place = lax.axis_index(WIDE)
    upper = wide_place % 2 == 1
    ada_rows = w_ada.shape[0]

    table = lax.dynamic_slice_in_dim(time_table, wide_place * ada_rows, ada_rows, 1)
    table = jnp.pad(table, ((0, -table.shape[0] % 128), (0, 0)))
    ts_tile = jnp.broadcast_to(timesteps[:, None], (8, 128)).astype(jnp.int32)
    (
        mod, cond_own, qkv_full, proj_full, route_full, activated, probs_full, mixed_low,
        attn_out, attn_low, mlp_low, grad_shared, gate_lanes,
        up_full, down_full, up_other, down_other, expert_in, grad_expert_out,
    ) = forward(
        ts_tile,
        table,
        jnp.transpose(w_ada, (1, 0, 2)),
        jnp.transpose(w_qkv, (1, 0, 2)),
        w_proj,
        jnp.pad(w_route, ((0, 0), (0, 128 - EXPERTS))),
        w_shared_up,
        w_shared_down,
        e_up,
        e_down,
        tokens,
        cotangent,
        routes,
    )
    got = backward(
        dict(
            ein=expert_in, eg=grad_expert_out, eup=e_up, upo=up_other, edn=e_down, dno=down_other,
            mlp=mlp_low, gsh=grad_shared, up=up_full, down=down_full,
            attn=attn_out, attnlow=attn_low, act=activated,
            probs=probs_full, mixed=mixed_low, qkvw=qkv_full, projw=proj_full, routew=route_full,
        ),
        dict(tok=tokens, cot=cotangent, mod=mod, cond=cond_own, routes=routes, gates=gate_lanes),
    )
    return (
        got.out_o,
        got.tokens_o,
        jnp.transpose(got.ada_o, (1, 0, 2)),
        jnp.transpose(got.qkv_o, (1, 0, 2)),
        got.proj_o,
        got.route_o[:, :EXPERTS],
        got.up_o,
        got.down_o,
        got.eup_o,
        got.edown_o,
    )


def solution(mesh):
    placed = (
        P(WIDE, None),
        P(WIDE, None),
        P(),
        P(WIDE),
        P(WIDE, None),
        P(WIDE, None, None),
        P(WIDE, None, NARROW),
        P(WIDE, NARROW),
        P(WIDE, None),
        P(WIDE, NARROW),
        P(WIDE, NARROW),
        P(WIDE, NARROW),
        P(WIDE, NARROW),
    )
    direct = mesh.shape[WIDE] == 16 and mesh.shape[NARROW] == 2
    return jax.shard_map(
        per_device_direct if direct else per_device,
        mesh=mesh,
        in_specs=placed,
        out_specs=(
            P(WIDE, None),
            P(WIDE, None),
            P(WIDE, None, None),
            P(WIDE, None, NARROW),
            P(WIDE, NARROW),
            P(WIDE, None),
            P(WIDE, NARROW),
            P(WIDE, NARROW),
            P(WIDE, NARROW),
            P(WIDE, NARROW),
        ),
        check_vma=False,
    )
```

```python
import functools
import types

import jax
import jax.numpy as jnp
from jax import lax
from jax.experimental import pallas as pl
from jax.experimental.pallas import tpu as pltpu
from jax.sharding import PartitionSpec as P

WIDE, NARROW = "wide", "narrow"
HEADS = 12
EXPERTS = 8
CAP = 96


epsilon = 1e-06
highest = lax.Precision.HIGHEST


def swapped(shard, axis, distance):
    return lax.ppermute(shard, axis, [(i, i ^ 1 << distance) for i in range(lax.axis_size(axis))])


def normalize(values):
    centre = jnp.mean(values, axis=-1, keepdims=True)
    shifted = values - centre
    spread = jnp.mean(shifted * shifted, axis=-1, keepdims=True)
    return shifted * lax.rsqrt(spread + epsilon)


def modulate(values, offset, factor):
    return normalize(values) * (1.0 + factor[:, None, :]) + offset[:, None, :]


def gelu_tanh(values):
    return jax.nn.gelu(values, approximate=True)


def gelu_back(values, gradient):
    return jax.vjp(gelu_tanh, values)[1](gradient)[0]


def contract(left_side, right_side, left_dims, right_dims):
    return lax.dot_general(
        left_side,
        right_side,
        ((left_dims, right_dims), ((), ())),
        preferred_element_type=jnp.float32,
    )


def slot_table(route_block):
    flat_routes = route_block.reshape(-1)
    matches = (flat_routes[:, None] == jnp.arange(EXPERTS, dtype=jnp.int32)[None, :]).astype(
        jnp.int32
    )
    earlier = jnp.cumsum(matches, axis=0, dtype=jnp.int32) - matches
    ranking = jnp.sum(earlier * matches, axis=1, dtype=jnp.int32)
    return flat_routes * CAP + ranking


def join_halves(stacked, bit_level, wide_place):
    partner = swapped(stacked, WIDE, bit_level)
    upper = wide_place >> bit_level & 1 == 1
    return jnp.where(
        upper,
        jnp.concatenate([partner, stacked], axis=1),
        jnp.concatenate([stacked, partner], axis=1),
    )


def split_halves(stacked, bit_level, wide_place):
    half_rows = stacked.shape[1] // 2
    upper = wide_place >> bit_level & 1 == 1
    lower_part = stacked[:, :half_rows]
    upper_part = stacked[:, half_rows:]
    kept = jnp.where(upper, upper_part, lower_part)
    given = jnp.where(upper, lower_part, upper_part)
    return kept + swapped(given.astype(jnp.bfloat16), WIDE, bit_level).astype(given.dtype)


def per_device(
    tokens,
    cotangent,
    time_table,
    timesteps,
    routes,
    w_ada,
    w_qkv,
    w_proj,
    w_route,
    w_shared_up,
    w_shared_down,
    e_up,
    e_down,
):
    images = timesteps.shape[0]
    row_count = tokens.shape[0]
    model_width = tokens.shape[1]
    patches = row_count // images
    core_count = lax.axis_size(NARROW)
    wide_count = lax.axis_size(WIDE)
    group_size = wide_count // EXPERTS
    levels = group_size.bit_length() - 1
    slice_rows = CAP // group_size
    heads_here = HEADS // core_count
    head_dim = model_width // HEADS
    head_width = heads_here * head_dim
    scale_factor = head_dim ** (-0.5)
    wide_place = lax.axis_index(WIDE)
    ada_rows = w_ada.shape[0]
    step_onehot = (
        timesteps[:, None] == jnp.arange(time_table.shape[0], dtype=jnp.int32)[None, :]
    ).astype(jnp.bfloat16)
    cond = jnp.dot(step_onehot, time_table, preferred_element_type=jnp.float32)
    cond_act = jax.nn.silu(cond).astype(jnp.bfloat16)
    qkv_full, proj_full, route_full, up_full, down_full = (
        lax.all_gather(w_qkv, WIDE, axis=0, tiled=True),
        lax.all_gather(w_proj, WIDE, axis=0, tiled=True),
        lax.all_gather(w_route, WIDE, axis=0, tiled=True),
        lax.all_gather(w_shared_up, WIDE, axis=0, tiled=True),
        lax.all_gather(w_shared_down, WIDE, axis=0, tiled=True),
    )
    cond_every = lax.all_gather(cond_act, WIDE, axis=0, tiled=True)
    cond_own = lax.dynamic_slice_in_dim(cond_every, wide_place * ada_rows, ada_rows, 1)
    modulation_terms = jnp.dot(
        cond_own, w_ada.reshape(ada_rows, 6 * model_width), preferred_element_type=jnp.float32
    )
    modulation = lax.psum_scatter(modulation_terms, WIDE, scatter_dimension=0, tiled=True)
    modulation = modulation.reshape(images, 6, model_width)
    expert_weights = jnp.stack([e_up, e_down])
    for bit_level in range(levels):
        expert_weights = join_halves(expert_weights, bit_level, wide_place)
    expert_up = expert_weights[0]
    expert_down = expert_weights[1]
    inputs = tokens.astype(jnp.float32).reshape(images, patches, model_width)
    attn_in, pull_first = jax.vjp(modulate, inputs, modulation[:, 0], modulation[:, 1])
    attn_low = attn_in.reshape(row_count, model_width).astype(jnp.bfloat16)
    projected = jnp.dot(
        attn_low, qkv_full.reshape(model_width, 3 * head_width), preferred_element_type=jnp.float32
    )
    projected = projected.reshape(images, patches, 3, heads_here, head_dim).astype(jnp.bfloat16)
    queries = projected[:, :, 0]
    keys = projected[:, :, 1]
    values = projected[:, :, 2]
    scores = (
        jnp.einsum("bqhd,bkhd->bhqk", queries, keys, preferred_element_type=jnp.float32)
        * scale_factor
    )
    highest_score = jnp.max(scores, axis=-1, keepdims=True)
    log_total = highest_score + jnp.log(
        jnp.sum(jnp.exp(scores - highest_score), axis=-1, keepdims=True)
    )
    probs_low = jnp.exp(scores - log_total).astype(jnp.bfloat16)
    mixed = jnp.einsum("bhqk,bkhd->bqhd", probs_low, values, preferred_element_type=jnp.float32)
    mixed_low = mixed.astype(jnp.bfloat16).reshape(row_count, head_width)
    attn_part = contract(mixed_low, proj_full, (1,), (1,))
    attn_out = lax.psum(attn_part.astype(jnp.bfloat16), NARROW).astype(jnp.float32)
    attn_three = attn_out.reshape(images, patches, model_width)
    hidden_state = inputs + modulation[:, 2][:, None, :] * attn_three
    mlp_in, pull_second = jax.vjp(modulate, hidden_state, modulation[:, 3], modulation[:, 4])
    mlp_low = mlp_in.reshape(row_count, model_width).astype(jnp.bfloat16)
    logits = jnp.dot(mlp_low, route_full, preferred_element_type=jnp.float32)
    selector = (routes[:, :, None] == jnp.arange(EXPERTS, dtype=jnp.int32)[None, None, :]).astype(
        jnp.float32
    )
    chosen = jnp.sum(logits[:, None, :] * selector, axis=-1)
    gate_values, pull_gate = jax.vjp(
        lambda picked_logits: jax.nn.softmax(picked_logits, axis=-1), chosen
    )
    slot_index = slot_table(routes)
    outgoing = (
        jnp.zeros((EXPERTS * CAP, model_width), jnp.bfloat16)
        .at[slot_index]
        .set(jnp.repeat(mlp_low, 2, axis=0))
    )
    arrived = lax.all_to_all(
        outgoing.reshape(wide_count, slice_rows, model_width),
        WIDE,
        split_axis=0,
        concat_axis=0,
        tiled=True,
    )
    expert_in = arrived.reshape(wide_count * slice_rows, model_width)
    shared_pre = jnp.dot(mlp_low, up_full, preferred_element_type=jnp.float32)
    shared_act = gelu_tanh(shared_pre).astype(jnp.bfloat16)
    shared_part = contract(shared_act, down_full, (1,), (1,))
    expert_pre = jnp.dot(expert_in, expert_up, preferred_element_type=jnp.float32)
    expert_act = gelu_tanh(expert_pre).astype(jnp.bfloat16)
    expert_part = contract(expert_act, expert_down, (1,), (1,))
    expert_sum, shared_out = (
        lax.psum(expert_part.astype(jnp.bfloat16), NARROW).astype(jnp.float32),
        lax.psum(shared_part.astype(jnp.bfloat16), NARROW).astype(jnp.float32),
    )
    expert_out = expert_sum.astype(jnp.bfloat16)
    returned = lax.all_to_all(
        expert_out.reshape(wide_count, slice_rows, model_width),
        WIDE,
        split_axis=0,
        concat_axis=0,
        tiled=True,
    )
    returned = returned.reshape(EXPERTS * CAP, model_width)
    picked = returned[slot_index].astype(jnp.float32).reshape(row_count, 2, model_width)
    mixture = jnp.sum(gate_values[:, :, None] * picked, axis=1)
    branch = (shared_out + mixture).reshape(images, patches, model_width)
    output = hidden_state + modulation[:, 5][:, None, :] * branch
    grad_out = cotangent.astype(jnp.float32).reshape(images, patches, model_width)
    grad_branch = (modulation[:, 5][:, None, :] * grad_out).reshape(row_count, model_width)
    grad_gate2 = jnp.sum(grad_out * branch, axis=1)
    grad_pick = jnp.sum(grad_branch[:, None, :] * picked, axis=-1)
    grad_rows = (
        (gate_values[:, :, None] * grad_branch[:, None, :])
        .astype(jnp.bfloat16)
        .reshape(row_count * 2, model_width)
    )
    grad_slots = jnp.zeros((EXPERTS * CAP, model_width), jnp.bfloat16).at[slot_index].set(grad_rows)
    grad_expert_out = lax.all_to_all(
        grad_slots.reshape(wide_count, slice_rows, model_width),
        WIDE,
        split_axis=0,
        concat_axis=0,
        tiled=True,
    )
    grad_expert_out = grad_expert_out.reshape(wide_count * slice_rows, model_width)
    grad_shared = grad_branch.astype(jnp.bfloat16)
    shared_down_grad = contract(grad_shared, shared_act, (0,), (0,))
    grad_shared_act = jnp.dot(grad_shared, down_full, preferred_element_type=jnp.float32)
    grad_shared_pre = gelu_back(shared_pre, grad_shared_act).astype(jnp.bfloat16)
    shared_up_grad = contract(mlp_low, grad_shared_pre, (0,), (0,))
    grad_in_shared = contract(grad_shared_pre, up_full, (1,), (1,))
    grad_chosen = pull_gate(grad_pick)[0]
    grad_logits = jnp.sum(grad_chosen[:, :, None] * selector, axis=1).astype(jnp.bfloat16)
    route_grad = contract(mlp_low, grad_logits, (0,), (0,))
    grad_in_route = contract(grad_logits, route_full, (1,), (1,))
    expert_down_grad = contract(grad_expert_out, expert_act, (0,), (0,))
    grad_expert_act = jnp.dot(grad_expert_out, expert_down, preferred_element_type=jnp.float32)
    grad_expert_pre = gelu_back(expert_pre, grad_expert_act).astype(jnp.bfloat16)
    expert_up_grad = contract(expert_in, grad_expert_pre, (0,), (0,))
    grad_in_part = contract(grad_expert_pre, expert_up, (1,), (1,))
    grad_in_rows, grad_in_shared_sum = (
        lax.psum(grad_in_part.astype(jnp.bfloat16), NARROW).astype(jnp.float32),
        lax.psum(grad_in_shared.astype(jnp.bfloat16), NARROW).astype(jnp.float32),
    )
    back_rows = lax.all_to_all(
        grad_in_rows.astype(jnp.bfloat16).reshape(wide_count, slice_rows, model_width),
        WIDE,
        split_axis=0,
        concat_axis=0,
        tiled=True,
    )
    back_rows = back_rows.reshape(EXPERTS * CAP, model_width)
    grad_in_expert = jnp.sum(
        back_rows[slot_index].astype(jnp.float32).reshape(row_count, 2, model_width), axis=1
    )
    grad_mlp_in = grad_in_shared_sum + grad_in_route + grad_in_expert
    grad_hidden_norm, grad_shift2, grad_scale2 = pull_second(
        grad_mlp_in.reshape(images, patches, model_width)
    )
    grad_hidden = grad_out + grad_hidden_norm
    grad_gate1 = jnp.sum(grad_hidden * attn_three, axis=1)
    grad_attn = (
        (modulation[:, 2][:, None, :] * grad_hidden)
        .reshape(row_count, model_width)
        .astype(jnp.bfloat16)
    )
    proj_grad = contract(grad_attn, mixed_low, (0,), (0,))
    grad_mixed = jnp.dot(grad_attn, proj_full, preferred_element_type=jnp.float32).astype(
        jnp.bfloat16
    )
    grad_mixed = grad_mixed.reshape(images, patches, heads_here, head_dim)
    again_scores = (
        jnp.einsum("bqhd,bkhd->bhqk", queries, keys, preferred_element_type=jnp.float32)
        * scale_factor
    )
    probs_full = jnp.exp(again_scores - log_total)
    again_low = probs_full.astype(jnp.bfloat16)
    grad_probs = jnp.einsum(
        "bqhd,bkhd->bhqk", grad_mixed, values, preferred_element_type=jnp.float32
    )
    grad_values = jnp.einsum(
        "bhqk,bqhd->bkhd", again_low, grad_mixed, preferred_element_type=jnp.float32
    )
    weighted_sum = jnp.sum(probs_full * grad_probs, axis=-1, keepdims=True)
    grad_scores = (probs_full * (grad_probs - weighted_sum)).astype(jnp.bfloat16)
    grad_queries = (
        jnp.einsum("bhqk,bkhd->bqhd", grad_scores, keys, preferred_element_type=jnp.float32)
        * scale_factor
    )
    grad_keys = (
        jnp.einsum("bhqk,bqhd->bkhd", grad_scores, queries, preferred_element_type=jnp.float32)
        * scale_factor
    )
    grad_qkv = jnp.stack([grad_queries, grad_keys, grad_values], axis=2).astype(jnp.bfloat16)
    grad_qkv = grad_qkv.reshape(row_count, 3 * head_width)
    qkv_grad = contract(attn_low, grad_qkv, (0,), (0,)).reshape(model_width, 3, head_width)
    grad_attn_part = contract(grad_qkv, qkv_full.reshape(model_width, 3 * head_width), (1,), (1,))
    grad_attn_in = lax.psum(grad_attn_part.astype(jnp.bfloat16), NARROW).astype(jnp.float32)
    grad_input_norm, grad_shift1, grad_scale1 = pull_first(
        grad_attn_in.reshape(images, patches, model_width)
    )
    tokens_grad = (grad_hidden + grad_input_norm).reshape(row_count, model_width)
    grad_modulation = jnp.stack(
        [grad_shift1, grad_scale1, grad_gate1, grad_shift2, grad_scale2, grad_gate2], axis=1
    )
    grad_modulation = grad_modulation.reshape(images, 6 * model_width)
    grad_mod_every = lax.all_gather(grad_modulation, WIDE, axis=0, tiled=True)
    ada_part = jnp.dot(cond_own.astype(jnp.float32).T, grad_mod_every, precision=highest).reshape(
        ada_rows, 6, model_width
    )
    qkv_part, proj_part, route_part, shared_up_part, shared_down_part = (
        lax.psum_scatter(qkv_grad, WIDE, scatter_dimension=0, tiled=True),
        lax.psum_scatter(proj_grad, WIDE, scatter_dimension=0, tiled=True),
        lax.psum_scatter(route_grad, WIDE, scatter_dimension=0, tiled=True),
        lax.psum_scatter(shared_up_grad, WIDE, scatter_dimension=0, tiled=True),
        lax.psum_scatter(shared_down_grad, WIDE, scatter_dimension=0, tiled=True),
    )
    expert_grads = jnp.stack([expert_up_grad, expert_down_grad])
    for bit_level in reversed(range(levels)):
        expert_grads = split_halves(expert_grads, bit_level, wide_place)
    return (
        output.reshape(row_count, model_width).astype(jnp.bfloat16),
        tokens_grad,
        ada_part,
        qkv_part,
        proj_part,
        route_part,
        shared_up_part,
        shared_down_part,
        expert_grads[0],
        expert_grads[1],
    )


MESH = pl.DeviceIdType.MESH
F32 = jnp.float32
BF16 = jnp.bfloat16
Z_SIZE, Y_SIZE, X_SIZE = 4, 2, 2
VMEM_LIMIT = 60 * 1024 * 1024


def place(index):
    return lax.div(index, 4), lax.rem(lax.div(index, 2), 2), lax.rem(index, 2)


def at_place(z, y, x):
    return z * 4 + y * 2 + x


class Sends:
    def __init__(self):
        self.items = []

    def go(self, make, when=None):
        self.items.append((make, when))
        guarded(when, lambda: make().start())

    def drain(self):
        for make, when in self.items:
            guarded(when, lambda make=make: make().wait_send())


def guarded(when, action):
    if when is None:
        action()
        return

    @pl.when(when)
    def _():
        action()


def both(first, second):
    if first is None:
        return second
    if second is None:
        return first
    return jnp.logical_and(first, second)


def remote(src, dst, send_sem, recv_sem, target):
    return pltpu.make_async_remote_copy(
        src_ref=src,
        dst_ref=dst,
        send_sem=send_sem,
        recv_sem=recv_sem,
        device_id=target,
        device_id_type=MESH,
    )


def greet(targets):
    barrier = pltpu.get_barrier_semaphore()
    for target in targets:
        pl.semaphore_signal(barrier, inc=1, device_id=target, device_id_type=MESH)
    pl.semaphore_wait(barrier, len(targets))


class Gather:
    def __init__(self, streams, send_sem, recv_sem, sends):
        self.streams, self.ss, self.rs, self.sends = streams, send_sem, recv_sem, sends
        self.count = [0] * len(streams)
        self.core = lax.axis_index(NARROW)
        self.me = lax.axis_index(WIDE)
        self.z, self.y, self.x = place(self.me)
        self.to_x = at_place(self.z, self.y, 1 - self.x)
        self.to_y = at_place(self.z, 1 - self.y, self.x)
        self.can_up, self.can_down = self.z < Z_SIZE - 1, self.z > 0
        self.up, self.down = self.me + 4, self.me - 4

    def block(self, s, origin):
        shard, full, start, width = self.streams[s][:4]
        rows = shard.shape[0]
        return full.at[pl.ds(pl.multiple_of(origin * rows, 16), rows), pl.ds(start, width)]

    def send(self, s, origin, target, when=None, own=False, over_x=False):
        shard, full, start, width, _, parted = self.streams[s]
        index = self.count[s]
        self.count[s] += 1

        def make():
            dst = self.block(s, origin)
            first = start
            if parted:
                first = pl.multiple_of((1 - self.x if over_x else self.x) * full.shape[1] + start, 128)
            src = shard.at[:, pl.ds(first, width)] if own else dst
            return remote(src, dst, self.ss.at[s, index], self.rs.at[s, origin], (target, self.core))

        self.sends.go(make, when)

    def wait(self, s, origin, when=None):
        def action():
            ref = self.block(s, origin)
            remote(
                ref, ref, self.ss.at[s, 0], self.rs.at[s, origin], (self.to_x, self.core)
            ).wait_recv()

        guarded(when, action)

    def spread(self, s, origin, when=None, own=False, up=True, down=True, over_y=True):
        if up:
            self.send(s, origin, self.up, both(when, self.can_up), own)
        if down:
            self.send(s, origin, self.down, both(when, self.can_down), own)
        if over_y:
            self.send(s, origin, self.to_y, when, own)

    def begin_x(self, s):
        self.send(s, self.me, self.to_x, own=True, over_x=True)

    def begin(self, s):
        self.begin_x(s)
        self.spread(s, self.me, own=True)

    def after_x(self, s):
        self.wait(s, self.to_x)
        self.spread(s, self.to_x)

    def y_pair(self, s):
        if self.streams[s][4] == "xyz":
            for xx in (self.x, 1 - self.x):
                origin = at_place(self.z, 1 - self.y, xx)
                self.wait(s, origin)
                self.spread(s, origin, over_y=False)

    def after_z(self, s, distance):
        order = self.streams[s][4]
        ys = (self.y,) if order == "xzy" else (self.y, 1 - self.y)
        for step, ok in ((-distance, self.z >= distance), (distance, self.z + distance < Z_SIZE)):
            for yy in ys:
                for xx in (self.x, 1 - self.x):
                    origin = at_place(self.z + step, yy, xx)
                    self.wait(s, origin, ok)
                    self.spread(s, origin, ok, up=step < 0, down=step > 0, over_y=order == "xzy")

    def finish(self, s):
        if self.streams[s][4] == "xzy":
            for zz in range(Z_SIZE):
                for xx in range(X_SIZE):
                    self.wait(s, at_place(zz, 1 - self.y, xx))


def vmem(count):
    return [pl.BlockSpec(memory_space=pltpu.VMEM)] * count


def hbm(count):
    return [pl.BlockSpec(memory_space=pl.ANY)] * count


def params(collective_id, vmem_limit=VMEM_LIMIT):
    return pltpu.CompilerParams(
        collective_id=collective_id, has_side_effects=True, vmem_limit_bytes=vmem_limit
    )


def peers_far_first(me):
    z, y, x = place(me)
    found = []
    for dz in range(Z_SIZE):
        for dy in range(Y_SIZE):
            for dx in range(X_SIZE):
                if dz or dy or dx:
                    zz = lax.rem(z + dz, Z_SIZE)
                    found.append(at_place(zz, lax.rem(y + dy, 2), lax.rem(x + dx, 2)))
    return found[::-1]


def lanes_of(ref, vector):
    rows = ref.shape[0] // 6
    return jnp.concatenate(
        [ref[rows * vector + i : rows * vector + i + 1, :] for i in range(rows)], axis=1
    )


def head_masks(rows):
    lane = lax.broadcasted_iota(jnp.int32, (rows, 128), 1)
    first = (lane < 64).astype(F32)
    return first, 1.0 - first


def diagonal(rows):
    down = lax.broadcasted_iota(jnp.int32, (rows, 128), 0)
    return (down == lax.broadcasted_iota(jnp.int32, (rows, 128), 1)).astype(F32)


def choice_masks(routes_ref):
    rows = routes_ref.shape[1]
    lane = lax.broadcasted_iota(jnp.int32, (rows, 128), 1)
    routes = contract(
        routes_ref[...].astype(F32).astype(BF16), diagonal(2).astype(BF16), (0,), (0,)
    )
    named = [(routes[:, k : k + 1] == lane.astype(F32)).astype(F32) for k in range(2)]
    above = lax.broadcasted_iota(jnp.int32, (rows, rows), 0)
    along = lax.broadcasted_iota(jnp.int32, (rows, rows), 1)
    before = jnp.dot(
        (along < above).astype(F32).astype(BF16),
        (named[0] + named[1]).astype(BF16),
        preferred_element_type=F32,
    )
    slot = lax.broadcasted_iota(jnp.int32, (rows, EXPERTS * CAP), 1)
    takes = []
    for k in range(2):
        rank = jnp.sum(before * named[k], axis=1, keepdims=True)
        own = routes[:, k : k + 1] * CAP + rank
        takes.append((slot == own.astype(jnp.int32)).astype(F32).astype(BF16))
    return named, takes


def attend(attn_low, qkv_ref, act_ref, probs_ref, mixed_ref, pump):
    rows, width = attn_low.shape[0], mixed_ref.shape[1]
    for j in range(3):
        act_ref[:, width * j : width * (j + 1)] = jnp.dot(
            attn_low, qkv_ref[:, width * j : width * (j + 1)], preferred_element_type=F32
        ).astype(BF16)
        pump()
    masks = head_masks(rows)
    scale_factor = 64 ** (-0.5)
    for pair in range(width // 128):
        q, k, v = [
            act_ref[:, width * j + 128 * pair : width * j + 128 * (pair + 1)] for j in range(3)
        ]
        mixed = None
        for h in range(2):
            scores = contract(q * masks[h].astype(BF16), k, (1,), (1,)) * scale_factor
            top = jnp.max(scores, axis=-1, keepdims=True)
            weights = jnp.exp(scores - top)
            probs = weights / jnp.sum(weights, axis=-1, keepdims=True)
            probs_ref[2 * pair + h] = probs
            part = jnp.dot(probs.astype(BF16), v, preferred_element_type=F32) * masks[h]
            mixed = part if mixed is None else mixed + part
            pump()
        mixed_ref[:, 128 * pair : 128 * (pair + 1)] = mixed.astype(BF16)


def forward_kernel(
    ts_ref, table_ref, ada_ref, qkv_ref, proj_ref, route_ref, up_ref, down_ref,
    eup_ref, edown_ref, tok_ref, cot_ref, routes_ref,
    mod_ref, cond_ref, qkv_out, proj_out, route_out, act_ref, probs_ref, mixed_ref,
    attn_ref, attn_low_ref, mlp_ref, gshared_ref, gates_ref,
    up_out, down_out, eup_out, edown_out, rows_out, grads_out,
    ts_all, terms, landed, part, theirs, gate_row, rows_send, grads_send,
    ts_ss, ts_rs, mod_ss, mod_rs, ag_ss, ag_rs, own_sem, join_ss, join_rs, swap_sem,
    ss, rs, pass_ss, pass_rs, own_a, pair_ss, pair_rs, ts_own, qkv_own, route_own,
):
    me, core = lax.axis_index(WIDE), lax.axis_index(NARROW)
    count = lax.axis_size(WIDE)
    others = peers_far_first(me)
    peer = (me, 1 - core)
    greet([(other, core) for other in others] + [peer])
    sends = Sends()
    ts_own[...] = jnp.full(ts_own.shape, ts_ref[0], jnp.int32)
    for k, other in enumerate(others):
        sends.go(lambda k=k, other=other: remote(ts_own, ts_all.at[me], ts_ss.at[k], ts_rs.at[me], (other, core)))
    half = down_out.shape[1] // 2
    streams = [
        (qkv_own, qkv_out, 0, qkv_own.shape[1], "xzy", False),
        (proj_ref, proj_out, 0, proj_ref.shape[1], "xzy", False),
        (route_own, route_out, 0, route_own.shape[1], "xzy", False),
        (up_ref, up_out, 0, up_out.shape[1], "xzy", True),
        (down_ref, down_out, 0, half, "xzy", True),
        (down_ref, down_out, half, half, "xyz", True),
    ]
    for j in range(3):
        at = qkv_ref.shape[2] * j
        qkv_own[:, at : at + qkv_ref.shape[2]] = qkv_ref[j]
    route_own[...] = contract(route_ref[...], diagonal(EXPERTS).astype(BF16), (0,), (0,)).astype(BF16)
    ag = Gather(streams, ag_ss, ag_rs, sends)
    for s in range(3):
        ag.begin(s)
    pieces = 8
    joins = []
    for a, (src, dst) in enumerate(((eup_ref, eup_out), (edown_ref, edown_out))):
        size = src.shape[0] // pieces
        for p in range(pieces):
            cut = pl.ds(p * size, size)
            joins.append(
                lambda a=a, p=p, src=src, dst=dst, cut=cut: remote(
                    src.at[cut, :], dst.at[cut, :],
                    join_ss.at[a * pieces + p], join_rs.at[a * pieces + p], (ag.to_x, core),
                )
            )
    waiting = joins[::2] + joins[1::2]

    def join(steps):
        for _ in range(steps):
            if waiting:
                sends.go(waiting.pop(0))

    join(1)
    own = []
    for i, (shard, full) in enumerate(
        ((qkv_own, qkv_out), (proj_ref, proj_out), (route_own, route_out), (up_ref, up_out), (down_ref, down_out))
    ):
        rows, wide = shard.shape[0], full.shape[1]
        side = pl.multiple_of(ag.x * wide, 128) if wide < shard.shape[1] else 0
        own.append(
            pltpu.make_async_copy(
                shard.at[:, pl.ds(side, wide)],
                full.at[pl.ds(pl.multiple_of(me * rows, 16), rows), :], own_sem.at[i]
            )
        )
        own[-1].start()

    tokens = tok_ref[...].astype(F32)
    normal1, _ = normalized(tokens)

    ts_all[me] = ts_own[...]
    for other in others[::-1]:
        remote(ts_own, ts_all.at[other], ts_ss.at[0], ts_rs.at[other], (other, core)).wait_recv()
    steps = jnp.max(ts_all[...], axis=1)[:, :1]
    onehot = (
        steps == lax.broadcasted_iota(jnp.int32, (count, table_ref.shape[0]), 1)
    ).astype(F32).astype(BF16)
    cond = jnp.dot(onehot, table_ref[...], preferred_element_type=F32)
    cond_act = (cond * jax.nn.sigmoid(cond)).astype(BF16)
    cond_ref[...] = cond_act.astype(F32)
    chunks = terms.shape[1] // 6
    for j in range(6):
        vector = jnp.dot(cond_act, ada_ref[j], preferred_element_type=F32)
        for i in range(chunks):
            terms[:, chunks * j + i, :] = vector[:, 128 * i : 128 * (i + 1)]
    for k, other in enumerate(others):
        sends.go(lambda k=k, other=other: remote(terms.at[other], landed.at[me], mod_ss.at[k], mod_rs.at[me], (other, core)))
    join(2)
    for s in range(3):
        ag.after_x(s)
    for s in range(3, len(streams)):
        ag.begin_x(s)
    join(2)

    for distance in range(1, Z_SIZE):
        for s in range(3):
            ag.after_z(s, distance)
        join(2)
    for s in range(3, len(streams)):
        ag.spread(s, ag.me, own=True)
    landed[me] = terms[me]
    for other in others[::-1]:
        remote(terms.at[me], landed.at[other], mod_ss.at[0], mod_rs.at[other], (other, core)).wait_recv()
    mod_ref[...] = jnp.sum(landed[...], axis=0)
    shift1, scale1, gate1, shift2, scale2, gate2 = [lanes_of(mod_ref, j) for j in range(6)]
    attn_low_ref[...] = (normal1 * (1.0 + scale1) + shift1).astype(BF16)
    patches = tok_ref.shape[0]
    first, second = pl.ds(0, patches), pl.ds(patches, patches)
    gate_row[...] = jnp.broadcast_to(gate2, gate_row.shape)
    gshared_ref[first, :] = (gate2 * cot_ref[...].astype(F32)).astype(BF16)
    width = rows_send.shape[1]
    mine = pl.ds(pl.multiple_of(core * width, 128), width)
    theirs_half = pl.ds(pl.multiple_of((1 - core) * width, 128), width)
    across = [
        remote(ref.at[first, mine], ref.at[second, mine], pair_ss.at[i], pair_rs.at[i], (ag.to_x, core))
        for i, ref in enumerate((gshared_ref, mlp_ref))
    ]
    handed = [
        remote(ref.at[second, mine], ref.at[second, mine], pair_ss.at[2 + i], pair_rs.at[2 + i], peer)
        for i, ref in enumerate((gshared_ref, mlp_ref))
    ]
    came = [
        remote(ref.at[second, theirs_half], ref.at[second, theirs_half], pair_ss.at[2 + i], pair_rs.at[2 + i], peer)
        for i, ref in enumerate((gshared_ref, mlp_ref))
    ]
    across[0].start()
    bulk = range(3, len(streams))
    queue = [lambda s=s: ag.after_x(s) for s in bulk]
    queue += [lambda s=s: ag.y_pair(s) for s in bulk]
    queue += [lambda s=s, d=d: ag.after_z(s, d) for d in range(1, Z_SIZE) for s in bulk]

    def pump():
        join(1)
        if queue:
            queue.pop(0)()

    ag.finish(0)
    own[0].wait()
    attend(attn_low_ref[...], qkv_out, act_ref, probs_ref, mixed_ref, pump)
    ag.finish(1)
    own[1].wait()
    part[...] = contract(mixed_ref[...], proj_out[...], (1,), (1,)).astype(BF16)
    swap = remote(part, theirs, swap_sem.at[0], swap_sem.at[1], peer)
    swap.start()
    named, takes = choice_masks(routes_ref)
    pump()
    swap.wait()
    attn_out = part[...].astype(F32) + theirs[...].astype(F32)
    attn_ref[...] = attn_out
    hidden = tok_ref[...].astype(F32) + gate1 * attn_out
    normal2, _ = normalized(hidden)
    mlp_ref[first, :] = (normal2 * (1.0 + scale2) + shift2).astype(BF16)
    ag.finish(2)
    own[2].wait()
    logits = jnp.dot(mlp_ref[first, :], route_out[...], preferred_element_type=F32)
    chosen = [jnp.sum(logits * named[k], axis=1, keepdims=True) for k in range(2)]
    peak = jnp.maximum(chosen[0], chosen[1])
    weight = [jnp.exp(chosen[k] - peak) for k in range(2)]
    total = weight[0] + weight[1]
    gates = [weight[k] / total for k in range(2)]
    lane = lax.broadcasted_iota(jnp.int32, gates_ref.shape, 1)
    gates_ref[...] = jnp.where(lane == 0, gates[0], jnp.where(lane == 1, gates[1], 0.0))
    grad_half = gate_row[0:1, mine] * cot_ref[:, mine].astype(F32)
    rows_send[...] = contract(takes[0] + takes[1], mlp_ref[first, mine], (0,), (0,)).astype(BF16)
    grads_send[...] = (
        contract(takes[0], (gates[0] * grad_half).astype(BF16), (0,), (0,))
        + contract(takes[1], (gates[1] * grad_half).astype(BF16), (0,), (0,))
    ).astype(BF16)

    size = rows_send.shape[0] // count

    def rows(index):
        return pl.ds(pl.multiple_of(index * size, 16), size)

    pairs = ((rows_send, rows_out), (grads_send, grads_out))
    for k, other in enumerate(others):
        for a, (src, dst) in enumerate(pairs):
            sends.go(
                lambda k=k, other=other, a=a, src=src, dst=dst: remote(
                    src.at[rows(other), :], dst.at[core, rows(me), :],
                    ss.at[a, k], rs.at[a, me], (other, core),
                )
            )
    across[1].start()
    across[0].wait()
    handed[0].start()
    join(len(joins))
    kept = []
    for a, (src, dst) in enumerate(pairs):
        sends.go(
            lambda a=a, src=src, dst=dst: remote(
                src.at[rows(me), :], dst.at[core, rows(me), :], pass_ss.at[a, 15], pass_rs.at[a, me], peer
            )
        )
        kept.append(pltpu.make_async_copy(src.at[rows(me), :], dst.at[core, rows(me), :], own_a.at[a]))
        kept[-1].start()
    while queue:
        pump()
    across[1].wait()
    handed[1].start()
    for k, other in enumerate(others[::-1]):
        for a, (src, dst) in enumerate(pairs):
            here = dst.at[core, rows(other), :]
            remote(here, here, ss.at[a, 0], rs.at[a, other], peer).wait_recv()
            sends.go(
                lambda k=k, other=other, a=a, here=here: remote(
                    here, here, pass_ss.at[a, k], pass_rs.at[a, other], peer
                )
            )
    for s in range(3, len(streams)):
        ag.finish(s)
    for i, make in enumerate(joins):
        make().wait_recv()
    for other in [me] + others[::-1]:
        for a, (src, dst) in enumerate(pairs):
            there = dst.at[1 - core, rows(other), :]
            remote(there, there, pass_ss.at[a, 0], pass_rs.at[a, other], peer).wait_recv()
    for i in range(2):
        handed[i].wait_send()
        came[i].wait_recv()
    for copy in own[3:] + kept:
        copy.wait()
    sends.drain()


def forward(ts_tile, table, ada, qkv, proj, route, up, down, e_up, e_down, tokens, cotangent, routes):
    count = 16
    shards = (qkv, proj, route, up, down)
    vectors = 6 * ada.shape[2] // 128
    patches, width = tokens.shape
    slots = EXPERTS * CAP
    dma = pltpu.SemaphoreType.DMA
    shape = jax.ShapeDtypeStruct

    def full(a):
        return shape((count * a.shape[0], a.shape[1]), a.dtype)

    def parted(a):
        return shape((count * a.shape[0], a.shape[1] // X_SIZE), a.dtype)

    return pl.pallas_call(
        forward_kernel,
        out_shape=[
            shape((vectors, 128), F32), shape((count, table.shape[1]), F32),
            shape((count * qkv.shape[1], 3 * qkv.shape[2]), BF16), full(proj), shape((count * qkv.shape[1], 128), BF16),
            shape((patches, 3 * qkv.shape[2]), BF16), shape((proj.shape[1] // 64, patches, patches), F32),
            shape((patches, proj.shape[1]), BF16), shape((patches, width), F32),
            shape((patches, width), BF16), shape((2 * patches, width), BF16),
            shape((2 * patches, width), BF16), shape((patches, 128), F32),
            parted(up), parted(down), shape(e_up.shape, BF16), shape(e_down.shape, BF16),
            shape((2, slots, width // 2), BF16), shape((2, slots, width // 2), BF16),
        ],
        in_specs=[pl.BlockSpec(memory_space=pltpu.SMEM)] + vmem(7) + hbm(2) + vmem(3),
        out_specs=vmem(13) + hbm(6),
        scratch_shapes=[
            pltpu.VMEM((count, 8, 128), jnp.int32),
            pltpu.VMEM((count, vectors, 128), F32),
            pltpu.VMEM((count, vectors, 128), F32),
            pltpu.VMEM((patches, width), BF16), pltpu.VMEM((patches, width), BF16),
            pltpu.VMEM((8, width), F32),
            pltpu.VMEM((slots, width // 2), BF16), pltpu.VMEM((slots, width // 2), BF16),
            dma((16,)), dma((16,)), dma((16,)), dma((16,)),
            dma((6, 40)), dma((6, 16)), dma((5,)), dma((16,)), dma((16,)), dma((2,)),
            dma((2, 16)), dma((2, 16)), dma((2, 16)), dma((2, 16)), dma((2,)), dma((4,)), dma((4,)),
            pltpu.VMEM((8, 128), jnp.int32),
            pltpu.VMEM((qkv.shape[1], 3 * qkv.shape[2]), BF16), pltpu.VMEM((qkv.shape[1], 128), BF16),
        ],
        compiler_params=params(1),
        name="forward",
    )(ts_tile, table, ada, *shards, e_up, e_down, tokens, cotangent, routes)


def normalized(values):
    centre = jnp.mean(values, axis=-1, keepdims=True)
    shifted = values - centre
    spread = jnp.mean(shifted * shifted, axis=-1, keepdims=True)
    rate = lax.rsqrt(spread + epsilon)
    return shifted * rate, rate


def norm_back(normal, rate, gradient):
    mean = jnp.mean(gradient, axis=-1, keepdims=True)
    along = jnp.mean(gradient * normal, axis=-1, keepdims=True)
    return rate * (gradient - mean - normal * along)


class Sums:
    def __init__(self, specs, r, sends):
        self.specs, self.r, self.sends = specs, r, sends
        self.me, self.core = lax.axis_index(WIDE), lax.axis_index(NARROW)
        self.z, self.y, self.x = place(self.me)
        z = self.z
        upper = z >= 2
        self.dest = [
            jnp.where(upper, 0, 3), jnp.where(upper, 1, 2), jnp.where(upper, 5 - z, 1 - z), z
        ]
        self.near = {
            "y": at_place(z, 1 - self.y, self.x), "x": at_place(z, self.y, 1 - self.x)
        }

    def part(self, ref, axis, zz, other):
        if axis == "y":
            return ref.at[zz, 1 - self.y if other else self.y]
        return ref.at[zz, :, 1 - self.x if other else self.x]

    def slot(self, zz, way, at):
        return jnp.where(jnp.logical_and(zz == at, way == 1), 4, zz)

    def landed(self, ref, sem):
        remote(ref, ref, self.r.first_ss.at[0, 0], sem, (self.near["x"], self.core)).wait_recv()

    def load(self, i, k):
        terms, axis, work = self.specs[i][:3]
        zz = self.dest[k]
        return pltpu.make_async_copy(
            self.part(terms, axis, zz, False), work.at[zz], self.r.load_sem.at[i, k]
        )

    def start(self, i, k):
        terms, axis, _, came = self.specs[i][:4]
        zz = self.dest[k]
        self.load(i, k).start()
        self.sends.go(
            lambda: remote(
                self.part(terms, axis, zz, True), came.at[zz],
                self.r.first_ss.at[i, k], self.r.first_rs.at[i, zz], (self.near[axis], self.core),
            )
        )

    def step(self, i, k):
        _, axis, work, came, along, last = self.specs[i][:6]
        z, zz, core = self.z, self.dest[k], self.core
        self.load(i, k).wait()
        self.landed(came.at[zz], self.r.first_rs.at[i, zz])
        if k < 3:
            rising = zz > z
            way = jnp.where(rising, 0, 1)
            more = jnp.where(rising, z > 0, z < 3)

            @pl.when(more)
            def _():
                self.landed(along.at[zz], self.r.z_rs.at[i, zz])
                add_blocks(work.at[zz], came.at[zz], along.at[zz])

            @pl.when(jnp.logical_not(more))
            def _():
                add_blocks(work.at[zz], came.at[zz])

            target = jnp.where(rising, self.me + 4, self.me - 4)
            slot = self.slot(zz, way, jnp.where(rising, z + 1, z - 1))
            self.sends.go(
                lambda: remote(
                    work.at[zz], along.at[slot],
                    self.r.z_ss.at[i, k], self.r.z_rs.at[i, slot], (target, core),
                )
            )
            return
        add_blocks(work.at[z], came.at[z])
        for way, there in ((0, z > 0), (1, z < 3)):

            @pl.when(there)
            def _(way=way):
                slot = self.slot(z, way, z)
                self.landed(along.at[slot], self.r.z_rs.at[i, slot])
                add_blocks(work.at[z], along.at[slot])

        side, final = (self.x, "x") if axis == "y" else (self.y, "y")
        self.sends.go(
            lambda: remote(
                work.at[z, 1 - side], last,
                self.r.last_ss.at[i], self.r.last_rs.at[i], (self.near[final], core),
            )
        )

    def finish(self, i):
        _, axis, work, _, _, last, store = self.specs[i]
        self.landed(last, self.r.last_rs.at[i])
        side = self.x if axis == "y" else self.y
        store(work[self.z, side].astype(F32), last[...].astype(F32))


def add_blocks(total, *terms):
    size = total.shape[1]
    per = size // 16

    def body(n, _):
        block, at = lax.div(n, per), pl.ds(pl.multiple_of(lax.rem(n, per) * 16, 16), 16)
        value = total[block, at, :].astype(F32)
        for term in terms:
            value = value + term[block, at, :].astype(F32)
        total[block, at, :] = value.astype(BF16)
        return 0

    lax.fori_loop(0, 2 * per, body, 0)


def gelu_pair(value, gradient):
    root = 0.7978845608028654
    square = value * value
    bend = jnp.tanh(root * (value + 0.044715 * value * square))
    half = 0.5 * (1.0 + bend)
    slope = half + 0.5 * value * (1.0 - bend * bend) * (root * (1.0 + 0.134145 * square))
    return (value * half).astype(BF16), (slope * gradient).astype(BF16)


def columns_of(total, tile, body):
    def turn(n, _):
        body(pl.ds(pl.multiple_of(n * tile, 128), tile))
        return 0

    lax.fori_loop(0, total // tile, turn, 0)


def backward_kernel(names, fetched, *refs):
    r = types.SimpleNamespace(**dict(zip(names, refs, strict=True)))
    me, core = lax.axis_index(WIDE), lax.axis_index(NARROW)
    count = lax.axis_size(WIDE)
    z, y, x = place(me)
    others = peers_far_first(me)
    peer = (me, 1 - core)
    across = (at_place(z, y, 1 - x), core)
    fetches = {}
    for n, name in enumerate(fetched):
        fetches[name] = pltpu.make_async_copy(getattr(r, name), getattr(r, name + "_v"), r.fetch_sem.at[n])
        fetches[name].start()
    greet([(other, core) for other in others] + [peer])
    sends = Sends()
    slots, width = r.their0.shape
    size = slots // count
    patches = r.tok.shape[0]
    mine = pl.ds(pl.multiple_of(core * width, 128), width)
    theirs_half = pl.ds(pl.multiple_of((1 - core) * width, 128), width)

    def rows(index):
        return pl.ds(pl.multiple_of(index * size, 16), size)

    def arrived(ref, sem):
        remote(ref, ref, r.near_ss.at[0, 0], sem, peer).wait_recv()

    for name in fetched[:6]:
        fetches[name].wait()
    hidden_units = r.eup_v.shape[1]
    for n in range(2):
        r.ein_t[n] = r.ein_v[n].T
        r.eg_t[n] = r.eg_v[n].T

    def expert_hidden(at):
        def through(rows_ref, own, other):
            return jnp.dot(rows_ref[x], own[:, at], preferred_element_type=F32) + jnp.dot(
                rows_ref[1 - x], other[:, at], preferred_element_type=F32
            )

        r.eact[:, at], r.epre[:, at] = gelu_pair(
            through(r.ein_v, r.eup_v, r.upo_v), through(r.eg_v, r.edn_v, r.dno_v)
        )

    columns_of(hidden_units, 256, expert_hidden)

    for target, left, own, other in (
        (r.ein_v, r.eact, r.edn_v, r.dno_v), (r.eg_v, r.epre, r.eup_v, r.upo_v),
    ):
        target[x] = contract(left[...], own[...], (1,), (1,)).astype(BF16)
        target[1 - x] = contract(left[...], other[...], (1,), (1,)).astype(BF16)

    triples = ((r.ein_v, r.their0, r.back0), (r.eg_v, r.their1, r.back1))
    order = others + [me]
    for k, other in enumerate(order):
        for a, (src, theirs, _) in enumerate(triples):
            sends.go(
                lambda k=k, other=other, a=a, src=src, theirs=theirs: remote(
                    src.at[1 - core, rows(other), :], theirs.at[rows(other), :],
                    r.near_ss.at[a, k], r.near_rs.at[a, other], peer,
                )
            )
    def given_terms(at):
        r.eup_v[:, at] = jnp.dot(r.ein_t[1 - x], r.epre[:, at], preferred_element_type=F32).astype(BF16)
        r.upo_v[:, at] = jnp.dot(r.eg_t[1 - x], r.eact[:, at], preferred_element_type=F32).astype(BF16)

    columns_of(hidden_units, 256, given_terms)
    pieces = 2
    cut = r.eup_v.shape[0] // pieces
    trades = []
    for a, (give, take) in enumerate(((r.eup_v, r.take0), (r.upo_v, r.take1))):
        for p in range(pieces):
            piece = pl.ds(p * cut, cut)
            trades.append(
                lambda a=a, p=p, give=give, take=take, piece=piece: remote(
                    give.at[piece, :], take.at[piece, :],
                    r.trade_ss.at[a * pieces + p], r.trade_rs.at[a * pieces + p], across,
                )
            )
    for k, other in enumerate(order):
        for a, (src, theirs, back) in enumerate(triples):
            arrived(theirs.at[rows(other), :], r.near_rs.at[a, other])
            both_cores = (
                src[core, rows(other), :].astype(F32) + theirs[rows(other), :].astype(F32)
            ).astype(BF16)
            if k < len(others):
                src[core, rows(other), :] = both_cores
                sends.go(
                    lambda k=k, other=other, a=a, src=src, back=back: remote(
                        src.at[core, rows(other), :], back.at[rows(me), :],
                        r.ss.at[a, k], r.rs.at[a, me], (other, core),
                    )
                )
            else:
                back[rows(me), :] = both_cores

    for name in fetched[6:10]:
        fetches[name].wait()
    r.mlp_t[...] = r.mlp_v[...].T
    r.gsh_t[...] = r.gsh_v[...].T

    def shared_hidden(at):
        r.sact[:, at], r.spre[:, at] = gelu_pair(
            jnp.dot(r.mlp_v[...], r.up_v[:, at], preferred_element_type=F32),
            jnp.dot(r.gsh_v[...], r.down_v[:, at], preferred_element_type=F32),
        )

    columns_of(r.up_v.shape[1], 256, shared_hidden)
    blocks = (2, 2, 2, size)

    def shared_terms(at):
        for target, left, right in ((r.up_t, r.mlp_t, r.spre), (r.down_t, r.gsh_t, r.sact)):
            for h in range(2):
                value = jnp.dot(
                    left[384 * h : 384 * (h + 1), :], right[:, at], preferred_element_type=F32
                )
                target[2 * h : 2 * h + 2, :, :, :, at] = value.astype(BF16).reshape(
                    *blocks, value.shape[1]
                )

    columns_of(r.up_v.shape[1], 256, shared_terms)

    def shared_out(at):
        r.part0[:, at] = contract(r.sact[...], r.down_v[at, :], (1,), (1,)).astype(BF16)
        r.gsh_v[:, at] = contract(r.spre[...], r.up_v[at, :], (1,), (1,)).astype(BF16)

    columns_of(r.part0.shape[1], 256, shared_out)

    def store_to(ref):
        def store(own, came):
            ref[...] = own + came

        return store

    def store_route(own, came):
        r.route_o[...] = lax.dot_general(
            diagonal(EXPERTS), own + came, (((1,), (1,)), ((), ())),
            precision=highest, preferred_element_type=F32,
        )

    def store_sides(ref):
        def store(own, came):
            half = own.shape[1]
            ref[:, pl.ds(pl.multiple_of(x * half, 128), half)] = own
            ref[:, pl.ds(pl.multiple_of((1 - x) * half, 128), half)] = came

        return store

    def store_qkv(own, came):
        for j in range(3):
            at = slice(width * j, width * (j + 1))
            r.qkv_o[j] = own[:, at] + came[:, at]

    specs = [
        (r.up_t, "y", r.up_w, r.up_c, r.up_a, r.up_l, store_sides(r.up_o)),
        (r.down_t, "y", r.down_w, r.down_c, r.down_a, r.down_l, store_sides(r.down_o)),
        (r.proj_t, "y", r.proj_w, r.proj_c, r.proj_a, r.proj_l, store_to(r.proj_o)),
        (r.route_t, "y", r.route_w, r.route_c, r.route_a, r.route_l, store_route),
        (r.qkv_t, "y", r.qkv_w, r.qkv_c, r.qkv_a, r.qkv_l, store_qkv),
    ]
    sums = Sums(specs, r, sends)
    small = ((r.part0, r.their2, r.branch, r.pass0, r.came0), (r.gsh_v, r.their3, r.gmlp, r.pass1, r.came1))
    for a, (part, theirs, _, _, _) in enumerate(small):
        sends.go(
            lambda a=a, part=part, theirs=theirs: remote(
                part.at[:, theirs_half], theirs, r.near_ss.at[a, 16], r.near_rs.at[a, 16], peer
            )
        )
    for k in range(4):
        for i in range(2):
            sums.start(i, k)
    for a, (part, theirs, total, passed, came) in enumerate(small):
        arrived(theirs, r.near_rs.at[a, 16])
        total[:, mine] = part[:patches, mine].astype(F32) + theirs[:patches, :].astype(F32)
        passed[...] = (part[patches:, mine].astype(F32) + theirs[patches:, :].astype(F32)).astype(BF16)
        sends.go(
            lambda a=a, passed=passed, came=came: remote(
                passed, came, r.pass_ss.at[a], r.pass_rs.at[a], across
            )
        )
    for trade in trades:
        sends.go(trade)
    queue = [lambda i=i, k=k: sums.step(i, k) for k in range(4) for i in range(2)]

    def pump(steps=1):
        for _ in range(steps):
            if queue:
                queue.pop(0)()

    shift1, scale1, gate1, shift2, scale2, gate2 = [lanes_of(r.mod, j) for j in range(6)]
    named, takes = choice_masks(r.routes)
    gates = [r.gates[:, k : k + 1] for k in range(2)]
    pump(2)
    for other in others[::-1]:
        for a, (_, _, back) in enumerate(triples):
            arrived(back.at[rows(other), :], r.rs.at[a, other])
    for a in range(2):
        arrived(small[a][4], r.pass_rs.at[a])
    picked = [jnp.dot(takes[k], r.back0[...], preferred_element_type=F32) for k in range(2)]
    r.branch[:, mine] = (
        r.branch[:, mine] + r.came0[...].astype(F32)
        + gates[0] * picked[0] + gates[1] * picked[1]
    )
    r.gmlp[:, mine] = (
        r.gmlp[:, mine] + r.came1[...].astype(F32)
        + jnp.dot(takes[0] + takes[1], r.back1[...], preferred_element_type=F32)
    )
    for k in range(6):
        r.gate_row[k : k + 1, :] = lanes_of(r.mod, k)
    grad_half = r.gate_row[5:6, mine] * r.cot[:, mine].astype(F32)
    terms = [jnp.sum(grad_half * picked[k], axis=-1, keepdims=True) for k in range(2)]
    lane = lax.broadcasted_iota(jnp.int32, r.gsum.shape, 1)
    r.gsum[...] = jnp.where(lane == 0, terms[0], jnp.where(lane == 1, terms[1], 0.0))
    swaps = [
        remote(r.branch.at[:, mine], r.branch.at[:, mine], r.swap_ss.at[0], r.swap_rs.at[0], peer),
        remote(r.gmlp.at[:, mine], r.gmlp.at[:, mine], r.swap_ss.at[1], r.swap_rs.at[1], peer),
        remote(r.gsum, r.gsum_c, r.swap_ss.at[2], r.swap_rs.at[2], peer),
    ]
    for swap in swaps:
        swap.start()
    for name in fetched[10:]:
        fetches[name].wait()
    hidden = r.tok[...].astype(F32) + gate1 * r.attn_v[...]
    normal2, rate2 = normalized(hidden)
    r.normal[...] = normal2
    grad_out = r.cot[...].astype(F32)
    arrived(r.branch.at[:, theirs_half], r.swap_rs.at[0])
    arrived(r.gmlp.at[:, theirs_half], r.swap_rs.at[1])
    arrived(r.gsum_c, r.swap_rs.at[2])
    for swap in swaps:
        swap.wait_send()

    def put(vector, value):
        for i in range(value.shape[1] // 128):
            at = value.shape[1] // 128 * vector + i
            r.vec[at : at + 1, :] = value[:, 128 * i : 128 * (i + 1)]

    branch = r.branch[...]
    r.out_o[...] = (hidden + gate2 * branch).astype(BF16)
    put(5, jnp.sum(grad_out * branch, axis=0, keepdims=True))
    grad_gates = [r.gsum[:, k : k + 1] + r.gsum_c[:, k : k + 1] for k in range(2)]
    inner = gates[0] * grad_gates[0] + gates[1] * grad_gates[1]
    grad_chosen = [gates[k] * (grad_gates[k] - inner) for k in range(2)]
    grad_logits = (grad_chosen[0] * named[0] + grad_chosen[1] * named[1]).astype(BF16)
    grad_mlp = r.gmlp[...] + contract(grad_logits, r.routew_v[...], (1,), (1,))
    normal2 = r.normal[...]
    put(3, jnp.sum(grad_mlp, axis=0, keepdims=True))
    put(4, jnp.sum(grad_mlp * normal2, axis=0, keepdims=True))
    r.ghid[...] = grad_out + norm_back(normal2, rate2, grad_mlp * (1.0 + scale2))
    grad_hidden = r.ghid[...]
    put(2, jnp.sum(grad_hidden * r.attn_v[...], axis=0, keepdims=True))
    r.gattn[...] = (gate1 * grad_hidden).astype(BF16)

    def weight_terms(target, left, right):
        columns = right.shape[1]
        cut = 384
        for n in range(columns // cut if columns > cut else 1):
            lo, hi = cut * n, min(columns, cut * (n + 1))
            for h in range(2):
                value = contract(left[:, 384 * h : 384 * (h + 1)], right[:, lo:hi], (0,), (0,))
                target[2 * h : 2 * h + 2, :, :, :, lo:hi] = value.astype(BF16).reshape(
                    *blocks, hi - lo
                )

    weight_terms(r.proj_t, r.gattn, r.mixed_v)
    weight_terms(r.route_t, r.mlp_v[:patches, :], grad_logits)
    pump(1)
    r.gmix[...] = jnp.dot(r.gattn[...], r.projw_v[...], preferred_element_type=F32).astype(BF16)
    for k in range(4):
        for i in (2, 3):
            sums.start(i, k)
    masks = head_masks(r.gmix.shape[0])
    scale_factor = 64 ** (-0.5)
    for pair in range(width // 128):
        at = [slice(width * j + 128 * pair, width * j + 128 * (pair + 1)) for j in range(3)]
        q, k, v = [r.act_v[:, at[j]] for j in range(3)]
        gm = r.gmix[:, at[0]]
        found = [None] * 3
        for h in range(2):
            probs = r.probs_v[2 * pair + h]
            grad_probs = contract(gm * masks[h].astype(BF16), v, (1,), (1,))
            weighted = jnp.sum(probs * grad_probs, axis=-1, keepdims=True)
            grad_scores = (probs * (grad_probs - weighted)).astype(BF16)
            parts = (
                jnp.dot(grad_scores, k, preferred_element_type=F32) * scale_factor,
                contract(grad_scores, q, (0,), (0,)) * scale_factor,
                contract(probs.astype(BF16), gm, (0,), (0,)),
            )
            found = [
                part * masks[h] if old is None else old + part * masks[h]
                for part, old in zip(parts, found, strict=True)
            ]
            pump(1)
        for j in range(3):
            r.gqkv[:, at[j]] = found[j].astype(BF16)
    r.gpart[...] = contract(r.gqkv[...], r.qkvw_v[...], (1,), (1,)).astype(BF16)
    swap = remote(r.gpart, r.gpart_c, r.swap_ss.at[3], r.swap_rs.at[3], peer)
    swap.start()
    weight_terms(r.qkv_t, r.attnlow_v, r.gqkv)
    for k in range(4):
        sums.start(4, k)
    tokens = r.tok[...].astype(F32)
    normal1, rate1 = normalized(tokens)
    swap.wait()
    grad_in = r.gpart[...].astype(F32) + r.gpart_c[...].astype(F32)
    put(0, jnp.sum(grad_in, axis=0, keepdims=True))
    put(1, jnp.sum(grad_in * normal1, axis=0, keepdims=True))
    for k, other in enumerate(others):
        sends.go(
            lambda k=k, other=other: remote(
                r.vec, r.every.at[me], r.vec_ss.at[k], r.vec_rs.at[me], (other, core)
            )
        )
    r.tokens_o[...] = r.ghid[...] + norm_back(normal1, rate1, grad_in * (1.0 + scale1))
    while queue:
        pump()
    for k in range(4):
        for i in (2, 3, 4):
            sums.step(i, k)
    for a in range(2 * pieces):
        take = (r.take0, r.take1)[a // pieces]
        arrived(take.at[pl.ds(a % pieces * cut, cut), :], r.trade_rs.at[a])
    for left, right, take, result in (
        (r.ein_t, r.epre, r.take0, r.eup_o), (r.eg_t, r.eact, r.take1, r.edown_o),
    ):

        def outward(n, slot, result=result):
            at = pl.ds(pl.multiple_of(n * 512 + slot * 256, 128), 256)
            return at, pltpu.make_async_copy(r.stage.at[slot], result.at[:, at], r.keep_sem.at[slot])

        def turn(n, _, left=left, right=right, take=take, outward=outward):
            for slot in range(2):
                at, copy = outward(n, slot)
                guarded(n > 0, lambda: outward(n - 1, slot)[1].wait())
                r.stage[slot] = jnp.dot(
                    left[x], right[:, at], preferred_element_type=F32
                ) + take[:, at].astype(F32)
                copy.start()
            return 0

        turns = hidden_units // 512
        lax.fori_loop(0, turns, turn, 0)
        for slot in range(2):
            outward(turns - 1, slot)[1].wait()
    for i in range(2):
        sums.finish(i)
    r.every[me] = r.vec[...]
    for other in others[::-1]:
        arrived(r.every.at[other], r.vec_rs.at[other])
    cond = r.cond[...]
    chunks = r.vec.shape[0] // 6
    for j in range(6):
        for i in range(chunks):
            r.ada_o[j, :, 128 * i : 128 * (i + 1)] = lax.dot_general(
                cond, r.every[:, chunks * j + i, :], (((0,), (0,)), ((), ())),
                precision=highest, preferred_element_type=F32,
            )
    for i in (2, 3, 4):
        sums.finish(i)
    sends.drain()


def backward(given, near):
    count = 16
    dma = pltpu.SemaphoreType.DMA
    shape = jax.ShapeDtypeStruct
    operands = given | near
    a = types.SimpleNamespace(**operands)
    patches, width = a.tok.shape
    slots, half = a.ein.shape[1:]
    head_width = a.mixed.shape[1]
    hidden = a.eup.shape[1]
    quarter = a.up.shape[1]
    size = slots // count
    vectors = a.mod.shape[0]
    columns = dict(up=quarter, down=quarter, proj=head_width, route=128, qkv=3 * head_width)
    results = dict(
        out_o=shape((patches, width), BF16),
        tokens_o=shape((patches, width), F32),
        ada_o=shape((6, size, width), F32),
        qkv_o=shape((3, size, head_width), F32),
        proj_o=shape((size, head_width), F32),
        route_o=shape((EXPERTS, size), F32),
        up_o=shape((size, 2 * quarter), F32),
        down_o=shape((size, 2 * quarter), F32),
        eup_o=shape((half, hidden), F32),
        edown_o=shape((half, hidden), F32),
    )
    v = pltpu.VMEM
    scratch = {name + "_v": v(array.shape, array.dtype) for name, array in given.items()}
    for name, wide in columns.items():
        scratch[name + "_w"] = v((4, 2, size, wide), BF16)
        scratch[name + "_c"] = v((4, 2, size, wide), BF16)
        scratch[name + "_a"] = v((5, 2, size, wide), BF16)
        scratch[name + "_l"] = v((size, wide), BF16)
        scratch[name + "_t"] = v((4, 2, 2, size, wide), BF16)

    def low(*sizes):
        return v(sizes, BF16)

    def full(*sizes):
        return v(sizes, F32)

    scratch |= dict(
        ein_t=low(2, half, slots), eg_t=low(2, half, slots),
        eact=low(slots, hidden), epre=low(slots, hidden),
        take0=low(half, hidden), take1=low(half, hidden),
        stage=full(2, half, 256),
        their0=low(slots, half), their1=low(slots, half), back0=low(slots, half), back1=low(slots, half),
        mlp_t=low(width, 2 * patches), gsh_t=low(width, 2 * patches),
        sact=low(2 * patches, quarter), spre=low(2 * patches, quarter),
        part0=low(2 * patches, width),
        their2=low(2 * patches, half), their3=low(2 * patches, half),
        pass0=low(patches, half), pass1=low(patches, half), came0=low(patches, half), came1=low(patches, half),
        branch=full(patches, width), gmlp=full(patches, width),
        normal=full(patches, width), ghid=full(patches, width),
        gattn=low(patches, width), gpart=low(patches, width), gpart_c=low(patches, width),
        gmix=low(patches, head_width), gqkv=low(patches, 3 * head_width),
        gsum=full(patches, 128), gsum_c=full(patches, 128), gate_row=full(8, width),
        vec=full(vectors, 128), every=full(count, vectors, 128),
        near_ss=dma((2, 17)), near_rs=dma((2, 17)), ss=dma((2, 16)), rs=dma((2, 16)),
        fetch_sem=dma((len(given),)), keep_sem=dma((2,)), trade_ss=dma((4,)), trade_rs=dma((4,)),
        first_ss=dma((5, 4)), first_rs=dma((5, 4)), load_sem=dma((5, 4)),
        z_ss=dma((5, 3)), z_rs=dma((5, 5)), last_ss=dma((5,)), last_rs=dma((5,)),
        swap_ss=dma((4,)), swap_rs=dma((4,)), vec_ss=dma((16,)), vec_rs=dma((16,)),
        pass_ss=dma((2,)), pass_rs=dma((2,)),
    )
    names = tuple(operands) + tuple(results) + tuple(scratch)
    found = pl.pallas_call(
        functools.partial(backward_kernel, names, tuple(given)),
        out_shape=list(results.values()),
        in_specs=hbm(len(given)) + vmem(len(near)),
        out_specs=vmem(8) + hbm(2),
        scratch_shapes=list(scratch.values()),
        compiler_params=params(3, 64_000_000),
        name="backward",
    )(*operands.values())
    return types.SimpleNamespace(**dict(zip(results, found, strict=True)))


def per_device_direct(
    tokens, cotangent, time_table, timesteps, routes, w_ada, w_qkv, w_proj,
    w_route, w_shared_up, w_shared_down, e_up, e_down,
):
    row_count, model_width = tokens.shape
    core = lax.axis_index(NARROW)
    core_count = lax.axis_size(NARROW)
    wide_count = lax.axis_size(WIDE)
    heads_here = HEADS // core_count
    head_dim = model_width // HEADS
    head_width = heads_here * head_dim
    half = model_width // 2
    scale_factor = head_dim ** (-0.5)
    wide_place = lax.axis_index(WIDE)
    upper = wide_place % 2 == 1
    ada_rows = w_ada.shape[0]

    table = lax.dynamic_slice_in_dim(time_table, wide_place * ada_rows, ada_rows, 1)
    table = jnp.pad(table, ((0, -table.shape[0] % 128), (0, 0)))
    (
        mod, cond_own, qkv_full, proj_full, route_full, activated, probs_full, mixed_low,
        attn_out, attn_low, mlp_low, grad_shared, gate_lanes,
        up_full, down_full, up_other, down_other, expert_in, grad_expert_out,
    ) = forward(
        timesteps,
        table,
        jnp.transpose(w_ada, (1, 0, 2)),
        jnp.transpose(w_qkv, (1, 0, 2)),
        w_proj,
        w_route.T,
        w_shared_up,
        w_shared_down,
        e_up,
        e_down,
        tokens,
        cotangent,
        routes.T,
    )
    got = backward(
        dict(
            ein=expert_in, eg=grad_expert_out, eup=e_up, upo=up_other, edn=e_down, dno=down_other,
            mlp=mlp_low, gsh=grad_shared, up=up_full, down=down_full,
            attn=attn_out, attnlow=attn_low, act=activated,
            probs=probs_full, mixed=mixed_low, qkvw=qkv_full, projw=proj_full, routew=route_full,
        ),
        dict(tok=tokens, cot=cotangent, mod=mod, cond=cond_own, routes=routes.T, gates=gate_lanes),
    )
    return (
        got.out_o,
        got.tokens_o,
        jnp.transpose(got.ada_o, (1, 0, 2)),
        jnp.transpose(got.qkv_o, (1, 0, 2)),
        got.proj_o,
        got.route_o.T,
        got.up_o,
        got.down_o,
        got.eup_o,
        got.edown_o,
    )


def solution(mesh):
    placed = (
        P(WIDE, None),
        P(WIDE, None),
        P(),
        P(WIDE),
        P(WIDE, None),
        P(WIDE, None, None),
        P(WIDE, None, NARROW),
        P(WIDE, NARROW),
        P(WIDE, None),
        P(WIDE, NARROW),
        P(WIDE, NARROW),
        P(WIDE, NARROW),
        P(WIDE, NARROW),
    )
    direct = mesh.shape[WIDE] == 16 and mesh.shape[NARROW] == 2
    return jax.shard_map(
        per_device_direct if direct else per_device,
        mesh=mesh,
        in_specs=placed,
        out_specs=(
            P(WIDE, None),
            P(WIDE, None),
            P(WIDE, None, None),
            P(WIDE, None, NARROW),
            P(WIDE, NARROW),
            P(WIDE, None),
            P(WIDE, NARROW),
            P(WIDE, NARROW),
            P(WIDE, NARROW),
            P(WIDE, NARROW),
        ),
        check_vma=False,
    )
```

```python
import functools
import types

import jax
import jax.numpy as jnp
from jax import lax
from jax.experimental import pallas as pl
from jax.experimental.pallas import tpu as pltpu
from jax.sharding import PartitionSpec as P

WIDE, NARROW = "wide", "narrow"
HEADS = 12
EXPERTS = 8
CAP = 96


epsilon = 1e-06
highest = lax.Precision.HIGHEST


def swapped(shard, axis, distance):
    return lax.ppermute(shard, axis, [(i, i ^ 1 << distance) for i in range(lax.axis_size(axis))])


def normalize(values):
    centre = jnp.mean(values, axis=-1, keepdims=True)
    shifted = values - centre
    spread = jnp.mean(shifted * shifted, axis=-1, keepdims=True)
    return shifted * lax.rsqrt(spread + epsilon)


def modulate(values, offset, factor):
    return normalize(values) * (1.0 + factor[:, None, :]) + offset[:, None, :]


def gelu_tanh(values):
    return jax.nn.gelu(values, approximate=True)


def gelu_back(values, gradient):
    return jax.vjp(gelu_tanh, values)[1](gradient)[0]


def contract(left_side, right_side, left_dims, right_dims):
    return lax.dot_general(
        left_side,
        right_side,
        ((left_dims, right_dims), ((), ())),
        preferred_element_type=jnp.float32,
    )


def slot_table(route_block):
    flat_routes = route_block.reshape(-1)
    matches = (flat_routes[:, None] == jnp.arange(EXPERTS, dtype=jnp.int32)[None, :]).astype(
        jnp.int32
    )
    earlier = jnp.cumsum(matches, axis=0, dtype=jnp.int32) - matches
    ranking = jnp.sum(earlier * matches, axis=1, dtype=jnp.int32)
    return flat_routes * CAP + ranking


def join_halves(stacked, bit_level, wide_place):
    partner = swapped(stacked, WIDE, bit_level)
    upper = wide_place >> bit_level & 1 == 1
    return jnp.where(
        upper,
        jnp.concatenate([partner, stacked], axis=1),
        jnp.concatenate([stacked, partner], axis=1),
    )


def split_halves(stacked, bit_level, wide_place):
    half_rows = stacked.shape[1] // 2
    upper = wide_place >> bit_level & 1 == 1
    lower_part = stacked[:, :half_rows]
    upper_part = stacked[:, half_rows:]
    kept = jnp.where(upper, upper_part, lower_part)
    given = jnp.where(upper, lower_part, upper_part)
    return kept + swapped(given.astype(jnp.bfloat16), WIDE, bit_level).astype(given.dtype)


def per_device(
    tokens,
    cotangent,
    time_table,
    timesteps,
    routes,
    w_ada,
    w_qkv,
    w_proj,
    w_route,
    w_shared_up,
    w_shared_down,
    e_up,
    e_down,
):
    images = timesteps.shape[0]
    row_count = tokens.shape[0]
    model_width = tokens.shape[1]
    patches = row_count // images
    core_count = lax.axis_size(NARROW)
    wide_count = lax.axis_size(WIDE)
    group_size = wide_count // EXPERTS
    levels = group_size.bit_length() - 1
    slice_rows = CAP // group_size
    heads_here = HEADS // core_count
    head_dim = model_width // HEADS
    head_width = heads_here * head_dim
    scale_factor = head_dim ** (-0.5)
    wide_place = lax.axis_index(WIDE)
    ada_rows = w_ada.shape[0]
    step_onehot = (
        timesteps[:, None] == jnp.arange(time_table.shape[0], dtype=jnp.int32)[None, :]
    ).astype(jnp.bfloat16)
    cond = jnp.dot(step_onehot, time_table, preferred_element_type=jnp.float32)
    cond_act = jax.nn.silu(cond).astype(jnp.bfloat16)
    qkv_full, proj_full, route_full, up_full, down_full = (
        lax.all_gather(w_qkv, WIDE, axis=0, tiled=True),
        lax.all_gather(w_proj, WIDE, axis=0, tiled=True),
        lax.all_gather(w_route, WIDE, axis=0, tiled=True),
        lax.all_gather(w_shared_up, WIDE, axis=0, tiled=True),
        lax.all_gather(w_shared_down, WIDE, axis=0, tiled=True),
    )
    cond_every = lax.all_gather(cond_act, WIDE, axis=0, tiled=True)
    cond_own = lax.dynamic_slice_in_dim(cond_every, wide_place * ada_rows, ada_rows, 1)
    modulation_terms = jnp.dot(
        cond_own, w_ada.reshape(ada_rows, 6 * model_width), preferred_element_type=jnp.float32
    )
    modulation = lax.psum_scatter(modulation_terms, WIDE, scatter_dimension=0, tiled=True)
    modulation = modulation.reshape(images, 6, model_width)
    expert_weights = jnp.stack([e_up, e_down])
    for bit_level in range(levels):
        expert_weights = join_halves(expert_weights, bit_level, wide_place)
    expert_up = expert_weights[0]
    expert_down = expert_weights[1]
    inputs = tokens.astype(jnp.float32).reshape(images, patches, model_width)
    attn_in, pull_first = jax.vjp(modulate, inputs, modulation[:, 0], modulation[:, 1])
    attn_low = attn_in.reshape(row_count, model_width).astype(jnp.bfloat16)
    projected = jnp.dot(
        attn_low, qkv_full.reshape(model_width, 3 * head_width), preferred_element_type=jnp.float32
    )
    projected = projected.reshape(images, patches, 3, heads_here, head_dim).astype(jnp.bfloat16)
    queries = projected[:, :, 0]
    keys = projected[:, :, 1]
    values = projected[:, :, 2]
    scores = (
        jnp.einsum("bqhd,bkhd->bhqk", queries, keys, preferred_element_type=jnp.float32)
        * scale_factor
    )
    highest_score = jnp.max(scores, axis=-1, keepdims=True)
    log_total = highest_score + jnp.log(
        jnp.sum(jnp.exp(scores - highest_score), axis=-1, keepdims=True)
    )
    probs_low = jnp.exp(scores - log_total).astype(jnp.bfloat16)
    mixed = jnp.einsum("bhqk,bkhd->bqhd", probs_low, values, preferred_element_type=jnp.float32)
    mixed_low = mixed.astype(jnp.bfloat16).reshape(row_count, head_width)
    attn_part = contract(mixed_low, proj_full, (1,), (1,))
    attn_out = lax.psum(attn_part.astype(jnp.bfloat16), NARROW).astype(jnp.float32)
    attn_three = attn_out.reshape(images, patches, model_width)
    hidden_state = inputs + modulation[:, 2][:, None, :] * attn_three
    mlp_in, pull_second = jax.vjp(modulate, hidden_state, modulation[:, 3], modulation[:, 4])
    mlp_low = mlp_in.reshape(row_count, model_width).astype(jnp.bfloat16)
    logits = jnp.dot(mlp_low, route_full, preferred_element_type=jnp.float32)
    selector = (routes[:, :, None] == jnp.arange(EXPERTS, dtype=jnp.int32)[None, None, :]).astype(
        jnp.float32
    )
    chosen = jnp.sum(logits[:, None, :] * selector, axis=-1)
    gate_values, pull_gate = jax.vjp(
        lambda picked_logits: jax.nn.softmax(picked_logits, axis=-1), chosen
    )
    slot_index = slot_table(routes)
    outgoing = (
        jnp.zeros((EXPERTS * CAP, model_width), jnp.bfloat16)
        .at[slot_index]
        .set(jnp.repeat(mlp_low, 2, axis=0))
    )
    arrived = lax.all_to_all(
        outgoing.reshape(wide_count, slice_rows, model_width),
        WIDE,
        split_axis=0,
        concat_axis=0,
        tiled=True,
    )
    expert_in = arrived.reshape(wide_count * slice_rows, model_width)
    shared_pre = jnp.dot(mlp_low, up_full, preferred_element_type=jnp.float32)
    shared_act = gelu_tanh(shared_pre).astype(jnp.bfloat16)
    shared_part = contract(shared_act, down_full, (1,), (1,))
    expert_pre = jnp.dot(expert_in, expert_up, preferred_element_type=jnp.float32)
    expert_act = gelu_tanh(expert_pre).astype(jnp.bfloat16)
    expert_part = contract(expert_act, expert_down, (1,), (1,))
    expert_sum, shared_out = (
        lax.psum(expert_part.astype(jnp.bfloat16), NARROW).astype(jnp.float32),
        lax.psum(shared_part.astype(jnp.bfloat16), NARROW).astype(jnp.float32),
    )
    expert_out = expert_sum.astype(jnp.bfloat16)
    returned = lax.all_to_all(
        expert_out.reshape(wide_count, slice_rows, model_width),
        WIDE,
        split_axis=0,
        concat_axis=0,
        tiled=True,
    )
    returned = returned.reshape(EXPERTS * CAP, model_width)
    picked = returned[slot_index].astype(jnp.float32).reshape(row_count, 2, model_width)
    mixture = jnp.sum(gate_values[:, :, None] * picked, axis=1)
    branch = (shared_out + mixture).reshape(images, patches, model_width)
    output = hidden_state + modulation[:, 5][:, None, :] * branch
    grad_out = cotangent.astype(jnp.float32).reshape(images, patches, model_width)
    grad_branch = (modulation[:, 5][:, None, :] * grad_out).reshape(row_count, model_width)
    grad_gate2 = jnp.sum(grad_out * branch, axis=1)
    grad_pick = jnp.sum(grad_branch[:, None, :] * picked, axis=-1)
    grad_rows = (
        (gate_values[:, :, None] * grad_branch[:, None, :])
        .astype(jnp.bfloat16)
        .reshape(row_count * 2, model_width)
    )
    grad_slots = jnp.zeros((EXPERTS * CAP, model_width), jnp.bfloat16).at[slot_index].set(grad_rows)
    grad_expert_out = lax.all_to_all(
        grad_slots.reshape(wide_count, slice_rows, model_width),
        WIDE,
        split_axis=0,
        concat_axis=0,
        tiled=True,
    )
    grad_expert_out = grad_expert_out.reshape(wide_count * slice_rows, model_width)
    grad_shared = grad_branch.astype(jnp.bfloat16)
    shared_down_grad = contract(grad_shared, shared_act, (0,), (0,))
    grad_shared_act = jnp.dot(grad_shared, down_full, preferred_element_type=jnp.float32)
    grad_shared_pre = gelu_back(shared_pre, grad_shared_act).astype(jnp.bfloat16)
    shared_up_grad = contract(mlp_low, grad_shared_pre, (0,), (0,))
    grad_in_shared = contract(grad_shared_pre, up_full, (1,), (1,))
    grad_chosen = pull_gate(grad_pick)[0]
    grad_logits = jnp.sum(grad_chosen[:, :, None] * selector, axis=1).astype(jnp.bfloat16)
    route_grad = contract(mlp_low, grad_logits, (0,), (0,))
    grad_in_route = contract(grad_logits, route_full, (1,), (1,))
    expert_down_grad = contract(grad_expert_out, expert_act, (0,), (0,))
    grad_expert_act = jnp.dot(grad_expert_out, expert_down, preferred_element_type=jnp.float32)
    grad_expert_pre = gelu_back(expert_pre, grad_expert_act).astype(jnp.bfloat16)
    expert_up_grad = contract(expert_in, grad_expert_pre, (0,), (0,))
    grad_in_part = contract(grad_expert_pre, expert_up, (1,), (1,))
    grad_in_rows, grad_in_shared_sum = (
        lax.psum(grad_in_part.astype(jnp.bfloat16), NARROW).astype(jnp.float32),
        lax.psum(grad_in_shared.astype(jnp.bfloat16), NARROW).astype(jnp.float32),
    )
    back_rows = lax.all_to_all(
        grad_in_rows.astype(jnp.bfloat16).reshape(wide_count, slice_rows, model_width),
        WIDE,
        split_axis=0,
        concat_axis=0,
        tiled=True,
    )
    back_rows = back_rows.reshape(EXPERTS * CAP, model_width)
    grad_in_expert = jnp.sum(
        back_rows[slot_index].astype(jnp.float32).reshape(row_count, 2, model_width), axis=1
    )
    grad_mlp_in = grad_in_shared_sum + grad_in_route + grad_in_expert
    grad_hidden_norm, grad_shift2, grad_scale2 = pull_second(
        grad_mlp_in.reshape(images, patches, model_width)
    )
    grad_hidden = grad_out + grad_hidden_norm
    grad_gate1 = jnp.sum(grad_hidden * attn_three, axis=1)
    grad_attn = (
        (modulation[:, 2][:, None, :] * grad_hidden)
        .reshape(row_count, model_width)
        .astype(jnp.bfloat16)
    )
    proj_grad = contract(grad_attn, mixed_low, (0,), (0,))
    grad_mixed = jnp.dot(grad_attn, proj_full, preferred_element_type=jnp.float32).astype(
        jnp.bfloat16
    )
    grad_mixed = grad_mixed.reshape(images, patches, heads_here, head_dim)
    again_scores = (
        jnp.einsum("bqhd,bkhd->bhqk", queries, keys, preferred_element_type=jnp.float32)
        * scale_factor
    )
    probs_full = jnp.exp(again_scores - log_total)
    again_low = probs_full.astype(jnp.bfloat16)
    grad_probs = jnp.einsum(
        "bqhd,bkhd->bhqk", grad_mixed, values, preferred_element_type=jnp.float32
    )
    grad_values = jnp.einsum(
        "bhqk,bqhd->bkhd", again_low, grad_mixed, preferred_element_type=jnp.float32
    )
    weighted_sum = jnp.sum(probs_full * grad_probs, axis=-1, keepdims=True)
    grad_scores = (probs_full * (grad_probs - weighted_sum)).astype(jnp.bfloat16)
    grad_queries = (
        jnp.einsum("bhqk,bkhd->bqhd", grad_scores, keys, preferred_element_type=jnp.float32)
        * scale_factor
    )
    grad_keys = (
        jnp.einsum("bhqk,bqhd->bkhd", grad_scores, queries, preferred_element_type=jnp.float32)
        * scale_factor
    )
    grad_qkv = jnp.stack([grad_queries, grad_keys, grad_values], axis=2).astype(jnp.bfloat16)
    grad_qkv = grad_qkv.reshape(row_count, 3 * head_width)
    qkv_grad = contract(attn_low, grad_qkv, (0,), (0,)).reshape(model_width, 3, head_width)
    grad_attn_part = contract(grad_qkv, qkv_full.reshape(model_width, 3 * head_width), (1,), (1,))
    grad_attn_in = lax.psum(grad_attn_part.astype(jnp.bfloat16), NARROW).astype(jnp.float32)
    grad_input_norm, grad_shift1, grad_scale1 = pull_first(
        grad_attn_in.reshape(images, patches, model_width)
    )
    tokens_grad = (grad_hidden + grad_input_norm).reshape(row_count, model_width)
    grad_modulation = jnp.stack(
        [grad_shift1, grad_scale1, grad_gate1, grad_shift2, grad_scale2, grad_gate2], axis=1
    )
    grad_modulation = grad_modulation.reshape(images, 6 * model_width)
    grad_mod_every = lax.all_gather(grad_modulation, WIDE, axis=0, tiled=True)
    ada_part = jnp.dot(cond_own.astype(jnp.float32).T, grad_mod_every, precision=highest).reshape(
        ada_rows, 6, model_width
    )
    qkv_part, proj_part, route_part, shared_up_part, shared_down_part = (
        lax.psum_scatter(qkv_grad, WIDE, scatter_dimension=0, tiled=True),
        lax.psum_scatter(proj_grad, WIDE, scatter_dimension=0, tiled=True),
        lax.psum_scatter(route_grad, WIDE, scatter_dimension=0, tiled=True),
        lax.psum_scatter(shared_up_grad, WIDE, scatter_dimension=0, tiled=True),
        lax.psum_scatter(shared_down_grad, WIDE, scatter_dimension=0, tiled=True),
    )
    expert_grads = jnp.stack([expert_up_grad, expert_down_grad])
    for bit_level in reversed(range(levels)):
        expert_grads = split_halves(expert_grads, bit_level, wide_place)
    return (
        output.reshape(row_count, model_width).astype(jnp.bfloat16),
        tokens_grad,
        ada_part,
        qkv_part,
        proj_part,
        route_part,
        shared_up_part,
        shared_down_part,
        expert_grads[0],
        expert_grads[1],
    )


MESH = pl.DeviceIdType.MESH
F32 = jnp.float32
BF16 = jnp.bfloat16
Z_SIZE, Y_SIZE, X_SIZE = 4, 2, 2
VMEM_LIMIT = 60 * 1024 * 1024


def place(index):
    return lax.div(index, 4), lax.rem(lax.div(index, 2), 2), lax.rem(index, 2)


def at_place(z, y, x):
    return z * 4 + y * 2 + x


class Sends:
    def __init__(self):
        self.items = []

    def go(self, make, when=None):
        self.items.append((make, when))
        guarded(when, lambda: make().start())

    def drain(self):
        for make, when in self.items:
            guarded(when, lambda make=make: make().wait_send())


def guarded(when, action):
    if when is None:
        action()
        return

    @pl.when(when)
    def _():
        action()


def both(first, second):
    if first is None:
        return second
    if second is None:
        return first
    return jnp.logical_and(first, second)


def remote(src, dst, send_sem, recv_sem, target):
    return pltpu.make_async_remote_copy(
        src_ref=src,
        dst_ref=dst,
        send_sem=send_sem,
        recv_sem=recv_sem,
        device_id=target,
        device_id_type=MESH,
    )


def greet(targets):
    barrier = pltpu.get_barrier_semaphore()
    for target in targets:
        pl.semaphore_signal(barrier, inc=1, device_id=target, device_id_type=MESH)
    pl.semaphore_wait(barrier, len(targets))


class Gather:
    def __init__(self, streams, send_sem, recv_sem, sends):
        self.streams, self.ss, self.rs, self.sends = streams, send_sem, recv_sem, sends
        self.count = [0] * len(streams)
        self.core = lax.axis_index(NARROW)
        self.me = lax.axis_index(WIDE)
        self.z, self.y, self.x = place(self.me)
        self.to_x = at_place(self.z, self.y, 1 - self.x)
        self.to_y = at_place(self.z, 1 - self.y, self.x)
        self.can_up, self.can_down = self.z < Z_SIZE - 1, self.z > 0
        self.up, self.down = self.me + 4, self.me - 4

    def block(self, s, origin):
        shard, full, start, width = self.streams[s][:4]
        rows = shard.shape[0]
        return full.at[pl.ds(pl.multiple_of(origin * rows, 16), rows), pl.ds(start, width)]

    def send(self, s, origin, target, when=None, own=False, over_x=False):
        shard, full, start, width, _, parted = self.streams[s]
        index = self.count[s]
        self.count[s] += 1

        def make():
            dst = self.block(s, origin)
            first = start
            if parted:
                first = pl.multiple_of((1 - self.x if over_x else self.x) * full.shape[1] + start, 128)
            src = shard.at[:, pl.ds(first, width)] if own else dst
            return remote(src, dst, self.ss.at[s, index], self.rs.at[s, origin], (target, self.core))

        self.sends.go(make, when)

    def wait(self, s, origin, when=None):
        def action():
            ref = self.block(s, origin)
            remote(
                ref, ref, self.ss.at[s, 0], self.rs.at[s, origin], (self.to_x, self.core)
            ).wait_recv()

        guarded(when, action)

    def spread(self, s, origin, when=None, own=False, up=True, down=True, over_y=True):
        if up:
            self.send(s, origin, self.up, both(when, self.can_up), own)
        if down:
            self.send(s, origin, self.down, both(when, self.can_down), own)
        if over_y:
            self.send(s, origin, self.to_y, when, own)

    def begin_x(self, s):
        self.send(s, self.me, self.to_x, own=True, over_x=True)

    def begin(self, s):
        self.begin_x(s)
        self.spread(s, self.me, own=True)

    def after_x(self, s):
        self.wait(s, self.to_x)
        self.spread(s, self.to_x)

    def y_pair(self, s):
        if self.streams[s][4] == "xyz":
            for xx in (self.x, 1 - self.x):
                origin = at_place(self.z, 1 - self.y, xx)
                self.wait(s, origin)
                self.spread(s, origin, over_y=False)

    def after_z(self, s, distance):
        order = self.streams[s][4]
        ys = (self.y,) if order == "xzy" else (self.y, 1 - self.y)
        for step, ok in ((-distance, self.z >= distance), (distance, self.z + distance < Z_SIZE)):
            for yy in ys:
                for xx in (self.x, 1 - self.x):
                    origin = at_place(self.z + step, yy, xx)
                    self.wait(s, origin, ok)
                    self.spread(s, origin, ok, up=step < 0, down=step > 0, over_y=order == "xzy")

    def finish(self, s):
        if self.streams[s][4] == "xzy":
            for zz in range(Z_SIZE):
                for xx in range(X_SIZE):
                    self.wait(s, at_place(zz, 1 - self.y, xx))


def vmem(count):
    return [pl.BlockSpec(memory_space=pltpu.VMEM)] * count


def hbm(count):
    return [pl.BlockSpec(memory_space=pl.ANY)] * count


def params(collective_id, vmem_limit=VMEM_LIMIT):
    return pltpu.CompilerParams(
        collective_id=collective_id, has_side_effects=True, vmem_limit_bytes=vmem_limit
    )


def peers_far_first(me):
    z, y, x = place(me)
    found = []
    for dz in range(Z_SIZE):
        for dy in range(Y_SIZE):
            for dx in range(X_SIZE):
                if dz or dy or dx:
                    zz = lax.rem(z + dz, Z_SIZE)
                    found.append(at_place(zz, lax.rem(y + dy, 2), lax.rem(x + dx, 2)))
    return found[::-1]


def lanes_of(ref, vector):
    rows = ref.shape[0] // 6
    return jnp.concatenate(
        [ref[rows * vector + i : rows * vector + i + 1, :] for i in range(rows)], axis=1
    )


def head_masks(rows):
    lane = lax.broadcasted_iota(jnp.int32, (rows, 128), 1)
    first = (lane < 64).astype(F32)
    return first, 1.0 - first


def diagonal(rows):
    down = lax.broadcasted_iota(jnp.int32, (rows, 128), 0)
    return (down == lax.broadcasted_iota(jnp.int32, (rows, 128), 1)).astype(F32)


def choice_masks(routes_ref):
    rows = routes_ref.shape[1]
    lane = lax.broadcasted_iota(jnp.int32, (rows, 128), 1)
    routes = contract(
        routes_ref[...].astype(F32).astype(BF16), diagonal(2).astype(BF16), (0,), (0,)
    )
    named = [(routes[:, k : k + 1] == lane.astype(F32)).astype(F32) for k in range(2)]
    above = lax.broadcasted_iota(jnp.int32, (rows, rows), 0)
    along = lax.broadcasted_iota(jnp.int32, (rows, rows), 1)
    before = jnp.dot(
        (along < above).astype(F32).astype(BF16),
        (named[0] + named[1]).astype(BF16),
        preferred_element_type=F32,
    )
    slot = lax.broadcasted_iota(jnp.int32, (rows, EXPERTS * CAP), 1)
    takes = []
    for k in range(2):
        rank = jnp.sum(before * named[k], axis=1, keepdims=True)
        own = routes[:, k : k + 1] * CAP + rank
        takes.append((slot == own.astype(jnp.int32)).astype(F32).astype(BF16))
    return named, takes


def attend(attn_low, qkv_ref, act_ref, probs_ref, mixed_ref, pump):
    rows, width = attn_low.shape[0], mixed_ref.shape[1]
    for j in range(3):
        act_ref[:, width * j : width * (j + 1)] = jnp.dot(
            attn_low, qkv_ref[:, width * j : width * (j + 1)], preferred_element_type=F32
        ).astype(BF16)
        pump()
    masks = head_masks(rows)
    scale_factor = 64 ** (-0.5)
    for pair in range(width // 128):
        q, k, v = [
            act_ref[:, width * j + 128 * pair : width * j + 128 * (pair + 1)] for j in range(3)
        ]
        mixed = None
        for h in range(2):
            scores = contract(q * masks[h].astype(BF16), k, (1,), (1,)) * scale_factor
            top = jnp.max(scores, axis=-1, keepdims=True)
            weights = jnp.exp(scores - top)
            probs = weights / jnp.sum(weights, axis=-1, keepdims=True)
            probs_ref[2 * pair + h] = probs
            part = jnp.dot(probs.astype(BF16), v, preferred_element_type=F32) * masks[h]
            mixed = part if mixed is None else mixed + part
            pump()
        mixed_ref[:, 128 * pair : 128 * (pair + 1)] = mixed.astype(BF16)


def forward_kernel(
    ts_ref, table_ref, ada_ref, qkv_ref, proj_ref, route_ref, up_ref, down_ref,
    eup_ref, edown_ref, tok_ref, cot_ref, routes_ref,
    mod_ref, cond_ref, qkv_out, proj_out, route_out, act_ref, probs_ref, mixed_ref,
    attn_ref, attn_low_ref, mlp_ref, gshared_ref, gates_ref,
    up_out, down_out, eup_out, edown_out, rows_out, grads_out,
    ts_all, terms, landed, part, theirs, gate_row, rows_send, grads_send,
    ts_ss, ts_rs, mod_ss, mod_rs, ag_ss, ag_rs, own_sem, join_ss, join_rs, swap_sem,
    ss, rs, pass_ss, pass_rs, own_a, pair_ss, pair_rs, ts_own, qkv_own, route_own,
):
    me, core = lax.axis_index(WIDE), lax.axis_index(NARROW)
    count = lax.axis_size(WIDE)
    others = peers_far_first(me)
    peer = (me, 1 - core)
    greet([(other, core) for other in others] + [peer])
    sends = Sends()
    ts_own[...] = jnp.full(ts_own.shape, ts_ref[0], jnp.int32)
    for k, other in enumerate(others):
        sends.go(lambda k=k, other=other: remote(ts_own, ts_all.at[me], ts_ss.at[k], ts_rs.at[me], (other, core)))
    half = down_out.shape[1] // 2
    streams = [
        (qkv_own, qkv_out, 0, qkv_own.shape[1], "xzy", False),
        (proj_ref, proj_out, 0, proj_ref.shape[1], "xzy", False),
        (route_own, route_out, 0, route_own.shape[1], "xzy", False),
        (up_ref, up_out, 0, up_out.shape[1], "xzy", True),
        (down_ref, down_out, 0, half, "xzy", True),
        (down_ref, down_out, half, half, "xyz", True),
    ]
    for j in range(3):
        at = qkv_ref.shape[2] * j
        qkv_own[:, at : at + qkv_ref.shape[2]] = qkv_ref[j]
    route_own[...] = contract(route_ref[...], diagonal(EXPERTS).astype(BF16), (0,), (0,)).astype(BF16)
    ag = Gather(streams, ag_ss, ag_rs, sends)
    for s in range(3):
        ag.begin(s)
    pieces = 8
    joins = []
    for a, (src, dst) in enumerate(((eup_ref, eup_out), (edown_ref, edown_out))):
        size = src.shape[0] // pieces
        for p in range(pieces):
            cut = pl.ds(p * size, size)
            joins.append(
                lambda a=a, p=p, src=src, dst=dst, cut=cut: remote(
                    src.at[cut, :], dst.at[cut, :],
                    join_ss.at[a * pieces + p], join_rs.at[a * pieces + p], (ag.to_x, core),
                )
            )
    waiting = joins[::2] + joins[1::2]

    def join(steps):
        for _ in range(steps):
            if waiting:
                sends.go(waiting.pop(0))

    join(1)
    own = []
    for i, (shard, full) in enumerate(
        ((qkv_own, qkv_out), (proj_ref, proj_out), (route_own, route_out), (up_ref, up_out), (down_ref, down_out))
    ):
        rows, wide = shard.shape[0], full.shape[1]
        side = pl.multiple_of(ag.x * wide, 128) if wide < shard.shape[1] else 0
        own.append(
            pltpu.make_async_copy(
                shard.at[:, pl.ds(side, wide)],
                full.at[pl.ds(pl.multiple_of(me * rows, 16), rows), :], own_sem.at[i]
            )
        )
        own[-1].start()

    tokens = tok_ref[...].astype(F32)
    normal1, _ = normalized(tokens)

    ts_all[me] = ts_own[...]
    for other in others[::-1]:
        remote(ts_own, ts_all.at[other], ts_ss.at[0], ts_rs.at[other], (other, core)).wait_recv()
    steps = jnp.max(ts_all[...], axis=1)[:, :1]
    onehot = (
        steps == lax.broadcasted_iota(jnp.int32, (count, table_ref.shape[0]), 1)
    ).astype(F32).astype(BF16)
    cond = jnp.dot(onehot, table_ref[...], preferred_element_type=F32)
    cond_act = (cond * jax.nn.sigmoid(cond)).astype(BF16)
    cond_ref[...] = cond_act.astype(F32)
    chunks = terms.shape[1] // 6
    for j in range(6):
        vector = jnp.dot(cond_act, ada_ref[j], preferred_element_type=F32)
        for i in range(chunks):
            terms[:, chunks * j + i, :] = vector[:, 128 * i : 128 * (i + 1)]
    for k, other in enumerate(others):
        sends.go(lambda k=k, other=other: remote(terms.at[other], landed.at[me], mod_ss.at[k], mod_rs.at[me], (other, core)))
    join(2)
    for s in range(3):
        ag.after_x(s)
    for s in range(3, len(streams)):
        ag.begin_x(s)
    join(2)

    for distance in range(1, Z_SIZE):
        for s in range(3):
            ag.after_z(s, distance)
        join(2)
    for s in range(3, len(streams)):
        ag.spread(s, ag.me, own=True)
    landed[me] = terms[me]
    for other in others[::-1]:
        remote(terms.at[me], landed.at[other], mod_ss.at[0], mod_rs.at[other], (other, core)).wait_recv()
    mod_ref[...] = jnp.sum(landed[...], axis=0)
    shift1, scale1, gate1, shift2, scale2, gate2 = [lanes_of(mod_ref, j) for j in range(6)]
    attn_low_ref[...] = (normal1 * (1.0 + scale1) + shift1).astype(BF16)
    patches = tok_ref.shape[0]
    first, second = pl.ds(0, patches), pl.ds(patches, patches)
    gate_row[...] = jnp.broadcast_to(gate2, gate_row.shape)
    gshared_ref[first, :] = (gate2 * cot_ref[...].astype(F32)).astype(BF16)
    width = rows_send.shape[1]
    mine = pl.ds(pl.multiple_of(core * width, 128), width)
    theirs_half = pl.ds(pl.multiple_of((1 - core) * width, 128), width)
    across = [
        remote(ref.at[first, mine], ref.at[second, mine], pair_ss.at[i], pair_rs.at[i], (ag.to_x, core))
        for i, ref in enumerate((gshared_ref, mlp_ref))
    ]
    handed = [
        remote(ref.at[second, mine], ref.at[second, mine], pair_ss.at[2 + i], pair_rs.at[2 + i], peer)
        for i, ref in enumerate((gshared_ref, mlp_ref))
    ]
    came = [
        remote(ref.at[second, theirs_half], ref.at[second, theirs_half], pair_ss.at[2 + i], pair_rs.at[2 + i], peer)
        for i, ref in enumerate((gshared_ref, mlp_ref))
    ]
    across[0].start()
    bulk = range(3, len(streams))
    queue = [lambda s=s: ag.after_x(s) for s in bulk]
    queue += [lambda s=s: ag.y_pair(s) for s in bulk]
    queue += [lambda s=s, d=d: ag.after_z(s, d) for d in range(1, Z_SIZE) for s in bulk]

    def pump():
        join(1)
        if queue:
            queue.pop(0)()

    ag.finish(0)
    own[0].wait()
    attend(attn_low_ref[...], qkv_out, act_ref, probs_ref, mixed_ref, pump)
    ag.finish(1)
    own[1].wait()
    part[...] = contract(mixed_ref[...], proj_out[...], (1,), (1,)).astype(BF16)
    swap = remote(part, theirs, swap_sem.at[0], swap_sem.at[1], peer)
    swap.start()
    named, takes = choice_masks(routes_ref)
    pump()
    swap.wait()
    attn_out = part[...].astype(F32) + theirs[...].astype(F32)
    attn_ref[...] = attn_out
    hidden = tok_ref[...].astype(F32) + gate1 * attn_out
    normal2, _ = normalized(hidden)
    mlp_ref[first, :] = (normal2 * (1.0 + scale2) + shift2).astype(BF16)
    ag.finish(2)
    own[2].wait()
    logits = jnp.dot(mlp_ref[first, :], route_out[...], preferred_element_type=F32)
    chosen = [jnp.sum(logits * named[k], axis=1, keepdims=True) for k in range(2)]
    peak = jnp.maximum(chosen[0], chosen[1])
    weight = [jnp.exp(chosen[k] - peak) for k in range(2)]
    total = weight[0] + weight[1]
    gates = [weight[k] / total for k in range(2)]
    lane = lax.broadcasted_iota(jnp.int32, gates_ref.shape, 1)
    gates_ref[...] = jnp.where(lane == 0, gates[0], jnp.where(lane == 1, gates[1], 0.0))
    grad_half = gate_row[0:1, mine] * cot_ref[:, mine].astype(F32)
    rows_send[...] = contract(takes[0] + takes[1], mlp_ref[first, mine], (0,), (0,)).astype(BF16)
    grads_send[...] = (
        contract(takes[0], (gates[0] * grad_half).astype(BF16), (0,), (0,))
        + contract(takes[1], (gates[1] * grad_half).astype(BF16), (0,), (0,))
    ).astype(BF16)

    size = rows_send.shape[0] // count

    def rows(index):
        return pl.ds(pl.multiple_of(index * size, 16), size)

    pairs = ((rows_send, rows_out), (grads_send, grads_out))
    for k, other in enumerate(others):
        for a, (src, dst) in enumerate(pairs):
            sends.go(
                lambda k=k, other=other, a=a, src=src, dst=dst: remote(
                    src.at[rows(other), :], dst.at[core, rows(me), :],
                    ss.at[a, k], rs.at[a, me], (other, core),
                )
            )
    across[1].start()
    across[0].wait()
    handed[0].start()
    join(len(joins))
    kept = []
    for a, (src, dst) in enumerate(pairs):
        sends.go(
            lambda a=a, src=src, dst=dst: remote(
                src.at[rows(me), :], dst.at[core, rows(me), :], pass_ss.at[a, 15], pass_rs.at[a, me], peer
            )
        )
        kept.append(pltpu.make_async_copy(src.at[rows(me), :], dst.at[core, rows(me), :], own_a.at[a]))
        kept[-1].start()
    while queue:
        pump()
    across[1].wait()
    handed[1].start()
    for k, other in enumerate(others[::-1]):
        for a, (src, dst) in enumerate(pairs):
            here = dst.at[core, rows(other), :]
            remote(here, here, ss.at[a, 0], rs.at[a, other], peer).wait_recv()
            sends.go(
                lambda k=k, other=other, a=a, here=here: remote(
                    here, here, pass_ss.at[a, k], pass_rs.at[a, other], peer
                )
            )
    for s in range(3, len(streams)):
        ag.finish(s)
    for i, make in enumerate(joins):
        make().wait_recv()
    for other in [me] + others[::-1]:
        for a, (src, dst) in enumerate(pairs):
            there = dst.at[1 - core, rows(other), :]
            remote(there, there, pass_ss.at[a, 0], pass_rs.at[a, other], peer).wait_recv()
    for i in range(2):
        handed[i].wait_send()
        came[i].wait_recv()
    for copy in own[3:] + kept:
        copy.wait()
    sends.drain()


def forward(ts_tile, table, ada, qkv, proj, route, up, down, e_up, e_down, tokens, cotangent, routes):
    count = 16
    shards = (qkv, proj, route, up, down)
    vectors = 6 * ada.shape[2] // 128
    patches, width = tokens.shape
    slots = EXPERTS * CAP
    dma = pltpu.SemaphoreType.DMA
    shape = jax.ShapeDtypeStruct

    def full(a):
        return shape((count * a.shape[0], a.shape[1]), a.dtype)

    def parted(a):
        return shape((count * a.shape[0], a.shape[1] // X_SIZE), a.dtype)

    return pl.pallas_call(
        forward_kernel,
        out_shape=[
            shape((vectors, 128), F32), shape((count, table.shape[1]), F32),
            shape((count * qkv.shape[1], 3 * qkv.shape[2]), BF16), full(proj), shape((count * qkv.shape[1], 128), BF16),
            shape((patches, 3 * qkv.shape[2]), BF16), shape((proj.shape[1] // 64, patches, patches), F32),
            shape((patches, proj.shape[1]), BF16), shape((patches, width), F32),
            shape((patches, width), BF16), shape((2 * patches, width), BF16),
            shape((2 * patches, width), BF16), shape((patches, 128), F32),
            parted(up), parted(down), shape(e_up.shape, BF16), shape(e_down.shape, BF16),
            shape((2, slots, width // 2), BF16), shape((2, slots, width // 2), BF16),
        ],
        in_specs=[pl.BlockSpec(memory_space=pltpu.SMEM)] + vmem(7) + hbm(2) + vmem(3),
        out_specs=vmem(13) + hbm(6),
        scratch_shapes=[
            pltpu.VMEM((count, 8, 128), jnp.int32),
            pltpu.VMEM((count, vectors, 128), F32),
            pltpu.VMEM((count, vectors, 128), F32),
            pltpu.VMEM((patches, width), BF16), pltpu.VMEM((patches, width), BF16),
            pltpu.VMEM((8, width), F32),
            pltpu.VMEM((slots, width // 2), BF16), pltpu.VMEM((slots, width // 2), BF16),
            dma((16,)), dma((16,)), dma((16,)), dma((16,)),
            dma((6, 40)), dma((6, 16)), dma((5,)), dma((16,)), dma((16,)), dma((2,)),
            dma((2, 16)), dma((2, 16)), dma((2, 16)), dma((2, 16)), dma((2,)), dma((4,)), dma((4,)),
            pltpu.VMEM((8, 128), jnp.int32),
            pltpu.VMEM((qkv.shape[1], 3 * qkv.shape[2]), BF16), pltpu.VMEM((qkv.shape[1], 128), BF16),
        ],
        compiler_params=params(1),
        name="forward",
    )(ts_tile, table, ada, *shards, e_up, e_down, tokens, cotangent, routes)


def normalized(values):
    centre = jnp.mean(values, axis=-1, keepdims=True)
    shifted = values - centre
    spread = jnp.mean(shifted * shifted, axis=-1, keepdims=True)
    rate = lax.rsqrt(spread + epsilon)
    return shifted * rate, rate


def norm_back(normal, rate, gradient):
    mean = jnp.mean(gradient, axis=-1, keepdims=True)
    along = jnp.mean(gradient * normal, axis=-1, keepdims=True)
    return rate * (gradient - mean - normal * along)


class Sums:
    def __init__(self, specs, r, sends):
        self.specs, self.r, self.sends = specs, r, sends
        self.me, self.core = lax.axis_index(WIDE), lax.axis_index(NARROW)
        self.z, self.y, self.x = place(self.me)
        z = self.z
        upper = z >= 2
        self.dest = [
            jnp.where(upper, 0, 3), jnp.where(upper, 1, 2), jnp.where(upper, 5 - z, 1 - z), z
        ]
        self.near = {
            "y": at_place(z, 1 - self.y, self.x), "x": at_place(z, self.y, 1 - self.x)
        }

    def part(self, ref, axis, zz, other):
        if axis == "y":
            return ref.at[zz, 1 - self.y if other else self.y]
        return ref.at[zz, :, 1 - self.x if other else self.x]

    def slot(self, zz, way, at):
        return jnp.where(jnp.logical_and(zz == at, way == 1), 4, zz)

    def landed(self, ref, sem):
        remote(ref, ref, self.r.first_ss.at[0, 0], sem, (self.near["x"], self.core)).wait_recv()

    def load(self, i, k):
        terms, axis, work = self.specs[i][:3]
        zz = self.dest[k]
        return pltpu.make_async_copy(
            self.part(terms, axis, zz, False), work.at[zz], self.r.load_sem.at[i, k]
        )

    def start(self, i, k):
        terms, axis, _, came = self.specs[i][:4]
        zz = self.dest[k]
        self.load(i, k).start()
        self.sends.go(
            lambda: remote(
                self.part(terms, axis, zz, True), came.at[zz],
                self.r.first_ss.at[i, k], self.r.first_rs.at[i, zz], (self.near[axis], self.core),
            )
        )

    def step(self, i, k):
        _, axis, work, came, along, last = self.specs[i][:6]
        z, zz, core = self.z, self.dest[k], self.core
        self.load(i, k).wait()
        self.landed(came.at[zz], self.r.first_rs.at[i, zz])
        if k < 3:
            rising = zz > z
            way = jnp.where(rising, 0, 1)
            more = jnp.where(rising, z > 0, z < 3)

            @pl.when(more)
            def _():
                self.landed(along.at[zz], self.r.z_rs.at[i, zz])
                add_blocks(work.at[zz], came.at[zz], along.at[zz])

            @pl.when(jnp.logical_not(more))
            def _():
                add_blocks(work.at[zz], came.at[zz])

            target = jnp.where(rising, self.me + 4, self.me - 4)
            slot = self.slot(zz, way, jnp.where(rising, z + 1, z - 1))
            self.sends.go(
                lambda: remote(
                    work.at[zz], along.at[slot],
                    self.r.z_ss.at[i, k], self.r.z_rs.at[i, slot], (target, core),
                )
            )
            return
        add_blocks(work.at[z], came.at[z])
        for way, there in ((0, z > 0), (1, z < 3)):

            @pl.when(there)
            def _(way=way):
                slot = self.slot(z, way, z)
                self.landed(along.at[slot], self.r.z_rs.at[i, slot])
                add_blocks(work.at[z], along.at[slot])

        side, final = (self.x, "x") if axis == "y" else (self.y, "y")
        self.sends.go(
            lambda: remote(
                work.at[z, 1 - side], last,
                self.r.last_ss.at[i], self.r.last_rs.at[i], (self.near[final], core),
            )
        )

    def finish(self, i):
        _, axis, work, _, _, last, store = self.specs[i]
        self.landed(last, self.r.last_rs.at[i])
        side = self.x if axis == "y" else self.y
        store(work[self.z, side].astype(F32), last[...].astype(F32))


def add_blocks(total, *terms):
    size = total.shape[1]
    per = size // 16

    def body(n, _):
        block, at = lax.div(n, per), pl.ds(pl.multiple_of(lax.rem(n, per) * 16, 16), 16)
        value = total[block, at, :].astype(F32)
        for term in terms:
            value = value + term[block, at, :].astype(F32)
        total[block, at, :] = value.astype(BF16)
        return 0

    lax.fori_loop(0, 2 * per, body, 0)


def gelu_pair(value, gradient):
    root = 0.7978845608028654
    square = value * value
    bend = jnp.tanh(root * (value + 0.044715 * value * square))
    half = 0.5 * (1.0 + bend)
    slope = half + 0.5 * value * (1.0 - bend * bend) * (root * (1.0 + 0.134145 * square))
    return (value * half).astype(BF16), (slope * gradient).astype(BF16)


def columns_of(total, tile, body):
    def turn(n, _):
        body(pl.ds(pl.multiple_of(n * tile, 128), tile))
        return 0

    lax.fori_loop(0, total // tile, turn, 0)


def backward_kernel(names, fetched, *refs):
    r = types.SimpleNamespace(**dict(zip(names, refs, strict=True)))
    me, core = lax.axis_index(WIDE), lax.axis_index(NARROW)
    count = lax.axis_size(WIDE)
    z, y, x = place(me)
    others = peers_far_first(me)
    peer = (me, 1 - core)
    across = (at_place(z, y, 1 - x), core)
    fetches = {}
    for n, name in enumerate(fetched):
        fetches[name] = pltpu.make_async_copy(getattr(r, name), getattr(r, name + "_v"), r.fetch_sem.at[n])
        fetches[name].start()
    greet([(other, core) for other in others] + [peer])
    sends = Sends()
    slots, width = r.their0.shape
    size = slots // count
    patches = r.tok.shape[0]
    mine = pl.ds(pl.multiple_of(core * width, 128), width)
    theirs_half = pl.ds(pl.multiple_of((1 - core) * width, 128), width)

    def rows(index):
        return pl.ds(pl.multiple_of(index * size, 16), size)

    def arrived(ref, sem):
        remote(ref, ref, r.near_ss.at[0, 0], sem, peer).wait_recv()

    for name in fetched[:6]:
        fetches[name].wait()
    hidden_units = r.eup_v.shape[1]
    for n in range(2):
        r.ein_t[n] = r.ein_v[n].T
        r.eg_t[n] = r.eg_v[n].T

    def expert_hidden(at):
        def through(rows_ref, own, other):
            return jnp.dot(rows_ref[x], own[:, at], preferred_element_type=F32) + jnp.dot(
                rows_ref[1 - x], other[:, at], preferred_element_type=F32
            )

        r.eact[:, at], r.epre[:, at] = gelu_pair(
            through(r.ein_v, r.eup_v, r.upo_v), through(r.eg_v, r.edn_v, r.dno_v)
        )

    columns_of(hidden_units, 256, expert_hidden)

    for target, left, own, other in (
        (r.ein_v, r.eact, r.edn_v, r.dno_v), (r.eg_v, r.epre, r.eup_v, r.upo_v),
    ):
        target[x] = contract(left[...], own[...], (1,), (1,)).astype(BF16)
        target[1 - x] = contract(left[...], other[...], (1,), (1,)).astype(BF16)

    triples = ((r.ein_v, r.their0, r.back0), (r.eg_v, r.their1, r.back1))
    order = others + [me]
    for k, other in enumerate(order):
        for a, (src, theirs, _) in enumerate(triples):
            sends.go(
                lambda k=k, other=other, a=a, src=src, theirs=theirs: remote(
                    src.at[1 - core, rows(other), :], theirs.at[rows(other), :],
                    r.near_ss.at[a, k], r.near_rs.at[a, other], peer,
                )
            )
    def given_terms(at):
        r.eup_v[:, at] = jnp.dot(r.ein_t[1 - x], r.epre[:, at], preferred_element_type=F32).astype(BF16)
        r.upo_v[:, at] = jnp.dot(r.eg_t[1 - x], r.eact[:, at], preferred_element_type=F32).astype(BF16)

    columns_of(hidden_units, 256, given_terms)
    pieces = 2
    cut = r.eup_v.shape[0] // pieces
    trades = []
    for a, (give, take) in enumerate(((r.eup_v, r.take0), (r.upo_v, r.take1))):
        for p in range(pieces):
            piece = pl.ds(p * cut, cut)
            trades.append(
                lambda a=a, p=p, give=give, take=take, piece=piece: remote(
                    give.at[piece, :], take.at[piece, :],
                    r.trade_ss.at[a * pieces + p], r.trade_rs.at[a * pieces + p], across,
                )
            )
    for k, other in enumerate(order):
        for a, (src, theirs, back) in enumerate(triples):
            arrived(theirs.at[rows(other), :], r.near_rs.at[a, other])
            both_cores = (
                src[core, rows(other), :].astype(F32) + theirs[rows(other), :].astype(F32)
            ).astype(BF16)
            if k < len(others):
                src[core, rows(other), :] = both_cores
                sends.go(
                    lambda k=k, other=other, a=a, src=src, back=back: remote(
                        src.at[core, rows(other), :], back.at[rows(me), :],
                        r.ss.at[a, k], r.rs.at[a, me], (other, core),
                    )
                )
            else:
                back[rows(me), :] = both_cores

    for name in fetched[6:10]:
        fetches[name].wait()
    r.mlp_t[...] = r.mlp_v[...].T
    r.gsh_t[...] = r.gsh_v[...].T

    def shared_hidden(at):
        r.sact[:, at], r.spre[:, at] = gelu_pair(
            jnp.dot(r.mlp_v[...], r.up_v[:, at], preferred_element_type=F32),
            jnp.dot(r.gsh_v[...], r.down_v[:, at], preferred_element_type=F32),
        )

    columns_of(r.up_v.shape[1], 256, shared_hidden)
    blocks = (2, 2, 2, size)

    def shared_terms(at):
        for target, left, right in ((r.up_t, r.mlp_t, r.spre), (r.down_t, r.gsh_t, r.sact)):
            for h in range(2):
                value = jnp.dot(
                    left[384 * h : 384 * (h + 1), :], right[:, at], preferred_element_type=F32
                )
                target[2 * h : 2 * h + 2, :, :, :, at] = value.astype(BF16).reshape(
                    *blocks, value.shape[1]
                )

    columns_of(r.up_v.shape[1], 256, shared_terms)

    def shared_out(at):
        r.part0[:, at] = contract(r.sact[...], r.down_v[at, :], (1,), (1,)).astype(BF16)
        r.gsh_v[:, at] = contract(r.spre[...], r.up_v[at, :], (1,), (1,)).astype(BF16)

    columns_of(r.part0.shape[1], 256, shared_out)

    def store_to(ref):
        def store(own, came):
            ref[...] = own + came

        return store

    def store_route(own, came):
        r.route_o[...] = lax.dot_general(
            diagonal(EXPERTS), own + came, (((1,), (1,)), ((), ())),
            precision=highest, preferred_element_type=F32,
        )

    def store_sides(ref):
        def store(own, came):
            half = own.shape[1]
            ref[:, pl.ds(pl.multiple_of(x * half, 128), half)] = own
            ref[:, pl.ds(pl.multiple_of((1 - x) * half, 128), half)] = came

        return store

    def store_qkv(own, came):
        for j in range(3):
            at = slice(width * j, width * (j + 1))
            r.qkv_o[j] = own[:, at] + came[:, at]

    specs = [
        (r.up_t, "y", r.up_w, r.up_c, r.up_a, r.up_l, store_sides(r.up_o)),
        (r.down_t, "y", r.down_w, r.down_c, r.down_a, r.down_l, store_sides(r.down_o)),
        (r.proj_t, "y", r.proj_w, r.proj_c, r.proj_a, r.proj_l, store_to(r.proj_o)),
        (r.route_t, "y", r.route_w, r.route_c, r.route_a, r.route_l, store_route),
        (r.qkv_t, "y", r.qkv_w, r.qkv_c, r.qkv_a, r.qkv_l, store_qkv),
    ]
    sums = Sums(specs, r, sends)
    small = ((r.part0, r.their2, r.branch, r.pass0, r.came0), (r.gsh_v, r.their3, r.gmlp, r.pass1, r.came1))
    for a, (part, theirs, _, _, _) in enumerate(small):
        sends.go(
            lambda a=a, part=part, theirs=theirs: remote(
                part.at[:, theirs_half], theirs, r.near_ss.at[a, 16], r.near_rs.at[a, 16], peer
            )
        )
    for k in range(4):
        for i in range(2):
            sums.start(i, k)
    for a, (part, theirs, total, passed, came) in enumerate(small):
        arrived(theirs, r.near_rs.at[a, 16])
        total[:, mine] = part[:patches, mine].astype(F32) + theirs[:patches, :].astype(F32)
        passed[...] = (part[patches:, mine].astype(F32) + theirs[patches:, :].astype(F32)).astype(BF16)
        sends.go(
            lambda a=a, passed=passed, came=came: remote(
                passed, came, r.pass_ss.at[a], r.pass_rs.at[a], across
            )
        )
    for trade in trades:
        sends.go(trade)
    queue = [lambda i=i, k=k: sums.step(i, k) for k in range(4) for i in range(2)]

    def pump(steps=1):
        for _ in range(steps):
            if queue:
                queue.pop(0)()

    shift1, scale1, gate1, shift2, scale2, gate2 = [lanes_of(r.mod, j) for j in range(6)]
    named, takes = choice_masks(r.routes)
    gates = [r.gates[:, k : k + 1] for k in range(2)]
    pump(2)
    for other in others[::-1]:
        for a, (_, _, back) in enumerate(triples):
            arrived(back.at[rows(other), :], r.rs.at[a, other])
    for a in range(2):
        arrived(small[a][4], r.pass_rs.at[a])
    picked = [jnp.dot(takes[k], r.back0[...], preferred_element_type=F32) for k in range(2)]
    r.branch[:, mine] = (
        r.branch[:, mine] + r.came0[...].astype(F32)
        + gates[0] * picked[0] + gates[1] * picked[1]
    )
    r.gmlp[:, mine] = (
        r.gmlp[:, mine] + r.came1[...].astype(F32)
        + jnp.dot(takes[0] + takes[1], r.back1[...], preferred_element_type=F32)
    )
    for k in range(6):
        r.gate_row[k : k + 1, :] = lanes_of(r.mod, k)
    grad_half = r.gate_row[5:6, mine] * r.cot[:, mine].astype(F32)
    terms = [jnp.sum(grad_half * picked[k], axis=-1, keepdims=True) for k in range(2)]
    lane = lax.broadcasted_iota(jnp.int32, r.gsum.shape, 1)
    r.gsum[...] = jnp.where(lane == 0, terms[0], jnp.where(lane == 1, terms[1], 0.0))
    swaps = [
        remote(r.branch.at[:, mine], r.branch.at[:, mine], r.swap_ss.at[0], r.swap_rs.at[0], peer),
        remote(r.gmlp.at[:, mine], r.gmlp.at[:, mine], r.swap_ss.at[1], r.swap_rs.at[1], peer),
        remote(r.gsum, r.gsum_c, r.swap_ss.at[2], r.swap_rs.at[2], peer),
    ]
    for swap in swaps:
        swap.start()
    for name in fetched[10:]:
        fetches[name].wait()
    hidden = r.tok[...].astype(F32) + gate1 * r.attn_v[...]
    normal2, rate2 = normalized(hidden)
    r.normal[...] = normal2
    grad_out = r.cot[...].astype(F32)
    arrived(r.branch.at[:, theirs_half], r.swap_rs.at[0])
    arrived(r.gmlp.at[:, theirs_half], r.swap_rs.at[1])
    arrived(r.gsum_c, r.swap_rs.at[2])
    for swap in swaps:
        swap.wait_send()

    def put(vector, value):
        for i in range(value.shape[1] // 128):
            at = value.shape[1] // 128 * vector + i
            r.vec[at : at + 1, :] = value[:, 128 * i : 128 * (i + 1)]

    branch = r.branch[...]
    r.out_o[...] = (hidden + gate2 * branch).astype(BF16)
    put(5, jnp.sum(grad_out * branch, axis=0, keepdims=True))
    grad_gates = [r.gsum[:, k : k + 1] + r.gsum_c[:, k : k + 1] for k in range(2)]
    inner = gates[0] * grad_gates[0] + gates[1] * grad_gates[1]
    grad_chosen = [gates[k] * (grad_gates[k] - inner) for k in range(2)]
    grad_logits = (grad_chosen[0] * named[0] + grad_chosen[1] * named[1]).astype(BF16)
    grad_mlp = r.gmlp[...] + contract(grad_logits, r.routew_v[...], (1,), (1,))
    normal2 = r.normal[...]
    put(3, jnp.sum(grad_mlp, axis=0, keepdims=True))
    put(4, jnp.sum(grad_mlp * normal2, axis=0, keepdims=True))
    r.ghid[...] = grad_out + norm_back(normal2, rate2, grad_mlp * (1.0 + scale2))
    grad_hidden = r.ghid[...]
    put(2, jnp.sum(grad_hidden * r.attn_v[...], axis=0, keepdims=True))
    r.gattn[...] = (gate1 * grad_hidden).astype(BF16)

    def weight_terms(target, left, right):
        columns = right.shape[1]
        cut = 384
        for n in range(columns // cut if columns > cut else 1):
            lo, hi = cut * n, min(columns, cut * (n + 1))
            for h in range(2):
                value = contract(left[:, 384 * h : 384 * (h + 1)], right[:, lo:hi], (0,), (0,))
                target[2 * h : 2 * h + 2, :, :, :, lo:hi] = value.astype(BF16).reshape(
                    *blocks, hi - lo
                )

    weight_terms(r.proj_t, r.gattn, r.mixed_v)
    weight_terms(r.route_t, r.mlp_v[:patches, :], grad_logits)
    pump(1)
    r.gmix[...] = jnp.dot(r.gattn[...], r.projw_v[...], preferred_element_type=F32).astype(BF16)
    for k in range(4):
        for i in (2, 3):
            sums.start(i, k)
    masks = head_masks(r.gmix.shape[0])
    scale_factor = 64 ** (-0.5)
    for pair in range(width // 128):
        at = [slice(width * j + 128 * pair, width * j + 128 * (pair + 1)) for j in range(3)]
        q, k, v = [r.act_v[:, at[j]] for j in range(3)]
        gm = r.gmix[:, at[0]]
        found = [None] * 3
        for h in range(2):
            probs = r.probs_v[2 * pair + h]
            grad_probs = contract(gm * masks[h].astype(BF16), v, (1,), (1,))
            weighted = jnp.sum(probs * grad_probs, axis=-1, keepdims=True)
            grad_scores = (probs * (grad_probs - weighted)).astype(BF16)
            parts = (
                jnp.dot(grad_scores, k, preferred_element_type=F32) * scale_factor,
                contract(grad_scores, q, (0,), (0,)) * scale_factor,
                contract(probs.astype(BF16), gm, (0,), (0,)),
            )
            found = [
                part * masks[h] if old is None else old + part * masks[h]
                for part, old in zip(parts, found, strict=True)
            ]
            pump(1)
        for j in range(3):
            r.gqkv[:, at[j]] = found[j].astype(BF16)
    r.gpart[...] = contract(r.gqkv[...], r.qkvw_v[...], (1,), (1,)).astype(BF16)
    swap = remote(r.gpart, r.gpart_c, r.swap_ss.at[3], r.swap_rs.at[3], peer)
    swap.start()
    weight_terms(r.qkv_t, r.attnlow_v, r.gqkv)
    for k in range(4):
        sums.start(4, k)
    tokens = r.tok[...].astype(F32)
    normal1, rate1 = normalized(tokens)
    swap.wait()
    grad_in = r.gpart[...].astype(F32) + r.gpart_c[...].astype(F32)
    put(0, jnp.sum(grad_in, axis=0, keepdims=True))
    put(1, jnp.sum(grad_in * normal1, axis=0, keepdims=True))
    for k, other in enumerate(others):
        sends.go(
            lambda k=k, other=other: remote(
                r.vec, r.every.at[me], r.vec_ss.at[k], r.vec_rs.at[me], (other, core)
            )
        )
    r.tokens_o[...] = r.ghid[...] + norm_back(normal1, rate1, grad_in * (1.0 + scale1))
    while queue:
        pump()
    for k in range(4):
        for i in (2, 3, 4):
            sums.step(i, k)
    for a, (left, right, take, result) in enumerate((
        (r.ein_t, r.epre, r.take0, r.eup_o), (r.eg_t, r.eact, r.take1, r.edown_o),
    )):
        for p in range(pieces):
            arrived(take.at[pl.ds(p * cut, cut), :], r.trade_rs.at[a * pieces + p])

        def outward(n, slot, result=result):
            at = pl.ds(pl.multiple_of(n * 512 + slot * 256, 128), 256)
            return at, pltpu.make_async_copy(r.stage.at[slot], result.at[:, at], r.keep_sem.at[slot])

        def turn(n, _, left=left, right=right, take=take, outward=outward):
            for slot in range(2):
                at, copy = outward(n, slot)
                guarded(n > 0, lambda: outward(n - 1, slot)[1].wait())
                r.stage[slot] = jnp.dot(
                    left[x], right[:, at], preferred_element_type=F32
                ) + take[:, at].astype(F32)
                copy.start()
            return 0

        turns = hidden_units // 512
        lax.fori_loop(0, turns, turn, 0)
        for slot in range(2):
            outward(turns - 1, slot)[1].wait()
    for i in range(2):
        sums.finish(i)
    r.every[me] = r.vec[...]
    for other in others[::-1]:
        arrived(r.every.at[other], r.vec_rs.at[other])
    cond = r.cond[...]
    chunks = r.vec.shape[0] // 6
    for j in range(6):
        for i in range(chunks):
            r.ada_o[j, :, 128 * i : 128 * (i + 1)] = lax.dot_general(
                cond, r.every[:, chunks * j + i, :], (((0,), (0,)), ((), ())),
                precision=highest, preferred_element_type=F32,
            )
    for i in (2, 3, 4):
        sums.finish(i)
    sends.drain()


def backward(given, near):
    count = 16
    dma = pltpu.SemaphoreType.DMA
    shape = jax.ShapeDtypeStruct
    operands = given | near
    a = types.SimpleNamespace(**operands)
    patches, width = a.tok.shape
    slots, half = a.ein.shape[1:]
    head_width = a.mixed.shape[1]
    hidden = a.eup.shape[1]
    quarter = a.up.shape[1]
    size = slots // count
    vectors = a.mod.shape[0]
    columns = dict(up=quarter, down=quarter, proj=head_width, route=128, qkv=3 * head_width)
    results = dict(
        out_o=shape((patches, width), BF16),
        tokens_o=shape((patches, width), F32),
        ada_o=shape((6, size, width), F32),
        qkv_o=shape((3, size, head_width), F32),
        proj_o=shape((size, head_width), F32),
        route_o=shape((EXPERTS, size), F32),
        up_o=shape((size, 2 * quarter), F32),
        down_o=shape((size, 2 * quarter), F32),
        eup_o=shape((half, hidden), F32),
        edown_o=shape((half, hidden), F32),
    )
    v = pltpu.VMEM
    scratch = {name + "_v": v(array.shape, array.dtype) for name, array in given.items()}
    for name, wide in columns.items():
        scratch[name + "_w"] = v((4, 2, size, wide), BF16)
        scratch[name + "_c"] = v((4, 2, size, wide), BF16)
        scratch[name + "_a"] = v((5, 2, size, wide), BF16)
        scratch[name + "_l"] = v((size, wide), BF16)
        scratch[name + "_t"] = v((4, 2, 2, size, wide), BF16)

    def low(*sizes):
        return v(sizes, BF16)

    def full(*sizes):
        return v(sizes, F32)

    scratch |= dict(
        ein_t=low(2, half, slots), eg_t=low(2, half, slots),
        eact=low(slots, hidden), epre=low(slots, hidden),
        take0=low(half, hidden), take1=low(half, hidden),
        stage=full(2, half, 256),
        their0=low(slots, half), their1=low(slots, half), back0=low(slots, half), back1=low(slots, half),
        mlp_t=low(width, 2 * patches), gsh_t=low(width, 2 * patches),
        sact=low(2 * patches, quarter), spre=low(2 * patches, quarter),
        part0=low(2 * patches, width),
        their2=low(2 * patches, half), their3=low(2 * patches, half),
        pass0=low(patches, half), pass1=low(patches, half), came0=low(patches, half), came1=low(patches, half),
        branch=full(patches, width), gmlp=full(patches, width),
        normal=full(patches, width), ghid=full(patches, width),
        gattn=low(patches, width), gpart=low(patches, width), gpart_c=low(patches, width),
        gmix=low(patches, head_width), gqkv=low(patches, 3 * head_width),
        gsum=full(patches, 128), gsum_c=full(patches, 128), gate_row=full(8, width),
        vec=full(vectors, 128), every=full(count, vectors, 128),
        near_ss=dma((2, 17)), near_rs=dma((2, 17)), ss=dma((2, 16)), rs=dma((2, 16)),
        fetch_sem=dma((len(given),)), keep_sem=dma((2,)), trade_ss=dma((4,)), trade_rs=dma((4,)),
        first_ss=dma((5, 4)), first_rs=dma((5, 4)), load_sem=dma((5, 4)),
        z_ss=dma((5, 3)), z_rs=dma((5, 5)), last_ss=dma((5,)), last_rs=dma((5,)),
        swap_ss=dma((4,)), swap_rs=dma((4,)), vec_ss=dma((16,)), vec_rs=dma((16,)),
        pass_ss=dma((2,)), pass_rs=dma((2,)),
    )
    names = tuple(operands) + tuple(results) + tuple(scratch)
    found = pl.pallas_call(
        functools.partial(backward_kernel, names, tuple(given)),
        out_shape=list(results.values()),
        in_specs=hbm(len(given)) + vmem(len(near)),
        out_specs=vmem(8) + hbm(2),
        scratch_shapes=list(scratch.values()),
        compiler_params=params(3, 64_000_000),
        name="backward",
    )(*operands.values())
    return types.SimpleNamespace(**dict(zip(results, found, strict=True)))


def per_device_direct(
    tokens, cotangent, time_table, timesteps, routes, w_ada, w_qkv, w_proj,
    w_route, w_shared_up, w_shared_down, e_up, e_down,
):
    row_count, model_width = tokens.shape
    core = lax.axis_index(NARROW)
    core_count = lax.axis_size(NARROW)
    wide_count = lax.axis_size(WIDE)
    heads_here = HEADS // core_count
    head_dim = model_width // HEADS
    head_width = heads_here * head_dim
    half = model_width // 2
    scale_factor = head_dim ** (-0.5)
    wide_place = lax.axis_index(WIDE)
    upper = wide_place % 2 == 1
    ada_rows = w_ada.shape[0]

    table = lax.dynamic_slice_in_dim(time_table, wide_place * ada_rows, ada_rows, 1)
    table = jnp.pad(table, ((0, -table.shape[0] % 128), (0, 0)))
    (
        mod, cond_own, qkv_full, proj_full, route_full, activated, probs_full, mixed_low,
        attn_out, attn_low, mlp_low, grad_shared, gate_lanes,
        up_full, down_full, up_other, down_other, expert_in, grad_expert_out,
    ) = forward(
        timesteps,
        table,
        jnp.transpose(w_ada, (1, 0, 2)),
        jnp.transpose(w_qkv, (1, 0, 2)),
        w_proj,
        w_route.T,
        w_shared_up,
        w_shared_down,
        e_up,
        e_down,
        tokens,
        cotangent,
        routes.T,
    )
    got = backward(
        dict(
            ein=expert_in, eg=grad_expert_out, eup=e_up, upo=up_other, edn=e_down, dno=down_other,
            mlp=mlp_low, gsh=grad_shared, up=up_full, down=down_full,
            attn=attn_out, attnlow=attn_low, act=activated,
            probs=probs_full, mixed=mixed_low, qkvw=qkv_full, projw=proj_full, routew=route_full,
        ),
        dict(tok=tokens, cot=cotangent, mod=mod, cond=cond_own, routes=routes.T, gates=gate_lanes),
    )
    return (
        got.out_o,
        got.tokens_o,
        jnp.transpose(got.ada_o, (1, 0, 2)),
        jnp.transpose(got.qkv_o, (1, 0, 2)),
        got.proj_o,
        got.route_o.T,
        got.up_o,
        got.down_o,
        got.eup_o,
        got.edown_o,
    )


def solution(mesh):
    placed = (
        P(WIDE, None),
        P(WIDE, None),
        P(),
        P(WIDE),
        P(WIDE, None),
        P(WIDE, None, None),
        P(WIDE, None, NARROW),
        P(WIDE, NARROW),
        P(WIDE, None),
        P(WIDE, NARROW),
        P(WIDE, NARROW),
        P(WIDE, NARROW),
        P(WIDE, NARROW),
    )
    direct = mesh.shape[WIDE] == 16 and mesh.shape[NARROW] == 2
    return jax.shard_map(
        per_device_direct if direct else per_device,
        mesh=mesh,
        in_specs=placed,
        out_specs=(
            P(WIDE, None),
            P(WIDE, None),
            P(WIDE, None, None),
            P(WIDE, None, NARROW),
            P(WIDE, NARROW),
            P(WIDE, None),
            P(WIDE, NARROW),
            P(WIDE, NARROW),
            P(WIDE, NARROW),
            P(WIDE, NARROW),
        ),
        check_vma=False,
    )
```
